32 devices in a mesh: dp: 8 (over y, x, core), tensor: 4 (over z).
Axes of the slice: x: 2, y: 2, z: 4, core: 2. Of those that a mesh axis runs over, the one named last changes fastest.
Arguments:
- tokens: bfloat16 [18432, 768], P(('dp', 'tensor')), may hold values from -6 to 6
- segment_ids: int32 [8, 2304], P('dp'), may hold values from 0 to 7, never falling along the last dimension, each value on 1 to 1152 neighbouring positions
- ln1_gain: float32 [768], replicated, may hold values from 0.5 to 1.5
- ln1_bias: float32 [768], replicated, may hold values from -3 to 3
- qkv_weight: bfloat16 [3, 768, 768], P(None, None, 'tensor'), may hold values from -0.21875 to 0.21875
- qv_bias: float32 [2, 768], P(None, 'tensor'), may hold values from -3 to 3
- proj_weight: bfloat16 [768, 768], P('tensor'), may hold values from -0.875 to 0.875
- proj_bias: float32 [768], replicated, may hold values from -1.75 to 1.75
- scale_one: float32 [768], replicated, may hold values from 0.3 to 1.5
- ln2_gain: float32 [768], replicated, may hold values from 0.5 to 1.5
- ln2_bias: float32 [768], replicated, may hold values from -3 to 3
- fc1_weight: bfloat16 [768, 3072], P(None, 'tensor'), may hold values from -0.21875 to 0.21875
- fc1_bias: float32 [3072], P('tensor'), may hold values from -3 to 3
- fc2_weight: bfloat16 [3072, 768], P('tensor'), may hold values from -0.15625 to 0.15625
- fc2_bias: float32 [768], replicated, may hold values from -1.75 to 1.75
- scale_two: float32 [768], replicated, may hold values from 0.3 to 1.5
- cotangent: bfloat16 [18432, 768], P(('dp', 'tensor')), may hold values from -6 to 6
Outputs:
- block_out: bfloat16 [18432, 768], P(('dp', 'tensor'))
- grad_tokens: float32 [18432, 768], P(('dp', 'tensor'))
- grad_ln1_gain: float32 [768], replicated
- grad_ln1_bias: float32 [768], replicated
- grad_qkv_weight: float32 [3, 768, 768], P(None, None, 'tensor')
- grad_qv_bias: float32 [2, 768], P(None, 'tensor')
- grad_proj_weight: float32 [768, 768], P('tensor')
- grad_proj_bias: float32 [768], replicated
- grad_scale_one: float32 [768], replicated
- grad_ln2_gain: float32 [768], replicated
- grad_ln2_bias: float32 [768], replicated
- grad_fc1_weight: float32 [768, 3072], P(None, 'tensor')
- grad_fc1_bias: float32 [3072], P('tensor')
- grad_fc2_weight: float32 [3072, 768], P('tensor')
- grad_fc2_bias: float32 [768], replicated
- grad_scale_two: float32 [768], replicated
The draws below stay inside these ranges and needn't reach their ends.
Inputs may be any that keep to these rules, and one draw needn't show every extreme that they name: `segment_ids`: within a sequence the ids never fall; every segment holds at most 1152 tokens, and some segment holds exactly 1152.
All inputs are finite; a program needn't handle non-finite values.
Results may differ from the reference program's by a relative error of at most 0.015.
Values may be sent and summed in bfloat16 or wider, within the bound.
A program may use at most 128 MiB of HBM per device.

```python
import math
import jax
import jax.numpy as jnp
import numpy as np
from jax import lax

D = 768
HEADS = 12
HEAD_DIM = 64
FF = 3072
SEQ = 2304
IMAGES = 8
MOST_IMG = 1152
TOKENS = 18432
N_DP = 8


def block_levels(own_key, shape, cuts, low, largest):
    level = 1.0
    for axis_at, parts in cuts:
        draws = jax.random.uniform(jax.random.fold_in(jax.random.fold_in(own_key, 6), axis_at), (parts,), jnp.float32, low / len(cuts), largest / len(cuts))
        level = level * jnp.repeat(jnp.exp(draws), shape[axis_at] // parts).reshape((-1,) + (1,) * (len(shape) - 1 - axis_at))
    return level


def profile(amount, total, reach, slope):
    weights = [(1 << 20) // math.isqrt(rank ** slope) + 1 for rank in range(2, amount + 1)]
    spare, given = total - reach - (amount - 1), [1] * (amount - 1)
    while spare > 0:
        movable = [i for i in range(amount - 1) if given[i] < reach]
        pool, remaining = sum([weights[i] for i in movable]), spare
        for i in movable:
            more = min(reach - given[i], max(1, remaining * weights[i] // pool), spare)
            given[i] = given[i] + more
            spare = spare - more
    return np.array([reach] + given)


def uneven_parts(own_key, amount, total, most, slope):
    if amount == 2:
        one = jax.random.randint(own_key, (), max(1, total - most), min(most, total - 1) + 1)
        return jnp.stack([one, total - one])
    lengths = jnp.asarray(profile(amount, total, most, slope), jnp.int32)
    couples = (amount - 1) // 2
    giver, taker = lengths[1:1 + 2 * couples:2], lengths[2:2 + 2 * couples:2]
    slack = jnp.minimum(giver - 1, most - taker)
    moved = jax.random.randint(jax.random.fold_in(own_key, 1), (couples,), 0, 1 << 20) % (slack + 1)
    lengths = lengths.at[1:1 + 2 * couples:2].set(giver - moved).at[2:2 + 2 * couples:2].set(taker + moved)
    return lengths[jax.random.permutation(jax.random.fold_in(own_key, 2), amount)]


def gaussian(rng, shape, scale, most, split=(), dtype=jnp.bfloat16):
    entries = scale * jax.random.normal(rng, shape, jnp.float32)
    if split:
        entries = entries * block_levels(rng, shape, split, -0.22, 0.18)
    return jnp.clip(entries, -most, most).astype(dtype)


def setup_inputs(seed: int = 0) -> dict:
    splits = jax.random.split(jax.random.key(seed), 18)
    tokens = gaussian(splits[0], (TOKENS, D), 1.0, 6.0, ((0, 32),))
    segment_ids = jax.vmap(lambda own: jnp.searchsorted(jnp.cumsum(uneven_parts(own, IMAGES, SEQ, MOST_IMG, 2)), jnp.arange(SEQ), side="right"))(jax.random.split(splits[1], N_DP)).reshape((N_DP, SEQ)).astype(jnp.int32)
    ln1_gain = jnp.clip(1.0 + 0.1 * jax.random.normal(splits[2], (D,), jnp.float32), 0.5, 1.5)
    ln1_bias = gaussian(splits[3], (D,), 0.5, 3.0, (), jnp.float32)
    qkv_weight = gaussian(splits[4], (3, D, D), D ** -0.5, 0.21875, ((2, 4),))
    qv_bias = gaussian(splits[5], (2, D), 0.5, 3.0, ((1, 4),), jnp.float32)
    proj_weight = gaussian(splits[6], (D, D), (D // 16) ** -0.5, 0.875, ((0, 4),))
    proj_bias = gaussian(splits[7], (D,), 0.3, 1.75, (), jnp.float32)
    scale_one = jnp.clip(jnp.exp(jax.random.uniform(splits[8], (D,), jnp.float32, math.log(0.3), math.log(1.5))), 0.3, 1.5)
    ln2_gain = jnp.clip(1.0 + 0.1 * jax.random.normal(splits[9], (D,), jnp.float32), 0.5, 1.5)
    ln2_bias = gaussian(splits[10], (D,), 0.5, 3.0, (), jnp.float32)
    fc1_weight = gaussian(splits[11], (D, FF), D ** -0.5, 0.21875, ((1, 4),))
    fc1_bias = gaussian(splits[12], (FF,), 0.5, 3.0, ((0, 4),), jnp.float32)
    fc2_weight = gaussian(splits[13], (FF, D), (FF // 2) ** -0.5, 0.15625, ((0, 4),))
    fc2_bias = gaussian(splits[14], (D,), 0.3, 1.75, (), jnp.float32)
    scale_two = jnp.clip(jnp.exp(jax.random.uniform(splits[15], (D,), jnp.float32, math.log(0.3), math.log(1.5))), 0.3, 1.5)
    cotangent = gaussian(splits[16], (TOKENS, D), 1.0, 6.0, ((0, 32),))
    return dict(tokens=tokens, segment_ids=segment_ids, ln1_gain=ln1_gain, ln1_bias=ln1_bias, qkv_weight=qkv_weight, qv_bias=qv_bias, proj_weight=proj_weight, proj_bias=proj_bias, scale_one=scale_one, ln2_gain=ln2_gain, ln2_bias=ln2_bias, fc1_weight=fc1_weight, fc1_bias=fc1_bias, fc2_weight=fc2_weight, fc2_bias=fc2_bias, scale_two=scale_two, cotangent=cotangent)


eps_norm = 1e-06
precise = lax.Precision.HIGHEST

@jax.custom_vjp
def low(v):
    return lax.optimization_barrier(v.astype(jnp.bfloat16)).astype(jnp.float32)

@jax.custom_vjp
def low_back(v):
    return v

def low_keep(v):
    return (low(v), None)

def low_pass(kept, grad):
    return (grad,)

def back_keep(v):
    return (v, None)

def back_low(kept, grad):
    return (low(grad),)
low.defvjp(low_keep, low_pass)
low_back.defvjp(back_keep, back_low)

def layer_norm(rows_in, gain, shift):
    row_mean = lax.optimization_barrier(jnp.mean(rows_in, axis=-1, keepdims=True))
    centred = rows_in - row_mean
    spread = lax.optimization_barrier(jnp.mean(centred * centred, axis=-1, keepdims=True))
    return centred * lax.rsqrt(spread + eps_norm) * gain + shift

def attention(queries, key_rows, value_rows, image_ids):
    block_rows = 576 if SEQ % 576 == 0 else SEQ
    block_count = SEQ // block_rows
    query_blocks = queries.reshape(block_count, block_rows, HEADS, HEAD_DIM)
    id_blocks = image_ids.reshape(block_count, block_rows)
    score_scale = HEAD_DIM ** (-0.5)

    def one_block(pair):
        query_part, id_part = pair
        raw_scores = jnp.einsum('qhd,khd->hqk', query_part, key_rows, precision=precise) * score_scale
        raw_scores = low_back(raw_scores)
        same_image = id_part[:, None] == image_ids[None, :]
        masked = jnp.where(same_image[None], raw_scores, -1e+30)
        row_peak = lax.optimization_barrier(jnp.max(masked, axis=-1, keepdims=True))
        weights = jnp.exp(masked - row_peak)
        softmax = weights / lax.optimization_barrier(jnp.sum(weights, axis=-1, keepdims=True))
        return jnp.einsum('hqk,khd->qhd', low(softmax), value_rows, precision=precise)
    mixture = lax.map(jax.checkpoint(one_block), (query_blocks, id_blocks))
    return mixture.reshape(SEQ, HEADS * HEAD_DIM)

def forward(rows_in, params, image_ids):
    ln1_gain, ln1_bias, qkv_weight, qv_bias, proj_weight, proj_bias, scale_one, ln2_gain, ln2_bias, fc1_weight, fc1_bias, fc2_weight, fc2_bias, scale_two = params
    normed1 = low(layer_norm(rows_in, ln1_gain, ln1_bias))
    queries = low(low_back(jnp.dot(normed1, qkv_weight[0], precision=precise, preferred_element_type=jnp.float32) + qv_bias[0]))
    key_rows = low(low_back(jnp.dot(normed1, qkv_weight[1], precision=precise, preferred_element_type=jnp.float32)))
    value_rows = low(low_back(jnp.dot(normed1, qkv_weight[2], precision=precise, preferred_element_type=jnp.float32) + qv_bias[1]))
    attended = attention(queries.reshape(SEQ, HEADS, HEAD_DIM), key_rows.reshape(SEQ, HEADS, HEAD_DIM), value_rows.reshape(SEQ, HEADS, HEAD_DIM), image_ids)
    attended = low(low_back(attended))
    branch = low_back(jnp.dot(attended, proj_weight, precision=precise, preferred_element_type=jnp.float32) + proj_bias)
    hidden = rows_in + scale_one * branch
    normed2 = low(layer_norm(hidden, ln2_gain, ln2_bias))
    pre_act = low_back(jnp.dot(normed2, fc1_weight, precision=precise, preferred_element_type=jnp.float32) + fc1_bias)
    active = low(jax.nn.gelu(pre_act, approximate=False))
    mlp_out = low_back(jnp.dot(active, fc2_weight, precision=precise, preferred_element_type=jnp.float32) + fc2_bias)
    return hidden + scale_two * mlp_out

def reference(tokens, segment_ids, ln1_gain, ln1_bias, qkv_weight, qv_bias, proj_weight, proj_bias, scale_one, ln2_gain, ln2_bias, fc1_weight, fc1_bias, fc2_weight, fc2_bias, scale_two, cotangent):
    params = (ln1_gain.astype(jnp.float32), ln1_bias.astype(jnp.float32), qkv_weight.astype(jnp.float32), qv_bias.astype(jnp.float32), proj_weight.astype(jnp.float32), proj_bias.astype(jnp.float32), scale_one.astype(jnp.float32), ln2_gain.astype(jnp.float32), ln2_bias.astype(jnp.float32), fc1_weight.astype(jnp.float32), fc1_bias.astype(jnp.float32), fc2_weight.astype(jnp.float32), fc2_bias.astype(jnp.float32), scale_two.astype(jnp.float32))
    token_rows = tokens.astype(jnp.float32).reshape(N_DP, SEQ, D)
    cot_rows = cotangent.astype(jnp.float32).reshape(N_DP, SEQ, D)

    def one_sequence(totals, block_item):
        rows_in, image_ids, cot_in = block_item

        def run_layer(inputs, weights):
            return forward(inputs, weights, image_ids)
        result, pullback = jax.vjp(run_layer, rows_in, params)
        grad_rows, grad_params = pullback(cot_in)
        return (jax.tree.map(jnp.add, totals, grad_params), (result, grad_rows))
    start_totals = jax.tree.map(jnp.zeros_like, params)
    totals, (results, grad_rows) = lax.scan(one_sequence, start_totals, (token_rows, segment_ids, cot_rows))
    return (results.reshape(TOKENS, D).astype(jnp.bfloat16), grad_rows.reshape(TOKENS, D), totals[0], totals[1], totals[2], totals[3], totals[4], totals[5], totals[6], totals[7], totals[8], totals[9], totals[10], totals[11], totals[12], totals[13])
```

```python
from functools import partial
import jax, jax.numpy as jnp
from jax import lax
from jax.experimental import pallas as pl
from jax.experimental.pallas import tpu as pltpu

from jax.sharding import PartitionSpec as P

HEAD_DIM = 64
LANES = 128
MASKED = -(2.0**100)


def split_three(value):
    high = value.astype(jnp.bfloat16)
    rest = value - high.astype(jnp.float32)
    middle = rest.astype(jnp.bfloat16)
    low = (rest - middle.astype(jnp.float32)).astype(jnp.bfloat16)
    return (high, middle, low)


def join_heads(parts, low_half):
    tiles = []
    for at in range(0, len(parts), 2):
        if at + 1 < len(parts):
            tiles.append(jnp.where(low_half, parts[at], pltpu.roll(parts[at + 1], HEAD_DIM, 1)))
        else:
            tiles.append(parts[at])
    return tiles


def attend_kernel(key_block, bounds_ref, q_ref, k_ref, v_ref, out_ref, q_back_ref, peak_ref, acc_ref):
    step = pl.program_id(0)
    heads, count, _ = q_ref.shape
    peak_ref[...] = jnp.full_like(peak_ref, -3e38)
    acc_ref[...] = jnp.zeros_like(acc_ref)

    def visit(at, carry):
        keys = pl.ds(pl.multiple_of(at * key_block, key_block), key_block)
        for head in range(heads):
            scores = lax.dot_general(
                q_ref[head],
                k_ref[head, keys, :],
                (((1,), (1,)), ((), ())),
                preferred_element_type=jnp.float32,
            )
            old_peak = peak_ref[head]
            new_peak = jnp.maximum(old_peak, jnp.max(scores, axis=1, keepdims=True))
            weights = jnp.exp(scores - new_peak[:, :1]).astype(jnp.bfloat16)
            mixed = jnp.dot(weights, v_ref[head, keys, :], preferred_element_type=jnp.float32)
            acc_ref[head] = acc_ref[head] * jnp.exp(old_peak - new_peak) + mixed
            peak_ref[head] = new_peak
        return carry

    lax.fori_loop(bounds_ref[0, step], bounds_ref[1, step], visit, 0)
    lane = lax.broadcasted_iota(jnp.int32, (count, LANES), 1)
    low_half = lane < HEAD_DIM
    parts = []
    for head in range(heads):
        acc = acc_ref[head]
        total = acc[:, HEAD_DIM : HEAD_DIM + 1]
        parts.append(acc / total)
        log_total = -(peak_ref[head] + jnp.log(total))
        high, middle, low = split_three(log_total)
        kept = q_ref[head].astype(jnp.float32)
        kept = jnp.where(lane == HEAD_DIM + 8, high.astype(jnp.float32), kept)
        kept = jnp.where(lane == HEAD_DIM + 9, middle.astype(jnp.float32), kept)
        kept = jnp.where(lane == HEAD_DIM + 10, low.astype(jnp.float32), kept)
        q_back_ref[head] = kept.astype(jnp.bfloat16)
    for at, tile in enumerate(join_heads(parts, low_half)):
        wide = min(LANES, heads * HEAD_DIM - at * LANES)
        out_ref[:, at * LANES : at * LANES + wide] = tile[:, :wide].astype(jnp.bfloat16)


def attend(bounds, queries, keys, values, key_block):
    heads, seq_len, _ = queries.shape
    steps = bounds.shape[1]
    block = seq_len // steps
    q_spec = pl.BlockSpec((heads, block, LANES), lambda i, b: (0, i, 0))
    full = pl.BlockSpec((heads, seq_len, LANES), lambda i, b: (0, 0, 0))
    return pl.pallas_call(
        partial(attend_kernel, key_block),
        grid_spec=pltpu.PrefetchScalarGridSpec(
            num_scalar_prefetch=1,
            grid=(steps,),
            in_specs=[q_spec, full, full],
            out_specs=[pl.BlockSpec((block, heads * HEAD_DIM), lambda i, b: (i, 0)), q_spec],
            scratch_shapes=[
                pltpu.VMEM((heads, block, LANES), jnp.float32),
                pltpu.VMEM((heads, block, LANES), jnp.float32),
            ],
        ),
        out_shape=[
            jax.ShapeDtypeStruct((seq_len, heads * HEAD_DIM), jnp.bfloat16),
            jax.ShapeDtypeStruct((heads, seq_len, LANES), jnp.bfloat16),
        ],
        name="attend",
        cost_estimate=pl.CostEstimate(
            flops=4 * heads * seq_len * seq_len * LANES // 2, transcendentals=heads * seq_len * seq_len // 2,
            bytes_accessed=8 * heads * seq_len * LANES,
        ),
    )(bounds, queries, keys, values)


def attend_back_kernel(
    query_block, bounds_ref, q_ref, k_ref, v_ref, mixed_ref, grad_ref, out_ref, grad_heads_ref, dq_ref, dk_ref, dv_ref, k0_ref
):
    step = pl.program_id(0)
    heads, count, _ = k_ref.shape
    seq_len = q_ref.shape[1]
    blocks = seq_len // query_block

    @pl.when(step == 0)
    def _():
        dq_ref[...] = jnp.zeros_like(dq_ref)

        def prepare(at, carry):
            rows = pl.ds(pl.multiple_of(at * query_block, query_block), query_block)
            lane = lax.broadcasted_iota(jnp.int32, (query_block, LANES), 1)
            for head in range(heads):
                first = (head // 2) * LANES
                wide = min(LANES, heads * HEAD_DIM - first)
                grad = grad_ref[rows, first : first + wide].astype(jnp.float32)
                mixed = mixed_ref[rows, first : first + wide].astype(jnp.float32)
                if wide < LANES:
                    blank = jnp.zeros((query_block, LANES - wide), jnp.float32)
                    grad = jnp.concatenate([grad, blank], axis=1)
                    mixed = jnp.concatenate([mixed, blank], axis=1)
                if head % 2:
                    grad = pltpu.roll(grad, HEAD_DIM, 1)
                    mixed = pltpu.roll(mixed, HEAD_DIM, 1)
                inside = lane < HEAD_DIM
                shared = -jnp.sum(jnp.where(inside, grad * mixed, 0.0), axis=1, keepdims=True)
                high, middle, low = split_three(shared)
                grad = jnp.where(inside, grad, 0.0)
                grad = jnp.where(lane == HEAD_DIM, high.astype(jnp.float32), grad)
                grad = jnp.where(lane == HEAD_DIM + 1, middle.astype(jnp.float32), grad)
                grad = jnp.where(lane == HEAD_DIM + 2, low.astype(jnp.float32), grad)
                grad_heads_ref[head, rows, :] = grad.astype(jnp.bfloat16)
            return carry

        lax.fori_loop(0, blocks, prepare, 0)

    dk_ref[...] = jnp.zeros_like(dk_ref)
    dv_ref[...] = jnp.zeros_like(dv_ref)

    def visit(at, carry):
        rows = pl.ds(pl.multiple_of(at * query_block, query_block), query_block)
        for head in range(heads):
            queries = q_ref[head, rows, :]
            grads = grad_heads_ref[head, rows, :]
            keys = k_ref[head]
            contract = (((1,), (1,)), ((), ()))
            scores = lax.dot_general(keys, queries, contract, preferred_element_type=jnp.float32)
            probs = jnp.exp(scores)
            grad_probs = lax.dot_general(
                v_ref[head], grads, contract, preferred_element_type=jnp.float32
            )
            grad_scores = (probs * grad_probs).astype(jnp.bfloat16)
            dv_ref[head] += jnp.dot(
                probs.astype(jnp.bfloat16), grads, preferred_element_type=jnp.float32
            )
            dk_ref[head] += jnp.dot(grad_scores, queries, preferred_element_type=jnp.float32)
            dq_ref[head, rows, :] += lax.dot_general(
                grad_scores, keys, (((0,), (0,)), ((), ())), preferred_element_type=jnp.float32
            )
        return carry

    lax.fori_loop(bounds_ref[0, step], bounds_ref[1, step], visit, 0)
    lane = lax.broadcasted_iota(jnp.int32, (count, LANES), 1)
    low_half = lane < HEAD_DIM
    here = pl.ds(pl.multiple_of(step * count, count), count)
    k0_ref[here, :] = dk_ref[0]
    out_ref[here, 256:384] = jnp.where(
        low_half, dk_ref[1], pltpu.roll(dk_ref[2], HEAD_DIM, 1)
    ).astype(jnp.bfloat16)
    out_ref[here, 384:512] = jnp.where(
        low_half, dv_ref[0], pltpu.roll(dv_ref[1], HEAD_DIM, 1)
    ).astype(jnp.bfloat16)
    out_ref[here, 512:576] = dv_ref[2][:, :HEAD_DIM].astype(jnp.bfloat16)

    @pl.when(step == pl.num_programs(0) - 1)
    def _():
        def finish(at, carry):
            rows = pl.ds(pl.multiple_of(at * query_block, query_block), query_block)
            lane = lax.broadcasted_iota(jnp.int32, (query_block, LANES), 1)
            low_half = lane < HEAD_DIM
            scale = HEAD_DIM**-0.5
            out_ref[rows, 0:128] = (
                jnp.where(low_half, dq_ref[0, rows, :], pltpu.roll(dq_ref[1, rows, :], HEAD_DIM, 1))
                * scale
            ).astype(jnp.bfloat16)
            out_ref[rows, 128:256] = jnp.where(
                low_half, dq_ref[2, rows, :] * scale, pltpu.roll(k0_ref[rows, :], HEAD_DIM, 1)
            ).astype(jnp.bfloat16)
            return carry

        lax.fori_loop(0, blocks, finish, 0)


def attend_back(bounds, queries, keys, values, mixed, grads, query_block):
    heads, seq_len, _ = queries.shape
    steps = bounds.shape[1]
    block = seq_len // steps
    k_spec = pl.BlockSpec((heads, block, LANES), lambda i, b: (0, i, 0))
    full = pl.BlockSpec((heads, seq_len, LANES), lambda i, b: (0, 0, 0))
    flat = pl.BlockSpec((seq_len, heads * HEAD_DIM), lambda i, b: (0, 0))
    return pl.pallas_call(
        partial(attend_back_kernel, query_block),
        grid_spec=pltpu.PrefetchScalarGridSpec(
            num_scalar_prefetch=1,
            grid=(steps,),
            in_specs=[full, k_spec, k_spec, flat, flat],
            out_specs=pl.BlockSpec((seq_len, 3 * heads * HEAD_DIM), lambda i, b: (0, 0)),
            scratch_shapes=[
                pltpu.VMEM((heads, seq_len, LANES), jnp.bfloat16),
                pltpu.VMEM((heads, seq_len, LANES), jnp.float32),
                pltpu.VMEM((heads, block, LANES), jnp.float32),
                pltpu.VMEM((heads, block, LANES), jnp.float32),
                pltpu.VMEM((seq_len, LANES), jnp.float32),
            ],
        ),
        out_shape=jax.ShapeDtypeStruct((seq_len, 3 * heads * HEAD_DIM), jnp.bfloat16),
        name="attend_back",
        cost_estimate=pl.CostEstimate(
            flops=10 * heads * seq_len * seq_len * LANES // 2, transcendentals=heads * seq_len * seq_len // 2,
            bytes_accessed=12 * heads * seq_len * LANES,
        ),
    )(bounds, queries, keys, values, mixed, grads)


def visit_bounds(ids, steps, block):
    seq_len = ids.shape[0]
    count = seq_len // steps
    first = ids[::count][:steps]
    last = ids[count - 1 :: count]
    start = jnp.sum(ids[None, :] < first[:, None], axis=1, dtype=jnp.int32)
    end = jnp.sum(ids[None, :] <= last[:, None], axis=1, dtype=jnp.int32)
    return jnp.stack([start // block, (end + block - 1) // block])


MESH = pl.DeviceIdType.MESH
PIECES = 8
PIECE_BITS = 3


def contract_rows(left, right):
    return lax.dot_general(left, right, (((0,), (0,)), ((), ())), preferred_element_type=jnp.float32)


def times_transposed(left, right, precision=None):
    return lax.dot_general(
        left, right, (((1,), (1,)), ((), ())), preferred_element_type=jnp.float32, precision=precision
    )


def rounded_sum(left, right):
    return (left.astype(jnp.float32) + right.astype(jnp.float32)).astype(jnp.bfloat16)


def bit_of(index, bit):
    return lax.rem(index // (1 << bit), 2)


def partner_of(index, bit):
    return index + (1 - 2 * bit_of(index, bit)) * (1 << bit)


def greet(dp_bits, shards):
    barrier = pltpu.get_barrier_semaphore()
    member, here = lax.axis_index("dp"), lax.axis_index("tensor")
    peers = [{"dp": partner_of(member, bit)} for bit in range(dp_bits)]
    peers += [{"tensor": lax.rem(here + shift, shards)} for shift in range(1, shards)]
    for peer in peers:
        pl.semaphore_signal(barrier, inc=1, device_id=peer, device_id_type=MESH)
    pl.semaphore_wait(barrier, len(peers))


def weight_grad_kernel(
    normed_ref, pre_ref, active_ref, mlp_ref, attended_ref, branch_ref, keep_ref, send_ref, wide_ref
):
    core = bit_of(lax.axis_index("dp"), 0)
    half = PIECES // 2
    first = 0
    for left, right in (
        (normed_ref[...], pre_ref[...]),
        (active_ref[...], mlp_ref[...]),
        (attended_ref[0], branch_ref[...]),
    ):
        product = contract_rows(left, right)
        count = product.shape[0] // PIECES
        wide_ref[: product.shape[0], :] = product
        for piece in range(half):
            for out_ref, side in ((keep_ref, core), (send_ref, 1 - core)):
                start = pl.multiple_of((side * half + piece) * count, 8)
                out_ref[piece, 0, first : first + count, :] = wide_ref[
                    pl.ds(start, count), :
                ].astype(jnp.bfloat16)
        first += count
    for piece in range(half):
        for out_ref in (keep_ref, send_ref):
            blank = out_ref.shape[2] - first
            out_ref[piece, 0, first:, :] = jnp.zeros((blank, out_ref.shape[3]), jnp.bfloat16)


def weight_grads(normed, grad_pre, active, grad_mlp, attended, grad_branch):
    shards, count, columns = attended.shape
    width = normed.shape[1]
    hidden_here = grad_pre.shape[1] // shards
    rows = -(-(2 * width + columns) // PIECES // 16) * 16
    whole = pl.BlockSpec((count, width), lambda t: (0, 0))
    part = pl.BlockSpec((count, hidden_here), lambda t: (0, t))
    out_spec = pl.BlockSpec((PIECES // 2, 1, rows, width), lambda t: (0, t, 0, 0))
    out = jax.ShapeDtypeStruct((PIECES // 2, shards, rows, width), jnp.bfloat16)
    return pl.pallas_call(
        weight_grad_kernel,
        grid=(shards,),
        in_specs=[whole, part, part, whole, pl.BlockSpec((1, count, columns), lambda t: (t, 0, 0)), whole],
        out_specs=[out_spec, out_spec],
        out_shape=[out, out],
        scratch_shapes=[pltpu.VMEM((width, width), jnp.float32)],
        name="weight_grads",
        cost_estimate=pl.CostEstimate(
            flops=2 * count * width * shards * (2 * hidden_here + columns),
            transcendentals=0,
            bytes_accessed=4 * PIECES * shards * rows * width,
        ),
    )(normed, grad_pre, active, grad_mlp, attended, grad_branch)


def finish_kernel(
    shards,
    dp_bits,
    grads_ref,
    rows_ref,
    weight_ref,
    gain_ref,
    shift_ref,
    vectors_ref,
    tokens_ref,
    hidden_ref,
    a_keep,
    a_got,
    b_keep,
    b_got,
    tokens_out,
    vectors_out,
    qkv_out,
    weights_out,
    part,
    from_left,
    from_right,
    q_wide,
    q_all,
    q_half,
    q_quarter,
    q_got_core,
    q_got_x,
    q_got_y,
    q_got_more,
    v_now,
    v_got,
    v_shards,
    a_sum,
    b_sum,
    a_second,
    b_second,
    pieces,
    pieces_more,
    z_got,
    send,
    recv,
):
    f32, bf16 = jnp.float32, jnp.bfloat16
    member, here = lax.axis_index("dp"), lax.axis_index("tensor")
    core, x_bit, y_bit = bit_of(member, 0), bit_of(member, 1), bit_of(member, 2)
    own_piece = core * 4 + x_bit * 2 + y_bit
    block = part.shape[1]
    width = part.shape[2]
    columns = grads_ref.shape[1]
    half_rows = weights_out.shape[1] // 2
    last = shards - 1
    slots = iter(range(send.shape[0]))
    pending = []

    def copy_to(src, dst, at, **peer):
        return pltpu.make_async_remote_copy(
            src_ref=src, dst_ref=dst, send_sem=send.at[at], recv_sem=recv.at[at], device_id=peer, device_id_type=MESH
        )

    def start_dp(src, dst, bit, keep=True):
        copy = copy_to(src, dst, next(slots), dp=partner_of(member, bit))
        copy.start()
        if keep:
            pending.append(copy)
        return copy

    greet(dp_bits, shards)

    def add_into(out, left, right):
        def step(at, carry):
            out[at] = rounded_sum(left[at], right[at])
            return carry

        lax.fori_loop(0, out.shape[0], step, 0)

    def sum_pairs(out, left, right):
        def step(at, carry):
            one, two = at // out.shape[1], lax.rem(at, out.shape[1])
            out[one, two] = rounded_sum(left[one, two], right[one, two])
            return carry

        lax.fori_loop(0, out.shape[0] * out.shape[1], step, 0)

    sum_pairs(a_sum, a_keep, a_got)
    sum_pairs(b_sum, b_keep, b_got)
    second_a = start_dp(a_sum.at[1 - y_bit], a_second, 2)
    second_b = start_dp(b_sum.at[1 - x_bit], b_second, 1)

    right_slots = [next(slots) for _ in range(shards)]
    left_slots = [next(slots) for _ in range(shards)]

    def to_right(owner):
        return copy_to(part.at[owner], from_left.at[owner], right_slots[owner], tensor=lax.rem(here + 1, shards))

    def to_left(owner):
        return copy_to(
            part.at[owner], from_right.at[owner], left_slots[owner], tensor=lax.rem(here + last, shards)
        )

    def add_arrived(owner, arrived):
        def step(at, carry):
            rows = pl.ds(pl.multiple_of(at * (block // 4), 16), block // 4)
            part[owner, rows, :] = rounded_sum(part[owner, rows, :], arrived[owner, rows, :])
            return carry

        lax.fori_loop(0, 4, step, 0)

    order = []
    for near in range((shards + 1) // 2):
        for owner in (last - near, near):
            if owner not in order:
                order.append(owner)
    for owner in order:
        product = times_transposed(grads_ref[owner * block : (owner + 1) * block, :], weight_ref[...])
        part[owner] = product.astype(bf16)
        if owner > 0:

            @pl.when(here == 0)
            def _():
                to_right(owner).start()

        if owner < last:

            @pl.when(here == last)
            def _():
                to_left(owner).start()

    def hop(time):
        for owner in range(shards):
            at = time - (last - owner)
            if 0 < at < owner:

                @pl.when(here == at)
                def _():
                    to_right(owner).wait_recv()
                    add_arrived(owner, from_left)
                    to_right(owner).start()

            at = last + owner - time
            if owner < at < last:

                @pl.when(here == at)
                def _():
                    to_left(owner).wait_recv()
                    add_arrived(owner, from_right)
                    to_left(owner).start()

    q_wide[...] = jnp.zeros_like(q_wide)

    def grow(at, carry):
        rows = pl.ds(pl.multiple_of(at * block, 16), block)
        q_wide[...] += contract_rows(rows_ref[rows, :], grads_ref[rows, :])
        return carry

    lax.fori_loop(0, shards, grow, 0)
    sums = jnp.dot(jnp.ones((8, grads_ref.shape[0]), bf16), grads_ref[...], preferred_element_type=f32)
    exact = lax.Precision.HIGHEST
    weight = weight_ref[...].astype(f32)
    shift_sum = times_transposed(sums, weight, exact)[0:1]
    gain_sum = times_transposed(jnp.ones((8, columns), f32), weight * q_wide[...], exact)[0:1]
    v_now[0] = vectors_ref[...]
    v_now[0, 0:1, :] = (gain_sum - shift_ref[...] * shift_sum) / gain_ref[...]
    v_now[0, 1:2, :] = shift_sum
    v_now[0, pl.ds(12 + here, 1), 0:columns] = sums[0:1]
    count = q_all.shape[1]
    for piece in range(PIECES):
        q_all[piece] = q_wide[piece * count : (piece + 1) * count, :].astype(bf16)

    def vector_stage(bit):
        return start_dp(v_now.at[bit], v_got.at[bit], bit)

    q_core = start_dp(q_all.at[pl.ds((1 - core) * 4, 4)], q_got_core, 0)
    v_copy = vector_stage(0)

    second_a.wait_recv()
    second_b.wait_recv()
    pairs = shards // 2
    for at in range(pairs):
        pieces[at] = rounded_sum(a_sum[y_bit, at], a_second[at])
        pieces[pairs + at] = rounded_sum(b_sum[x_bit, at], b_second[at])
    for bit in range(PIECE_BITS, dp_bits):
        extra = start_dp(pieces, pieces_more.at[bit - PIECE_BITS], bit, False)
        extra.wait_recv()
        extra.wait_send()
        add_into(pieces, pieces, pieces_more.at[bit - PIECE_BITS])
    z_copies = []
    for shift in range(1, shards):
        target = lax.rem(here + shift, shards)
        copy = copy_to(pieces.at[target], z_got.at[shift - 1], next(slots), tensor=target)
        copy.start()
        z_copies.append(copy)
    pending.extend(z_copies)

    q_core.wait_recv()
    for at in range(4):
        q_half[at] = rounded_sum(q_all[core * 4 + at], q_got_core[at])
    q_x = start_dp(q_half.at[pl.ds((1 - x_bit) * 2, 2)], q_got_x, 1)
    v_copy.wait_recv()
    v_now[1] = v_now[0] + v_got[0]
    v_copy = vector_stage(1)
    if last > 1:
        hop(1)
    q_x.wait_recv()
    for at in range(2):
        q_quarter[at] = rounded_sum(q_half[x_bit * 2 + at], q_got_x[at])
    q_y = start_dp(q_quarter.at[1 - y_bit], q_got_y, 2)
    v_copy.wait_recv()
    v_now[2] = v_now[1] + v_got[1]
    v_copy = vector_stage(2)
    q_y.wait_recv()
    qkv_out[own_piece] = rounded_sum(q_quarter[y_bit], q_got_y[...])
    v_copy.wait_recv()
    v_now[3] = v_now[2] + v_got[2]
    for bit in range(PIECE_BITS, dp_bits):
        extra = start_dp(qkv_out.at[own_piece], q_got_more.at[bit - PIECE_BITS], bit, False)
        v_copy = vector_stage(bit)
        extra.wait_recv()
        extra.wait_send()
        qkv_out[own_piece] = rounded_sum(qkv_out[own_piece], q_got_more[bit - PIECE_BITS])
        v_copy.wait_recv()
        v_now[bit + 1] = v_now[bit] + v_got[bit]
    v_shards[here] = v_now[dp_bits]
    for shift in range(1, shards):
        copy = copy_to(
            v_now.at[dp_bits], v_shards.at[here], next(slots), tensor=lax.rem(here + shift, shards)
        )
        copy.start()
        pending.append(copy)
    v_waits = pending[-last:]
    q_back = start_dp(qkv_out.at[own_piece], qkv_out.at[own_piece], 2)
    q_back.wait_recv()
    q_back = start_dp(
        qkv_out.at[pl.ds(core * 4 + x_bit * 2, 2)], qkv_out.at[pl.ds(core * 4 + x_bit * 2, 2)], 1
    )
    for time in range(2, last):
        hop(time)
    q_back.wait_recv()
    q_back = start_dp(qkv_out.at[pl.ds(core * 4, 4)], qkv_out.at[pl.ds(core * 4, 4)], 0)

    for copy in z_copies:
        copy.wait_recv()
    total = pieces[here].astype(f32)
    for shift in range(1, shards):
        total = total + z_got[shift - 1].astype(f32)
    weights_out[own_piece] = total.astype(bf16)

    def own_half(low, *index):
        rows = pl.ds(0 if low else half_rows, half_rows)
        return weights_out.at[index[0], rows]

    back_a = start_dp(own_half(True, own_piece), own_half(True, own_piece), 2)
    back_b = start_dp(own_half(False, own_piece), own_half(False, own_piece), 1)
    back_a.wait_recv()
    span = pl.ds(core * 4 + x_bit * 2, 2)
    back_a = start_dp(own_half(True, span), own_half(True, span), 1)
    back_b.wait_recv()
    back_c = [
        start_dp(own_half(False, core * 4 + 2 * at + y_bit), own_half(False, core * 4 + 2 * at + y_bit), 2)
        for at in range(2)
    ]
    back_a.wait_recv()
    for copy in back_c:
        copy.wait_recv()
    span = pl.ds(core * 4, 4)
    back_core = start_dp(weights_out.at[span], weights_out.at[span], 0)

    for copy in v_waits:
        copy.wait_recv()
    vectors_sum = v_shards[0]
    for at in range(1, shards):
        vectors_sum = vectors_sum + v_shards[at]
    vectors_out[...] = vectors_sum

    for owner in range(shards):

        @pl.when(here == owner)
        def _():
            if owner > 0:
                to_right(owner).wait_recv()
                add_arrived(owner, from_left)
            if owner < last:
                to_left(owner).wait_recv()
                add_arrived(owner, from_right)

    def close(at, carry):
        rows = pl.ds(pl.multiple_of(at * (block // 4), 16), block // 4)
        tokens = tokens_ref[rows, :].astype(f32)
        centred = tokens - jnp.mean(tokens, axis=1, keepdims=True)
        inverse = lax.rsqrt(jnp.mean(centred * centred, axis=1, keepdims=True) + eps_norm)
        unit = centred * inverse
        scaled = part[here, rows, :].astype(f32) * gain_ref[...]
        inner = (
            scaled
            - jnp.mean(scaled, axis=1, keepdims=True)
            - unit * jnp.mean(scaled * unit, axis=1, keepdims=True)
        )
        tokens_out[rows, :] = hidden_ref[rows, :] + inverse * inner
        return carry

    lax.fori_loop(0, 4, close, 0)
    q_back.wait_recv()
    back_core.wait_recv()
    for copy in pending:
        copy.wait_send()
    for owner in range(shards):

        @pl.when(here < owner)
        def _():
            to_right(owner).wait_send()

        @pl.when(here > owner)
        def _():
            to_left(owner).wait_send()


def finish(shards, members, grads, rows, weight, gain, shift, vectors, tokens, grad_hidden, a_keep, a_got, b_keep, b_got):
    dp_bits = members.bit_length() - 1
    assert members == 1 << dp_bits and dp_bits >= PIECE_BITS
    f32, bf16 = jnp.float32, jnp.bfloat16
    seq_len, columns = grads.shape
    block, width = tokens.shape
    piece_rows = a_keep.shape[2]
    count = width // PIECES
    more = max(1, dp_bits - PIECE_BITS)
    copies = 16 + 2 * shards + 2 * (shards - 1) + 3 * dp_bits
    vm = pltpu.VMEM
    return pl.pallas_call(
        partial(finish_kernel, shards, dp_bits),
        in_specs=[pl.BlockSpec(memory_space=vm)] * 12,
        out_specs=[pl.BlockSpec(memory_space=vm)] * 4,
        out_shape=[
            jax.ShapeDtypeStruct((block, width), f32),
            jax.ShapeDtypeStruct(vectors.shape, f32),
            jax.ShapeDtypeStruct((PIECES, count, columns), bf16),
            jax.ShapeDtypeStruct((PIECES, piece_rows, width), bf16),
        ],
        scratch_shapes=[
            vm((shards, block, width), bf16),
            vm((shards, block, width), bf16),
            vm((shards, block, width), bf16),
            vm((width, columns), f32),
            vm((PIECES, count, columns), bf16),
            vm((4, count, columns), bf16),
            vm((2, count, columns), bf16),
            vm((4, count, columns), bf16),
            vm((2, count, columns), bf16),
            vm((count, columns), bf16),
            vm((more, count, columns), bf16),
            vm((dp_bits + 1,) + vectors.shape, f32),
            vm((dp_bits,) + vectors.shape, f32),
            vm((shards,) + vectors.shape, f32),
            vm(a_keep.shape, bf16),
            vm(b_keep.shape, bf16),
            vm(a_keep.shape[1:], bf16),
            vm(b_keep.shape[1:], bf16),
            vm((shards, piece_rows, width), bf16),
            vm((more, shards, piece_rows, width), bf16),
            vm((shards - 1, piece_rows, width), bf16),
            pltpu.SemaphoreType.DMA((copies,)),
            pltpu.SemaphoreType.DMA((copies,)),
        ],
        compiler_params=pltpu.CompilerParams(
            collective_id=1, has_side_effects=True, vmem_limit_bytes=64 * 1024 * 1024 - 2048 * 1024
        ),
        name="finish",
        cost_estimate=pl.CostEstimate(
            flops=4 * seq_len * columns * width, transcendentals=0, bytes_accessed=40 * block * width
        ),
    )(grads, rows, weight, gain, shift, vectors, tokens, grad_hidden, a_keep, a_got, b_keep, b_got)


def start_kernel(
    shards,
    dp_bits,
    tokens_ref,
    ids_ref,
    gain_ref,
    shift_ref,
    qkv_ref,
    qv_bias_ref,
    fc1_ref,
    fc2_ref,
    proj_ref,
    fc1_bias_ref,
    normed_out,
    q_out,
    k_out,
    v_out,
    weights_out,
    bias_out,
    blocks,
    q_extra,
    k_extra,
    own,
    chain,
    send,
    recv,
    local,
):
    f32, bf16 = jnp.float32, jnp.bfloat16
    member, here = lax.axis_index("dp"), lax.axis_index("tensor")
    core, x_bit, y_bit = bit_of(member, 0), bit_of(member, 1), bit_of(member, 2)
    own_piece = core * 4 + x_bit * 2 + y_bit
    block, width = tokens_ref.shape
    heads = q_out.shape[0]
    seq_len = ids_ref.shape[1]
    last = shards - 1
    slots = iter(range(send.shape[0]))
    pending = []

    def copy_to(src, dst, at, **peer):
        return pltpu.make_async_remote_copy(
            src_ref=src, dst_ref=dst, send_sem=send.at[at], recv_sem=recv.at[at], device_id=peer, device_id_type=MESH
        )

    def start_dp(src, dst, bit):
        copy = copy_to(src, dst, next(slots), dp=partner_of(member, bit))
        copy.start()
        pending.append(copy)
        return copy

    fc1_rows, fc2_rows, proj_rows = (ref.shape[0] // PIECES for ref in (fc1_ref, fc2_ref, proj_ref))
    loads = []
    for at, (ref, first, count) in enumerate(
        ((fc1_ref, 0, fc1_rows), (fc2_ref, fc1_rows, fc2_rows))
    ):
        rows = pl.ds(pl.multiple_of(own_piece * count, 16), count)
        loads.append(pltpu.make_async_copy(ref.at[rows], own.at[first : first + count], local.at[at]))
        loads[-1].start()
    used = fc1_rows + fc2_rows
    rows = pl.ds(pl.multiple_of(own_piece * proj_rows, 8), proj_rows)
    own[used : used + proj_rows, :] = proj_ref[rows, :]
    used += proj_rows
    own[used:, :] = jnp.zeros((own.shape[0] - used, width), bf16)
    greet(dp_bits, shards)
    for load in loads:
        load.wait()

    chains = {}
    for name, first, rest in (("w", own, chain), ("t", tokens_ref, blocks)):
        chains[name] = (
            first,
            rest,
            [next(slots) for _ in range(shards)],
            [next(slots) for _ in range(shards)],
        )

    def hop_copy(name, owner, rightward, from_own):
        first, rest, right_slots, left_slots = chains[name]
        src = first if from_own else rest.at[owner]
        step = 1 if rightward else last
        at = (right_slots if rightward else left_slots)[owner]
        return copy_to(src, rest.at[owner], at, tensor=lax.rem(here + step, shards))

    def send_own(name, rightward):
        for owner in range(shards):
            if owner != (last if rightward else 0):

                @pl.when(here == owner)
                def _():
                    hop_copy(name, owner, rightward, True).start()

    def hop(name, time, then=None):
        for at in range(shards):
            for rightward, owner, end in ((True, at - time, last), (False, at + time, 0)):
                if 0 <= owner <= last:

                    @pl.when(here == at)
                    def _():
                        hop_copy(name, owner, rightward, False).wait_recv()
                        if at != end:
                            hop_copy(name, owner, rightward, False).start()
                            if then is not None and owner in (0, last):
                                hop_copy(then, at, rightward, True).start()

    send_own("w", True)
    send_own("w", False)

    @pl.when(here == 0)
    def _():
        hop_copy("t", 0, True, True).start()

    @pl.when(here == last)
    def _():
        hop_copy("t", last, False, True).start()

    bias_copies = []
    bias_out[here] = fc1_bias_ref[...]
    for shift in range(1, shards):
        copy = copy_to(
            fc1_bias_ref, bias_out.at[here], next(slots), tensor=lax.rem(here + shift, shards)
        )
        copy.start()
        bias_copies.append(copy)
    pending.extend(bias_copies)

    large = -MASKED
    segments = lax.broadcasted_iota(jnp.int32, (8, seq_len), 0)
    same = jnp.where(segments == ids_ref[...], 1.0, 0.0).astype(bf16)
    select = lax.broadcasted_iota(jnp.int32, (8, LANES), 1) - HEAD_DIM == lax.broadcasted_iota(
        jnp.int32, (8, LANES), 0
    )
    matched = contract_rows(same, jnp.where(select, 1.0, 0.0).astype(bf16))
    lane = lax.broadcasted_iota(jnp.int32, (seq_len, LANES), 1)
    segment_lane = (lane >= HEAD_DIM) & (lane < HEAD_DIM + 8)
    ones_lane = (lane >= HEAD_DIM + 8) & (lane < HEAD_DIM + 11)
    q_extra[...] = jnp.where(segment_lane, (matched - 1.0) * large, 0.0).astype(bf16)
    k_extra[...] = jnp.where(ones_lane, 1.0, matched).astype(bf16)
    low_half = lax.broadcasted_iota(jnp.int32, (block, LANES), 1) < HEAD_DIM
    v_lane = lax.broadcasted_iota(jnp.int32, (block, LANES), 1)
    v_extra = jnp.where((v_lane >= HEAD_DIM) & (v_lane < HEAD_DIM + 3), 1.0, 0.0).astype(bf16)

    def project_block(source, owner):
        tokens = source.astype(f32)
        centred = tokens - jnp.mean(tokens, axis=1, keepdims=True)
        inverse = lax.rsqrt(jnp.mean(centred * centred, axis=1, keepdims=True) + eps_norm)
        normed = (centred * inverse * gain_ref[...] + shift_ref[...]).astype(bf16)
        rows = pl.ds(pl.multiple_of(owner * block, 16), block)
        normed_out[rows, :] = normed
        for which, out in ((0, q_out), (1, k_out), (2, v_out)):
            product = jnp.dot(normed, qkv_ref[which], preferred_element_type=f32)
            if which != 1:
                product = product + qv_bias_ref[which // 2 : which // 2 + 1, :]
            if which == 0:
                product = product.astype(bf16).astype(f32) * HEAD_DIM**-0.5
            extra = v_extra if which == 2 else (q_extra if which == 0 else k_extra)[rows, :]
            for head in range(heads):
                first = (head // 2) * LANES
                tile = product[:, first : first + LANES]
                if tile.shape[1] < LANES:
                    blank = jnp.zeros((block, LANES - tile.shape[1]), f32)
                    tile = jnp.concatenate([tile, blank], axis=1)
                if head % 2:
                    tile = pltpu.roll(tile, HEAD_DIM, 1)
                out[head, rows, :] = jnp.where(low_half, tile, extra.astype(f32)).astype(bf16)

    project_block(tokens_ref[...], here)
    for time in range(1, shards):
        hop("w", time, "t")

    half = shards // 2
    out_a = [weights_out.at[own_piece, 0:half]]
    stores = []
    for owner in range(shards):
        at = 2 + owner

        @pl.when(here == owner)
        def _():
            pltpu.make_async_copy(own, weights_out.at[own_piece, owner], local.at[at]).start()

        @pl.when(here != owner)
        def _():
            pltpu.make_async_copy(chain.at[owner], weights_out.at[own_piece, owner], local.at[at]).start()

        stores.append(pltpu.make_async_copy(own, weights_out.at[own_piece, owner], local.at[at]))
    for store in stores:
        store.wait()

    def part(low, pieces):
        owners = pl.ds(0, half) if low else pl.ds(half, shards - half)
        return weights_out.at[pieces, owners]

    def gather_stage(low, pieces, bit):
        return [start_dp(part(low, at), part(low, at), bit) for at in pieces]

    def wait_all(copies):
        for copy in copies:
            copy.wait_recv()

    stage = gather_stage(True, [own_piece], 2) + gather_stage(False, [own_piece], 1)

    def arrived(time):
        for way in (-1, 1):
            owner = here + way * time

            @pl.when((owner >= 0) & (owner <= last))
            def _():
                project_block(blocks[owner], owner)

    for time in range(1, shards):
        hop("t", time)
        if time == 1:
            arrived(time)
            wait_all(stage)
            stage = gather_stage(True, [pl.ds(core * 4 + x_bit * 2, 2)], 1) + gather_stage(
                False, [core * 4 + 2 * at + y_bit for at in range(2)], 2
            )
        elif time == 2:
            arrived(time)
            wait_all(stage)
            stage = [start_dp(weights_out.at[pl.ds(core * 4, 4)], weights_out.at[pl.ds(core * 4, 4)], 0)]
        else:
            arrived(time)
    wait_all(stage)
    wait_all(bias_copies)
    for copy in pending:
        copy.wait_send()
    for name in chains:
        for at in range(shards):
            for owner in range(shards):
                if owner <= at < last:

                    @pl.when(here == at)
                    def _():
                        hop_copy(name, owner, True, False).wait_send()

                if owner >= at > 0:

                    @pl.when(here == at)
                    def _():
                        hop_copy(name, owner, False, False).wait_send()


def start(shards, members, tokens, ids, gain, shift, qkv, qv_bias, fc1, fc2, proj, fc1_bias):
    dp_bits = members.bit_length() - 1
    assert members == 1 << dp_bits and dp_bits >= PIECE_BITS and shards >= 3
    f32, bf16 = jnp.float32, jnp.bfloat16
    block, width = tokens.shape
    seq_len = block * shards
    heads = qkv.shape[2] // HEAD_DIM
    rows = -(-(fc1.shape[0] + fc2.shape[0] + proj.shape[0]) // PIECES // 16) * 16
    copies = 4 * shards + (shards - 1) + 6
    vm = pltpu.VMEM
    on_chip = pl.BlockSpec(memory_space=vm)
    anywhere = pl.BlockSpec(memory_space=pl.ANY)
    head_rows = jax.ShapeDtypeStruct((heads, seq_len, LANES), bf16)
    return pl.pallas_call(
        partial(start_kernel, shards, dp_bits),
        in_specs=[on_chip] * 6 + [anywhere] * 2 + [on_chip] * 2,
        out_specs=[on_chip] * 4 + [anywhere, on_chip],
        out_shape=[
            jax.ShapeDtypeStruct((seq_len, width), bf16),
            head_rows,
            head_rows,
            head_rows,
            jax.ShapeDtypeStruct((PIECES, shards, rows, width), bf16),
            jax.ShapeDtypeStruct((shards,) + fc1_bias.shape, f32),
        ],
        scratch_shapes=[
            vm((shards, block, width), bf16),
            vm((seq_len, LANES), bf16),
            vm((seq_len, LANES), bf16),
            vm((rows, width), bf16),
            vm((shards, rows, width), bf16),
            pltpu.SemaphoreType.DMA((copies,)),
            pltpu.SemaphoreType.DMA((copies,)),
            pltpu.SemaphoreType.DMA((2 + shards,)),
        ],
        compiler_params=pltpu.CompilerParams(collective_id=0, has_side_effects=True),
        name="start",
        cost_estimate=pl.CostEstimate(
            flops=6 * seq_len * width * heads * HEAD_DIM, transcendentals=0, bytes_accessed=40 * block * width
        ),
    )(tokens, ids, gain, shift, qkv, qv_bias, fc1, fc2, proj, fc1_bias)


eps_norm = 1e-06


def normalize(rows_in, gain, shift):
    row_mean = jnp.mean(rows_in, axis=1, keepdims=True)
    centred = rows_in - row_mean
    inverse = lax.rsqrt(jnp.mean(centred * centred, axis=1, keepdims=True) + eps_norm)
    unit_rows = centred * inverse
    return (unit_rows * gain + shift, unit_rows, inverse)


def normalize_back(grad_rows, unit_rows, inverse, gain):
    scaled = grad_rows * gain
    inner = (
        scaled
        - jnp.mean(scaled, axis=1, keepdims=True)
        - unit_rows * jnp.mean(scaled * unit_rows, axis=1, keepdims=True)
    )
    return (inverse * inner, jnp.sum(grad_rows * unit_rows, axis=0), jnp.sum(grad_rows, axis=0))


def exchange(blocks, count):
    here = lax.axis_index("tensor")
    result = blocks
    for shift in range(1, count):
        target = lax.rem(here + shift, count)
        source = lax.rem(here + count - shift, count)
        piece = lax.dynamic_index_in_dim(blocks, target, 0, keepdims=False)
        got = lax.ppermute(piece, "tensor", [(j, (j + shift) % count) for j in range(count)])
        result = lax.dynamic_update_index_in_dim(result, got, source, 0)
    return result


def on_device(
    shards,
    members,
    tokens,
    segment_ids,
    ln1_gain,
    ln1_bias,
    qkv_weight,
    qv_bias,
    proj_weight,
    proj_bias,
    scale_one,
    ln2_gain,
    ln2_bias,
    fc1_weight,
    fc1_bias,
    fc2_weight,
    fc2_bias,
    scale_two,
    cotangent,
):
    f32, bf16 = jnp.float32, jnp.bfloat16
    seq_len = segment_ids.shape[1]
    rows_here, width = tokens.shape
    head_columns = qkv_weight.shape[2]
    heads = head_columns // HEAD_DIM
    hidden_here = fc1_weight.shape[1]
    ids = segment_ids[0]
    here = lax.axis_index("tensor")

    inputs = tokens.astype(f32)
    full_one, queries, keys, values, gathered, fc1_bias_full = start(
        shards,
        members,
        tokens,
        segment_ids,
        ln1_gain[None],
        ln1_bias[None],
        qkv_weight,
        qv_bias,
        fc1_weight,
        fc2_weight,
        proj_weight,
        fc1_bias[None],
    )
    fc_rows, proj_count = width // PIECES, head_columns // PIECES
    fc1_full = gathered[:, :, :fc_rows].transpose(1, 0, 2, 3).reshape(shards, width, hidden_here)
    fc2_rows = (
        gathered[:, :, fc_rows : 2 * fc_rows]
        .transpose(1, 0, 2, 3)
        .reshape(shards * hidden_here, width)
    )
    proj_rows = (
        gathered[:, :, 2 * fc_rows : 2 * fc_rows + proj_count]
        .transpose(1, 0, 2, 3)
        .reshape(shards * head_columns, width)
    )
    fc1_full = fc1_full.transpose(1, 0, 2).reshape(width, shards * hidden_here)
    fc1_bias_full = fc1_bias_full.reshape(shards * hidden_here)
    bounds = visit_bounds(ids, 8, seq_len // 9)
    mixed, queries_back = attend(bounds, queries, keys, values, seq_len // 9)

    attended_blocks = exchange(mixed.reshape(shards, rows_here, head_columns), shards)
    attended = attended_blocks.transpose(1, 0, 2).reshape(rows_here, shards * head_columns)
    branch = jnp.dot(attended, proj_rows, preferred_element_type=f32) + proj_bias
    hidden = inputs + scale_one * branch
    normed2, unit_two, inverse_two = normalize(hidden, ln2_gain, ln2_bias)
    normed2 = normed2.astype(bf16)
    pre_act = (
        jnp.dot(normed2, fc1_full, preferred_element_type=f32) + fc1_bias_full
    )
    active = jax.nn.gelu(pre_act, approximate=False).astype(bf16)
    mlp_out = jnp.dot(active, fc2_rows, preferred_element_type=f32) + fc2_bias
    block_out = (hidden + scale_two * mlp_out).astype(bf16)
    grad_out = cotangent.astype(f32)
    grad_scale_two = jnp.sum(grad_out * mlp_out, axis=0)
    grad_mlp = (grad_out * scale_two).astype(bf16)
    grad_fc2_bias = jnp.sum(grad_mlp.astype(f32), axis=0)
    grad_active = jnp.einsum("sd,fd->sf", grad_mlp, fc2_rows, preferred_element_type=f32)
    gelu_value, gelu_back = jax.vjp(partial(jax.nn.gelu, approximate=False), pre_act)
    grad_pre = gelu_back(grad_active)[0].astype(bf16)
    grad_fc1_bias = jnp.sum(grad_pre.astype(f32), axis=0)
    grad_normed2 = jnp.einsum("sf,df->sd", grad_pre, fc1_full, preferred_element_type=f32)
    grad_ln2_in, grad_ln2_gain, grad_ln2_bias = normalize_back(
        grad_normed2, unit_two, inverse_two, ln2_gain
    )
    grad_hidden = grad_out + grad_ln2_in
    grad_scale_one = jnp.sum(grad_hidden * branch, axis=0)
    grad_branch = (grad_hidden * scale_one).astype(bf16)
    grad_proj_bias = jnp.sum(grad_branch.astype(f32), axis=0)
    grad_attended = jnp.einsum(
        "sd,ed->se", grad_branch, proj_rows, preferred_element_type=f32
    ).astype(bf16)
    grad_blocks = grad_attended.reshape(rows_here, shards, head_columns).transpose(1, 0, 2)
    grad_mixed = exchange(grad_blocks, shards).reshape(seq_len, head_columns)

    keep, away = weight_grads(
        normed2,
        grad_pre,
        active,
        grad_mlp,
        attended_blocks,
        grad_branch,
    )
    member = lax.axis_index("dp")
    x_bit, y_bit = bit_of(member, 1), bit_of(member, 2)

    def swap(value, bit):
        return lax.ppermute(value, "dp", [(j, j ^ (1 << bit)) for j in range(members)])

    def pick(value, at, axis):
        return lax.dynamic_index_in_dim(value, at, axis, keepdims=False)

    got = swap(away, 0)
    pair = (2, 2) + keep.shape[1:]
    both = rounded_sum(keep, got).reshape(pair)
    half_a, half_b = both[:, :, : shards // 2], both[:, :, shards // 2 :]
    a_got = swap(pick(half_a, 1 - x_bit, 0), 1)
    b_got = swap(pick(half_b, 1 - y_bit, 1), 2)
    a_keep, b_keep = pick(half_a, x_bit, 0), pick(half_b, y_bit, 1)

    grad_heads = attend_back(
        bounds, queries_back, keys, values, mixed, grad_mixed, seq_len // 9
    )
    vectors = jnp.concatenate(
        [
            jnp.zeros((2, width), f32),
            jnp.stack(
                [
                    grad_proj_bias,
                    grad_scale_one,
                    grad_ln2_gain,
                    grad_ln2_bias,
                    grad_fc2_bias,
                    grad_scale_two,
                ]
            ),
            grad_fc1_bias.reshape(shards, hidden_here),
            jnp.zeros((shards, width), f32),
        ]
    )
    grad_tokens, totals, qkv_pieces, weight_pieces = finish(
        shards,
        members,
        grad_heads,
        full_one,
        qkv_weight.transpose(1, 0, 2).reshape(width, 3 * head_columns),
        ln1_gain[None],
        ln1_bias[None],
        vectors,
        tokens,
        grad_hidden,
        a_keep,
        a_got,
        b_keep,
        b_got,
    )
    grad_qkv_weight = (
        qkv_pieces.reshape(width, 3, head_columns).transpose(1, 0, 2).astype(f32)
    )
    fc_rows, proj_count = width // PIECES, head_columns // PIECES
    grad_fc1_weight = weight_pieces[:, :fc_rows].reshape(width, hidden_here).astype(f32)
    grad_fc2_weight = (
        weight_pieces[:, fc_rows : 2 * fc_rows].reshape(hidden_here, width).astype(f32)
    )
    grad_proj_weight = (
        weight_pieces[:, 2 * fc_rows : 2 * fc_rows + proj_count]
        .reshape(head_columns, width)
        .astype(f32)
    )
    vectors = totals
    grad_fc1_bias = lax.dynamic_index_in_dim(totals, 8 + here, 0, keepdims=False)
    qv_sums = lax.dynamic_index_in_dim(totals, 12 + here, 0, keepdims=False)
    grad_qv_bias = jnp.stack([qv_sums[:head_columns], qv_sums[2 * head_columns : 3 * head_columns]])
    return (
        block_out,
        grad_tokens,
        vectors[0],
        vectors[1],
        grad_qkv_weight,
        grad_qv_bias,
        grad_proj_weight,
        vectors[2],
        vectors[3],
        vectors[4],
        vectors[5],
        grad_fc1_weight,
        grad_fc1_bias,
        grad_fc2_weight,
        vectors[6],
        vectors[7],
    )


def solution(mesh):
    rows = P(("dp", "tensor"), None)
    columns = P(None, "tensor")
    return jax.shard_map(
        partial(on_device, mesh.shape["tensor"], mesh.shape["dp"]),
        mesh=mesh,
        in_specs=(
            rows,
            P("dp", None),
            P(),
            P(),
            P(None, None, "tensor"),
            columns,
            P("tensor", None),
            P(),
            P(),
            P(),
            P(),
            columns,
            P("tensor"),
            P("tensor", None),
            P(),
            P(),
            rows,
        ),
        out_specs=(
            rows,
            rows,
            P(),
            P(),
            P(None, None, "tensor"),
            columns,
            P("tensor", None),
            P(),
            P(),
            P(),
            P(),
            columns,
            P("tensor"),
            P("tensor", None),
            P(),
            P(),
        ),
        check_vma=False,
    )
```

```python
from functools import partial
import math

import jax, jax.numpy as jnp
from jax import lax
from jax.experimental import pallas as pl
from jax.experimental.pallas import tpu as pltpu

from jax.sharding import PartitionSpec as P

HEAD_DIM = 64
LANES = 128
MASKED = -(2.0**100)


def split_three(value):
    high = value.astype(jnp.bfloat16)
    rest = value - high.astype(jnp.float32)
    middle = rest.astype(jnp.bfloat16)
    low = (rest - middle.astype(jnp.float32)).astype(jnp.bfloat16)
    return (high, middle, low)


def join_heads(parts, low_half):
    tiles = []
    for at in range(0, len(parts), 2):
        if at + 1 < len(parts):
            tiles.append(jnp.where(low_half, parts[at], pltpu.roll(parts[at + 1], HEAD_DIM, 1)))
        else:
            tiles.append(parts[at])
    return tiles


def attend_kernel(key_block, bounds_ref, q_ref, k_ref, v_ref, out_ref, q_back_ref, peak_ref, acc_ref):
    step = pl.program_id(0)
    heads, count, _ = q_ref.shape
    peak_ref[...] = jnp.full_like(peak_ref, -3e38)
    acc_ref[...] = jnp.zeros_like(acc_ref)

    def visit(at, carry):
        keys = pl.ds(pl.multiple_of(at * key_block, key_block), key_block)
        for head in range(heads):
            scores = lax.dot_general(
                q_ref[head],
                k_ref[head, keys, :],
                (((1,), (1,)), ((), ())),
                preferred_element_type=jnp.float32,
            )
            old_peak = peak_ref[head]
            new_peak = jnp.maximum(old_peak, jnp.max(scores, axis=1, keepdims=True))
            weights = jnp.exp(scores - new_peak[:, :1]).astype(jnp.bfloat16)
            mixed = jnp.dot(weights, v_ref[head, keys, :], preferred_element_type=jnp.float32)
            acc_ref[head] = acc_ref[head] * jnp.exp(old_peak - new_peak) + mixed
            peak_ref[head] = new_peak
        return carry

    lax.fori_loop(bounds_ref[0, step], bounds_ref[1, step], visit, 0)
    lane = lax.broadcasted_iota(jnp.int32, (count, LANES), 1)
    low_half = lane < HEAD_DIM
    parts = []
    for head in range(heads):
        acc = acc_ref[head]
        total = acc[:, HEAD_DIM : HEAD_DIM + 1]
        parts.append(acc / total)
        log_total = -(peak_ref[head] + jnp.log(total))
        high, middle, low = split_three(log_total)
        kept = q_ref[head].astype(jnp.float32)
        kept = jnp.where(lane == HEAD_DIM + 8, high.astype(jnp.float32), kept)
        kept = jnp.where(lane == HEAD_DIM + 9, middle.astype(jnp.float32), kept)
        kept = jnp.where(lane == HEAD_DIM + 10, low.astype(jnp.float32), kept)
        q_back_ref[head] = kept.astype(jnp.bfloat16)
    for at, tile in enumerate(join_heads(parts, low_half)):
        wide = min(LANES, heads * HEAD_DIM - at * LANES)
        out_ref[:, at * LANES : at * LANES + wide] = tile[:, :wide].astype(jnp.bfloat16)


def attend(bounds, queries, keys, values, key_block):
    heads, seq_len, _ = queries.shape
    steps = bounds.shape[1]
    block = seq_len // steps
    q_spec = pl.BlockSpec((heads, block, LANES), lambda i, b: (0, i, 0))
    full = pl.BlockSpec((heads, seq_len, LANES), lambda i, b: (0, 0, 0))
    return pl.pallas_call(
        partial(attend_kernel, key_block),
        grid_spec=pltpu.PrefetchScalarGridSpec(
            num_scalar_prefetch=1,
            grid=(steps,),
            in_specs=[q_spec, full, full],
            out_specs=[pl.BlockSpec((block, heads * HEAD_DIM), lambda i, b: (i, 0)), q_spec],
            scratch_shapes=[
                pltpu.VMEM((heads, block, LANES), jnp.float32),
                pltpu.VMEM((heads, block, LANES), jnp.float32),
            ],
        ),
        out_shape=[
            jax.ShapeDtypeStruct((seq_len, heads * HEAD_DIM), jnp.bfloat16),
            jax.ShapeDtypeStruct((heads, seq_len, LANES), jnp.bfloat16),
        ],
        name="attend",
        cost_estimate=pl.CostEstimate(
            flops=4 * heads * seq_len * seq_len * LANES // 2, transcendentals=heads * seq_len * seq_len // 2,
            bytes_accessed=8 * heads * seq_len * LANES,
        ),
    )(bounds, queries, keys, values)


def attend_back_kernel(
    query_block, bounds_ref, q_ref, k_ref, v_ref, mixed_ref, grad_ref, out_ref, grad_heads_ref, dq_ref, dk_ref, dv_ref, k0_ref
):
    step = pl.program_id(0)
    heads, count, _ = k_ref.shape
    seq_len = q_ref.shape[1]
    blocks = seq_len // query_block

    @pl.when(step == 0)
    def _():
        dq_ref[...] = jnp.zeros_like(dq_ref)

        def prepare(at, carry):
            rows = pl.ds(pl.multiple_of(at * query_block, query_block), query_block)
            lane = lax.broadcasted_iota(jnp.int32, (query_block, LANES), 1)
            for head in range(heads):
                first = (head // 2) * LANES
                wide = min(LANES, heads * HEAD_DIM - first)
                grad = grad_ref[rows, first : first + wide].astype(jnp.float32)
                mixed = mixed_ref[rows, first : first + wide].astype(jnp.float32)
                if wide < LANES:
                    blank = jnp.zeros((query_block, LANES - wide), jnp.float32)
                    grad = jnp.concatenate([grad, blank], axis=1)
                    mixed = jnp.concatenate([mixed, blank], axis=1)
                if head % 2:
                    grad = pltpu.roll(grad, HEAD_DIM, 1)
                    mixed = pltpu.roll(mixed, HEAD_DIM, 1)
                inside = lane < HEAD_DIM
                shared = -jnp.sum(jnp.where(inside, grad * mixed, 0.0), axis=1, keepdims=True)
                high, middle, low = split_three(shared)
                grad = jnp.where(inside, grad, 0.0)
                grad = jnp.where(lane == HEAD_DIM, high.astype(jnp.float32), grad)
                grad = jnp.where(lane == HEAD_DIM + 1, middle.astype(jnp.float32), grad)
                grad = jnp.where(lane == HEAD_DIM + 2, low.astype(jnp.float32), grad)
                grad_heads_ref[head, rows, :] = grad.astype(jnp.bfloat16)
            return carry

        lax.fori_loop(0, blocks, prepare, 0)

    dk_ref[...] = jnp.zeros_like(dk_ref)
    dv_ref[...] = jnp.zeros_like(dv_ref)

    def visit(at, carry):
        rows = pl.ds(pl.multiple_of(at * query_block, query_block), query_block)
        for head in range(heads):
            queries = q_ref[head, rows, :]
            grads = grad_heads_ref[head, rows, :]
            keys = k_ref[head]
            contract = (((1,), (1,)), ((), ()))
            scores = lax.dot_general(keys, queries, contract, preferred_element_type=jnp.float32)
            probs = jnp.exp(scores)
            grad_probs = lax.dot_general(
                v_ref[head], grads, contract, preferred_element_type=jnp.float32
            )
            grad_scores = (probs * grad_probs).astype(jnp.bfloat16)
            dv_ref[head] += jnp.dot(
                probs.astype(jnp.bfloat16), grads, preferred_element_type=jnp.float32
            )
            dk_ref[head] += jnp.dot(grad_scores, queries, preferred_element_type=jnp.float32)
            dq_ref[head, rows, :] += lax.dot_general(
                grad_scores, keys, (((0,), (0,)), ((), ())), preferred_element_type=jnp.float32
            )
        return carry

    lax.fori_loop(bounds_ref[0, step], bounds_ref[1, step], visit, 0)
    lane = lax.broadcasted_iota(jnp.int32, (count, LANES), 1)
    low_half = lane < HEAD_DIM
    here = pl.ds(pl.multiple_of(step * count, count), count)
    k0_ref[here, :] = dk_ref[0]
    out_ref[here, 256:384] = jnp.where(
        low_half, dk_ref[1], pltpu.roll(dk_ref[2], HEAD_DIM, 1)
    ).astype(jnp.bfloat16)
    out_ref[here, 384:512] = jnp.where(
        low_half, dv_ref[0], pltpu.roll(dv_ref[1], HEAD_DIM, 1)
    ).astype(jnp.bfloat16)
    out_ref[here, 512:576] = dv_ref[2][:, :HEAD_DIM].astype(jnp.bfloat16)

    @pl.when(step == pl.num_programs(0) - 1)
    def _():
        def finish(at, carry):
            rows = pl.ds(pl.multiple_of(at * query_block, query_block), query_block)
            lane = lax.broadcasted_iota(jnp.int32, (query_block, LANES), 1)
            low_half = lane < HEAD_DIM
            scale = HEAD_DIM**-0.5
            out_ref[rows, 0:128] = (
                jnp.where(low_half, dq_ref[0, rows, :], pltpu.roll(dq_ref[1, rows, :], HEAD_DIM, 1))
                * scale
            ).astype(jnp.bfloat16)
            out_ref[rows, 128:256] = jnp.where(
                low_half, dq_ref[2, rows, :] * scale, pltpu.roll(k0_ref[rows, :], HEAD_DIM, 1)
            ).astype(jnp.bfloat16)
            return carry

        lax.fori_loop(0, blocks, finish, 0)


def attend_back(bounds, queries, keys, values, mixed, grads, query_block):
    heads, seq_len, _ = queries.shape
    steps = bounds.shape[1]
    block = seq_len // steps
    k_spec = pl.BlockSpec((heads, block, LANES), lambda i, b: (0, i, 0))
    full = pl.BlockSpec((heads, seq_len, LANES), lambda i, b: (0, 0, 0))
    flat = pl.BlockSpec((seq_len, heads * HEAD_DIM), lambda i, b: (0, 0))
    return pl.pallas_call(
        partial(attend_back_kernel, query_block),
        grid_spec=pltpu.PrefetchScalarGridSpec(
            num_scalar_prefetch=1,
            grid=(steps,),
            in_specs=[full, k_spec, k_spec, flat, flat],
            out_specs=pl.BlockSpec((seq_len, 3 * heads * HEAD_DIM), lambda i, b: (0, 0)),
            scratch_shapes=[
                pltpu.VMEM((heads, seq_len, LANES), jnp.bfloat16),
                pltpu.VMEM((heads, seq_len, LANES), jnp.float32),
                pltpu.VMEM((heads, block, LANES), jnp.float32),
                pltpu.VMEM((heads, block, LANES), jnp.float32),
                pltpu.VMEM((seq_len, LANES), jnp.float32),
            ],
        ),
        out_shape=jax.ShapeDtypeStruct((seq_len, 3 * heads * HEAD_DIM), jnp.bfloat16),
        name="attend_back",
        cost_estimate=pl.CostEstimate(
            flops=10 * heads * seq_len * seq_len * LANES // 2, transcendentals=heads * seq_len * seq_len // 2,
            bytes_accessed=12 * heads * seq_len * LANES,
        ),
    )(bounds, queries, keys, values, mixed, grads)


def visit_bounds(ids, steps, block):
    seq_len = ids.shape[0]
    count = seq_len // steps
    first = ids[::count][:steps]
    last = ids[count - 1 :: count]
    start = jnp.sum(ids[None, :] < first[:, None], axis=1, dtype=jnp.int32)
    end = jnp.sum(ids[None, :] <= last[:, None], axis=1, dtype=jnp.int32)
    return jnp.stack([start // block, (end + block - 1) // block])


MESH = pl.DeviceIdType.MESH
PIECES = 8
PIECE_BITS = 3


def contract_rows(left, right):
    return lax.dot_general(left, right, (((0,), (0,)), ((), ())), preferred_element_type=jnp.float32)


def times_transposed(left, right, precision=None):
    return lax.dot_general(
        left, right, (((1,), (1,)), ((), ())), preferred_element_type=jnp.float32, precision=precision
    )


def rounded_sum(left, right):
    return (left.astype(jnp.float32) + right.astype(jnp.float32)).astype(jnp.bfloat16)


def bit_of(index, bit):
    return lax.rem(index // (1 << bit), 2)


def partner_of(index, bit):
    return index + (1 - 2 * bit_of(index, bit)) * (1 << bit)


def greet(dp_bits, shards):
    barrier = pltpu.get_barrier_semaphore()
    member, here = lax.axis_index("dp"), lax.axis_index("tensor")
    peers = [{"dp": partner_of(member, bit)} for bit in range(dp_bits)]
    peers += [{"tensor": lax.rem(here + shift, shards)} for shift in range(1, shards)]
    for peer in peers:
        pl.semaphore_signal(barrier, inc=1, device_id=peer, device_id_type=MESH)
    pl.semaphore_wait(barrier, len(peers))


def finish_kernel(
    shards,
    dp_bits,
    grads_ref,
    rows_ref,
    weight_ref,
    gain_ref,
    shift_ref,
    vectors_ref,
    tokens_ref,
    hidden_ref,
    a_keep,
    a_got,
    b_keep,
    b_got,
    tokens_out,
    vectors_out,
    qkv_out,
    weights_out,
    part,
    from_left,
    from_right,
    q_wide,
    q_all,
    q_half,
    q_quarter,
    q_got_core,
    q_got_x,
    q_got_y,
    q_got_more,
    v_now,
    v_got,
    v_shards,
    a_sum,
    b_sum,
    a_second,
    b_second,
    pieces,
    pieces_more,
    z_got,
    send,
    recv,
):
    f32, bf16 = jnp.float32, jnp.bfloat16
    member, here = lax.axis_index("dp"), lax.axis_index("tensor")
    core, x_bit, y_bit = bit_of(member, 0), bit_of(member, 1), bit_of(member, 2)
    own_piece = core * 4 + x_bit * 2 + y_bit
    block = part.shape[1]
    width = part.shape[2]
    columns = grads_ref.shape[1]
    half_rows = weights_out.shape[1] // 2
    last = shards - 1
    slots = iter(range(send.shape[0]))
    pending = []

    def copy_to(src, dst, at, **peer):
        return pltpu.make_async_remote_copy(
            src_ref=src, dst_ref=dst, send_sem=send.at[at], recv_sem=recv.at[at], device_id=peer, device_id_type=MESH
        )

    def start_dp(src, dst, bit, keep=True):
        copy = copy_to(src, dst, next(slots), dp=partner_of(member, bit))
        copy.start()
        if keep:
            pending.append(copy)
        return copy

    greet(dp_bits, shards)

    def add_into(out, left, right):
        def step(at, carry):
            out[at] = rounded_sum(left[at], right[at])
            return carry

        lax.fori_loop(0, out.shape[0], step, 0)

    def sum_pairs(out, left, right):
        def step(at, carry):
            one, two = at // out.shape[1], lax.rem(at, out.shape[1])
            out[one, two] = rounded_sum(left[one, two], right[one, two])
            return carry

        lax.fori_loop(0, out.shape[0] * out.shape[1], step, 0)

    sum_pairs(a_sum, a_keep, a_got)
    sum_pairs(b_sum, b_keep, b_got)
    second_a = start_dp(a_sum.at[1 - y_bit], a_second, 2)
    second_b = start_dp(b_sum.at[1 - x_bit], b_second, 1)

    right_slots = [next(slots) for _ in range(shards)]
    left_slots = [next(slots) for _ in range(shards)]

    def to_right(owner):
        return copy_to(part.at[owner], from_left.at[owner], right_slots[owner], tensor=lax.rem(here + 1, shards))

    def to_left(owner):
        return copy_to(
            part.at[owner], from_right.at[owner], left_slots[owner], tensor=lax.rem(here + last, shards)
        )

    def add_arrived(owner, arrived):
        def step(at, carry):
            rows = pl.ds(pl.multiple_of(at * (block // 4), 16), block // 4)
            part[owner, rows, :] = rounded_sum(part[owner, rows, :], arrived[owner, rows, :])
            return carry

        lax.fori_loop(0, 4, step, 0)

    order = []
    for near in range((shards + 1) // 2):
        for owner in (last - near, near):
            if owner not in order:
                order.append(owner)
    for owner in order:
        product = times_transposed(grads_ref[owner * block : (owner + 1) * block, :], weight_ref[...])
        part[owner] = product.astype(bf16)
        if owner > 0:

            @pl.when(here == 0)
            def _():
                to_right(owner).start()

        if owner < last:

            @pl.when(here == last)
            def _():
                to_left(owner).start()

    def hop(time):
        for owner in range(shards):
            at = time - (last - owner)
            if 0 < at < owner:

                @pl.when(here == at)
                def _():
                    to_right(owner).wait_recv()
                    add_arrived(owner, from_left)
                    to_right(owner).start()

            at = last + owner - time
            if owner < at < last:

                @pl.when(here == at)
                def _():
                    to_left(owner).wait_recv()
                    add_arrived(owner, from_right)
                    to_left(owner).start()

    q_wide[...] = jnp.zeros_like(q_wide)

    def grow(at, carry):
        rows = pl.ds(pl.multiple_of(at * block, 16), block)
        q_wide[...] += contract_rows(rows_ref[rows, :], grads_ref[rows, :])
        return carry

    lax.fori_loop(0, shards, grow, 0)
    sums = jnp.dot(jnp.ones((8, grads_ref.shape[0]), bf16), grads_ref[...], preferred_element_type=f32)
    exact = lax.Precision.HIGHEST
    weight = weight_ref[...].astype(f32)
    shift_sum = times_transposed(sums, weight, exact)[0:1]
    gain_sum = times_transposed(jnp.ones((8, columns), f32), weight * q_wide[...], exact)[0:1]
    v_now[0] = vectors_ref[...]
    v_now[0, 0:1, :] = (gain_sum - shift_ref[...] * shift_sum) / gain_ref[...]
    v_now[0, 1:2, :] = shift_sum
    v_now[0, pl.ds(12 + here, 1), 0:columns] = sums[0:1]
    count = q_all.shape[1]
    for piece in range(PIECES):
        q_all[piece] = q_wide[piece * count : (piece + 1) * count, :].astype(bf16)

    def vector_stage(bit):
        return start_dp(v_now.at[bit], v_got.at[bit], bit)

    q_core = start_dp(q_all.at[pl.ds((1 - core) * 4, 4)], q_got_core, 0)
    v_copy = vector_stage(0)

    second_a.wait_recv()
    second_b.wait_recv()
    pairs = shards // 2
    for at in range(pairs):
        pieces[at] = rounded_sum(a_sum[y_bit, at], a_second[at])
        pieces[pairs + at] = rounded_sum(b_sum[x_bit, at], b_second[at])
    for bit in range(PIECE_BITS, dp_bits):
        extra = start_dp(pieces, pieces_more.at[bit - PIECE_BITS], bit, False)
        extra.wait_recv()
        extra.wait_send()
        add_into(pieces, pieces, pieces_more.at[bit - PIECE_BITS])
    z_copies = []
    for shift in range(1, shards):
        target = lax.rem(here + shift, shards)
        copy = copy_to(pieces.at[target], z_got.at[shift - 1], next(slots), tensor=target)
        copy.start()
        z_copies.append(copy)
    pending.extend(z_copies)

    q_core.wait_recv()
    for at in range(4):
        q_half[at] = rounded_sum(q_all[core * 4 + at], q_got_core[at])
    q_x = start_dp(q_half.at[pl.ds((1 - x_bit) * 2, 2)], q_got_x, 1)
    v_copy.wait_recv()
    v_now[1] = v_now[0] + v_got[0]
    v_copy = vector_stage(1)
    if last > 1:
        hop(1)
    q_x.wait_recv()
    for at in range(2):
        q_quarter[at] = rounded_sum(q_half[x_bit * 2 + at], q_got_x[at])
    q_y = start_dp(q_quarter.at[1 - y_bit], q_got_y, 2)
    v_copy.wait_recv()
    v_now[2] = v_now[1] + v_got[1]
    v_copy = vector_stage(2)
    q_y.wait_recv()
    qkv_out[own_piece] = rounded_sum(q_quarter[y_bit], q_got_y[...])
    v_copy.wait_recv()
    v_now[3] = v_now[2] + v_got[2]
    for bit in range(PIECE_BITS, dp_bits):
        extra = start_dp(qkv_out.at[own_piece], q_got_more.at[bit - PIECE_BITS], bit, False)
        v_copy = vector_stage(bit)
        extra.wait_recv()
        extra.wait_send()
        qkv_out[own_piece] = rounded_sum(qkv_out[own_piece], q_got_more[bit - PIECE_BITS])
        v_copy.wait_recv()
        v_now[bit + 1] = v_now[bit] + v_got[bit]
    v_shards[here] = v_now[dp_bits]
    for shift in range(1, shards):
        copy = copy_to(
            v_now.at[dp_bits], v_shards.at[here], next(slots), tensor=lax.rem(here + shift, shards)
        )
        copy.start()
        pending.append(copy)
    v_waits = pending[-last:]
    q_back = start_dp(qkv_out.at[own_piece], qkv_out.at[own_piece], 2)
    q_back.wait_recv()
    q_back = start_dp(
        qkv_out.at[pl.ds(core * 4 + x_bit * 2, 2)], qkv_out.at[pl.ds(core * 4 + x_bit * 2, 2)], 1
    )
    for time in range(2, last):
        hop(time)
    q_back.wait_recv()
    q_back = start_dp(qkv_out.at[pl.ds(core * 4, 4)], qkv_out.at[pl.ds(core * 4, 4)], 0)

    for copy in z_copies:
        copy.wait_recv()
    total = pieces[here].astype(f32)
    for shift in range(1, shards):
        total = total + z_got[shift - 1].astype(f32)
    weights_out[own_piece] = total.astype(bf16)

    def own_half(low, *index):
        rows = pl.ds(0 if low else half_rows, half_rows)
        return weights_out.at[index[0], rows]

    back_a = start_dp(own_half(True, own_piece), own_half(True, own_piece), 2)
    back_b = start_dp(own_half(False, own_piece), own_half(False, own_piece), 1)
    back_a.wait_recv()
    span = pl.ds(core * 4 + x_bit * 2, 2)
    back_a = start_dp(own_half(True, span), own_half(True, span), 1)
    back_b.wait_recv()
    back_c = [
        start_dp(own_half(False, core * 4 + 2 * at + y_bit), own_half(False, core * 4 + 2 * at + y_bit), 2)
        for at in range(2)
    ]
    back_a.wait_recv()
    for copy in back_c:
        copy.wait_recv()
    span = pl.ds(core * 4, 4)
    back_core = start_dp(weights_out.at[span], weights_out.at[span], 0)

    for copy in v_waits:
        copy.wait_recv()
    vectors_sum = v_shards[0]
    for at in range(1, shards):
        vectors_sum = vectors_sum + v_shards[at]
    vectors_out[...] = vectors_sum

    for owner in range(shards):

        @pl.when(here == owner)
        def _():
            if owner > 0:
                to_right(owner).wait_recv()
                add_arrived(owner, from_left)
            if owner < last:
                to_left(owner).wait_recv()
                add_arrived(owner, from_right)

    def close(at, carry):
        rows = pl.ds(pl.multiple_of(at * (block // 4), 16), block // 4)
        tokens = tokens_ref[rows, :].astype(f32)
        centred = tokens - jnp.mean(tokens, axis=1, keepdims=True)
        inverse = lax.rsqrt(jnp.mean(centred * centred, axis=1, keepdims=True) + eps_norm)
        unit = centred * inverse
        scaled = part[here, rows, :].astype(f32) * gain_ref[...]
        inner = (
            scaled
            - jnp.mean(scaled, axis=1, keepdims=True)
            - unit * jnp.mean(scaled * unit, axis=1, keepdims=True)
        )
        tokens_out[rows, :] = hidden_ref[rows, :] + inverse * inner
        return carry

    lax.fori_loop(0, 4, close, 0)
    q_back.wait_recv()
    back_core.wait_recv()
    for copy in pending:
        copy.wait_send()
    for owner in range(shards):

        @pl.when(here < owner)
        def _():
            to_right(owner).wait_send()

        @pl.when(here > owner)
        def _():
            to_left(owner).wait_send()


def finish(shards, members, grads, rows, weight, gain, shift, vectors, tokens, grad_hidden, a_keep, a_got, b_keep, b_got):
    dp_bits = members.bit_length() - 1
    assert members == 1 << dp_bits and dp_bits >= PIECE_BITS
    f32, bf16 = jnp.float32, jnp.bfloat16
    seq_len, columns = grads.shape
    block, width = tokens.shape
    piece_rows = a_keep.shape[2]
    count = width // PIECES
    more = max(1, dp_bits - PIECE_BITS)
    copies = 16 + 2 * shards + 2 * (shards - 1) + 3 * dp_bits
    vm = pltpu.VMEM
    return pl.pallas_call(
        partial(finish_kernel, shards, dp_bits),
        in_specs=[pl.BlockSpec(memory_space=vm)] * 12,
        out_specs=[pl.BlockSpec(memory_space=vm)] * 4,
        out_shape=[
            jax.ShapeDtypeStruct((block, width), f32),
            jax.ShapeDtypeStruct(vectors.shape, f32),
            jax.ShapeDtypeStruct((PIECES, count, columns), bf16),
            jax.ShapeDtypeStruct((PIECES, piece_rows, width), bf16),
        ],
        scratch_shapes=[
            vm((shards, block, width), bf16),
            vm((shards, block, width), bf16),
            vm((shards, block, width), bf16),
            vm((width, columns), f32),
            vm((PIECES, count, columns), bf16),
            vm((4, count, columns), bf16),
            vm((2, count, columns), bf16),
            vm((4, count, columns), bf16),
            vm((2, count, columns), bf16),
            vm((count, columns), bf16),
            vm((more, count, columns), bf16),
            vm((dp_bits + 1,) + vectors.shape, f32),
            vm((dp_bits,) + vectors.shape, f32),
            vm((shards,) + vectors.shape, f32),
            vm(a_keep.shape, bf16),
            vm(b_keep.shape, bf16),
            vm(a_keep.shape[1:], bf16),
            vm(b_keep.shape[1:], bf16),
            vm((shards, piece_rows, width), bf16),
            vm((more, shards, piece_rows, width), bf16),
            vm((shards - 1, piece_rows, width), bf16),
            pltpu.SemaphoreType.DMA((copies,)),
            pltpu.SemaphoreType.DMA((copies,)),
        ],
        compiler_params=pltpu.CompilerParams(
            collective_id=1, has_side_effects=True, vmem_limit_bytes=64 * 1024 * 1024 - 2048 * 1024
        ),
        name="finish",
        cost_estimate=pl.CostEstimate(
            flops=4 * seq_len * columns * width, transcendentals=0, bytes_accessed=40 * block * width
        ),
    )(grads, rows, weight, gain, shift, vectors, tokens, grad_hidden, a_keep, a_got, b_keep, b_got)


def start_kernel(
    shards,
    dp_bits,
    tokens_ref,
    ids_ref,
    gain_ref,
    shift_ref,
    qkv_ref,
    qv_bias_ref,
    fc1_ref,
    fc2_ref,
    proj_ref,
    fc1_bias_ref,
    normed_out,
    q_out,
    k_out,
    v_out,
    weights_out,
    bias_out,
    blocks,
    q_extra,
    k_extra,
    own,
    chain,
    send,
    recv,
    local,
):
    f32, bf16 = jnp.float32, jnp.bfloat16
    member, here = lax.axis_index("dp"), lax.axis_index("tensor")
    core, x_bit, y_bit = bit_of(member, 0), bit_of(member, 1), bit_of(member, 2)
    own_piece = core * 4 + x_bit * 2 + y_bit
    block, width = tokens_ref.shape
    heads = q_out.shape[0]
    seq_len = ids_ref.shape[1]
    last = shards - 1
    slots = iter(range(send.shape[0]))
    pending = []

    def copy_to(src, dst, at, **peer):
        return pltpu.make_async_remote_copy(
            src_ref=src, dst_ref=dst, send_sem=send.at[at], recv_sem=recv.at[at], device_id=peer, device_id_type=MESH
        )

    def start_dp(src, dst, bit):
        copy = copy_to(src, dst, next(slots), dp=partner_of(member, bit))
        copy.start()
        pending.append(copy)
        return copy

    fc1_rows, fc2_rows, proj_rows = (ref.shape[0] // PIECES for ref in (fc1_ref, fc2_ref, proj_ref))
    loads = []
    for at, (ref, first, count) in enumerate(
        ((fc1_ref, 0, fc1_rows), (fc2_ref, fc1_rows, fc2_rows))
    ):
        rows = pl.ds(pl.multiple_of(own_piece * count, 16), count)
        loads.append(pltpu.make_async_copy(ref.at[rows], own.at[first : first + count], local.at[at]))
        loads[-1].start()
    used = fc1_rows + fc2_rows
    rows = pl.ds(pl.multiple_of(own_piece * proj_rows, 8), proj_rows)
    own[used : used + proj_rows, :] = proj_ref[rows, :]
    used += proj_rows
    own[used:, :] = jnp.zeros((own.shape[0] - used, width), bf16)
    greet(dp_bits, shards)
    for load in loads:
        load.wait()

    chains = {}
    for name, first, rest in (("w", own, chain), ("t", tokens_ref, blocks)):
        chains[name] = (
            first,
            rest,
            [next(slots) for _ in range(shards)],
            [next(slots) for _ in range(shards)],
        )

    def hop_copy(name, owner, rightward, from_own):
        first, rest, right_slots, left_slots = chains[name]
        src = first if from_own else rest.at[owner]
        step = 1 if rightward else last
        at = (right_slots if rightward else left_slots)[owner]
        return copy_to(src, rest.at[owner], at, tensor=lax.rem(here + step, shards))

    def send_own(name, rightward):
        for owner in range(shards):
            if owner != (last if rightward else 0):

                @pl.when(here == owner)
                def _():
                    hop_copy(name, owner, rightward, True).start()

    def hop(name, time, then=None):
        for at in range(shards):
            for rightward, owner, end in ((True, at - time, last), (False, at + time, 0)):
                if 0 <= owner <= last:

                    @pl.when(here == at)
                    def _():
                        hop_copy(name, owner, rightward, False).wait_recv()
                        if at != end:
                            hop_copy(name, owner, rightward, False).start()
                            if then is not None and owner in (0, last):
                                hop_copy(then, at, rightward, True).start()

    send_own("w", True)
    send_own("w", False)

    @pl.when(here == 0)
    def _():
        hop_copy("t", 0, True, True).start()

    @pl.when(here == last)
    def _():
        hop_copy("t", last, False, True).start()

    bias_copies = []
    bias_out[here] = fc1_bias_ref[...]
    for shift in range(1, shards):
        copy = copy_to(
            fc1_bias_ref, bias_out.at[here], next(slots), tensor=lax.rem(here + shift, shards)
        )
        copy.start()
        bias_copies.append(copy)
    pending.extend(bias_copies)

    large = -MASKED
    segments = lax.broadcasted_iota(jnp.int32, (8, seq_len), 0)
    same = jnp.where(segments == ids_ref[...], 1.0, 0.0).astype(bf16)
    select = lax.broadcasted_iota(jnp.int32, (8, LANES), 1) - HEAD_DIM == lax.broadcasted_iota(
        jnp.int32, (8, LANES), 0
    )
    matched = contract_rows(same, jnp.where(select, 1.0, 0.0).astype(bf16))
    lane = lax.broadcasted_iota(jnp.int32, (seq_len, LANES), 1)
    segment_lane = (lane >= HEAD_DIM) & (lane < HEAD_DIM + 8)
    ones_lane = (lane >= HEAD_DIM + 8) & (lane < HEAD_DIM + 11)
    q_extra[...] = jnp.where(segment_lane, (matched - 1.0) * large, 0.0).astype(bf16)
    k_extra[...] = jnp.where(ones_lane, 1.0, matched).astype(bf16)
    low_half = lax.broadcasted_iota(jnp.int32, (block, LANES), 1) < HEAD_DIM
    v_lane = lax.broadcasted_iota(jnp.int32, (block, LANES), 1)
    v_extra = jnp.where((v_lane >= HEAD_DIM) & (v_lane < HEAD_DIM + 3), 1.0, 0.0).astype(bf16)

    def project_block(source, owner):
        tokens = source.astype(f32)
        centred = tokens - jnp.mean(tokens, axis=1, keepdims=True)
        inverse = lax.rsqrt(jnp.mean(centred * centred, axis=1, keepdims=True) + eps_norm)
        normed = (centred * inverse * gain_ref[...] + shift_ref[...]).astype(bf16)
        rows = pl.ds(pl.multiple_of(owner * block, 16), block)
        normed_out[rows, :] = normed
        for which, out in ((0, q_out), (1, k_out), (2, v_out)):
            product = jnp.dot(normed, qkv_ref[which], preferred_element_type=f32)
            if which != 1:
                product = product + qv_bias_ref[which // 2 : which // 2 + 1, :]
            if which == 0:
                product = product.astype(bf16).astype(f32) * HEAD_DIM**-0.5
            extra = v_extra if which == 2 else (q_extra if which == 0 else k_extra)[rows, :]
            for head in range(heads):
                first = (head // 2) * LANES
                tile = product[:, first : first + LANES]
                if tile.shape[1] < LANES:
                    blank = jnp.zeros((block, LANES - tile.shape[1]), f32)
                    tile = jnp.concatenate([tile, blank], axis=1)
                if head % 2:
                    tile = pltpu.roll(tile, HEAD_DIM, 1)
                out[head, rows, :] = jnp.where(low_half, tile, extra.astype(f32)).astype(bf16)

    project_block(tokens_ref[...], here)
    for time in range(1, shards):
        hop("w", time, "t")

    half = shards // 2
    out_a = [weights_out.at[own_piece, 0:half]]
    stores = []
    for owner in range(shards):
        at = 2 + owner

        @pl.when(here == owner)
        def _():
            pltpu.make_async_copy(own, weights_out.at[own_piece, owner], local.at[at]).start()

        @pl.when(here != owner)
        def _():
            pltpu.make_async_copy(chain.at[owner], weights_out.at[own_piece, owner], local.at[at]).start()

        stores.append(pltpu.make_async_copy(own, weights_out.at[own_piece, owner], local.at[at]))
    for store in stores:
        store.wait()

    def part(low, pieces):
        owners = pl.ds(0, half) if low else pl.ds(half, shards - half)
        return weights_out.at[pieces, owners]

    def gather_stage(low, pieces, bit):
        return [start_dp(part(low, at), part(low, at), bit) for at in pieces]

    def wait_all(copies):
        for copy in copies:
            copy.wait_recv()

    stage = gather_stage(True, [own_piece], 2) + gather_stage(False, [own_piece], 1)

    def arrived(time):
        for way in (-1, 1):
            owner = here + way * time

            @pl.when((owner >= 0) & (owner <= last))
            def _():
                project_block(blocks[owner], owner)

    for time in range(1, shards):
        hop("t", time)
        if time == 1:
            arrived(time)
            wait_all(stage)
            stage = gather_stage(True, [pl.ds(core * 4 + x_bit * 2, 2)], 1) + gather_stage(
                False, [core * 4 + 2 * at + y_bit for at in range(2)], 2
            )
        elif time == 2:
            arrived(time)
            wait_all(stage)
            stage = [start_dp(weights_out.at[pl.ds(core * 4, 4)], weights_out.at[pl.ds(core * 4, 4)], 0)]
        else:
            arrived(time)
    wait_all(stage)
    wait_all(bias_copies)
    for copy in pending:
        copy.wait_send()
    for name in chains:
        for at in range(shards):
            for owner in range(shards):
                if owner <= at < last:

                    @pl.when(here == at)
                    def _():
                        hop_copy(name, owner, True, False).wait_send()

                if owner >= at > 0:

                    @pl.when(here == at)
                    def _():
                        hop_copy(name, owner, False, False).wait_send()


def start(shards, members, tokens, ids, gain, shift, qkv, qv_bias, fc1, fc2, proj, fc1_bias):
    dp_bits = members.bit_length() - 1
    assert members == 1 << dp_bits and dp_bits >= PIECE_BITS and shards >= 3
    f32, bf16 = jnp.float32, jnp.bfloat16
    block, width = tokens.shape
    seq_len = block * shards
    heads = qkv.shape[2] // HEAD_DIM
    rows = -(-(fc1.shape[0] + fc2.shape[0] + proj.shape[0]) // PIECES // 16) * 16
    copies = 4 * shards + (shards - 1) + 6
    vm = pltpu.VMEM
    on_chip = pl.BlockSpec(memory_space=vm)
    anywhere = pl.BlockSpec(memory_space=pl.ANY)
    head_rows = jax.ShapeDtypeStruct((heads, seq_len, LANES), bf16)
    return pl.pallas_call(
        partial(start_kernel, shards, dp_bits),
        in_specs=[on_chip] * 6 + [anywhere] * 2 + [on_chip] * 2,
        out_specs=[on_chip] * 4 + [anywhere, on_chip],
        out_shape=[
            jax.ShapeDtypeStruct((seq_len, width), bf16),
            head_rows,
            head_rows,
            head_rows,
            jax.ShapeDtypeStruct((PIECES, shards, rows, width), bf16),
            jax.ShapeDtypeStruct((shards,) + fc1_bias.shape, f32),
        ],
        scratch_shapes=[
            vm((shards, block, width), bf16),
            vm((seq_len, LANES), bf16),
            vm((seq_len, LANES), bf16),
            vm((rows, width), bf16),
            vm((shards, rows, width), bf16),
            pltpu.SemaphoreType.DMA((copies,)),
            pltpu.SemaphoreType.DMA((copies,)),
            pltpu.SemaphoreType.DMA((2 + shards,)),
        ],
        compiler_params=pltpu.CompilerParams(collective_id=0, has_side_effects=True),
        name="start",
        cost_estimate=pl.CostEstimate(
            flops=6 * seq_len * width * heads * HEAD_DIM, transcendentals=0, bytes_accessed=40 * block * width
        ),
    )(tokens, ids, gain, shift, qkv, qv_bias, fc1, fc2, proj, fc1_bias)


CHUNK = 32


def middle_kernel(
    shards,
    dp_bits,
    mixed_ref,
    weights_ref,
    fc1_bias_ref,
    params_ref,
    tokens_ref,
    cotangent_ref,
    block_out,
    hidden_grad_out,
    mixed_grad_out,
    vectors_out,
    a_keep,
    a_away,
    b_keep,
    b_away,
    weights,
    attended,
    branch,
    hidden,
    normed,
    wide,
    total,
    active,
    slope,
    grad_pre,
    grad_mlp,
    grad_branch,
    grad_attended,
    got,
    send,
    recv,
    local,
):
    f32, bf16 = jnp.float32, jnp.bfloat16
    member, here = lax.axis_index("dp"), lax.axis_index("tensor")
    core, x_bit, y_bit = bit_of(member, 0), bit_of(member, 1), bit_of(member, 2)
    block, width = tokens_ref.shape
    columns = mixed_ref.shape[1]
    half = PIECES // 2
    fc_rows, proj_rows = width // PIECES, columns // PIECES
    proj_first = 2 * fc_rows
    slots = iter(range(send.shape[0]))
    proj_bias, scale_one, gain, shift, fc2_bias, scale_two = (
        params_ref[at : at + 1, :] for at in range(6)
    )

    def copy_to(src, dst, at, **peer):
        return pltpu.make_async_remote_copy(
            src_ref=src, dst_ref=dst, send_sem=send.at[at], recv_sem=recv.at[at], device_id=peer, device_id_type=MESH
        )

    loads = []
    for owner in range(shards):
        load = pltpu.make_async_copy(weights_ref.at[:, owner], weights.at[:, owner], local.at[owner])
        load.start()
        loads.append(load)
    greet(dp_bits, shards)

    def rows_of(owner):
        return pl.ds(pl.multiple_of(owner * block, 16), block)

    copies = []
    for way in range(1, shards):
        target = lax.rem(here + way, shards)
        copy = copy_to(mixed_ref.at[rows_of(target)], attended.at[here], next(slots), tensor=target)
        copy.start()
        copies.append(copy)
    attended[here] = mixed_ref[rows_of(here), :]
    for load in loads:
        load.wait()

    def fc1_of(owner):
        return weights[:, owner, :fc_rows, :].reshape(width, width)

    def fc2_of(owner):
        return weights[:, owner, fc_rows:proj_first, :].reshape(width, width)

    def proj_of(owner):
        return weights[:, owner, proj_first : proj_first + proj_rows, :].reshape(columns, width)

    def chunk(at):
        return pl.ds(pl.multiple_of(at * CHUNK, CHUNK), CHUNK)

    def each_chunk(body, init):
        return lax.fori_loop(0, block // CHUNK, body, init)

    def column_sum(value):
        return jnp.sum(value, axis=0, keepdims=True)

    def unit_of(value):
        centred = value - jnp.mean(value, axis=1, keepdims=True)
        inverse = lax.rsqrt(jnp.mean(centred * centred, axis=1, keepdims=True) + eps_norm)
        return centred * inverse, inverse

    for copy in copies:
        copy.wait_recv()
    product = jnp.dot(attended[0], proj_of(0), preferred_element_type=f32)
    for owner in range(1, shards):
        product += jnp.dot(attended[owner], proj_of(owner), preferred_element_type=f32)
    branch[...] = product

    def enter(at, carry):
        rows = chunk(at)
        value = branch[rows, :] + proj_bias
        branch[rows, :] = value
        value = tokens_ref[rows, :].astype(f32) + scale_one * value
        hidden[rows, :] = value
        unit, _ = unit_of(value)
        normed[rows, :] = (unit * gain + shift).astype(bf16)
        return carry

    each_chunk(enter, 0)

    def forward(owner, carry):
        wide[...] = jnp.dot(normed[...], fc1_of(owner), preferred_element_type=f32)
        bias = fc1_bias_ref[owner]

        def activate(at, carry):
            rows = chunk(at)
            value = wide[rows, :] + bias
            below = 0.5 * (1.0 + lax.erf(value * 0.5**0.5))
            active[owner, rows, :] = (value * below).astype(bf16)
            density = jnp.exp(value * value * -0.5) * (0.5 / math.pi) ** 0.5
            slope[owner, rows, :] = below + value * density
            return carry

        each_chunk(activate, 0)
        product = jnp.dot(active[owner], fc2_of(owner), preferred_element_type=f32)
        total[...] = jnp.where(owner == 0, product, total[...] + product)
        return carry

    lax.fori_loop(0, shards, forward, 0)
    empty = jnp.zeros((1, width), f32)

    def turn(at, sums):
        rows = chunk(at)
        value = total[rows, :] + fc2_bias
        block_out[rows, :] = (hidden[rows, :] + scale_two * value).astype(bf16)
        grad = cotangent_ref[rows, :].astype(f32)
        grad_mlp[rows, :] = (grad * scale_two).astype(bf16)
        return (
            sums[0] + column_sum(grad * value),
            sums[1] + column_sum(grad_mlp[rows, :].astype(f32)),
        )

    scale_two_sum, fc2_bias_sum = each_chunk(turn, (empty, empty))

    def backward(owner, carry):
        wide[...] = times_transposed(grad_mlp[...], fc2_of(owner))

        def slopes(at, sums):
            rows = chunk(at)
            value = (wide[rows, :] * slope[owner, rows, :]).astype(bf16)
            grad_pre[owner, rows, :] = value
            return sums + column_sum(value.astype(f32))

        vectors_out[pl.ds(8 + owner, 1), :] = each_chunk(slopes, empty)
        product = times_transposed(grad_pre[owner], fc1_of(owner))
        total[...] = jnp.where(owner == 0, product, total[...] + product)
        return carry

    lax.fori_loop(0, shards, backward, 0)

    def leave(at, sums):
        rows = chunk(at)
        grad = total[rows, :]
        unit, inverse = unit_of(hidden[rows, :])
        scaled = grad * gain
        inner = (
            scaled
            - jnp.mean(scaled, axis=1, keepdims=True)
            - unit * jnp.mean(scaled * unit, axis=1, keepdims=True)
        )
        value = cotangent_ref[rows, :].astype(f32) + inverse * inner
        hidden_grad_out[rows, :] = value
        rounded = (value * scale_one).astype(bf16)
        grad_branch[rows, :] = rounded
        return (
            sums[0] + column_sum(grad * unit),
            sums[1] + column_sum(grad),
            sums[2] + column_sum(value * branch[rows, :]),
            sums[3] + column_sum(rounded.astype(f32)),
        )

    gain_sum, shift_sum, scale_one_sum, proj_bias_sum = each_chunk(leave, (empty,) * 4)
    for at, value in enumerate(
        (empty, empty, proj_bias_sum, scale_one_sum, gain_sum, shift_sum, fc2_bias_sum, scale_two_sum)
    ):
        vectors_out[at : at + 1, :] = value
    vectors_out[12:, :] = jnp.zeros((vectors_out.shape[0] - 12, width), f32)

    back = []
    for way in (*range(1, shards), 0):
        target = lax.rem(here + way, shards)
        grad_attended[target] = times_transposed(grad_branch[...], proj_of(target)).astype(bf16)
        if way:
            copy = copy_to(grad_attended.at[target], mixed_grad_out.at[here], next(slots), tensor=target)
            copy.start()
            back.append(copy)
    mixed_grad_out[here] = grad_attended[here]

    first_slot = next(slots)

    def core_copy(owner):
        return pltpu.make_async_remote_copy(
            src_ref=weights.at[pl.ds((1 - core) * half, half), owner],
            dst_ref=got.at[:, owner],
            send_sem=send.at[first_slot + owner],
            recv_sem=recv.at[first_slot + owner],
            device_id={"dp": partner_of(member, 0)},
            device_id_type=MESH,
        )

    def weight_grads(owner, carry):
        for left, right, first, count in (
            (normed[...], grad_pre[owner], 0, fc_rows),
            (active[owner], grad_mlp[...], fc_rows, fc_rows),
            (attended[owner], grad_branch[...], proj_first, proj_rows),
        ):
            product = contract_rows(left, right).astype(bf16)
            weights[:, owner, first : first + count, :] = product.reshape(PIECES, count, width)
        core_copy(owner).start()
        return carry

    lax.fori_loop(0, shards, weight_grads, 0)
    pairs = shards // 2
    for owner in range(shards):
        core_copy(owner).wait_recv()
        if owner < pairs:
            for y in range(2):
                for out, x in ((a_keep, x_bit), (a_away, 1 - x_bit)):
                    out[y, owner] = rounded_sum(weights[core * half + x * 2 + y, owner], got[x * 2 + y, owner])
        else:
            for x in range(2):
                for out, y in ((b_keep, y_bit), (b_away, 1 - y_bit)):
                    out[x, owner - pairs] = rounded_sum(
                        weights[core * half + x * 2 + y, owner], got[x * 2 + y, owner]
                    )
    for copy in back:
        copy.wait_recv()
    for copy in copies + back:
        copy.wait_send()
    for owner in range(shards):
        core_copy(owner).wait_send()


def middle(shards, members, mixed, weights, fc1_bias, params, tokens, cotangent):
    dp_bits = members.bit_length() - 1
    f32, bf16 = jnp.float32, jnp.bfloat16
    block, width = tokens.shape
    columns = mixed.shape[1]
    rows = weights.shape[2]
    vm = pltpu.VMEM
    on_chip = pl.BlockSpec(memory_space=vm)
    quarter = jax.ShapeDtypeStruct((2, shards // 2, rows, width), bf16)
    copies = 2 * (shards - 1) + shards
    return pl.pallas_call(
        partial(middle_kernel, shards, dp_bits),
        in_specs=[on_chip, pl.BlockSpec(memory_space=pl.ANY)] + [on_chip] * 4,
        out_specs=[on_chip] * 8,
        out_shape=[
            jax.ShapeDtypeStruct((block, width), bf16),
            jax.ShapeDtypeStruct((block, width), f32),
            jax.ShapeDtypeStruct((shards, block, columns), bf16),
            jax.ShapeDtypeStruct((16, width), f32),
            quarter,
            quarter,
            quarter,
            quarter,
        ],
        scratch_shapes=[
            vm(weights.shape, bf16),
            vm((shards, block, columns), bf16),
            vm((block, width), f32),
            vm((block, width), f32),
            vm((block, width), bf16),
            vm((block, width), f32),
            vm((block, width), f32),
            vm((shards, block, width), bf16),
            vm((shards, block, width), f32),
            vm((shards, block, width), bf16),
            vm((block, width), bf16),
            vm((block, width), bf16),
            vm((shards, block, columns), bf16),
            vm((PIECES // 2, shards, rows, width), bf16),
            pltpu.SemaphoreType.DMA((copies,)),
            pltpu.SemaphoreType.DMA((copies,)),
            pltpu.SemaphoreType.DMA((shards,)),
        ],
        compiler_params=pltpu.CompilerParams(
            collective_id=2, has_side_effects=True, vmem_limit_bytes=62 * 1024 * 1024
        ),
        name="middle",
        cost_estimate=pl.CostEstimate(
            flops=12 * block * width * width * shards, transcendentals=0, bytes_accessed=40 * block * width
        ),
    )(mixed, weights, fc1_bias, params, tokens, cotangent)


eps_norm = 1e-06


def on_device(
    shards,
    members,
    tokens,
    segment_ids,
    ln1_gain,
    ln1_bias,
    qkv_weight,
    qv_bias,
    proj_weight,
    proj_bias,
    scale_one,
    ln2_gain,
    ln2_bias,
    fc1_weight,
    fc1_bias,
    fc2_weight,
    fc2_bias,
    scale_two,
    cotangent,
):
    f32, bf16 = jnp.float32, jnp.bfloat16
    seq_len = segment_ids.shape[1]
    rows_here, width = tokens.shape
    head_columns = qkv_weight.shape[2]
    heads = head_columns // HEAD_DIM
    hidden_here = fc1_weight.shape[1]
    ids = segment_ids[0]
    here = lax.axis_index("tensor")

    full_one, queries, keys, values, gathered, fc1_bias_full = start(
        shards,
        members,
        tokens,
        segment_ids,
        ln1_gain[None],
        ln1_bias[None],
        qkv_weight,
        qv_bias,
        fc1_weight,
        fc2_weight,
        proj_weight,
        fc1_bias[None],
    )
    bounds = visit_bounds(ids, 8, seq_len // 9)
    mixed, queries_back = attend(bounds, queries, keys, values, seq_len // 9)

    params = jnp.stack([proj_bias, scale_one, ln2_gain, ln2_bias, fc2_bias, scale_two])
    block_out, grad_hidden, grad_mixed, vectors, a_keep, a_away, b_keep, b_away = middle(
        shards, members, mixed, gathered, fc1_bias_full, params, tokens, cotangent
    )
    grad_mixed = grad_mixed.reshape(seq_len, head_columns)

    def swap(value, bit):
        return lax.ppermute(value, "dp", [(j, j ^ (1 << bit)) for j in range(members)])

    a_got, b_got = swap(a_away, 1), swap(b_away, 2)
    grad_heads = attend_back(
        bounds, queries_back, keys, values, mixed, grad_mixed, seq_len // 9
    )
    grad_tokens, totals, qkv_pieces, weight_pieces = finish(
        shards,
        members,
        grad_heads,
        full_one,
        qkv_weight.transpose(1, 0, 2).reshape(width, 3 * head_columns),
        ln1_gain[None],
        ln1_bias[None],
        vectors,
        tokens,
        grad_hidden,
        a_keep,
        a_got,
        b_keep,
        b_got,
    )
    grad_qkv_weight = (
        qkv_pieces.reshape(width, 3, head_columns).transpose(1, 0, 2).astype(f32)
    )
    fc_rows, proj_count = width // PIECES, head_columns // PIECES
    grad_fc1_weight = weight_pieces[:, :fc_rows].reshape(width, hidden_here).astype(f32)
    grad_fc2_weight = (
        weight_pieces[:, fc_rows : 2 * fc_rows].reshape(hidden_here, width).astype(f32)
    )
    grad_proj_weight = (
        weight_pieces[:, 2 * fc_rows : 2 * fc_rows + proj_count]
        .reshape(head_columns, width)
        .astype(f32)
    )
    vectors = totals
    grad_fc1_bias = lax.dynamic_index_in_dim(totals, 8 + here, 0, keepdims=False)
    qv_sums = lax.dynamic_index_in_dim(totals, 12 + here, 0, keepdims=False)
    grad_qv_bias = jnp.stack([qv_sums[:head_columns], qv_sums[2 * head_columns : 3 * head_columns]])
    return (
        block_out,
        grad_tokens,
        vectors[0],
        vectors[1],
        grad_qkv_weight,
        grad_qv_bias,
        grad_proj_weight,
        vectors[2],
        vectors[3],
        vectors[4],
        vectors[5],
        grad_fc1_weight,
        grad_fc1_bias,
        grad_fc2_weight,
        vectors[6],
        vectors[7],
    )


def solution(mesh):
    rows = P(("dp", "tensor"), None)
    columns = P(None, "tensor")
    return jax.shard_map(
        partial(on_device, mesh.shape["tensor"], mesh.shape["dp"]),
        mesh=mesh,
        in_specs=(
            rows,
            P("dp", None),
            P(),
            P(),
            P(None, None, "tensor"),
            columns,
            P("tensor", None),
            P(),
            P(),
            P(),
            P(),
            columns,
            P("tensor"),
            P("tensor", None),
            P(),
            P(),
            rows,
        ),
        out_specs=(
            rows,
            rows,
            P(),
            P(),
            P(None, None, "tensor"),
            columns,
            P("tensor", None),
            P(),
            P(),
            P(),
            P(),
            columns,
            P("tensor"),
            P("tensor", None),
            P(),
            P(),
        ),
        check_vma=False,
    )
```

```python
from functools import partial
import math

import jax, jax.numpy as jnp
from jax import lax
from jax.experimental import pallas as pl
from jax.experimental.pallas import tpu as pltpu

from jax.sharding import PartitionSpec as P

HEAD_DIM = 64
LANES = 128
MASKED = -(2.0**100)


def contract_rows(left, right):
    return lax.dot_general(left, right, (((0,), (0,)), ((), ())), preferred_element_type=jnp.float32)


def times_transposed(left, right, precision=None):
    return lax.dot_general(
        left, right, (((1,), (1,)), ((), ())), preferred_element_type=jnp.float32, precision=precision
    )


def split_three(value):
    high = value.astype(jnp.bfloat16)
    rest = value - high.astype(jnp.float32)
    middle = rest.astype(jnp.bfloat16)
    low = (rest - middle.astype(jnp.float32)).astype(jnp.bfloat16)
    return (high, middle, low)


def join_heads(parts, low_half):
    tiles = []
    for at in range(0, len(parts), 2):
        if at + 1 < len(parts):
            tiles.append(jnp.where(low_half, parts[at], pltpu.roll(parts[at + 1], HEAD_DIM, 1)))
        else:
            tiles.append(parts[at])
    return tiles


def attend_kernel(
    key_block, bounds_ref, q_ref, k_ref, v_ref, out_ref, q_back_ref, peak_ref, acc_ref, score_ref, weight_ref
):
    step = pl.program_id(0)
    heads, count, _ = q_ref.shape
    repeats = key_block // LANES
    peak_ref[...] = jnp.full_like(peak_ref, -3e38)
    acc_ref[...] = jnp.zeros_like(acc_ref)

    def visit(at, carry):
        keys = pl.ds(pl.multiple_of(at * key_block, key_block), key_block)
        for head in range(heads):
            score_ref[head] = times_transposed(q_ref[head], k_ref[head, keys, :])
        for head in range(heads):
            old_peak = peak_ref[head]
            new_peak = jnp.maximum(old_peak, jnp.max(score_ref[head], axis=1, keepdims=True))
            peak_ref[head] = new_peak
            spread = jnp.concatenate([new_peak] * repeats, axis=1)
            weight_ref[head] = jnp.exp(score_ref[head] - spread).astype(jnp.bfloat16)
            acc_ref[head] = acc_ref[head] * jnp.exp(old_peak - new_peak)
        for head in range(heads):
            acc_ref[head] += jnp.dot(
                weight_ref[head], v_ref[head, keys, :], preferred_element_type=jnp.float32
            )
        return carry

    lax.fori_loop(bounds_ref[0, step], bounds_ref[1, step], visit, 0)
    lane = lax.broadcasted_iota(jnp.int32, (count, LANES), 1)
    low_half = lane < HEAD_DIM
    parts = []
    for head in range(heads):
        acc = acc_ref[head]
        total = acc[:, HEAD_DIM : HEAD_DIM + 1]
        parts.append(acc / total)
        log_total = -(peak_ref[head] + jnp.log(total))
        high, middle, low = split_three(log_total)
        kept = q_ref[head].astype(jnp.float32)
        kept = jnp.where(lane == HEAD_DIM + 8, high.astype(jnp.float32), kept)
        kept = jnp.where(lane == HEAD_DIM + 9, middle.astype(jnp.float32), kept)
        kept = jnp.where(lane == HEAD_DIM + 10, low.astype(jnp.float32), kept)
        q_back_ref[head] = kept.astype(jnp.bfloat16)
    for at, tile in enumerate(join_heads(parts, low_half)):
        wide = min(LANES, heads * HEAD_DIM - at * LANES)
        out_ref[:, at * LANES : at * LANES + wide] = tile[:, :wide].astype(jnp.bfloat16)


def attend(bounds, queries, keys, values, key_block):
    heads, seq_len, _ = queries.shape
    steps = bounds.shape[1]
    block = seq_len // steps
    q_spec = pl.BlockSpec((heads, block, LANES), lambda i, b: (0, i, 0))
    full = pl.BlockSpec((heads, seq_len, LANES), lambda i, b: (0, 0, 0))
    return pl.pallas_call(
        partial(attend_kernel, key_block),
        grid_spec=pltpu.PrefetchScalarGridSpec(
            num_scalar_prefetch=1,
            grid=(steps,),
            in_specs=[q_spec, full, full],
            out_specs=[pl.BlockSpec((block, heads * HEAD_DIM), lambda i, b: (i, 0)), q_spec],
            scratch_shapes=[
                pltpu.VMEM((heads, block, LANES), jnp.float32),
                pltpu.VMEM((heads, block, LANES), jnp.float32),
                pltpu.VMEM((heads, block, key_block), jnp.float32),
                pltpu.VMEM((heads, block, key_block), jnp.bfloat16),
            ],
        ),
        out_shape=[
            jax.ShapeDtypeStruct((seq_len, heads * HEAD_DIM), jnp.bfloat16),
            jax.ShapeDtypeStruct((heads, seq_len, LANES), jnp.bfloat16),
        ],
        name="attend",
        cost_estimate=pl.CostEstimate(
            flops=4 * heads * seq_len * seq_len * LANES // 2, transcendentals=heads * seq_len * seq_len // 2,
            bytes_accessed=8 * heads * seq_len * LANES,
        ),
    )(bounds, queries, keys, values)


def attend_back_kernel(
    query_block,
    bounds_ref,
    q_ref,
    k_ref,
    v_ref,
    mixed_ref,
    grad_ref,
    out_ref,
    grad_heads_ref,
    dq_ref,
    dk_ref,
    dv_ref,
    k0_ref,
    prob_ref,
    grad_score_ref,
):
    f32, bf16 = jnp.float32, jnp.bfloat16
    step = pl.program_id(0)
    heads, count, _ = k_ref.shape
    seq_len = q_ref.shape[1]
    blocks = seq_len // query_block

    @pl.when(step == 0)
    def _():
        dq_ref[...] = jnp.zeros_like(dq_ref)
        source = lax.broadcasted_iota(jnp.int32, (LANES, LANES), 0)
        target = lax.broadcasted_iota(jnp.int32, (LANES, LANES), 1)
        gathers = (target >= HEAD_DIM) & (target < HEAD_DIM + 3)
        picks = []
        for odd in range(2):
            own = (source >= HEAD_DIM * odd) & (source < HEAD_DIM * (odd + 1))
            summing = jnp.where(own & gathers, -1.0, 0.0).astype(bf16)
            moving = jnp.where(own & (source - HEAD_DIM * odd == target), 1.0, 0.0).astype(bf16)
            picks.append((summing, moving))
        lane = lax.broadcasted_iota(jnp.int32, (query_block, LANES), 1)

        def prepare(at, carry):
            rows = pl.ds(pl.multiple_of(at * query_block, query_block), query_block)
            for first in range(0, heads * HEAD_DIM, LANES):
                wide = min(LANES, heads * HEAD_DIM - first)
                grad = grad_ref[rows, first : first + wide]
                mixed = mixed_ref[rows, first : first + wide]
                product = grad.astype(f32) * mixed.astype(f32)
                high = product.astype(bf16)
                low = (product - high.astype(f32)).astype(bf16)
                for odd in range(-(-wide // HEAD_DIM)):
                    summing, moving = (pick[:wide] for pick in picks[odd])
                    shared = jnp.dot(high, summing, preferred_element_type=f32) + jnp.dot(
                        low, summing, preferred_element_type=f32
                    )
                    first_part, second_part, third_part = split_three(shared)
                    moved = jnp.dot(grad, moving, preferred_element_type=f32)
                    moved = jnp.where(lane == HEAD_DIM, first_part.astype(f32), moved)
                    moved = jnp.where(lane == HEAD_DIM + 1, second_part.astype(f32), moved)
                    moved = jnp.where(lane == HEAD_DIM + 2, third_part.astype(f32), moved)
                    grad_heads_ref[first // HEAD_DIM + odd, rows, :] = moved.astype(bf16)
            return carry

        lax.fori_loop(0, blocks, prepare, 0)

    dk_ref[...] = jnp.zeros_like(dk_ref)
    dv_ref[...] = jnp.zeros_like(dv_ref)

    def visit(at, carry):
        rows = pl.ds(pl.multiple_of(at * query_block, query_block), query_block)
        for head in range(heads):
            probs = jnp.exp(times_transposed(k_ref[head], q_ref[head, rows, :]))
            grad_probs = times_transposed(v_ref[head], grad_heads_ref[head, rows, :])
            prob_ref[head] = probs.astype(bf16)
            grad_score_ref[head] = (probs * grad_probs).astype(bf16)
        for head in range(heads):
            dv_ref[head] += jnp.dot(
                prob_ref[head], grad_heads_ref[head, rows, :], preferred_element_type=f32
            )
            dk_ref[head] += jnp.dot(
                grad_score_ref[head], q_ref[head, rows, :], preferred_element_type=f32
            )
            dq_ref[head, rows, :] += contract_rows(grad_score_ref[head], k_ref[head])
        return carry

    lax.fori_loop(bounds_ref[0, step], bounds_ref[1, step], visit, 0)
    lane = lax.broadcasted_iota(jnp.int32, (count, LANES), 1)
    low_half = lane < HEAD_DIM
    here = pl.ds(pl.multiple_of(step * count, count), count)
    k0_ref[here, :] = dk_ref[0].astype(bf16)
    out_ref[here, 256:384] = jnp.where(
        low_half, dk_ref[1], pltpu.roll(dk_ref[2], HEAD_DIM, 1)
    ).astype(bf16)
    out_ref[here, 384:512] = jnp.where(
        low_half, dv_ref[0], pltpu.roll(dv_ref[1], HEAD_DIM, 1)
    ).astype(bf16)
    out_ref[here, 512:576] = dv_ref[2][:, :HEAD_DIM].astype(bf16)

    @pl.when(step == pl.num_programs(0) - 1)
    def _():
        scale = HEAD_DIM**-0.5

        def close(at, carry):
            rows = pl.ds(pl.multiple_of(at * query_block, query_block), query_block)
            low_half = lax.broadcasted_iota(jnp.int32, (query_block, LANES), 1) < HEAD_DIM
            second = pltpu.roll(dq_ref[1, rows, :], HEAD_DIM, 1)
            out_ref[rows, 0:128] = (
                jnp.where(low_half, dq_ref[0, rows, :], second) * scale
            ).astype(bf16)
            first_keys = pltpu.roll(k0_ref[rows, :].astype(f32), HEAD_DIM, 1)
            out_ref[rows, 128:256] = jnp.where(
                low_half, dq_ref[2, rows, :] * scale, first_keys
            ).astype(bf16)
            return carry

        lax.fori_loop(0, blocks, close, 0)


def attend_back(bounds, queries, keys, values, mixed, grads, query_block):
    heads, seq_len, _ = queries.shape
    steps = bounds.shape[1]
    block = seq_len // steps
    k_spec = pl.BlockSpec((heads, block, LANES), lambda i, b: (0, i, 0))
    full = pl.BlockSpec((heads, seq_len, LANES), lambda i, b: (0, 0, 0))
    flat = pl.BlockSpec((seq_len, heads * HEAD_DIM), lambda i, b: (0, 0))
    return pl.pallas_call(
        partial(attend_back_kernel, query_block),
        grid_spec=pltpu.PrefetchScalarGridSpec(
            num_scalar_prefetch=1,
            grid=(steps,),
            in_specs=[full, k_spec, k_spec, flat, flat],
            out_specs=pl.BlockSpec((seq_len, 3 * heads * HEAD_DIM), lambda i, b: (0, 0)),
            scratch_shapes=[
                pltpu.VMEM((heads, seq_len, LANES), jnp.bfloat16),
                pltpu.VMEM((heads, seq_len, LANES), jnp.float32),
                pltpu.VMEM((heads, block, LANES), jnp.float32),
                pltpu.VMEM((heads, block, LANES), jnp.float32),
                pltpu.VMEM((seq_len, LANES), jnp.bfloat16),
                pltpu.VMEM((heads, block, query_block), jnp.bfloat16),
                pltpu.VMEM((heads, block, query_block), jnp.bfloat16),
            ],
        ),
        out_shape=jax.ShapeDtypeStruct((seq_len, 3 * heads * HEAD_DIM), jnp.bfloat16),
        name="attend_back",
        cost_estimate=pl.CostEstimate(
            flops=10 * heads * seq_len * seq_len * LANES // 2, transcendentals=heads * seq_len * seq_len // 2,
            bytes_accessed=12 * heads * seq_len * LANES,
        ),
    )(bounds, queries, keys, values, mixed, grads)


MESH = pl.DeviceIdType.MESH
PIECES = 8
PIECE_BITS = 3


def rounded_sum(left, right):
    return (left.astype(jnp.float32) + right.astype(jnp.float32)).astype(jnp.bfloat16)


def bit_of(index, bit):
    return lax.rem(index // (1 << bit), 2)


def partner_of(index, bit):
    return index + (1 - 2 * bit_of(index, bit)) * (1 << bit)


def greet(dp_bits, shards):
    barrier = pltpu.get_barrier_semaphore()
    member, here = lax.axis_index("dp"), lax.axis_index("tensor")
    peers = [{"dp": partner_of(member, bit)} for bit in range(dp_bits)]
    peers += [{"tensor": lax.rem(here + way, shards)} for way in range(1, shards)]
    for peer in peers:
        pl.semaphore_signal(barrier, inc=1, device_id=peer, device_id_type=MESH)
    pl.semaphore_wait(barrier, len(peers))


def finish_kernel(
    shards,
    dp_bits,
    grads_ref,
    rows_ref,
    weight_ref,
    gain_ref,
    shift_ref,
    vectors_ref,
    tokens_ref,
    hidden_ref,
    a_keep,
    a_got,
    b_keep,
    b_got,
    tokens_out,
    vectors_out,
    qkv_out,
    weights_out,
    part,
    from_left,
    from_right,
    q_wide,
    q_all,
    q_half,
    q_quarter,
    q_got_core,
    q_got_x,
    q_got_y,
    q_got_more,
    v_now,
    v_got,
    v_shards,
    a_sum,
    b_sum,
    a_second,
    b_second,
    pieces,
    pieces_more,
    z_got,
    send,
    recv,
):
    f32, bf16 = jnp.float32, jnp.bfloat16
    member, here = lax.axis_index("dp"), lax.axis_index("tensor")
    core, x_bit, y_bit = bit_of(member, 0), bit_of(member, 1), bit_of(member, 2)
    own_piece = core * 4 + x_bit * 2 + y_bit
    block = part.shape[1]
    width = part.shape[2]
    columns = grads_ref.shape[1]
    half_rows = weights_out.shape[1] // 2
    last = shards - 1
    gain, shift = (ref[...].reshape(1, width) for ref in (gain_ref, shift_ref))
    slots = iter(range(send.shape[0]))
    pending = []

    def copy_to(src, dst, at, **peer):
        return pltpu.make_async_remote_copy(
            src_ref=src, dst_ref=dst, send_sem=send.at[at], recv_sem=recv.at[at], device_id=peer, device_id_type=MESH
        )

    def start_dp(src, dst, bit, keep=True):
        copy = copy_to(src, dst, next(slots), dp=partner_of(member, bit))
        copy.start()
        if keep:
            pending.append(copy)
        return copy

    greet(dp_bits, shards)

    def add_into(out, left, right):
        def step(at, carry):
            out[at] = rounded_sum(left[at], right[at])
            return carry

        lax.fori_loop(0, out.shape[0], step, 0)

    def sum_pairs(out, left, right):
        def step(at, carry):
            one, two = at // out.shape[1], lax.rem(at, out.shape[1])
            out[one, two] = rounded_sum(left[one, two], right[one, two])
            return carry

        lax.fori_loop(0, out.shape[0] * out.shape[1], step, 0)

    sum_pairs(a_sum, a_keep, a_got)
    sum_pairs(b_sum, b_keep, b_got)
    second_a = start_dp(a_sum.at[1 - y_bit], a_second, 2)
    second_b = start_dp(b_sum.at[1 - x_bit], b_second, 1)

    right_slots = [next(slots) for _ in range(shards)]
    left_slots = [next(slots) for _ in range(shards)]

    def to_right(owner):
        return copy_to(part.at[owner], from_left.at[owner], right_slots[owner], tensor=lax.rem(here + 1, shards))

    def to_left(owner):
        return copy_to(
            part.at[owner], from_right.at[owner], left_slots[owner], tensor=lax.rem(here + last, shards)
        )

    def add_arrived(owner, arrived):
        def step(at, carry):
            rows = pl.ds(pl.multiple_of(at * (block // 4), 16), block // 4)
            part[owner, rows, :] = rounded_sum(part[owner, rows, :], arrived[owner, rows, :])
            return carry

        lax.fori_loop(0, 4, step, 0)

    order = []
    for near in range((shards + 1) // 2):
        for owner in (last - near, near):
            if owner not in order:
                order.append(owner)
    for owner in order:
        product = jnp.dot(
            grads_ref[owner * block : (owner + 1) * block, :], weight_ref[...], preferred_element_type=f32
        )
        part[owner] = product.astype(bf16)
        if owner > 0:

            @pl.when(here == 0)
            def _():
                to_right(owner).start()

        if owner < last:

            @pl.when(here == last)
            def _():
                to_left(owner).start()

    def hop(time):
        for owner in range(shards):
            at = time - (last - owner)
            if 0 < at < owner:

                @pl.when(here == at)
                def _():
                    to_right(owner).wait_recv()
                    add_arrived(owner, from_left)
                    to_right(owner).start()

            at = last + owner - time
            if owner < at < last:

                @pl.when(here == at)
                def _():
                    to_left(owner).wait_recv()
                    add_arrived(owner, from_right)
                    to_left(owner).start()

    q_wide[...] = jnp.zeros_like(q_wide)

    def grow(at, carry):
        rows = pl.ds(pl.multiple_of(at * block, 16), block)
        q_wide[...] += contract_rows(grads_ref[rows, :], rows_ref[rows, :])
        return carry

    lax.fori_loop(0, shards, grow, 0)
    sums = jnp.dot(jnp.ones((8, grads_ref.shape[0]), bf16), grads_ref[...], preferred_element_type=f32)
    weight = weight_ref[...].astype(f32)
    shift_sum = jnp.dot(
        sums, weight, preferred_element_type=f32, precision=lax.Precision.HIGHEST
    )[0:1]
    gain_sum = jnp.sum(weight * q_wide[...], axis=0, keepdims=True)
    v_now[0] = vectors_ref[...]
    v_now[0, 0:1, :] = (gain_sum - shift * shift_sum) / gain
    v_now[0, 1:2, :] = shift_sum
    v_now[0, pl.ds(12 + here, 1), 0:columns] = sums[0:1]
    count = q_all.shape[1]
    for piece in range(PIECES):
        q_all[piece] = q_wide[piece * count : (piece + 1) * count, :].astype(bf16)

    def vector_stage(bit):
        return start_dp(v_now.at[bit], v_got.at[bit], bit)

    q_core = start_dp(q_all.at[pl.ds((1 - core) * 4, 4)], q_got_core, 0)
    v_copy = vector_stage(0)

    second_a.wait_recv()
    second_b.wait_recv()
    pairs = shards // 2
    for at in range(pairs):
        pieces[at] = rounded_sum(a_sum[y_bit, at], a_second[at])
        pieces[pairs + at] = rounded_sum(b_sum[x_bit, at], b_second[at])
    for bit in range(PIECE_BITS, dp_bits):
        extra = start_dp(pieces, pieces_more.at[bit - PIECE_BITS], bit, False)
        extra.wait_recv()
        extra.wait_send()
        add_into(pieces, pieces, pieces_more.at[bit - PIECE_BITS])
    z_copies = []
    for way in range(1, shards):
        target = lax.rem(here + way, shards)
        copy = copy_to(pieces.at[target], z_got.at[way - 1], next(slots), tensor=target)
        copy.start()
        z_copies.append(copy)
    pending.extend(z_copies)

    q_core.wait_recv()
    for at in range(4):
        q_half[at] = rounded_sum(q_all[core * 4 + at], q_got_core[at])
    q_x = start_dp(q_half.at[pl.ds((1 - x_bit) * 2, 2)], q_got_x, 1)
    v_copy.wait_recv()
    v_now[1] = v_now[0] + v_got[0]
    v_copy = vector_stage(1)
    if last > 1:
        hop(1)
    q_x.wait_recv()
    for at in range(2):
        q_quarter[at] = rounded_sum(q_half[x_bit * 2 + at], q_got_x[at])
    q_y = start_dp(q_quarter.at[1 - y_bit], q_got_y, 2)
    v_copy.wait_recv()
    v_now[2] = v_now[1] + v_got[1]
    v_copy = vector_stage(2)
    q_y.wait_recv()
    qkv_out[own_piece] = rounded_sum(q_quarter[y_bit], q_got_y[...])
    v_copy.wait_recv()
    v_now[3] = v_now[2] + v_got[2]
    for bit in range(PIECE_BITS, dp_bits):
        extra = start_dp(qkv_out.at[own_piece], q_got_more.at[bit - PIECE_BITS], bit, False)
        v_copy = vector_stage(bit)
        extra.wait_recv()
        extra.wait_send()
        qkv_out[own_piece] = rounded_sum(qkv_out[own_piece], q_got_more[bit - PIECE_BITS])
        v_copy.wait_recv()
        v_now[bit + 1] = v_now[bit] + v_got[bit]
    v_shards[here] = v_now[dp_bits]
    for way in range(1, shards):
        copy = copy_to(
            v_now.at[dp_bits], v_shards.at[here], next(slots), tensor=lax.rem(here + way, shards)
        )
        copy.start()
        pending.append(copy)
    v_waits = pending[-last:]
    q_back = start_dp(qkv_out.at[own_piece], qkv_out.at[own_piece], 2)
    q_back.wait_recv()
    q_back = start_dp(
        qkv_out.at[pl.ds(core * 4 + x_bit * 2, 2)], qkv_out.at[pl.ds(core * 4 + x_bit * 2, 2)], 1
    )
    for time in range(2, last):
        hop(time)
    q_back.wait_recv()
    q_back = start_dp(qkv_out.at[pl.ds(core * 4, 4)], qkv_out.at[pl.ds(core * 4, 4)], 0)

    for copy in z_copies:
        copy.wait_recv()
    total = pieces[here].astype(f32)
    for way in range(1, shards):
        total = total + z_got[way - 1].astype(f32)
    weights_out[own_piece] = total.astype(bf16)

    def own_half(low, *index):
        rows = pl.ds(0 if low else half_rows, half_rows)
        return weights_out.at[index[0], rows]

    back_a = start_dp(own_half(True, own_piece), own_half(True, own_piece), 2)
    back_b = start_dp(own_half(False, own_piece), own_half(False, own_piece), 1)
    back_a.wait_recv()
    span = pl.ds(core * 4 + x_bit * 2, 2)
    back_a = start_dp(own_half(True, span), own_half(True, span), 1)
    back_b.wait_recv()
    back_c = [
        start_dp(own_half(False, core * 4 + 2 * at + y_bit), own_half(False, core * 4 + 2 * at + y_bit), 2)
        for at in range(2)
    ]
    back_a.wait_recv()
    for copy in back_c:
        copy.wait_recv()
    span = pl.ds(core * 4, 4)
    back_core = start_dp(weights_out.at[span], weights_out.at[span], 0)

    for copy in v_waits:
        copy.wait_recv()
    vectors_sum = v_shards[0]
    for at in range(1, shards):
        vectors_sum = vectors_sum + v_shards[at]
    vectors_out[...] = vectors_sum

    for owner in range(shards):

        @pl.when(here == owner)
        def _():
            if owner > 0:
                to_right(owner).wait_recv()
                add_arrived(owner, from_left)
            if owner < last:
                to_left(owner).wait_recv()
                add_arrived(owner, from_right)

    def close(at, carry):
        rows = pl.ds(pl.multiple_of(at * (block // 4), 16), block // 4)
        tokens = tokens_ref[rows, :].astype(f32)
        centred = tokens - jnp.mean(tokens, axis=1, keepdims=True)
        inverse = lax.rsqrt(jnp.mean(centred * centred, axis=1, keepdims=True) + eps_norm)
        unit = centred * inverse
        scaled = part[here, rows, :].astype(f32) * gain
        inner = (
            scaled
            - jnp.mean(scaled, axis=1, keepdims=True)
            - unit * jnp.mean(scaled * unit, axis=1, keepdims=True)
        )
        tokens_out[rows, :] = hidden_ref[rows, :] + inverse * inner
        return carry

    lax.fori_loop(0, 4, close, 0)
    q_back.wait_recv()
    back_core.wait_recv()
    for copy in pending:
        copy.wait_send()
    for owner in range(shards):

        @pl.when(here < owner)
        def _():
            to_right(owner).wait_send()

        @pl.when(here > owner)
        def _():
            to_left(owner).wait_send()


def finish(shards, members, grads, rows, weight, gain, shift, vectors, tokens, grad_hidden, a_keep, a_got, b_keep, b_got):
    dp_bits = members.bit_length() - 1
    assert members == 1 << dp_bits and dp_bits >= PIECE_BITS
    f32, bf16 = jnp.float32, jnp.bfloat16
    seq_len, columns = grads.shape
    block, width = tokens.shape
    piece_rows = a_keep.shape[2]
    count = columns // PIECES
    more = max(1, dp_bits - PIECE_BITS)
    copies = 16 + 2 * shards + 2 * (shards - 1) + 3 * dp_bits
    vm = pltpu.VMEM
    return pl.pallas_call(
        partial(finish_kernel, shards, dp_bits),
        in_specs=[pl.BlockSpec(memory_space=vm)] * 12,
        out_specs=[pl.BlockSpec(memory_space=vm)] * 4,
        out_shape=[
            jax.ShapeDtypeStruct((block, width), f32),
            jax.ShapeDtypeStruct(vectors.shape, f32),
            jax.ShapeDtypeStruct((PIECES, count, width), bf16),
            jax.ShapeDtypeStruct((PIECES, piece_rows, width), bf16),
        ],
        scratch_shapes=[
            vm((shards, block, width), bf16),
            vm((shards, block, width), bf16),
            vm((shards, block, width), bf16),
            vm((columns, width), f32),
            vm((PIECES, count, width), bf16),
            vm((4, count, width), bf16),
            vm((2, count, width), bf16),
            vm((4, count, width), bf16),
            vm((2, count, width), bf16),
            vm((count, width), bf16),
            vm((more, count, width), bf16),
            vm((dp_bits + 1,) + vectors.shape, f32),
            vm((dp_bits,) + vectors.shape, f32),
            vm((shards,) + vectors.shape, f32),
            vm(a_keep.shape, bf16),
            vm(b_keep.shape, bf16),
            vm(a_keep.shape[1:], bf16),
            vm(b_keep.shape[1:], bf16),
            vm((shards, piece_rows, width), bf16),
            vm((more, shards, piece_rows, width), bf16),
            vm((shards - 1, piece_rows, width), bf16),
            pltpu.SemaphoreType.DMA((copies,)),
            pltpu.SemaphoreType.DMA((copies,)),
        ],
        compiler_params=pltpu.CompilerParams(
            collective_id=1, has_side_effects=True, vmem_limit_bytes=64 * 1024 * 1024 - 2048 * 1024
        ),
        name="finish",
        cost_estimate=pl.CostEstimate(
            flops=4 * seq_len * columns * width, transcendentals=0, bytes_accessed=40 * block * width
        ),
    )(grads, rows, weight, gain, shift, vectors, tokens, grad_hidden, a_keep, a_got, b_keep, b_got)


def unpack_kernel(qkv_ref, weights_ref, totals_ref, fc1_out, fc2_out, proj_out, qkv_out, fc1_bias_out, *vector_outs):
    fc_rows, proj_rows = fc1_out.shape[0], proj_out.shape[0]
    fc1_out[...] = weights_ref[0, :fc_rows].astype(jnp.float32)
    fc2_out[...] = weights_ref[0, fc_rows : 2 * fc_rows].astype(jnp.float32)
    proj_out[...] = weights_ref[0, 2 * fc_rows : 2 * fc_rows + proj_rows].astype(jnp.float32)
    qkv_out[...] = qkv_ref[0].astype(jnp.float32)

    @pl.when(pl.program_id(0) == 0)
    def _():
        width = totals_ref.shape[1]
        for at, out in enumerate(vector_outs):
            out[...] = totals_ref[at : at + 1, :].reshape(width)
        here = lax.axis_index("tensor")
        fc1_bias_out[...] = totals_ref[pl.ds(8 + here, 1), :].reshape(width)


def unpack(qkv, weights, totals, fc_rows, proj_rows):
    f32 = jnp.float32
    _, rows, width = weights.shape
    qkv_rows = qkv.shape[1]
    counts = (fc_rows, fc_rows, proj_rows, qkv_rows)
    vector = pl.BlockSpec((width,), lambda i: (0,))
    return pl.pallas_call(
        unpack_kernel,
        grid=(PIECES,),
        in_specs=[
            pl.BlockSpec((1, qkv_rows, width), lambda i: (i, 0, 0)),
            pl.BlockSpec((1, rows, width), lambda i: (i, 0, 0)),
            pl.BlockSpec(totals.shape, lambda i: (0, 0)),
        ],
        out_specs=[pl.BlockSpec((count, width), lambda i: (i, 0)) for count in counts] + [vector] * 9,
        out_shape=[jax.ShapeDtypeStruct((PIECES * count, width), f32) for count in counts]
        + [jax.ShapeDtypeStruct((width,), f32)] * 9,
        name="unpack",
    )(qkv, weights, totals)


def start_kernel(
    shards,
    dp_bits,
    visit_block,
    tokens_ref,
    ids_ref,
    gain_ref,
    shift_ref,
    qkv_ref,
    qv_bias_ref,
    fc1_ref,
    fc2_ref,
    proj_ref,
    fc1_bias_ref,
    normed_out,
    q_out,
    k_out,
    v_out,
    weights_out,
    bias_out,
    bounds_out,
    blocks,
    q_extra,
    k_extra,
    own,
    chain,
    send,
    recv,
    local,
):
    f32, bf16 = jnp.float32, jnp.bfloat16
    member, here = lax.axis_index("dp"), lax.axis_index("tensor")
    core, x_bit, y_bit = bit_of(member, 0), bit_of(member, 1), bit_of(member, 2)
    own_piece = core * 4 + x_bit * 2 + y_bit
    block, width = tokens_ref.shape
    heads = q_out.shape[0]
    seq_len = ids_ref.shape[1]
    last = shards - 1
    slots = iter(range(send.shape[0]))
    pending = []

    def copy_to(src, dst, at, **peer):
        return pltpu.make_async_remote_copy(
            src_ref=src, dst_ref=dst, send_sem=send.at[at], recv_sem=recv.at[at], device_id=peer, device_id_type=MESH
        )

    def start_dp(src, dst, bit):
        copy = copy_to(src, dst, next(slots), dp=partner_of(member, bit))
        copy.start()
        pending.append(copy)
        return copy

    fc1_rows, fc2_rows, proj_rows = (ref.shape[0] // PIECES for ref in (fc1_ref, fc2_ref, proj_ref))
    loads = []
    for at, (ref, first, count) in enumerate(
        ((fc1_ref, 0, fc1_rows), (fc2_ref, fc1_rows, fc2_rows))
    ):
        rows = pl.ds(pl.multiple_of(own_piece * count, 16), count)
        loads.append(pltpu.make_async_copy(ref.at[rows], own.at[first : first + count], local.at[at]))
        loads[-1].start()
    used = fc1_rows + fc2_rows
    rows = pl.ds(pl.multiple_of(own_piece * proj_rows, 8), proj_rows)
    own[used : used + proj_rows, :] = proj_ref[rows, :]
    used += proj_rows
    own[used:, :] = jnp.zeros((own.shape[0] - used, width), bf16)
    gain, shift = (ref[...].reshape(1, width) for ref in (gain_ref, shift_ref))
    bias_out[here] = fc1_bias_ref[...].reshape(1, width)
    greet(dp_bits, shards)
    for load in loads:
        load.wait()

    chains = {}
    for name, first, rest in (("w", own, chain), ("t", tokens_ref, blocks)):
        chains[name] = (
            first,
            rest,
            [next(slots) for _ in range(shards)],
            [next(slots) for _ in range(shards)],
        )

    def hop_copy(name, owner, rightward, from_own):
        first, rest, right_slots, left_slots = chains[name]
        src = first if from_own else rest.at[owner]
        step = 1 if rightward else last
        at = (right_slots if rightward else left_slots)[owner]
        return copy_to(src, rest.at[owner], at, tensor=lax.rem(here + step, shards))

    def send_own(name, rightward):
        for owner in range(shards):
            if owner != (last if rightward else 0):

                @pl.when(here == owner)
                def _():
                    hop_copy(name, owner, rightward, True).start()

    def hop(name, time, then=None):
        for at in range(shards):
            for rightward, owner, end in ((True, at - time, last), (False, at + time, 0)):
                if 0 <= owner <= last:

                    @pl.when(here == at)
                    def _():
                        hop_copy(name, owner, rightward, False).wait_recv()
                        if at != end:
                            hop_copy(name, owner, rightward, False).start()
                            if then is not None and owner in (0, last):
                                hop_copy(then, at, rightward, True).start()

    send_own("w", True)
    send_own("w", False)

    @pl.when(here == 0)
    def _():
        hop_copy("t", 0, True, True).start()

    @pl.when(here == last)
    def _():
        hop_copy("t", last, False, True).start()

    bias_copies = []
    for way in range(1, shards):
        copy = copy_to(
            bias_out.at[here], bias_out.at[here], next(slots), tensor=lax.rem(here + way, shards)
        )
        copy.start()
        bias_copies.append(copy)
    pending.extend(bias_copies)

    large = -MASKED
    segments = lax.broadcasted_iota(jnp.int32, (8, seq_len), 0)
    same = jnp.where(segments == ids_ref[...], 1.0, 0.0).astype(bf16)
    select = lax.broadcasted_iota(jnp.int32, (8, LANES), 1) - HEAD_DIM == lax.broadcasted_iota(
        jnp.int32, (8, LANES), 0
    )
    matched = contract_rows(same, jnp.where(select, 1.0, 0.0).astype(bf16))
    lane = lax.broadcasted_iota(jnp.int32, (seq_len, LANES), 1)
    segment_lane = (lane >= HEAD_DIM) & (lane < HEAD_DIM + 8)
    ones_lane = (lane >= HEAD_DIM + 8) & (lane < HEAD_DIM + 11)
    q_extra[...] = jnp.where(segment_lane, (matched - 1.0) * large, 0.0).astype(bf16)
    k_extra[...] = jnp.where(ones_lane, 1.0, matched).astype(bf16)
    ids = ids_ref[...]
    groups = bounds_out.shape[1]
    for group in range(groups):
        first = group * (seq_len // groups)
        last_row = first + seq_len // groups - 1
        before = jnp.sum(jnp.where(ids < ids_ref[:, first : first + 1], 1.0, 0.0))
        within = jnp.sum(jnp.where(ids <= ids_ref[:, last_row : last_row + 1], 1.0, 0.0))
        bounds_out[0, group] = before.astype(jnp.int32) // visit_block
        bounds_out[1, group] = (within.astype(jnp.int32) + visit_block - 1) // visit_block
    low_half = lax.broadcasted_iota(jnp.int32, (block, LANES), 1) < HEAD_DIM
    v_lane = lax.broadcasted_iota(jnp.int32, (block, LANES), 1)
    v_extra = jnp.where((v_lane >= HEAD_DIM) & (v_lane < HEAD_DIM + 3), 1.0, 0.0).astype(bf16)

    def project_block(source, owner):
        tokens = source.astype(f32)
        centred = tokens - jnp.mean(tokens, axis=1, keepdims=True)
        inverse = lax.rsqrt(jnp.mean(centred * centred, axis=1, keepdims=True) + eps_norm)
        normed = (centred * inverse * gain + shift).astype(bf16)
        rows = pl.ds(pl.multiple_of(owner * block, 16), block)
        normed_out[rows, :] = normed
        for which, out in ((0, q_out), (1, k_out), (2, v_out)):
            product = times_transposed(normed, qkv_ref[which])
            if which != 1:
                product = product + qv_bias_ref[which // 2 : which // 2 + 1, :]
            if which == 0:
                product = product.astype(bf16).astype(f32) * HEAD_DIM**-0.5
            extra = v_extra if which == 2 else (q_extra if which == 0 else k_extra)[rows, :]
            for head in range(heads):
                first = (head // 2) * LANES
                tile = product[:, first : first + LANES]
                if tile.shape[1] < LANES:
                    blank = jnp.zeros((block, LANES - tile.shape[1]), f32)
                    tile = jnp.concatenate([tile, blank], axis=1)
                if head % 2:
                    tile = pltpu.roll(tile, HEAD_DIM, 1)
                out[head, rows, :] = jnp.where(low_half, tile, extra.astype(f32)).astype(bf16)

    project_block(tokens_ref[...], here)
    for time in range(1, shards):
        hop("w", time, "t")

    half = shards // 2
    out_a = [weights_out.at[own_piece, 0:half]]
    stores = []
    for owner in range(shards):
        at = 2 + owner

        @pl.when(here == owner)
        def _():
            pltpu.make_async_copy(own, weights_out.at[own_piece, owner], local.at[at]).start()

        @pl.when(here != owner)
        def _():
            pltpu.make_async_copy(chain.at[owner], weights_out.at[own_piece, owner], local.at[at]).start()

        stores.append(pltpu.make_async_copy(own, weights_out.at[own_piece, owner], local.at[at]))
    for store in stores:
        store.wait()

    def part(low, pieces):
        owners = pl.ds(0, half) if low else pl.ds(half, shards - half)
        return weights_out.at[pieces, owners]

    def gather_stage(low, pieces, bit):
        return [start_dp(part(low, at), part(low, at), bit) for at in pieces]

    def wait_all(copies):
        for copy in copies:
            copy.wait_recv()

    stage = gather_stage(True, [own_piece], 2) + gather_stage(False, [own_piece], 1)

    def arrived(time):
        for way in (-1, 1):
            owner = here + way * time

            @pl.when((owner >= 0) & (owner <= last))
            def _():
                project_block(blocks[owner], owner)

    for time in range(1, shards):
        hop("t", time)
        if time == 1:
            arrived(time)
            wait_all(stage)
            stage = gather_stage(True, [pl.ds(core * 4 + x_bit * 2, 2)], 1) + gather_stage(
                False, [core * 4 + 2 * at + y_bit for at in range(2)], 2
            )
        elif time == 2:
            arrived(time)
            wait_all(stage)
            stage = [start_dp(weights_out.at[pl.ds(core * 4, 4)], weights_out.at[pl.ds(core * 4, 4)], 0)]
        else:
            arrived(time)
    wait_all(stage)
    wait_all(bias_copies)
    for copy in pending:
        copy.wait_send()
    for name in chains:
        for at in range(shards):
            for owner in range(shards):
                if owner <= at < last:

                    @pl.when(here == at)
                    def _():
                        hop_copy(name, owner, True, False).wait_send()

                if owner >= at > 0:

                    @pl.when(here == at)
                    def _():
                        hop_copy(name, owner, False, False).wait_send()


def start(shards, members, visits, tokens, ids, gain, shift, qkv, qv_bias, fc1, fc2, proj, fc1_bias):
    dp_bits = members.bit_length() - 1
    assert members == 1 << dp_bits and dp_bits >= PIECE_BITS and shards >= 3
    f32, bf16 = jnp.float32, jnp.bfloat16
    block, width = tokens.shape
    seq_len = block * shards
    heads = qkv.shape[1] // HEAD_DIM
    rows = -(-(fc1.shape[0] + fc2.shape[0] + proj.shape[0]) // PIECES // 16) * 16
    copies = 4 * shards + (shards - 1) + 6
    vm = pltpu.VMEM
    on_chip = pl.BlockSpec(memory_space=vm)
    anywhere = pl.BlockSpec(memory_space=pl.ANY)
    head_rows = jax.ShapeDtypeStruct((heads, seq_len, LANES), bf16)
    return pl.pallas_call(
        partial(start_kernel, shards, dp_bits, visits[1]),
        in_specs=[on_chip] * 6 + [anywhere] * 2 + [on_chip] * 2,
        out_specs=[on_chip] * 4 + [anywhere, on_chip, pl.BlockSpec(memory_space=pltpu.SMEM)],
        out_shape=[
            jax.ShapeDtypeStruct((seq_len, width), bf16),
            head_rows,
            head_rows,
            head_rows,
            jax.ShapeDtypeStruct((PIECES, shards, rows, width), bf16),
            jax.ShapeDtypeStruct((shards, 1, width), f32),
            jax.ShapeDtypeStruct((2, visits[0]), jnp.int32),
        ],
        scratch_shapes=[
            vm((shards, block, width), bf16),
            vm((seq_len, LANES), bf16),
            vm((seq_len, LANES), bf16),
            vm((rows, width), bf16),
            vm((shards, rows, width), bf16),
            pltpu.SemaphoreType.DMA((copies,)),
            pltpu.SemaphoreType.DMA((copies,)),
            pltpu.SemaphoreType.DMA((2 + shards,)),
        ],
        compiler_params=pltpu.CompilerParams(collective_id=0, has_side_effects=True),
        name="start",
        cost_estimate=pl.CostEstimate(
            flops=6 * seq_len * width * heads * HEAD_DIM, transcendentals=0, bytes_accessed=40 * block * width
        ),
    )(tokens, ids, gain, shift, qkv, qv_bias, fc1, fc2, proj, fc1_bias)


CHUNK = 32


def middle_kernel(
    shards,
    dp_bits,
    mixed_ref,
    weights_ref,
    fc1_bias_ref,
    proj_bias_ref,
    scale_one_ref,
    gain_ref,
    shift_ref,
    fc2_bias_ref,
    scale_two_ref,
    tokens_ref,
    cotangent_ref,
    block_out,
    hidden_grad_out,
    mixed_grad_out,
    vectors_out,
    a_keep,
    a_away,
    b_keep,
    b_away,
    weights,
    attended,
    branch,
    hidden,
    normed,
    wide,
    total,
    active,
    slope,
    grad_pre,
    grad_mlp,
    grad_branch,
    grad_attended,
    got,
    send,
    recv,
    local,
):
    f32, bf16 = jnp.float32, jnp.bfloat16
    member, here = lax.axis_index("dp"), lax.axis_index("tensor")
    core, x_bit, y_bit = bit_of(member, 0), bit_of(member, 1), bit_of(member, 2)
    block, width = tokens_ref.shape
    columns = mixed_ref.shape[1]
    half = PIECES // 2
    fc_rows, proj_rows = width // PIECES, columns // PIECES
    proj_first = 2 * fc_rows
    slots = iter(range(send.shape[0]))
    proj_bias, scale_one, gain, shift, fc2_bias, scale_two = (
        ref[...].reshape(1, width)
        for ref in (proj_bias_ref, scale_one_ref, gain_ref, shift_ref, fc2_bias_ref, scale_two_ref)
    )

    def copy_to(src, dst, at, **peer):
        return pltpu.make_async_remote_copy(
            src_ref=src, dst_ref=dst, send_sem=send.at[at], recv_sem=recv.at[at], device_id=peer, device_id_type=MESH
        )

    loads = []
    for owner in range(shards):
        load = pltpu.make_async_copy(weights_ref.at[:, owner], weights.at[:, owner], local.at[owner])
        load.start()
        loads.append(load)
    greet(dp_bits, shards)

    def rows_of(owner):
        return pl.ds(pl.multiple_of(owner * block, 16), block)

    copies = []
    for way in range(1, shards):
        target = lax.rem(here + way, shards)
        copy = copy_to(mixed_ref.at[rows_of(target)], attended.at[here], next(slots), tensor=target)
        copy.start()
        copies.append(copy)
    attended[here] = mixed_ref[rows_of(here), :]
    for load in loads:
        load.wait()

    def fc1_of(owner):
        return weights[:, owner, :fc_rows, :].reshape(width, width)

    def fc2_of(owner):
        return weights[:, owner, fc_rows:proj_first, :].reshape(width, width)

    def proj_of(owner):
        return weights[:, owner, proj_first : proj_first + proj_rows, :].reshape(columns, width)

    def chunk(at):
        return pl.ds(pl.multiple_of(at * CHUNK, CHUNK), CHUNK)

    def each_chunk(body, init):
        return lax.fori_loop(0, block // CHUNK, body, init)

    def column_sum(value):
        return jnp.sum(value, axis=0, keepdims=True)

    def unit_of(value):
        centred = value - jnp.mean(value, axis=1, keepdims=True)
        inverse = lax.rsqrt(jnp.mean(centred * centred, axis=1, keepdims=True) + eps_norm)
        return centred * inverse, inverse

    for copy in copies:
        copy.wait_recv()
    product = jnp.dot(attended[0], proj_of(0), preferred_element_type=f32)
    for owner in range(1, shards):
        product += jnp.dot(attended[owner], proj_of(owner), preferred_element_type=f32)
    branch[...] = product

    def enter(at, carry):
        rows = chunk(at)
        value = branch[rows, :] + proj_bias
        branch[rows, :] = value
        value = tokens_ref[rows, :].astype(f32) + scale_one * value
        hidden[rows, :] = value
        unit, _ = unit_of(value)
        normed[rows, :] = (unit * gain + shift).astype(bf16)
        return carry

    each_chunk(enter, 0)

    def forward(owner, carry):
        wide[...] = jnp.dot(normed[...], fc1_of(owner), preferred_element_type=f32)
        bias = fc1_bias_ref[owner]

        def activate(at, carry):
            rows = chunk(at)
            value = wide[rows, :] + bias
            below = 0.5 * (1.0 + lax.erf(value * 0.5**0.5))
            active[owner, rows, :] = (value * below).astype(bf16)
            density = jnp.exp(value * value * -0.5) * (0.5 / math.pi) ** 0.5
            slope[owner, rows, :] = below + value * density
            return carry

        each_chunk(activate, 0)
        product = jnp.dot(active[owner], fc2_of(owner), preferred_element_type=f32)
        total[...] = jnp.where(owner == 0, product, total[...] + product)
        return carry

    lax.fori_loop(0, shards, forward, 0)
    empty = jnp.zeros((1, width), f32)

    def turn(at, sums):
        rows = chunk(at)
        value = total[rows, :] + fc2_bias
        block_out[rows, :] = (hidden[rows, :] + scale_two * value).astype(bf16)
        grad = cotangent_ref[rows, :].astype(f32)
        grad_mlp[rows, :] = (grad * scale_two).astype(bf16)
        return (
            sums[0] + column_sum(grad * value),
            sums[1] + column_sum(grad_mlp[rows, :].astype(f32)),
        )

    scale_two_sum, fc2_bias_sum = each_chunk(turn, (empty, empty))

    def backward(owner, carry):
        wide[...] = times_transposed(grad_mlp[...], fc2_of(owner))

        def slopes(at, sums):
            rows = chunk(at)
            value = (wide[rows, :] * slope[owner, rows, :]).astype(bf16)
            grad_pre[owner, rows, :] = value
            return sums + column_sum(value.astype(f32))

        vectors_out[pl.ds(8 + owner, 1), :] = each_chunk(slopes, empty)
        product = times_transposed(grad_pre[owner], fc1_of(owner))
        total[...] = jnp.where(owner == 0, product, total[...] + product)
        return carry

    lax.fori_loop(0, shards, backward, 0)

    def leave(at, sums):
        rows = chunk(at)
        grad = total[rows, :]
        unit, inverse = unit_of(hidden[rows, :])
        scaled = grad * gain
        inner = (
            scaled
            - jnp.mean(scaled, axis=1, keepdims=True)
            - unit * jnp.mean(scaled * unit, axis=1, keepdims=True)
        )
        value = cotangent_ref[rows, :].astype(f32) + inverse * inner
        hidden_grad_out[rows, :] = value
        rounded = (value * scale_one).astype(bf16)
        grad_branch[rows, :] = rounded
        return (
            sums[0] + column_sum(grad * unit),
            sums[1] + column_sum(grad),
            sums[2] + column_sum(value * branch[rows, :]),
            sums[3] + column_sum(rounded.astype(f32)),
        )

    gain_sum, shift_sum, scale_one_sum, proj_bias_sum = each_chunk(leave, (empty,) * 4)
    for at, value in enumerate(
        (empty, empty, proj_bias_sum, scale_one_sum, gain_sum, shift_sum, fc2_bias_sum, scale_two_sum)
    ):
        vectors_out[at : at + 1, :] = value
    vectors_out[12:, :] = jnp.zeros((vectors_out.shape[0] - 12, width), f32)

    back = []
    for way in (*range(1, shards), 0):
        target = lax.rem(here + way, shards)
        grad_attended[target] = times_transposed(grad_branch[...], proj_of(target)).astype(bf16)
        if way:
            copy = copy_to(grad_attended.at[target], mixed_grad_out.at[here], next(slots), tensor=target)
            copy.start()
            back.append(copy)
    mixed_grad_out[here] = grad_attended[here]

    first_slot = next(slots)

    def core_copy(owner):
        return pltpu.make_async_remote_copy(
            src_ref=weights.at[pl.ds((1 - core) * half, half), owner],
            dst_ref=got.at[:, owner],
            send_sem=send.at[first_slot + owner],
            recv_sem=recv.at[first_slot + owner],
            device_id={"dp": partner_of(member, 0)},
            device_id_type=MESH,
        )

    def weight_grads(owner, carry):
        for left, right, first, count in (
            (normed[...], grad_pre[owner], 0, fc_rows),
            (active[owner], grad_mlp[...], fc_rows, fc_rows),
            (attended[owner], grad_branch[...], proj_first, proj_rows),
        ):
            product = contract_rows(left, right).astype(bf16)
            weights[:, owner, first : first + count, :] = product.reshape(PIECES, count, width)
        core_copy(owner).start()
        return carry

    lax.fori_loop(0, shards, weight_grads, 0)
    pairs = shards // 2
    for owner in range(shards):
        core_copy(owner).wait_recv()
        if owner < pairs:
            for y in range(2):
                for out, x in ((a_keep, x_bit), (a_away, 1 - x_bit)):
                    out[y, owner] = rounded_sum(weights[core * half + x * 2 + y, owner], got[x * 2 + y, owner])
        else:
            for x in range(2):
                for out, y in ((b_keep, y_bit), (b_away, 1 - y_bit)):
                    out[x, owner - pairs] = rounded_sum(
                        weights[core * half + x * 2 + y, owner], got[x * 2 + y, owner]
                    )
    for copy in back:
        copy.wait_recv()
    for copy in copies + back:
        copy.wait_send()
    for owner in range(shards):
        core_copy(owner).wait_send()


def middle(shards, members, mixed, weights, fc1_bias, vectors, tokens, cotangent):
    dp_bits = members.bit_length() - 1
    f32, bf16 = jnp.float32, jnp.bfloat16
    block, width = tokens.shape
    columns = mixed.shape[1]
    rows = weights.shape[2]
    vm = pltpu.VMEM
    on_chip = pl.BlockSpec(memory_space=vm)
    quarter = jax.ShapeDtypeStruct((2, shards // 2, rows, width), bf16)
    copies = 2 * (shards - 1) + shards
    return pl.pallas_call(
        partial(middle_kernel, shards, dp_bits),
        in_specs=[on_chip, pl.BlockSpec(memory_space=pl.ANY)] + [on_chip] * 9,
        out_specs=[on_chip] * 8,
        out_shape=[
            jax.ShapeDtypeStruct((block, width), bf16),
            jax.ShapeDtypeStruct((block, width), f32),
            jax.ShapeDtypeStruct((shards, block, columns), bf16),
            jax.ShapeDtypeStruct((16, width), f32),
            quarter,
            quarter,
            quarter,
            quarter,
        ],
        scratch_shapes=[
            vm(weights.shape, bf16),
            vm((shards, block, columns), bf16),
            vm((block, width), f32),
            vm((block, width), f32),
            vm((block, width), bf16),
            vm((block, width), f32),
            vm((block, width), f32),
            vm((shards, block, width), bf16),
            vm((shards, block, width), f32),
            vm((shards, block, width), bf16),
            vm((block, width), bf16),
            vm((block, width), bf16),
            vm((shards, block, columns), bf16),
            vm((PIECES // 2, shards, rows, width), bf16),
            pltpu.SemaphoreType.DMA((copies,)),
            pltpu.SemaphoreType.DMA((copies,)),
            pltpu.SemaphoreType.DMA((shards,)),
        ],
        compiler_params=pltpu.CompilerParams(
            collective_id=2, has_side_effects=True, vmem_limit_bytes=62 * 1024 * 1024
        ),
        name="middle",
        cost_estimate=pl.CostEstimate(
            flops=12 * block * width * width * shards, transcendentals=0, bytes_accessed=40 * block * width
        ),
    )(mixed, weights, fc1_bias, *vectors, tokens, cotangent)


eps_norm = 1e-06


def on_device(
    shards,
    members,
    tokens,
    segment_ids,
    ln1_gain,
    ln1_bias,
    qkv_weight,
    qv_bias,
    proj_weight,
    proj_bias,
    scale_one,
    ln2_gain,
    ln2_bias,
    fc1_weight,
    fc1_bias,
    fc2_weight,
    fc2_bias,
    scale_two,
    cotangent,
):
    f32, bf16 = jnp.float32, jnp.bfloat16
    seq_len = segment_ids.shape[1]
    rows_here, width = tokens.shape
    head_columns = qkv_weight.shape[2]
    heads = head_columns // HEAD_DIM
    hidden_here = fc1_weight.shape[1]
    ids = segment_ids[0]
    here = lax.axis_index("tensor")

    visits = (4, seq_len // 6)
    turned = qkv_weight.transpose(0, 2, 1)
    full_one, queries, keys, values, gathered, fc1_bias_full, bounds = start(
        shards,
        members,
        visits,
        tokens,
        segment_ids,
        ln1_gain,
        ln1_bias,
        turned,
        qv_bias,
        fc1_weight,
        fc2_weight,
        proj_weight,
        fc1_bias,
    )
    mixed, queries_back = attend(bounds, queries, keys, values, visits[1])

    params = (proj_bias, scale_one, ln2_gain, ln2_bias, fc2_bias, scale_two)
    block_out, grad_hidden, grad_mixed, vectors, a_keep, a_away, b_keep, b_away = middle(
        shards, members, mixed, gathered, fc1_bias_full, params, tokens, cotangent
    )
    grad_mixed = grad_mixed.reshape(seq_len, head_columns)

    def swap(value, bit):
        return lax.ppermute(value, "dp", [(j, j ^ (1 << bit)) for j in range(members)])

    a_got, b_got = swap(a_away, 1), swap(b_away, 2)
    grad_heads = attend_back(bounds, queries_back, keys, values, mixed, grad_mixed, visits[1])
    grad_tokens, totals, qkv_pieces, weight_pieces = finish(
        shards,
        members,
        grad_heads,
        full_one,
        turned.reshape(3 * head_columns, width),
        ln1_gain,
        ln1_bias,
        vectors,
        tokens,
        grad_hidden,
        a_keep,
        a_got,
        b_keep,
        b_got,
    )
    fc1_grad, fc2_grad, proj_grad, qkv_grad, fc1_bias_grad, *sums = unpack(
        qkv_pieces, weight_pieces, totals, width // PIECES, head_columns // PIECES
    )
    qkv_grad = qkv_grad.reshape(3, head_columns, width).transpose(0, 2, 1)
    qv_sums = lax.dynamic_index_in_dim(totals, 12 + here, 0, keepdims=False)
    qv_grad = jnp.stack([qv_sums[:head_columns], qv_sums[2 * head_columns : 3 * head_columns]])
    return (
        block_out,
        grad_tokens,
        sums[0],
        sums[1],
        qkv_grad,
        qv_grad,
        proj_grad,
        sums[2],
        sums[3],
        sums[4],
        sums[5],
        fc1_grad,
        fc1_bias_grad,
        fc2_grad,
        sums[6],
        sums[7],
    )


def solution(mesh):
    rows = P(("dp", "tensor"), None)
    columns = P(None, "tensor")
    return jax.shard_map(
        partial(on_device, mesh.shape["tensor"], mesh.shape["dp"]),
        mesh=mesh,
        in_specs=(
            rows,
            P("dp", None),
            P(),
            P(),
            P(None, None, "tensor"),
            columns,
            P("tensor", None),
            P(),
            P(),
            P(),
            P(),
            columns,
            P("tensor"),
            P("tensor", None),
            P(),
            P(),
            rows,
        ),
        out_specs=(
            rows,
            rows,
            P(),
            P(),
            P(None, None, "tensor"),
            columns,
            P("tensor", None),
            P(),
            P(),
            P(),
            P(),
            columns,
            P("tensor"),
            P("tensor", None),
            P(),
            P(),
        ),
        check_vma=False,
    )
```

```python
from functools import partial
import math

import jax, jax.numpy as jnp
from jax import lax
from jax.experimental import pallas as pl
from jax.experimental.pallas import tpu as pltpu

from jax.sharding import PartitionSpec as P

HEAD_DIM = 64
LANES = 128
MASKED = -(2.0**100)


def contract_rows(left, right):
    return lax.dot_general(left, right, (((0,), (0,)), ((), ())), preferred_element_type=jnp.float32)


def times_transposed(left, right, precision=None):
    return lax.dot_general(
        left, right, (((1,), (1,)), ((), ())), preferred_element_type=jnp.float32, precision=precision
    )


def split_three(value):
    high = value.astype(jnp.bfloat16)
    rest = value - high.astype(jnp.float32)
    middle = rest.astype(jnp.bfloat16)
    low = (rest - middle.astype(jnp.float32)).astype(jnp.bfloat16)
    return (high, middle, low)


def join_lanes(low, high):
    lane = lax.broadcasted_iota(jnp.int32, low.shape, 1)
    return jnp.where(lane < HEAD_DIM, low, pltpu.roll(high, HEAD_DIM, 1))


def attend_kernel(
    key_block,
    bounds_ref,
    q_ref,
    k_ref,
    v_ref,
    pair_ref,
    single_ref,
    q_back_ref,
    peak_ref,
    acc_ref,
    score_ref,
    weight_ref,
):
    step = pl.program_id(0)
    heads, count, _ = q_ref.shape
    repeats = key_block // LANES
    peak_ref[...] = jnp.full_like(peak_ref, -3e38)
    acc_ref[...] = jnp.zeros_like(acc_ref)

    def visit(at, carry):
        keys = pl.ds(pl.multiple_of(at * key_block, key_block), key_block)
        for head in range(heads):
            score_ref[head] = times_transposed(q_ref[head], k_ref[head, keys, :])
        for head in range(heads):
            old_peak = peak_ref[head]
            new_peak = jnp.maximum(old_peak, jnp.max(score_ref[head], axis=1, keepdims=True))
            peak_ref[head] = new_peak
            spread = jnp.concatenate([new_peak] * repeats, axis=1)
            weight_ref[head] = jnp.exp(score_ref[head] - spread).astype(jnp.bfloat16)
            acc_ref[head] = acc_ref[head] * jnp.exp(old_peak - new_peak)
        for head in range(heads):
            acc_ref[head] += jnp.dot(
                weight_ref[head], v_ref[head, keys, :], preferred_element_type=jnp.float32
            )
        return carry

    lax.fori_loop(bounds_ref[0, step], bounds_ref[1, step], visit, 0)
    lane = lax.broadcasted_iota(jnp.int32, (count, LANES), 1)
    parts = []
    for head in range(heads):
        acc = acc_ref[head]
        total = acc[:, HEAD_DIM : HEAD_DIM + 1]
        parts.append(acc / total)
        log_total = -(peak_ref[head] + jnp.log(total))
        high, middle, low = split_three(log_total)
        kept = q_ref[head].astype(jnp.float32)
        kept = jnp.where(lane == HEAD_DIM + 8, high.astype(jnp.float32), kept)
        kept = jnp.where(lane == HEAD_DIM + 9, middle.astype(jnp.float32), kept)
        kept = jnp.where(lane == HEAD_DIM + 10, low.astype(jnp.float32), kept)
        q_back_ref[head] = kept.astype(jnp.bfloat16)
    pair_ref[...] = join_lanes(parts[0], parts[1]).astype(jnp.bfloat16)
    half = count // 2
    single_ref[...] = join_lanes(parts[2][:half], parts[2][half:]).astype(jnp.bfloat16)


def attend(bounds, queries, keys, values, key_block):
    heads, seq_len, _ = queries.shape
    steps = bounds.shape[1]
    block = seq_len // steps
    q_spec = pl.BlockSpec((heads, block, LANES), lambda i, b: (0, i, 0))
    full = pl.BlockSpec((heads, seq_len, LANES), lambda i, b: (0, 0, 0))
    return pl.pallas_call(
        partial(attend_kernel, key_block),
        grid_spec=pltpu.PrefetchScalarGridSpec(
            num_scalar_prefetch=1,
            grid=(steps,),
            in_specs=[q_spec, full, full],
            out_specs=[
                pl.BlockSpec((block, LANES), lambda i, b: (i, 0)),
                pl.BlockSpec((block // 2, LANES), lambda i, b: (i, 0)),
                q_spec,
            ],
            scratch_shapes=[
                pltpu.VMEM((heads, block, LANES), jnp.float32),
                pltpu.VMEM((heads, block, LANES), jnp.float32),
                pltpu.VMEM((heads, block, key_block), jnp.float32),
                pltpu.VMEM((heads, block, key_block), jnp.bfloat16),
            ],
        ),
        out_shape=[
            jax.ShapeDtypeStruct((seq_len, LANES), jnp.bfloat16),
            jax.ShapeDtypeStruct((seq_len // 2, LANES), jnp.bfloat16),
            jax.ShapeDtypeStruct((heads, seq_len, LANES), jnp.bfloat16),
        ],
        name="attend",
        cost_estimate=pl.CostEstimate(
            flops=4 * heads * seq_len * seq_len * LANES // 2, transcendentals=heads * seq_len * seq_len // 2,
            bytes_accessed=8 * heads * seq_len * LANES,
        ),
    )(bounds, queries, keys, values)


def attend_back_kernel(
    query_block,
    bounds_ref,
    q_ref,
    k_ref,
    v_ref,
    pair_ref,
    single_ref,
    pair_grad_ref,
    single_grad_ref,
    out_ref,
    grad_heads_ref,
    dq_ref,
    dk_ref,
    dv_ref,
    k0_ref,
    prob_ref,
    grad_score_ref,
):
    f32, bf16 = jnp.float32, jnp.bfloat16
    step = pl.program_id(0)
    heads, count, _ = k_ref.shape
    seq_len = q_ref.shape[1]
    blocks = seq_len // query_block

    @pl.when(step == 0)
    def _():
        dq_ref[...] = jnp.zeros_like(dq_ref)
        source = lax.broadcasted_iota(jnp.int32, (LANES, LANES), 0)
        target = lax.broadcasted_iota(jnp.int32, (LANES, LANES), 1)
        gathers = (target >= HEAD_DIM) & (target < HEAD_DIM + 3)
        picks = []
        for odd in range(2):
            own = (source >= HEAD_DIM * odd) & (source < HEAD_DIM * (odd + 1))
            summing = jnp.where(own & gathers, -1.0, 0.0).astype(bf16)
            moving = jnp.where(own & (source - HEAD_DIM * odd == target), 1.0, 0.0).astype(bf16)
            picks.append((summing, moving))
        half = count // 2
        lane = lax.broadcasted_iota(jnp.int32, (half, LANES), 1)

        def prepare(at, carry):
            for part in range(2):
                rows = pl.ds(pl.multiple_of((2 * at + part) * half, half), half)
                single_rows = pl.ds(pl.multiple_of(at * half, half), half)
                for head, odd, mixed, grad in (
                    (0, 0, pair_ref[rows, :], pair_grad_ref[rows, :]),
                    (1, 1, pair_ref[rows, :], pair_grad_ref[rows, :]),
                    (2, part, single_ref[single_rows, :], single_grad_ref[single_rows, :]),
                ):
                    summing, moving = picks[odd]
                    product = grad.astype(f32) * mixed.astype(f32)
                    high = product.astype(bf16)
                    low = (product - high.astype(f32)).astype(bf16)
                    shared = jnp.dot(high, summing, preferred_element_type=f32) + jnp.dot(
                        low, summing, preferred_element_type=f32
                    )
                    first_part, second_part, third_part = split_three(shared)
                    moved = jnp.dot(grad, moving, preferred_element_type=f32)
                    moved = jnp.where(lane == HEAD_DIM, first_part.astype(f32), moved)
                    moved = jnp.where(lane == HEAD_DIM + 1, second_part.astype(f32), moved)
                    moved = jnp.where(lane == HEAD_DIM + 2, third_part.astype(f32), moved)
                    grad_heads_ref[head, rows, :] = moved.astype(bf16)
            return carry

        lax.fori_loop(0, seq_len // count, prepare, 0)

    dk_ref[...] = jnp.zeros_like(dk_ref)
    dv_ref[...] = jnp.zeros_like(dv_ref)

    def visit(at, carry):
        rows = pl.ds(pl.multiple_of(at * query_block, query_block), query_block)
        for head in range(heads):
            probs = jnp.exp(times_transposed(k_ref[head], q_ref[head, rows, :]))
            grad_probs = times_transposed(v_ref[head], grad_heads_ref[head, rows, :])
            prob_ref[head] = probs.astype(bf16)
            grad_score_ref[head] = (probs * grad_probs).astype(bf16)
        for head in range(heads):
            dv_ref[head] += jnp.dot(
                prob_ref[head], grad_heads_ref[head, rows, :], preferred_element_type=f32
            )
            dk_ref[head] += jnp.dot(
                grad_score_ref[head], q_ref[head, rows, :], preferred_element_type=f32
            )
            dq_ref[head, rows, :] += contract_rows(grad_score_ref[head], k_ref[head])
        return carry

    lax.fori_loop(bounds_ref[0, step], bounds_ref[1, step], visit, 0)
    lane = lax.broadcasted_iota(jnp.int32, (count, LANES), 1)
    low_half = lane < HEAD_DIM
    here = pl.ds(pl.multiple_of(step * count, count), count)
    k0_ref[here, :] = dk_ref[0].astype(bf16)
    out_ref[here, 256:384] = jnp.where(
        low_half, dk_ref[1], pltpu.roll(dk_ref[2], HEAD_DIM, 1)
    ).astype(bf16)
    out_ref[here, 384:512] = jnp.where(
        low_half, dv_ref[0], pltpu.roll(dv_ref[1], HEAD_DIM, 1)
    ).astype(bf16)
    out_ref[here, 512:576] = dv_ref[2][:, :HEAD_DIM].astype(bf16)

    @pl.when(step == pl.num_programs(0) - 1)
    def _():
        scale = HEAD_DIM**-0.5

        def close(at, carry):
            rows = pl.ds(pl.multiple_of(at * query_block, query_block), query_block)
            low_half = lax.broadcasted_iota(jnp.int32, (query_block, LANES), 1) < HEAD_DIM
            second = pltpu.roll(dq_ref[1, rows, :], HEAD_DIM, 1)
            out_ref[rows, 0:128] = (
                jnp.where(low_half, dq_ref[0, rows, :], second) * scale
            ).astype(bf16)
            first_keys = pltpu.roll(k0_ref[rows, :].astype(f32), HEAD_DIM, 1)
            out_ref[rows, 128:256] = jnp.where(
                low_half, dq_ref[2, rows, :] * scale, first_keys
            ).astype(bf16)
            return carry

        lax.fori_loop(0, blocks, close, 0)


def attend_back(bounds, queries, keys, values, pairs, singles, pair_grads, single_grads, query_block):
    heads, seq_len, _ = queries.shape
    steps = bounds.shape[1]
    block = seq_len // steps
    k_spec = pl.BlockSpec((heads, block, LANES), lambda i, b: (0, i, 0))
    full = pl.BlockSpec((heads, seq_len, LANES), lambda i, b: (0, 0, 0))
    pair = pl.BlockSpec(pairs.shape, lambda i, b: (0, 0))
    single = pl.BlockSpec(singles.shape, lambda i, b: (0, 0))
    return pl.pallas_call(
        partial(attend_back_kernel, query_block),
        grid_spec=pltpu.PrefetchScalarGridSpec(
            num_scalar_prefetch=1,
            grid=(steps,),
            in_specs=[full, k_spec, k_spec, pair, single, pair, single],
            out_specs=pl.BlockSpec((seq_len, 3 * heads * HEAD_DIM), lambda i, b: (0, 0)),
            scratch_shapes=[
                pltpu.VMEM((heads, seq_len, LANES), jnp.bfloat16),
                pltpu.VMEM((heads, seq_len, LANES), jnp.float32),
                pltpu.VMEM((heads, block, LANES), jnp.float32),
                pltpu.VMEM((heads, block, LANES), jnp.float32),
                pltpu.VMEM((seq_len, LANES), jnp.bfloat16),
                pltpu.VMEM((heads, block, query_block), jnp.bfloat16),
                pltpu.VMEM((heads, block, query_block), jnp.bfloat16),
            ],
        ),
        out_shape=jax.ShapeDtypeStruct((seq_len, 3 * heads * HEAD_DIM), jnp.bfloat16),
        name="attend_back",
        cost_estimate=pl.CostEstimate(
            flops=10 * heads * seq_len * seq_len * LANES // 2, transcendentals=heads * seq_len * seq_len // 2,
            bytes_accessed=12 * heads * seq_len * LANES,
        ),
    )(bounds, queries, keys, values, pairs, singles, pair_grads, single_grads)


MESH = pl.DeviceIdType.MESH
PIECES = 8
PIECE_BITS = 3


def rounded_sum(left, right):
    return (left.astype(jnp.float32) + right.astype(jnp.float32)).astype(jnp.bfloat16)


def bit_of(index, bit):
    return lax.rem(index // (1 << bit), 2)


def partner_of(index, bit):
    return index + (1 - 2 * bit_of(index, bit)) * (1 << bit)


def greet(dp_bits, shards):
    barrier = pltpu.get_barrier_semaphore()
    member, here = lax.axis_index("dp"), lax.axis_index("tensor")
    peers = [{"dp": partner_of(member, bit)} for bit in range(dp_bits)]
    peers += [{"tensor": lax.rem(here + way, shards)} for way in range(1, shards)]
    for peer in peers:
        pl.semaphore_signal(barrier, inc=1, device_id=peer, device_id_type=MESH)
    pl.semaphore_wait(barrier, len(peers))


def finish_kernel(
    shards,
    dp_bits,
    grads_ref,
    rows_ref,
    weight_ref,
    gain_ref,
    shift_ref,
    vectors_ref,
    tokens_ref,
    hidden_ref,
    a_keep,
    a_got,
    b_keep,
    b_got,
    tokens_out,
    vectors_out,
    qkv_out,
    weights_out,
    rows_own,
    tokens_own,
    hidden_own,
    part,
    from_left,
    from_right,
    q_wide,
    q_all,
    q_half,
    q_quarter,
    q_got_core,
    q_got_x,
    q_got_y,
    q_got_more,
    v_now,
    v_got,
    v_shards,
    a_sum,
    b_sum,
    a_second,
    b_second,
    pieces,
    pieces_more,
    z_got,
    send,
    recv,
    local,
):
    f32, bf16 = jnp.float32, jnp.bfloat16
    loads = []
    for at, (source, landing) in enumerate(
        ((rows_ref, rows_own), (tokens_ref, tokens_own), (hidden_ref, hidden_own))
    ):
        loads.append(pltpu.make_async_copy(source, landing, local.at[at]))
        loads[-1].start()
    member, here = lax.axis_index("dp"), lax.axis_index("tensor")
    core, x_bit, y_bit = bit_of(member, 0), bit_of(member, 1), bit_of(member, 2)
    own_piece = core * 4 + x_bit * 2 + y_bit
    block = part.shape[1]
    width = part.shape[2]
    columns = grads_ref.shape[1]
    half_rows = weights_out.shape[1] // 2
    last = shards - 1
    gain, shift = (ref[...].reshape(1, width) for ref in (gain_ref, shift_ref))
    slots = iter(range(send.shape[0]))
    pending = []

    def copy_to(src, dst, at, **peer):
        return pltpu.make_async_remote_copy(
            src_ref=src, dst_ref=dst, send_sem=send.at[at], recv_sem=recv.at[at], device_id=peer, device_id_type=MESH
        )

    def start_dp(src, dst, bit, keep=True):
        copy = copy_to(src, dst, next(slots), dp=partner_of(member, bit))
        copy.start()
        if keep:
            pending.append(copy)
        return copy

    greet(dp_bits, shards)

    def add_into(out, left, right):
        def step(at, carry):
            out[at] = rounded_sum(left[at], right[at])
            return carry

        lax.fori_loop(0, out.shape[0], step, 0)

    def sum_pairs(out, left, right):
        def step(at, carry):
            one, two = at // out.shape[1], lax.rem(at, out.shape[1])
            out[one, two] = rounded_sum(left[one, two], right[one, two])
            return carry

        lax.fori_loop(0, out.shape[0] * out.shape[1], step, 0)

    sum_pairs(a_sum, a_keep, a_got)
    sum_pairs(b_sum, b_keep, b_got)
    second_a = start_dp(a_sum.at[1 - y_bit], a_second, 2)
    second_b = start_dp(b_sum.at[1 - x_bit], b_second, 1)

    right_slots = [next(slots) for _ in range(shards)]
    left_slots = [next(slots) for _ in range(shards)]

    def to_right(owner):
        return copy_to(part.at[owner], from_left.at[owner], right_slots[owner], tensor=lax.rem(here + 1, shards))

    def to_left(owner):
        return copy_to(
            part.at[owner], from_right.at[owner], left_slots[owner], tensor=lax.rem(here + last, shards)
        )

    def add_arrived(owner, arrived):
        def step(at, carry):
            rows = pl.ds(pl.multiple_of(at * (block // 4), 16), block // 4)
            part[owner, rows, :] = rounded_sum(part[owner, rows, :], arrived[owner, rows, :])
            return carry

        lax.fori_loop(0, 4, step, 0)

    order = []
    for near in range((shards + 1) // 2):
        for owner in (last - near, near):
            if owner not in order:
                order.append(owner)
    for owner in order:
        product = jnp.dot(
            grads_ref[owner * block : (owner + 1) * block, :], weight_ref[...], preferred_element_type=f32
        )
        part[owner] = product.astype(bf16)
        if owner == last:

            @pl.when(here == 0)
            def _():
                to_right(owner).start()

        if owner == 0:

            @pl.when(here == last)
            def _():
                to_left(owner).start()

    def end_sends():
        for owner in range(last - 1, 0, -1):

            @pl.when(here == 0)
            def _():
                to_right(owner).start()

        for owner in range(1, last):

            @pl.when(here == last)
            def _():
                to_left(owner).start()

    def hop(moved, nth):
        for owner, at, rightward in ((last - nth, moved, True), (nth, last - moved, False)):
            if (at < owner) if rightward else (at > owner):

                @pl.when(here == at)
                def _():
                    copy = to_right(owner) if rightward else to_left(owner)
                    copy.wait_recv()
                    add_arrived(owner, from_left if rightward else from_right)
                    copy.start()

    for load in loads:
        load.wait()
    q_wide[...] = jnp.zeros_like(q_wide)

    def grow(at, carry):
        rows = pl.ds(pl.multiple_of(at * block, 16), block)
        q_wide[...] += contract_rows(grads_ref[rows, :], rows_own[rows, :])
        return carry

    lax.fori_loop(0, shards, grow, 0)
    sums = jnp.dot(jnp.ones((8, grads_ref.shape[0]), bf16), grads_ref[...], preferred_element_type=f32)
    weight = weight_ref[...].astype(f32)
    shift_sum = jnp.dot(
        sums, weight, preferred_element_type=f32, precision=lax.Precision.HIGHEST
    )[0:1]
    gain_sum = jnp.sum(weight * q_wide[...], axis=0, keepdims=True)
    v_now[0] = vectors_ref[...]
    v_now[0, 0:1, :] = (gain_sum - shift * shift_sum) / gain
    v_now[0, 1:2, :] = shift_sum
    v_now[0, pl.ds(12 + here, 1), 0:columns] = sums[0:1]
    count = q_all.shape[1]
    for piece in range(PIECES):
        q_all[piece] = q_wide[piece * count : (piece + 1) * count, :].astype(bf16)

    def vector_stage(bit):
        return start_dp(v_now.at[bit], v_got.at[bit], bit)

    q_core = start_dp(q_all.at[pl.ds((1 - core) * 4, 4)], q_got_core, 0)
    v_copy = vector_stage(0)

    second_a.wait_recv()
    second_b.wait_recv()
    pairs = shards // 2
    for at in range(pairs):
        pieces[at] = rounded_sum(a_sum[y_bit, at], a_second[at])
        pieces[pairs + at] = rounded_sum(b_sum[x_bit, at], b_second[at])
    for bit in range(PIECE_BITS, dp_bits):
        extra = start_dp(pieces, pieces_more.at[bit - PIECE_BITS], bit, False)
        extra.wait_recv()
        extra.wait_send()
        add_into(pieces, pieces, pieces_more.at[bit - PIECE_BITS])
    z_copies = []
    for way in range(1, shards):
        target = lax.rem(here + way, shards)
        copy = copy_to(pieces.at[target], z_got.at[way - 1], next(slots), tensor=target)
        copy.start()
        z_copies.append(copy)
    pending.extend(z_copies)
    end_sends()

    q_core.wait_recv()
    for at in range(4):
        q_half[at] = rounded_sum(q_all[core * 4 + at], q_got_core[at])
    q_x = start_dp(q_half.at[pl.ds((1 - x_bit) * 2, 2)], q_got_x, 1)
    v_copy.wait_recv()
    v_now[1] = v_now[0] + v_got[0]
    v_copy = vector_stage(1)
    hop(1, 0)
    q_x.wait_recv()
    for at in range(2):
        q_quarter[at] = rounded_sum(q_half[x_bit * 2 + at], q_got_x[at])
    q_y = start_dp(q_quarter.at[1 - y_bit], q_got_y, 2)
    v_copy.wait_recv()
    v_now[2] = v_now[1] + v_got[1]
    v_copy = vector_stage(2)
    q_y.wait_recv()
    qkv_out[own_piece] = rounded_sum(q_quarter[y_bit], q_got_y[...])
    v_copy.wait_recv()
    v_now[3] = v_now[2] + v_got[2]
    for bit in range(PIECE_BITS, dp_bits):
        extra = start_dp(qkv_out.at[own_piece], q_got_more.at[bit - PIECE_BITS], bit, False)
        v_copy = vector_stage(bit)
        extra.wait_recv()
        extra.wait_send()
        qkv_out[own_piece] = rounded_sum(qkv_out[own_piece], q_got_more[bit - PIECE_BITS])
        v_copy.wait_recv()
        v_now[bit + 1] = v_now[bit] + v_got[bit]
    v_shards[here] = v_now[dp_bits]
    for way in range(1, shards):
        copy = copy_to(
            v_now.at[dp_bits], v_shards.at[here], next(slots), tensor=lax.rem(here + way, shards)
        )
        copy.start()
        pending.append(copy)
    v_waits = pending[-last:]
    q_back = start_dp(qkv_out.at[own_piece], qkv_out.at[own_piece], 2)
    q_back.wait_recv()
    q_back = start_dp(
        qkv_out.at[pl.ds(core * 4 + x_bit * 2, 2)], qkv_out.at[pl.ds(core * 4 + x_bit * 2, 2)], 1
    )
    q_back.wait_recv()
    q_back = start_dp(qkv_out.at[pl.ds(core * 4, 4)], qkv_out.at[pl.ds(core * 4, 4)], 0)

    for copy in z_copies:
        copy.wait_recv()
    total = pieces[here].astype(f32)
    for way in range(1, shards):
        total = total + z_got[way - 1].astype(f32)
    weights_out[own_piece] = total.astype(bf16)

    def own_half(low, *index):
        rows = pl.ds(0 if low else half_rows, half_rows)
        return weights_out.at[index[0], rows]

    back_a = start_dp(own_half(True, own_piece), own_half(True, own_piece), 2)
    back_b = start_dp(own_half(False, own_piece), own_half(False, own_piece), 1)
    back_a.wait_recv()
    span = pl.ds(core * 4 + x_bit * 2, 2)
    back_a = start_dp(own_half(True, span), own_half(True, span), 1)
    back_b.wait_recv()
    back_c = [
        start_dp(own_half(False, core * 4 + 2 * at + y_bit), own_half(False, core * 4 + 2 * at + y_bit), 2)
        for at in range(2)
    ]
    for moved in range(2, last):
        hop(moved, 0)
    for nth in range(1, last):
        for moved in range(1, last):
            hop(moved, nth)
    back_a.wait_recv()
    for copy in back_c:
        copy.wait_recv()
    span = pl.ds(core * 4, 4)
    back_core = start_dp(weights_out.at[span], weights_out.at[span], 0)

    for copy in v_waits:
        copy.wait_recv()
    vectors_sum = v_shards[0]
    for at in range(1, shards):
        vectors_sum = vectors_sum + v_shards[at]
    vectors_out[...] = vectors_sum

    for owner in range(shards):

        @pl.when(here == owner)
        def _():
            if owner > 0:
                to_right(owner).wait_recv()
                add_arrived(owner, from_left)
            if owner < last:
                to_left(owner).wait_recv()
                add_arrived(owner, from_right)

    def close(at, carry):
        rows = pl.ds(pl.multiple_of(at * (block // 4), 16), block // 4)
        tokens = tokens_own[rows, :].astype(f32)
        centred = tokens - jnp.mean(tokens, axis=1, keepdims=True)
        inverse = lax.rsqrt(jnp.mean(centred * centred, axis=1, keepdims=True) + eps_norm)
        unit = centred * inverse
        scaled = part[here, rows, :].astype(f32) * gain
        inner = (
            scaled
            - jnp.mean(scaled, axis=1, keepdims=True)
            - unit * jnp.mean(scaled * unit, axis=1, keepdims=True)
        )
        tokens_out[rows, :] = hidden_own[rows, :] + inverse * inner
        return carry

    lax.fori_loop(0, 4, close, 0)
    q_back.wait_recv()
    back_core.wait_recv()
    for copy in pending:
        copy.wait_send()
    for owner in range(shards):

        @pl.when(here < owner)
        def _():
            to_right(owner).wait_send()

        @pl.when(here > owner)
        def _():
            to_left(owner).wait_send()


def finish(shards, members, grads, rows, weight, gain, shift, vectors, tokens, grad_hidden, a_keep, a_got, b_keep, b_got):
    dp_bits = members.bit_length() - 1
    assert members == 1 << dp_bits and dp_bits >= PIECE_BITS
    f32, bf16 = jnp.float32, jnp.bfloat16
    seq_len, columns = grads.shape
    block, width = tokens.shape
    piece_rows = a_keep.shape[2]
    count = columns // PIECES
    more = max(1, dp_bits - PIECE_BITS)
    copies = 16 + 2 * shards + 2 * (shards - 1) + 3 * dp_bits
    vm = pltpu.VMEM
    return pl.pallas_call(
        partial(finish_kernel, shards, dp_bits),
        in_specs=[
            pl.BlockSpec(memory_space=pl.ANY if at in (1, 6, 7) else vm) for at in range(12)
        ],
        out_specs=[pl.BlockSpec(memory_space=vm)] * 4,
        out_shape=[
            jax.ShapeDtypeStruct((block, width), f32),
            jax.ShapeDtypeStruct(vectors.shape, f32),
            jax.ShapeDtypeStruct((PIECES, count, width), bf16),
            jax.ShapeDtypeStruct((PIECES, piece_rows, width), bf16),
        ],
        scratch_shapes=[
            vm((seq_len, width), bf16),
            vm((block, width), bf16),
            vm((block, width), f32),
            vm((shards, block, width), bf16),
            vm((shards, block, width), bf16),
            vm((shards, block, width), bf16),
            vm((columns, width), f32),
            vm((PIECES, count, width), bf16),
            vm((4, count, width), bf16),
            vm((2, count, width), bf16),
            vm((4, count, width), bf16),
            vm((2, count, width), bf16),
            vm((count, width), bf16),
            vm((more, count, width), bf16),
            vm((dp_bits + 1,) + vectors.shape, f32),
            vm((dp_bits,) + vectors.shape, f32),
            vm((shards,) + vectors.shape, f32),
            vm(a_keep.shape, bf16),
            vm(b_keep.shape, bf16),
            vm(a_keep.shape[1:], bf16),
            vm(b_keep.shape[1:], bf16),
            vm((shards, piece_rows, width), bf16),
            vm((more, shards, piece_rows, width), bf16),
            vm((shards - 1, piece_rows, width), bf16),
            pltpu.SemaphoreType.DMA((copies,)),
            pltpu.SemaphoreType.DMA((copies,)),
            pltpu.SemaphoreType.DMA((3,)),
        ],
        compiler_params=pltpu.CompilerParams(
            collective_id=1, has_side_effects=True, vmem_limit_bytes=64 * 1024 * 1024 - 2048 * 1024
        ),
        name="finish",
        cost_estimate=pl.CostEstimate(
            flops=4 * seq_len * columns * width, transcendentals=0, bytes_accessed=40 * block * width
        ),
    )(grads, rows, weight, gain, shift, vectors, tokens, grad_hidden, a_keep, a_got, b_keep, b_got)


def unpack_kernel(qkv_ref, weights_ref, totals_ref, fc1_out, fc2_out, proj_out, qkv_out, fc1_bias_out, *vector_outs):
    fc_rows, proj_rows = fc1_out.shape[0], proj_out.shape[0]
    fc1_out[...] = weights_ref[0, :fc_rows].astype(jnp.float32)
    fc2_out[...] = weights_ref[0, fc_rows : 2 * fc_rows].astype(jnp.float32)
    proj_out[...] = weights_ref[0, 2 * fc_rows : 2 * fc_rows + proj_rows].astype(jnp.float32)
    qkv_out[...] = qkv_ref[0].astype(jnp.float32)

    @pl.when(pl.program_id(0) == 0)
    def _():
        width = totals_ref.shape[1]
        for at, out in enumerate(vector_outs):
            out[...] = totals_ref[at : at + 1, :].reshape(width)
        here = lax.axis_index("tensor")
        fc1_bias_out[...] = totals_ref[pl.ds(8 + here, 1), :].reshape(width)


def unpack(qkv, weights, totals, fc_rows, proj_rows):
    f32 = jnp.float32
    _, rows, width = weights.shape
    qkv_rows = qkv.shape[1]
    counts = (fc_rows, fc_rows, proj_rows, qkv_rows)
    vector = pl.BlockSpec((width,), lambda i: (0,))
    return pl.pallas_call(
        unpack_kernel,
        grid=(PIECES,),
        in_specs=[
            pl.BlockSpec((1, qkv_rows, width), lambda i: (i, 0, 0)),
            pl.BlockSpec((1, rows, width), lambda i: (i, 0, 0)),
            pl.BlockSpec(totals.shape, lambda i: (0, 0)),
        ],
        out_specs=[pl.BlockSpec((count, width), lambda i: (i, 0)) for count in counts] + [vector] * 9,
        out_shape=[jax.ShapeDtypeStruct((PIECES * count, width), f32) for count in counts]
        + [jax.ShapeDtypeStruct((width,), f32)] * 9,
        name="unpack",
    )(qkv, weights, totals)


def start_kernel(
    shards,
    dp_bits,
    visit_block,
    tokens_ref,
    ids_ref,
    gain_ref,
    shift_ref,
    qkv_ref,
    qv_bias_ref,
    fc1_ref,
    fc2_ref,
    proj_ref,
    fc1_bias_ref,
    normed_out,
    q_out,
    k_out,
    v_out,
    weights_out,
    bias_out,
    bounds_out,
    blocks,
    q_extra,
    k_extra,
    own,
    chain,
    send,
    recv,
    local,
):
    f32, bf16 = jnp.float32, jnp.bfloat16
    member, here = lax.axis_index("dp"), lax.axis_index("tensor")
    core, x_bit, y_bit = bit_of(member, 0), bit_of(member, 1), bit_of(member, 2)
    own_piece = core * 4 + x_bit * 2 + y_bit
    block, width = tokens_ref.shape
    heads = q_out.shape[0]
    seq_len = ids_ref.shape[1]
    last = shards - 1
    slots = iter(range(send.shape[0]))
    pending = []

    def copy_to(src, dst, at, **peer):
        return pltpu.make_async_remote_copy(
            src_ref=src, dst_ref=dst, send_sem=send.at[at], recv_sem=recv.at[at], device_id=peer, device_id_type=MESH
        )

    def start_dp(src, dst, bit):
        copy = copy_to(src, dst, next(slots), dp=partner_of(member, bit))
        copy.start()
        pending.append(copy)
        return copy

    fc1_rows, fc2_rows, proj_rows = (ref.shape[0] // PIECES for ref in (fc1_ref, fc2_ref, proj_ref))
    loads = []
    for at, (ref, first, count) in enumerate(
        ((fc1_ref, 0, fc1_rows), (fc2_ref, fc1_rows, fc2_rows))
    ):
        rows = pl.ds(pl.multiple_of(own_piece * count, 16), count)
        loads.append(pltpu.make_async_copy(ref.at[rows], own.at[first : first + count], local.at[at]))
        loads[-1].start()
    used = fc1_rows + fc2_rows
    rows = pl.ds(pl.multiple_of(own_piece * proj_rows, 8), proj_rows)
    own[used : used + proj_rows, :] = proj_ref[rows, :]
    used += proj_rows
    own[used:, :] = jnp.zeros((own.shape[0] - used, width), bf16)
    gain, shift = (ref[...].reshape(1, width) for ref in (gain_ref, shift_ref))
    bias_out[here] = fc1_bias_ref[...].reshape(1, width)
    greet(dp_bits, shards)
    for load in loads:
        load.wait()

    chains = {}
    for name, first, rest in (("w", own, chain), ("t", tokens_ref, blocks)):
        chains[name] = (
            first,
            rest,
            [next(slots) for _ in range(shards)],
            [next(slots) for _ in range(shards)],
        )

    def hop_copy(name, owner, rightward, from_own):
        first, rest, right_slots, left_slots = chains[name]
        src = first if from_own else rest.at[owner]
        step = 1 if rightward else last
        at = (right_slots if rightward else left_slots)[owner]
        return copy_to(src, rest.at[owner], at, tensor=lax.rem(here + step, shards))

    def send_own(name, rightward):
        for owner in range(shards):
            if owner != (last if rightward else 0):

                @pl.when(here == owner)
                def _():
                    hop_copy(name, owner, rightward, True).start()

    def hop(name, time, then=None):
        for at in range(shards):
            for rightward, owner, end in ((True, at - time, last), (False, at + time, 0)):
                if 0 <= owner <= last:

                    @pl.when(here == at)
                    def _():
                        hop_copy(name, owner, rightward, False).wait_recv()
                        if at != end:
                            hop_copy(name, owner, rightward, False).start()
                            if then is not None and owner in (0, last):
                                hop_copy(then, at, rightward, True).start()

    send_own("w", True)
    send_own("w", False)

    @pl.when(here == 0)
    def _():
        hop_copy("t", 0, True, True).start()

    @pl.when(here == last)
    def _():
        hop_copy("t", last, False, True).start()

    bias_copies = []
    for way in range(1, shards):
        copy = copy_to(
            bias_out.at[here], bias_out.at[here], next(slots), tensor=lax.rem(here + way, shards)
        )
        copy.start()
        bias_copies.append(copy)
    pending.extend(bias_copies)

    large = -MASKED
    segments = lax.broadcasted_iota(jnp.int32, (8, seq_len), 0)
    same = jnp.where(segments == ids_ref[...], 1.0, 0.0).astype(bf16)
    select = lax.broadcasted_iota(jnp.int32, (8, LANES), 1) - HEAD_DIM == lax.broadcasted_iota(
        jnp.int32, (8, LANES), 0
    )
    matched = contract_rows(same, jnp.where(select, 1.0, 0.0).astype(bf16))
    lane = lax.broadcasted_iota(jnp.int32, (seq_len, LANES), 1)
    segment_lane = (lane >= HEAD_DIM) & (lane < HEAD_DIM + 8)
    ones_lane = (lane >= HEAD_DIM + 8) & (lane < HEAD_DIM + 11)
    q_extra[...] = jnp.where(segment_lane, (matched - 1.0) * large, 0.0).astype(bf16)
    k_extra[...] = jnp.where(ones_lane, 1.0, matched).astype(bf16)
    ids = ids_ref[...]
    groups = bounds_out.shape[1]
    for group in range(groups):
        first = group * (seq_len // groups)
        last_row = first + seq_len // groups - 1
        before = jnp.sum(jnp.where(ids < ids_ref[:, first : first + 1], 1.0, 0.0))
        within = jnp.sum(jnp.where(ids <= ids_ref[:, last_row : last_row + 1], 1.0, 0.0))
        bounds_out[0, group] = before.astype(jnp.int32) // visit_block
        bounds_out[1, group] = (within.astype(jnp.int32) + visit_block - 1) // visit_block
    low_half = lax.broadcasted_iota(jnp.int32, (block, LANES), 1) < HEAD_DIM
    v_lane = lax.broadcasted_iota(jnp.int32, (block, LANES), 1)
    v_extra = jnp.where((v_lane >= HEAD_DIM) & (v_lane < HEAD_DIM + 3), 1.0, 0.0).astype(bf16)

    def project_block(source, owner):
        tokens = source.astype(f32)
        centred = tokens - jnp.mean(tokens, axis=1, keepdims=True)
        inverse = lax.rsqrt(jnp.mean(centred * centred, axis=1, keepdims=True) + eps_norm)
        normed = (centred * inverse * gain + shift).astype(bf16)
        rows = pl.ds(pl.multiple_of(owner * block, 16), block)
        normed_out[rows, :] = normed
        for which, out in ((0, q_out), (1, k_out), (2, v_out)):
            product = times_transposed(normed, qkv_ref[which])
            if which != 1:
                product = product + qv_bias_ref[which // 2 : which // 2 + 1, :]
            if which == 0:
                product = product.astype(bf16).astype(f32) * HEAD_DIM**-0.5
            extra = v_extra if which == 2 else (q_extra if which == 0 else k_extra)[rows, :]
            for head in range(heads):
                first = (head // 2) * LANES
                tile = product[:, first : first + LANES]
                if tile.shape[1] < LANES:
                    blank = jnp.zeros((block, LANES - tile.shape[1]), f32)
                    tile = jnp.concatenate([tile, blank], axis=1)
                if head % 2:
                    tile = pltpu.roll(tile, HEAD_DIM, 1)
                out[head, rows, :] = jnp.where(low_half, tile, extra.astype(f32)).astype(bf16)

    project_block(tokens_ref[...], here)
    for time in range(1, shards):
        hop("w", time, "t")

    half = shards // 2
    out_a = [weights_out.at[own_piece, 0:half]]
    stores = []
    for owner in range(shards):
        at = 2 + owner

        @pl.when(here == owner)
        def _():
            pltpu.make_async_copy(own, weights_out.at[own_piece, owner], local.at[at]).start()

        @pl.when(here != owner)
        def _():
            pltpu.make_async_copy(chain.at[owner], weights_out.at[own_piece, owner], local.at[at]).start()

        stores.append(pltpu.make_async_copy(own, weights_out.at[own_piece, owner], local.at[at]))
    for store in stores:
        store.wait()

    def part(low, pieces):
        owners = pl.ds(0, half) if low else pl.ds(half, shards - half)
        return weights_out.at[pieces, owners]

    def gather_stage(low, pieces, bit):
        return [start_dp(part(low, at), part(low, at), bit) for at in pieces]

    def wait_all(copies):
        for copy in copies:
            copy.wait_recv()

    stage = gather_stage(True, [own_piece], 2) + gather_stage(False, [own_piece], 1)

    def arrived(time):
        for way in (-1, 1):
            owner = here + way * time

            @pl.when((owner >= 0) & (owner <= last))
            def _():
                project_block(blocks[owner], owner)

    for time in range(1, shards):
        hop("t", time)
        if time == 1:
            arrived(time)
            wait_all(stage)
            stage = gather_stage(True, [pl.ds(core * 4 + x_bit * 2, 2)], 1) + gather_stage(
                False, [core * 4 + 2 * at + y_bit for at in range(2)], 2
            )
        elif time == 2:
            arrived(time)
            wait_all(stage)
            stage = [start_dp(weights_out.at[pl.ds(core * 4, 4)], weights_out.at[pl.ds(core * 4, 4)], 0)]
        else:
            arrived(time)
    wait_all(stage)
    wait_all(bias_copies)
    for copy in pending:
        copy.wait_send()
    for name in chains:
        for at in range(shards):
            for owner in range(shards):
                if owner <= at < last:

                    @pl.when(here == at)
                    def _():
                        hop_copy(name, owner, True, False).wait_send()

                if owner >= at > 0:

                    @pl.when(here == at)
                    def _():
                        hop_copy(name, owner, False, False).wait_send()


def start(shards, members, visits, tokens, ids, gain, shift, qkv, qv_bias, fc1, fc2, proj, fc1_bias):
    dp_bits = members.bit_length() - 1
    assert members == 1 << dp_bits and dp_bits >= PIECE_BITS and shards >= 3
    f32, bf16 = jnp.float32, jnp.bfloat16
    block, width = tokens.shape
    seq_len = block * shards
    heads = qkv.shape[1] // HEAD_DIM
    rows = -(-(fc1.shape[0] + fc2.shape[0] + proj.shape[0]) // PIECES // 16) * 16
    copies = 4 * shards + (shards - 1) + 6
    vm = pltpu.VMEM
    on_chip = pl.BlockSpec(memory_space=vm)
    anywhere = pl.BlockSpec(memory_space=pl.ANY)
    head_rows = jax.ShapeDtypeStruct((heads, seq_len, LANES), bf16)
    return pl.pallas_call(
        partial(start_kernel, shards, dp_bits, visits[1]),
        in_specs=[on_chip] * 6 + [anywhere] * 2 + [on_chip] * 2,
        out_specs=[on_chip] * 4 + [anywhere, on_chip, pl.BlockSpec(memory_space=pltpu.SMEM)],
        out_shape=[
            jax.ShapeDtypeStruct((seq_len, width), bf16),
            head_rows,
            head_rows,
            head_rows,
            jax.ShapeDtypeStruct((PIECES, shards, rows, width), bf16),
            jax.ShapeDtypeStruct((shards, 1, width), f32),
            jax.ShapeDtypeStruct((2, visits[0]), jnp.int32),
        ],
        scratch_shapes=[
            vm((shards, block, width), bf16),
            vm((seq_len, LANES), bf16),
            vm((seq_len, LANES), bf16),
            vm((rows, width), bf16),
            vm((shards, rows, width), bf16),
            pltpu.SemaphoreType.DMA((copies,)),
            pltpu.SemaphoreType.DMA((copies,)),
            pltpu.SemaphoreType.DMA((2 + shards,)),
        ],
        compiler_params=pltpu.CompilerParams(collective_id=0, has_side_effects=True),
        name="start",
        cost_estimate=pl.CostEstimate(
            flops=6 * seq_len * width * heads * HEAD_DIM, transcendentals=0, bytes_accessed=40 * block * width
        ),
    )(tokens, ids, gain, shift, qkv, qv_bias, fc1, fc2, proj, fc1_bias)


CHUNK = 32


def middle_kernel(
    shards,
    dp_bits,
    pairs_ref,
    singles_ref,
    weights_ref,
    fc1_bias_ref,
    proj_bias_ref,
    scale_one_ref,
    gain_ref,
    shift_ref,
    fc2_bias_ref,
    scale_two_ref,
    tokens_ref,
    cotangent_ref,
    block_out,
    hidden_grad_out,
    pair_grads_out,
    single_grads_out,
    vectors_out,
    a_keep,
    a_away,
    b_keep,
    b_away,
    weights,
    pairs,
    singles,
    attended,
    proj,
    branch,
    hidden,
    normed,
    wide,
    total,
    active,
    slope,
    grad_pre,
    grad_mlp,
    grad_branch,
    pair_grads,
    single_grads,
    got,
    send,
    recv,
    local,
):
    f32, bf16 = jnp.float32, jnp.bfloat16
    member, here = lax.axis_index("dp"), lax.axis_index("tensor")
    core, x_bit, y_bit = bit_of(member, 0), bit_of(member, 1), bit_of(member, 2)
    block, width = tokens_ref.shape
    columns = width // shards
    half = PIECES // 2
    fc_rows, proj_rows = width // PIECES, columns // PIECES
    proj_first = 2 * fc_rows
    slots = iter(range(send.shape[0]))
    proj_bias, scale_one, gain, shift, fc2_bias, scale_two = (
        ref[...].reshape(1, width)
        for ref in (proj_bias_ref, scale_one_ref, gain_ref, shift_ref, fc2_bias_ref, scale_two_ref)
    )

    def copy_to(src, dst, at, **peer):
        return pltpu.make_async_remote_copy(
            src_ref=src, dst_ref=dst, send_sem=send.at[at], recv_sem=recv.at[at], device_id=peer, device_id_type=MESH
        )

    loads = []
    for owner in range(shards):
        load = pltpu.make_async_copy(weights_ref.at[:, owner], weights.at[:, owner], local.at[owner])
        load.start()
        loads.append(load)
    greet(dp_bits, shards)

    def rows_of(owner, count):
        return pl.ds(pl.multiple_of(owner * count, 16), count)

    copies = []
    for source, landing in ((pairs_ref, pairs), (singles_ref, singles)):
        count = landing.shape[1]
        for way in range(1, shards):
            target = lax.rem(here + way, shards)
            copy = copy_to(source.at[rows_of(target, count)], landing.at[here], next(slots), tensor=target)
            copy.start()
            copies.append(copy)
        landing[here] = source[rows_of(here, count), :]
    for load in loads:
        load.wait()

    def fc1_of(owner):
        return weights[:, owner, :fc_rows, :].reshape(width, width)

    def fc2_of(owner):
        return weights[:, owner, fc_rows:proj_first, :].reshape(width, width)

    def proj_of(owner):
        return weights[:, owner, proj_first : proj_first + proj_rows, :].reshape(columns, width)

    def chunk(at):
        return pl.ds(pl.multiple_of(at * CHUNK, CHUNK), CHUNK)

    def each_chunk(body, init):
        return lax.fori_loop(0, block // CHUNK, body, init)

    def column_sum(value):
        return jnp.sum(value, axis=0, keepdims=True)

    def unit_of(value):
        centred = value - jnp.mean(value, axis=1, keepdims=True)
        inverse = lax.rsqrt(jnp.mean(centred * centred, axis=1, keepdims=True) + eps_norm)
        return centred * inverse, inverse

    third = shards * LANES
    for owner in range(shards):
        own_proj = proj_of(owner)
        proj[owner * LANES : (owner + 1) * LANES, :] = own_proj[:LANES]
        proj[third + owner * HEAD_DIM : third + (owner + 1) * HEAD_DIM, :] = own_proj[LANES:]
    for copy in copies:
        copy.wait_recv()
    middle_row = block // 2
    for owner in range(shards):
        attended[:, owner * LANES : (owner + 1) * LANES] = pairs[owner]
    lane = lax.broadcasted_iota(jnp.int32, (middle_row, LANES), 1)
    low_half = lane < HEAD_DIM

    def swapped(value):
        return pltpu.roll(value, HEAD_DIM, 1)

    for at in range(shards // 2):
        one, two = singles[2 * at].astype(f32), singles[2 * at + 1].astype(f32)
        columns_here = slice(third + at * LANES, third + (at + 1) * LANES)
        attended[:middle_row, columns_here] = jnp.where(low_half, one, swapped(two)).astype(bf16)
        attended[middle_row:, columns_here] = jnp.where(low_half, swapped(one), two).astype(bf16)
    product = jnp.dot(attended[...], proj[...], preferred_element_type=f32)
    branch[...] = product

    def enter(at, carry):
        rows = chunk(at)
        value = branch[rows, :] + proj_bias
        branch[rows, :] = value
        value = tokens_ref[rows, :].astype(f32) + scale_one * value
        hidden[rows, :] = value
        unit, _ = unit_of(value)
        normed[rows, :] = (unit * gain + shift).astype(bf16)
        return carry

    each_chunk(enter, 0)

    def forward(owner, carry):
        wide[:block, :] = jnp.dot(normed[...], fc1_of(owner), preferred_element_type=f32)
        bias = fc1_bias_ref[owner]

        def activate(at, carry):
            rows = chunk(at)
            value = wide[rows, :] + bias
            below = 0.5 * (1.0 + lax.erf(value * 0.5**0.5))
            active[owner, rows, :] = (value * below).astype(bf16)
            density = jnp.exp(value * value * -0.5) * (0.5 / math.pi) ** 0.5
            slope[owner, rows, :] = below + value * density
            return carry

        each_chunk(activate, 0)
        product = jnp.dot(active[owner], fc2_of(owner), preferred_element_type=f32)
        total[...] = jnp.where(owner == 0, product, total[...] + product)
        return carry

    lax.fori_loop(0, shards, forward, 0)
    empty = jnp.zeros((1, width), f32)

    def turn(at, sums):
        rows = chunk(at)
        value = total[rows, :] + fc2_bias
        block_out[rows, :] = (hidden[rows, :] + scale_two * value).astype(bf16)
        grad = cotangent_ref[rows, :].astype(f32)
        grad_mlp[rows, :] = (grad * scale_two).astype(bf16)
        return (
            sums[0] + column_sum(grad * value),
            sums[1] + column_sum(grad_mlp[rows, :].astype(f32)),
        )

    scale_two_sum, fc2_bias_sum = each_chunk(turn, (empty, empty))

    def backward(owner, carry):
        wide[:block, :] = times_transposed(grad_mlp[...], fc2_of(owner))

        def slopes(at, sums):
            rows = chunk(at)
            value = (wide[rows, :] * slope[owner, rows, :]).astype(bf16)
            grad_pre[owner, rows, :] = value
            return sums + column_sum(value.astype(f32))

        vectors_out[pl.ds(8 + owner, 1), :] = each_chunk(slopes, empty)
        product = times_transposed(grad_pre[owner], fc1_of(owner))
        total[...] = jnp.where(owner == 0, product, total[...] + product)
        return carry

    lax.fori_loop(0, shards, backward, 0)

    def leave(at, sums):
        rows = chunk(at)
        grad = total[rows, :]
        unit, inverse = unit_of(hidden[rows, :])
        scaled = grad * gain
        inner = (
            scaled
            - jnp.mean(scaled, axis=1, keepdims=True)
            - unit * jnp.mean(scaled * unit, axis=1, keepdims=True)
        )
        value = cotangent_ref[rows, :].astype(f32) + inverse * inner
        hidden_grad_out[rows, :] = value
        rounded = (value * scale_one).astype(bf16)
        grad_branch[rows, :] = rounded
        return (
            sums[0] + column_sum(grad * unit),
            sums[1] + column_sum(grad),
            sums[2] + column_sum(value * branch[rows, :]),
            sums[3] + column_sum(rounded.astype(f32)),
        )

    gain_sum, shift_sum, scale_one_sum, proj_bias_sum = each_chunk(leave, (empty,) * 4)
    for at, value in enumerate(
        (empty, empty, proj_bias_sum, scale_one_sum, gain_sum, shift_sum, fc2_bias_sum, scale_two_sum)
    ):
        vectors_out[at : at + 1, :] = value
    vectors_out[12:, :] = jnp.zeros((vectors_out.shape[0] - 12, width), f32)

    wide[:block, :] = times_transposed(grad_branch[...], proj[...])
    for owner in range(shards):
        pair_grads[owner] = wide[:block, owner * LANES : (owner + 1) * LANES].astype(bf16)
    for at in range(shards // 2):
        columns_here = slice(third + at * LANES, third + (at + 1) * LANES)
        upper, lower = wide[:middle_row, columns_here], wide[middle_row:block, columns_here]
        single_grads[2 * at] = jnp.where(low_half, upper, swapped(lower)).astype(bf16)
        single_grads[2 * at + 1] = jnp.where(low_half, swapped(upper), lower).astype(bf16)
    back = []
    for source, out in ((pair_grads, pair_grads_out), (single_grads, single_grads_out)):
        for way in range(1, shards):
            target = lax.rem(here + way, shards)
            copy = copy_to(source.at[target], out.at[here], next(slots), tensor=target)
            copy.start()
            back.append(copy)
        out[here] = source[here]

    first_slot = next(slots)

    def core_copy(owner):
        return pltpu.make_async_remote_copy(
            src_ref=weights.at[pl.ds((1 - core) * half, half), owner],
            dst_ref=got.at[:, owner],
            send_sem=send.at[first_slot + owner],
            recv_sem=recv.at[first_slot + owner],
            device_id={"dp": partner_of(member, 0)},
            device_id_type=MESH,
        )

    wide[...] = contract_rows(attended[:, :], grad_branch[...])
    for owner in range(shards):
        for piece in range(PIECES):
            first, end = piece * proj_rows, (piece + 1) * proj_rows
            for low, high, start_row in ((0, LANES, owner * LANES), (LANES, columns, third + owner * HEAD_DIM)):
                begin, stop = max(first, low), min(end, high)
                if begin < stop:
                    rows = slice(start_row + begin - low, start_row + stop - low)
                    to = slice(proj_first + begin - first, proj_first + stop - first)
                    weights[piece, owner, to, :] = wide[rows, :].astype(bf16)

    def weight_grads(owner, carry):
        for left, right, first, count in (
            (normed[...], grad_pre[owner], 0, fc_rows),
            (active[owner], grad_mlp[...], fc_rows, fc_rows),
        ):
            product = contract_rows(left, right).astype(bf16)
            weights[:, owner, first : first + count, :] = product.reshape(PIECES, count, width)
        core_copy(owner).start()
        return carry

    lax.fori_loop(0, shards, weight_grads, 0)
    split = shards // 2
    for owner in range(shards):
        core_copy(owner).wait_recv()
        if owner < split:
            for y in range(2):
                for out, x in ((a_keep, x_bit), (a_away, 1 - x_bit)):
                    out[y, owner] = rounded_sum(weights[core * half + x * 2 + y, owner], got[x * 2 + y, owner])
        else:
            for x in range(2):
                for out, y in ((b_keep, y_bit), (b_away, 1 - y_bit)):
                    out[x, owner - split] = rounded_sum(
                        weights[core * half + x * 2 + y, owner], got[x * 2 + y, owner]
                    )
    for copy in back:
        copy.wait_recv()
    for copy in copies + back:
        copy.wait_send()
    for owner in range(shards):
        core_copy(owner).wait_send()


def middle(shards, members, pairs, singles, weights, fc1_bias, vectors, tokens, cotangent):
    dp_bits = members.bit_length() - 1
    f32, bf16 = jnp.float32, jnp.bfloat16
    block, width = tokens.shape
    rows = weights.shape[2]
    vm = pltpu.VMEM
    on_chip = pl.BlockSpec(memory_space=vm)
    quarter = jax.ShapeDtypeStruct((2, shards // 2, rows, width), bf16)
    copies = 4 * (shards - 1) + shards
    return pl.pallas_call(
        partial(middle_kernel, shards, dp_bits),
        in_specs=[on_chip, on_chip, pl.BlockSpec(memory_space=pl.ANY)] + [on_chip] * 9,
        out_specs=[on_chip] * 9,
        out_shape=[
            jax.ShapeDtypeStruct((block, width), bf16),
            jax.ShapeDtypeStruct((block, width), f32),
            jax.ShapeDtypeStruct((shards, block, LANES), bf16),
            jax.ShapeDtypeStruct((shards, block // 2, LANES), bf16),
            jax.ShapeDtypeStruct((16, width), f32),
            quarter,
            quarter,
            quarter,
            quarter,
        ],
        scratch_shapes=[
            vm(weights.shape, bf16),
            vm((shards, block, LANES), bf16),
            vm((shards, block // 2, LANES), bf16),
            vm((block, width), bf16),
            vm((width, width), bf16),
            vm((block, width), f32),
            vm((block, width), f32),
            vm((block, width), bf16),
            vm((width, width), f32),
            vm((block, width), f32),
            vm((shards, block, width), bf16),
            vm((shards, block, width), f32),
            vm((shards, block, width), bf16),
            vm((block, width), bf16),
            vm((block, width), bf16),
            vm((shards, block, LANES), bf16),
            vm((shards, block // 2, LANES), bf16),
            vm((PIECES // 2, shards, rows, width), bf16),
            pltpu.SemaphoreType.DMA((copies,)),
            pltpu.SemaphoreType.DMA((copies,)),
            pltpu.SemaphoreType.DMA((shards,)),
        ],
        compiler_params=pltpu.CompilerParams(
            collective_id=2, has_side_effects=True, vmem_limit_bytes=62 * 1024 * 1024
        ),
        name="middle",
        cost_estimate=pl.CostEstimate(
            flops=12 * block * width * width * shards, transcendentals=0, bytes_accessed=40 * block * width
        ),
    )(pairs, singles, weights, fc1_bias, *vectors, tokens, cotangent)


eps_norm = 1e-06


def on_device(
    shards,
    members,
    tokens,
    segment_ids,
    ln1_gain,
    ln1_bias,
    qkv_weight,
    qv_bias,
    proj_weight,
    proj_bias,
    scale_one,
    ln2_gain,
    ln2_bias,
    fc1_weight,
    fc1_bias,
    fc2_weight,
    fc2_bias,
    scale_two,
    cotangent,
):
    f32, bf16 = jnp.float32, jnp.bfloat16
    seq_len = segment_ids.shape[1]
    rows_here, width = tokens.shape
    head_columns = qkv_weight.shape[2]
    heads = head_columns // HEAD_DIM
    hidden_here = fc1_weight.shape[1]
    ids = segment_ids[0]
    here = lax.axis_index("tensor")

    visits = (shards, seq_len // 6)
    turned = qkv_weight.transpose(0, 2, 1)
    full_one, queries, keys, values, gathered, fc1_bias_full, bounds = start(
        shards,
        members,
        visits,
        tokens,
        segment_ids,
        ln1_gain,
        ln1_bias,
        turned,
        qv_bias,
        fc1_weight,
        fc2_weight,
        proj_weight,
        fc1_bias,
    )
    pairs, singles, queries_back = attend(bounds, queries, keys, values, visits[1])

    params = (proj_bias, scale_one, ln2_gain, ln2_bias, fc2_bias, scale_two)
    block_out, grad_hidden, pair_grads, single_grads, vectors, a_keep, a_away, b_keep, b_away = middle(
        shards, members, pairs, singles, gathered, fc1_bias_full, params, tokens, cotangent
    )
    pair_grads = pair_grads.reshape(seq_len, LANES)
    single_grads = single_grads.reshape(seq_len // 2, LANES)

    def swap(value, bit):
        return lax.ppermute(value, "dp", [(j, j ^ (1 << bit)) for j in range(members)])

    a_got, b_got = swap(a_away, 1), swap(b_away, 2)
    grad_heads = attend_back(bounds, queries_back, keys, values, pairs, singles, pair_grads, single_grads, visits[1])
    grad_tokens, totals, qkv_pieces, weight_pieces = finish(
        shards,
        members,
        grad_heads,
        full_one,
        turned.reshape(3 * head_columns, width),
        ln1_gain,
        ln1_bias,
        vectors,
        tokens,
        grad_hidden,
        a_keep,
        a_got,
        b_keep,
        b_got,
    )
    fc1_grad, fc2_grad, proj_grad, qkv_grad, fc1_bias_grad, *sums = unpack(
        qkv_pieces, weight_pieces, totals, width // PIECES, head_columns // PIECES
    )
    qkv_grad = qkv_grad.reshape(3, head_columns, width).transpose(0, 2, 1)
    qv_sums = lax.dynamic_index_in_dim(totals, 12 + here, 0, keepdims=False)
    qv_grad = jnp.stack([qv_sums[:head_columns], qv_sums[2 * head_columns : 3 * head_columns]])
    return (
        block_out,
        grad_tokens,
        sums[0],
        sums[1],
        qkv_grad,
        qv_grad,
        proj_grad,
        sums[2],
        sums[3],
        sums[4],
        sums[5],
        fc1_grad,
        fc1_bias_grad,
        fc2_grad,
        sums[6],
        sums[7],
    )


def solution(mesh):
    rows = P(("dp", "tensor"), None)
    columns = P(None, "tensor")
    return jax.shard_map(
        partial(on_device, mesh.shape["tensor"], mesh.shape["dp"]),
        mesh=mesh,
        in_specs=(
            rows,
            P("dp", None),
            P(),
            P(),
            P(None, None, "tensor"),
            columns,
            P("tensor", None),
            P(),
            P(),
            P(),
            P(),
            columns,
            P("tensor"),
            P("tensor", None),
            P(),
            P(),
            rows,
        ),
        out_specs=(
            rows,
            rows,
            P(),
            P(),
            P(None, None, "tensor"),
            columns,
            P("tensor", None),
            P(),
            P(),
            P(),
            P(),
            columns,
            P("tensor"),
            P("tensor", None),
            P(),
            P(),
        ),
        check_vma=False,
    )
```

```python
from functools import partial
import math

import jax, jax.numpy as jnp
from jax import lax
from jax.experimental import pallas as pl
from jax.experimental.pallas import tpu as pltpu

from jax.sharding import PartitionSpec as P

HEAD_DIM = 64
LANES = 128
MOST_TOKENS = 1152
MASKED = -(2.0**100)


def contract_rows(left, right):
    return lax.dot_general(left, right, (((0,), (0,)), ((), ())), preferred_element_type=jnp.float32)


def times_transposed(left, right, precision=None):
    return lax.dot_general(
        left, right, (((1,), (1,)), ((), ())), preferred_element_type=jnp.float32, precision=precision
    )


def split_three(value):
    high = value.astype(jnp.bfloat16)
    rest = value - high.astype(jnp.float32)
    middle = rest.astype(jnp.bfloat16)
    low = (rest - middle.astype(jnp.float32)).astype(jnp.bfloat16)
    return (high, middle, low)


def join_lanes(low, high):
    lane = lax.broadcasted_iota(jnp.int32, low.shape, 1)
    return jnp.where(lane < HEAD_DIM, low, pltpu.roll(high, HEAD_DIM, 1))


def attend_back_kernel(
    query_block,
    bounds_ref,
    q_ref,
    k_ref,
    v_ref,
    pair_ref,
    single_ref,
    pair_grad_ref,
    single_grad_ref,
    out_ref,
    grad_heads_ref,
    dq_ref,
    dk_ref,
    dv_ref,
    k0_ref,
    prob_ref,
    grad_score_ref,
):
    f32, bf16 = jnp.float32, jnp.bfloat16
    step = pl.program_id(0)
    heads, count, _ = k_ref.shape
    seq_len = q_ref.shape[1]
    blocks = seq_len // query_block

    @pl.when(step == 0)
    def _():
        dq_ref[...] = jnp.zeros_like(dq_ref)
        source = lax.broadcasted_iota(jnp.int32, (LANES, LANES), 0)
        target = lax.broadcasted_iota(jnp.int32, (LANES, LANES), 1)
        gathers = (target >= HEAD_DIM) & (target < HEAD_DIM + 3)
        picks = []
        for odd in range(2):
            own = (source >= HEAD_DIM * odd) & (source < HEAD_DIM * (odd + 1))
            summing = jnp.where(own & gathers, -1.0, 0.0).astype(bf16)
            moving = jnp.where(own & (source - HEAD_DIM * odd == target), 1.0, 0.0).astype(bf16)
            picks.append((summing, moving))
        half = count // 2
        lane = lax.broadcasted_iota(jnp.int32, (half, LANES), 1)

        def prepare(at, carry):
            for part in range(2):
                rows = pl.ds(pl.multiple_of((2 * at + part) * half, half), half)
                single_rows = pl.ds(pl.multiple_of(at * half, half), half)
                for head, odd, mixed, grad in (
                    (0, 0, pair_ref[rows, :], pair_grad_ref[rows, :]),
                    (1, 1, pair_ref[rows, :], pair_grad_ref[rows, :]),
                    (2, part, single_ref[single_rows, :], single_grad_ref[single_rows, :]),
                ):
                    summing, moving = picks[odd]
                    product = grad.astype(f32) * mixed.astype(f32)
                    high = product.astype(bf16)
                    low = (product - high.astype(f32)).astype(bf16)
                    shared = jnp.dot(high, summing, preferred_element_type=f32) + jnp.dot(
                        low, summing, preferred_element_type=f32
                    )
                    first_part, second_part, third_part = split_three(shared)
                    moved = jnp.dot(grad, moving, preferred_element_type=f32)
                    moved = jnp.where(lane == HEAD_DIM, first_part.astype(f32), moved)
                    moved = jnp.where(lane == HEAD_DIM + 1, second_part.astype(f32), moved)
                    moved = jnp.where(lane == HEAD_DIM + 2, third_part.astype(f32), moved)
                    grad_heads_ref[head, rows, :] = moved.astype(bf16)
            return carry

        lax.fori_loop(0, seq_len // count, prepare, 0)

    dk_ref[...] = jnp.zeros_like(dk_ref)
    dv_ref[...] = jnp.zeros_like(dv_ref)

    def visit(at, carry):
        rows = pl.ds(pl.multiple_of(at * query_block, query_block), query_block)
        for head in range(heads):
            probs = jnp.exp(times_transposed(k_ref[head], q_ref[head, rows, :]))
            grad_probs = times_transposed(v_ref[head], grad_heads_ref[head, rows, :])
            prob_ref[head] = probs.astype(bf16)
            grad_score_ref[head] = (probs * grad_probs).astype(bf16)
        for head in range(heads):
            dv_ref[head] += jnp.dot(
                prob_ref[head], grad_heads_ref[head, rows, :], preferred_element_type=f32
            )
            dk_ref[head] += jnp.dot(
                grad_score_ref[head], q_ref[head, rows, :], preferred_element_type=f32
            )
            dq_ref[head, rows, :] += contract_rows(grad_score_ref[head], k_ref[head])
        return carry

    lax.fori_loop(bounds_ref[0, step], bounds_ref[1, step], visit, 0)
    lane = lax.broadcasted_iota(jnp.int32, (count, LANES), 1)
    low_half = lane < HEAD_DIM
    here = pl.ds(pl.multiple_of(step * count, count), count)
    k0_ref[here, :] = dk_ref[0].astype(bf16)
    out_ref[here, 256:384] = jnp.where(
        low_half, dk_ref[1], pltpu.roll(dk_ref[2], HEAD_DIM, 1)
    ).astype(bf16)
    out_ref[here, 384:512] = jnp.where(
        low_half, dv_ref[0], pltpu.roll(dv_ref[1], HEAD_DIM, 1)
    ).astype(bf16)
    out_ref[here, 512:576] = dv_ref[2][:, :HEAD_DIM].astype(bf16)

    @pl.when(step == pl.num_programs(0) - 1)
    def _():
        scale = HEAD_DIM**-0.5

        def close(at, carry):
            rows = pl.ds(pl.multiple_of(at * query_block, query_block), query_block)
            low_half = lax.broadcasted_iota(jnp.int32, (query_block, LANES), 1) < HEAD_DIM
            second = pltpu.roll(dq_ref[1, rows, :], HEAD_DIM, 1)
            out_ref[rows, 0:128] = (
                jnp.where(low_half, dq_ref[0, rows, :], second) * scale
            ).astype(bf16)
            first_keys = pltpu.roll(k0_ref[rows, :].astype(f32), HEAD_DIM, 1)
            out_ref[rows, 128:256] = jnp.where(
                low_half, dq_ref[2, rows, :] * scale, first_keys
            ).astype(bf16)
            return carry

        lax.fori_loop(0, blocks, close, 0)


def attend_back(bounds, queries, keys, values, pairs, singles, pair_grads, single_grads, query_block):
    heads, seq_len, _ = queries.shape
    steps = bounds.shape[1]
    block = seq_len // steps
    k_spec = pl.BlockSpec((heads, block, LANES), lambda i, b: (0, i, 0))
    full = pl.BlockSpec((heads, seq_len, LANES), lambda i, b: (0, 0, 0))
    pair = pl.BlockSpec(pairs.shape, lambda i, b: (0, 0))
    single = pl.BlockSpec(singles.shape, lambda i, b: (0, 0))
    return pl.pallas_call(
        partial(attend_back_kernel, query_block),
        grid_spec=pltpu.PrefetchScalarGridSpec(
            num_scalar_prefetch=1,
            grid=(steps,),
            in_specs=[full, k_spec, k_spec, pair, single, pair, single],
            out_specs=pl.BlockSpec((seq_len, 3 * heads * HEAD_DIM), lambda i, b: (0, 0)),
            scratch_shapes=[
                pltpu.VMEM((heads, seq_len, LANES), jnp.bfloat16),
                pltpu.VMEM((heads, seq_len, LANES), jnp.float32),
                pltpu.VMEM((heads, block, LANES), jnp.float32),
                pltpu.VMEM((heads, block, LANES), jnp.float32),
                pltpu.VMEM((seq_len, LANES), jnp.bfloat16),
                pltpu.VMEM((heads, block, query_block), jnp.bfloat16),
                pltpu.VMEM((heads, block, query_block), jnp.bfloat16),
            ],
        ),
        out_shape=jax.ShapeDtypeStruct((seq_len, 3 * heads * HEAD_DIM), jnp.bfloat16),
        name="attend_back",
        cost_estimate=pl.CostEstimate(
            flops=10 * heads * seq_len * seq_len * LANES // 2, transcendentals=heads * seq_len * seq_len // 2,
            bytes_accessed=12 * heads * seq_len * LANES,
        ),
    )(bounds, queries, keys, values, pairs, singles, pair_grads, single_grads)


MESH = pl.DeviceIdType.MESH
PIECES = 8
PIECE_BITS = 3


def rounded_sum(left, right):
    return (left.astype(jnp.float32) + right.astype(jnp.float32)).astype(jnp.bfloat16)


def bit_of(index, bit):
    return lax.rem(index // (1 << bit), 2)


def partner_of(index, bit):
    return index + (1 - 2 * bit_of(index, bit)) * (1 << bit)


def greet(dp_bits, shards):
    barrier = pltpu.get_barrier_semaphore()
    member, here = lax.axis_index("dp"), lax.axis_index("tensor")
    peers = [{"dp": partner_of(member, bit)} for bit in range(dp_bits)]
    peers += [{"tensor": lax.rem(here + way, shards)} for way in range(1, shards)]
    for peer in peers:
        pl.semaphore_signal(barrier, inc=1, device_id=peer, device_id_type=MESH)
    pl.semaphore_wait(barrier, len(peers))


def finish_kernel(
    shards,
    dp_bits,
    grads_ref,
    rows_ref,
    weight_ref,
    gain_ref,
    shift_ref,
    vectors_ref,
    tokens_ref,
    hidden_ref,
    a_keep,
    a_got,
    b_keep,
    b_got,
    tokens_out,
    vectors_out,
    qkv_out,
    weights_out,
    rows_own,
    tokens_own,
    hidden_own,
    part,
    from_left,
    from_right,
    q_wide,
    q_all,
    q_half,
    q_quarter,
    q_got_core,
    q_got_x,
    q_got_y,
    q_got_more,
    v_now,
    v_got,
    v_shards,
    a_sum,
    b_sum,
    a_second,
    b_second,
    pieces,
    pieces_more,
    z_got,
    send,
    recv,
    local,
):
    f32, bf16 = jnp.float32, jnp.bfloat16
    loads = []
    for at, (source, landing) in enumerate(
        ((rows_ref, rows_own), (tokens_ref, tokens_own), (hidden_ref, hidden_own))
    ):
        loads.append(pltpu.make_async_copy(source, landing, local.at[at]))
        loads[-1].start()
    member, here = lax.axis_index("dp"), lax.axis_index("tensor")
    core, x_bit, y_bit = bit_of(member, 0), bit_of(member, 1), bit_of(member, 2)
    own_piece = core * 4 + x_bit * 2 + y_bit
    block = part.shape[1]
    width = part.shape[2]
    columns = grads_ref.shape[1]
    half_rows = weights_out.shape[1] // 2
    last = shards - 1
    gain, shift = (ref[...].reshape(1, width) for ref in (gain_ref, shift_ref))
    slots = iter(range(send.shape[0]))
    pending = []

    def copy_to(src, dst, at, **peer):
        return pltpu.make_async_remote_copy(
            src_ref=src, dst_ref=dst, send_sem=send.at[at], recv_sem=recv.at[at], device_id=peer, device_id_type=MESH
        )

    def start_dp(src, dst, bit, keep=True):
        copy = copy_to(src, dst, next(slots), dp=partner_of(member, bit))
        copy.start()
        if keep:
            pending.append(copy)
        return copy

    greet(dp_bits, shards)

    def add_into(out, left, right):
        def step(at, carry):
            out[at] = rounded_sum(left[at], right[at])
            return carry

        lax.fori_loop(0, out.shape[0], step, 0)

    def sum_pairs(out, left, right):
        def step(at, carry):
            one, two = at // out.shape[1], lax.rem(at, out.shape[1])
            out[one, two] = rounded_sum(left[one, two], right[one, two])
            return carry

        lax.fori_loop(0, out.shape[0] * out.shape[1], step, 0)

    sum_pairs(a_sum, a_keep, a_got)
    sum_pairs(b_sum, b_keep, b_got)
    second_a = start_dp(a_sum.at[1 - y_bit], a_second, 2)
    second_b = start_dp(b_sum.at[1 - x_bit], b_second, 1)

    right_slots = [next(slots) for _ in range(shards)]
    left_slots = [next(slots) for _ in range(shards)]

    def to_right(owner):
        return copy_to(part.at[owner], from_left.at[owner], right_slots[owner], tensor=lax.rem(here + 1, shards))

    def to_left(owner):
        return copy_to(
            part.at[owner], from_right.at[owner], left_slots[owner], tensor=lax.rem(here + last, shards)
        )

    def add_arrived(owner, arrived):
        def step(at, carry):
            rows = pl.ds(pl.multiple_of(at * (block // 4), 16), block // 4)
            part[owner, rows, :] = rounded_sum(part[owner, rows, :], arrived[owner, rows, :])
            return carry

        lax.fori_loop(0, 4, step, 0)

    order = []
    for near in range((shards + 1) // 2):
        for owner in (last - near, near):
            if owner not in order:
                order.append(owner)
    for owner in order:
        product = jnp.dot(
            grads_ref[owner * block : (owner + 1) * block, :], weight_ref[...], preferred_element_type=f32
        )
        part[owner] = product.astype(bf16)
        if owner == last:

            @pl.when(here == 0)
            def _():
                to_right(owner).start()

        if owner == 0:

            @pl.when(here == last)
            def _():
                to_left(owner).start()

    def end_sends():
        for owner in range(last - 1, 0, -1):

            @pl.when(here == 0)
            def _():
                to_right(owner).start()

        for owner in range(1, last):

            @pl.when(here == last)
            def _():
                to_left(owner).start()

    def hop(moved, nth):
        for owner, at, rightward in ((last - nth, moved, True), (nth, last - moved, False)):
            if (at < owner) if rightward else (at > owner):

                @pl.when(here == at)
                def _():
                    copy = to_right(owner) if rightward else to_left(owner)
                    copy.wait_recv()
                    add_arrived(owner, from_left if rightward else from_right)
                    copy.start()

    for load in loads:
        load.wait()
    q_wide[...] = jnp.zeros_like(q_wide)

    def grow(at, carry):
        rows = pl.ds(pl.multiple_of(at * block, 16), block)
        q_wide[...] += contract_rows(grads_ref[rows, :], rows_own[rows, :])
        return carry

    lax.fori_loop(0, shards, grow, 0)
    sums = jnp.dot(jnp.ones((8, grads_ref.shape[0]), bf16), grads_ref[...], preferred_element_type=f32)
    weight = weight_ref[...].astype(f32)
    shift_sum = jnp.dot(
        sums, weight, preferred_element_type=f32, precision=lax.Precision.HIGHEST
    )[0:1]
    gain_sum = jnp.sum(weight * q_wide[...], axis=0, keepdims=True)
    v_now[0] = vectors_ref[...]
    v_now[0, 0:1, :] = (gain_sum - shift * shift_sum) / gain
    v_now[0, 1:2, :] = shift_sum
    v_now[0, pl.ds(12 + here, 1), 0:columns] = sums[0:1]
    count = q_all.shape[1]
    for piece in range(PIECES):
        q_all[piece] = q_wide[piece * count : (piece + 1) * count, :].astype(bf16)

    def vector_stage(bit):
        return start_dp(v_now.at[bit], v_got.at[bit], bit)

    q_core = start_dp(q_all.at[pl.ds((1 - core) * 4, 4)], q_got_core, 0)
    v_copy = vector_stage(0)

    second_a.wait_recv()
    second_b.wait_recv()
    pairs = shards // 2
    for at in range(pairs):
        pieces[at] = rounded_sum(a_sum[y_bit, at], a_second[at])
        pieces[pairs + at] = rounded_sum(b_sum[x_bit, at], b_second[at])
    for bit in range(PIECE_BITS, dp_bits):
        extra = start_dp(pieces, pieces_more.at[bit - PIECE_BITS], bit, False)
        extra.wait_recv()
        extra.wait_send()
        add_into(pieces, pieces, pieces_more.at[bit - PIECE_BITS])
    z_copies = []
    for way in range(1, shards):
        target = lax.rem(here + way, shards)
        copy = copy_to(pieces.at[target], z_got.at[way - 1], next(slots), tensor=target)
        copy.start()
        z_copies.append(copy)
    pending.extend(z_copies)
    end_sends()

    q_core.wait_recv()
    for at in range(4):
        q_half[at] = rounded_sum(q_all[core * 4 + at], q_got_core[at])
    q_x = start_dp(q_half.at[pl.ds((1 - x_bit) * 2, 2)], q_got_x, 1)
    v_copy.wait_recv()
    v_now[1] = v_now[0] + v_got[0]
    v_copy = vector_stage(1)
    hop(1, 0)
    q_x.wait_recv()
    for at in range(2):
        q_quarter[at] = rounded_sum(q_half[x_bit * 2 + at], q_got_x[at])
    q_y = start_dp(q_quarter.at[1 - y_bit], q_got_y, 2)
    v_copy.wait_recv()
    v_now[2] = v_now[1] + v_got[1]
    v_copy = vector_stage(2)
    q_y.wait_recv()
    qkv_out[own_piece] = rounded_sum(q_quarter[y_bit], q_got_y[...])
    v_copy.wait_recv()
    v_now[3] = v_now[2] + v_got[2]
    for bit in range(PIECE_BITS, dp_bits):
        extra = start_dp(qkv_out.at[own_piece], q_got_more.at[bit - PIECE_BITS], bit, False)
        v_copy = vector_stage(bit)
        extra.wait_recv()
        extra.wait_send()
        qkv_out[own_piece] = rounded_sum(qkv_out[own_piece], q_got_more[bit - PIECE_BITS])
        v_copy.wait_recv()
        v_now[bit + 1] = v_now[bit] + v_got[bit]
    v_shards[here] = v_now[dp_bits]
    for way in range(1, shards):
        copy = copy_to(
            v_now.at[dp_bits], v_shards.at[here], next(slots), tensor=lax.rem(here + way, shards)
        )
        copy.start()
        pending.append(copy)
    v_waits = pending[-last:]
    q_back = start_dp(qkv_out.at[own_piece], qkv_out.at[own_piece], 2)
    q_back.wait_recv()
    q_back = start_dp(
        qkv_out.at[pl.ds(core * 4 + x_bit * 2, 2)], qkv_out.at[pl.ds(core * 4 + x_bit * 2, 2)], 1
    )
    q_back.wait_recv()
    q_back = start_dp(qkv_out.at[pl.ds(core * 4, 4)], qkv_out.at[pl.ds(core * 4, 4)], 0)

    for copy in z_copies:
        copy.wait_recv()
    total = pieces[here].astype(f32)
    for way in range(1, shards):
        total = total + z_got[way - 1].astype(f32)
    weights_out[own_piece] = total.astype(bf16)

    def own_half(low, *index):
        rows = pl.ds(0 if low else half_rows, half_rows)
        return weights_out.at[index[0], rows]

    back_a = start_dp(own_half(True, own_piece), own_half(True, own_piece), 2)
    back_b = start_dp(own_half(False, own_piece), own_half(False, own_piece), 1)
    back_a.wait_recv()
    span = pl.ds(core * 4 + x_bit * 2, 2)
    back_a = start_dp(own_half(True, span), own_half(True, span), 1)
    back_b.wait_recv()
    back_c = [
        start_dp(own_half(False, core * 4 + 2 * at + y_bit), own_half(False, core * 4 + 2 * at + y_bit), 2)
        for at in range(2)
    ]
    for moved in range(2, last):
        hop(moved, 0)
    for nth in range(1, last):
        for moved in range(1, last):
            hop(moved, nth)
    back_a.wait_recv()
    for copy in back_c:
        copy.wait_recv()
    span = pl.ds(core * 4, 4)
    back_core = start_dp(weights_out.at[span], weights_out.at[span], 0)

    for copy in v_waits:
        copy.wait_recv()
    vectors_sum = v_shards[0]
    for at in range(1, shards):
        vectors_sum = vectors_sum + v_shards[at]
    vectors_out[...] = vectors_sum

    for owner in range(shards):

        @pl.when(here == owner)
        def _():
            if owner > 0:
                to_right(owner).wait_recv()
                add_arrived(owner, from_left)
            if owner < last:
                to_left(owner).wait_recv()
                add_arrived(owner, from_right)

    def close(at, carry):
        rows = pl.ds(pl.multiple_of(at * (block // 4), 16), block // 4)
        tokens = tokens_own[rows, :].astype(f32)
        centred = tokens - jnp.mean(tokens, axis=1, keepdims=True)
        inverse = lax.rsqrt(jnp.mean(centred * centred, axis=1, keepdims=True) + eps_norm)
        unit = centred * inverse
        scaled = part[here, rows, :].astype(f32) * gain
        inner = (
            scaled
            - jnp.mean(scaled, axis=1, keepdims=True)
            - unit * jnp.mean(scaled * unit, axis=1, keepdims=True)
        )
        tokens_out[rows, :] = hidden_own[rows, :] + inverse * inner
        return carry

    lax.fori_loop(0, 4, close, 0)
    q_back.wait_recv()
    back_core.wait_recv()
    for copy in pending:
        copy.wait_send()
    for owner in range(shards):

        @pl.when(here < owner)
        def _():
            to_right(owner).wait_send()

        @pl.when(here > owner)
        def _():
            to_left(owner).wait_send()


def finish(shards, members, grads, rows, weight, gain, shift, vectors, tokens, grad_hidden, a_keep, a_got, b_keep, b_got):
    dp_bits = members.bit_length() - 1
    assert members == 1 << dp_bits and dp_bits >= PIECE_BITS
    f32, bf16 = jnp.float32, jnp.bfloat16
    seq_len, columns = grads.shape
    block, width = tokens.shape
    piece_rows = a_keep.shape[2]
    count = columns // PIECES
    more = max(1, dp_bits - PIECE_BITS)
    copies = 16 + 2 * shards + 2 * (shards - 1) + 3 * dp_bits
    vm = pltpu.VMEM
    return pl.pallas_call(
        partial(finish_kernel, shards, dp_bits),
        in_specs=[
            pl.BlockSpec(memory_space=pl.ANY if at in (1, 6, 7) else vm) for at in range(12)
        ],
        out_specs=[pl.BlockSpec(memory_space=vm)] * 4,
        out_shape=[
            jax.ShapeDtypeStruct((block, width), f32),
            jax.ShapeDtypeStruct(vectors.shape, f32),
            jax.ShapeDtypeStruct((PIECES, count, width), bf16),
            jax.ShapeDtypeStruct((PIECES, piece_rows, width), bf16),
        ],
        scratch_shapes=[
            vm((seq_len, width), bf16),
            vm((block, width), bf16),
            vm((block, width), f32),
            vm((shards, block, width), bf16),
            vm((shards, block, width), bf16),
            vm((shards, block, width), bf16),
            vm((columns, width), f32),
            vm((PIECES, count, width), bf16),
            vm((4, count, width), bf16),
            vm((2, count, width), bf16),
            vm((4, count, width), bf16),
            vm((2, count, width), bf16),
            vm((count, width), bf16),
            vm((more, count, width), bf16),
            vm((dp_bits + 1,) + vectors.shape, f32),
            vm((dp_bits,) + vectors.shape, f32),
            vm((shards,) + vectors.shape, f32),
            vm(a_keep.shape, bf16),
            vm(b_keep.shape, bf16),
            vm(a_keep.shape[1:], bf16),
            vm(b_keep.shape[1:], bf16),
            vm((shards, piece_rows, width), bf16),
            vm((more, shards, piece_rows, width), bf16),
            vm((shards - 1, piece_rows, width), bf16),
            pltpu.SemaphoreType.DMA((copies,)),
            pltpu.SemaphoreType.DMA((copies,)),
            pltpu.SemaphoreType.DMA((3,)),
        ],
        compiler_params=pltpu.CompilerParams(
            collective_id=1, has_side_effects=True, vmem_limit_bytes=64 * 1024 * 1024 - 2048 * 1024
        ),
        name="finish",
        cost_estimate=pl.CostEstimate(
            flops=4 * seq_len * columns * width, transcendentals=0, bytes_accessed=40 * block * width
        ),
    )(grads, rows, weight, gain, shift, vectors, tokens, grad_hidden, a_keep, a_got, b_keep, b_got)


def unpack_kernel(qkv_ref, weights_ref, totals_ref, fc1_out, fc2_out, proj_out, qkv_out, fc1_bias_out, *vector_outs):
    fc_rows, proj_rows = fc1_out.shape[0], proj_out.shape[0]
    fc1_out[...] = weights_ref[0, :fc_rows].astype(jnp.float32)
    fc2_out[...] = weights_ref[0, fc_rows : 2 * fc_rows].astype(jnp.float32)
    proj_out[...] = weights_ref[0, 2 * fc_rows : 2 * fc_rows + proj_rows].astype(jnp.float32)
    qkv_out[...] = qkv_ref[0].astype(jnp.float32)

    @pl.when(pl.program_id(0) == 0)
    def _():
        width = totals_ref.shape[1]
        for at, out in enumerate(vector_outs):
            out[...] = totals_ref[at : at + 1, :].reshape(width)
        here = lax.axis_index("tensor")
        fc1_bias_out[...] = totals_ref[pl.ds(8 + here, 1), :].reshape(width)


def unpack(qkv, weights, totals, fc_rows, proj_rows):
    f32 = jnp.float32
    _, rows, width = weights.shape
    qkv_rows = qkv.shape[1]
    counts = (fc_rows, fc_rows, proj_rows, qkv_rows)
    vector = pl.BlockSpec((width,), lambda i: (0,))
    return pl.pallas_call(
        unpack_kernel,
        grid=(PIECES,),
        in_specs=[
            pl.BlockSpec((1, qkv_rows, width), lambda i: (i, 0, 0)),
            pl.BlockSpec((1, rows, width), lambda i: (i, 0, 0)),
            pl.BlockSpec(totals.shape, lambda i: (0, 0)),
        ],
        out_specs=[pl.BlockSpec((count, width), lambda i: (i, 0)) for count in counts] + [vector] * 9,
        out_shape=[jax.ShapeDtypeStruct((PIECES * count, width), f32) for count in counts]
        + [jax.ShapeDtypeStruct((width,), f32)] * 9,
        name="unpack",
    )(qkv, weights, totals)


def start_kernel(
    shards,
    dp_bits,
    visit_block,
    tokens_ref,
    ids_ref,
    gain_ref,
    shift_ref,
    qkv_ref,
    qv_bias_ref,
    fc1_ref,
    fc2_ref,
    proj_ref,
    fc1_bias_ref,
    normed_out,
    q_out,
    k_out,
    v_out,
    pairs_out,
    singles_out,
    pairs_here,
    singles_here,
    weights_out,
    bias_out,
    bounds_out,
    blocks,
    normed_all,
    queries,
    keys,
    values,
    peaks,
    sums,
    scores,
    weights,
    q_extra,
    k_extra,
    own,
    chain,
    send,
    recv,
    local,
    stored,
):
    f32, bf16 = jnp.float32, jnp.bfloat16
    member, here = lax.axis_index("dp"), lax.axis_index("tensor")
    core, x_bit, y_bit = bit_of(member, 0), bit_of(member, 1), bit_of(member, 2)
    own_piece = core * 4 + x_bit * 2 + y_bit
    block, width = tokens_ref.shape
    heads = queries.shape[0]
    seq_len = ids_ref.shape[1]
    last = shards - 1
    reach = -(-(MOST_TOKENS - 1) // block)
    slots = iter(range(send.shape[0]))
    pending = []

    def copy_to(src, dst, at, **peer):
        return pltpu.make_async_remote_copy(
            src_ref=src, dst_ref=dst, send_sem=send.at[at], recv_sem=recv.at[at], device_id=peer, device_id_type=MESH
        )

    def start_dp(src, dst, bit):
        copy = copy_to(src, dst, next(slots), dp=partner_of(member, bit))
        copy.start()
        pending.append(copy)
        return copy

    fc1_rows, fc2_rows, proj_rows = (ref.shape[0] // PIECES for ref in (fc1_ref, fc2_ref, proj_ref))
    loads = []
    for at, (ref, first, count) in enumerate(
        ((fc1_ref, 0, fc1_rows), (fc2_ref, fc1_rows, fc2_rows))
    ):
        rows = pl.ds(pl.multiple_of(own_piece * count, 16), count)
        loads.append(pltpu.make_async_copy(ref.at[rows], own.at[first : first + count], local.at[at]))
        loads[-1].start()
    used = fc1_rows + fc2_rows
    rows = pl.ds(pl.multiple_of(own_piece * proj_rows, 8), proj_rows)
    own[used : used + proj_rows, :] = proj_ref[rows, :]
    used += proj_rows
    own[used:, :] = jnp.zeros((own.shape[0] - used, width), bf16)
    gain, shift = (ref[...].reshape(1, width) for ref in (gain_ref, shift_ref))
    bias_out[here] = fc1_bias_ref[...].reshape(1, width)
    greet(dp_bits, shards)
    for load in loads:
        load.wait()

    chains = {}
    for name, first, rest in (("w", own, chain), ("t", tokens_ref, blocks)):
        chains[name] = (
            first,
            rest,
            [next(slots) for _ in range(shards)],
            [next(slots) for _ in range(shards)],
        )

    def hop_copy(name, owner, rightward, from_own):
        first, rest, right_slots, left_slots = chains[name]
        src = first if from_own else rest.at[owner]
        step = 1 if rightward else last
        at = (right_slots if rightward else left_slots)[owner]
        return copy_to(src, rest.at[owner], at, tensor=lax.rem(here + step, shards))

    def send_own(name, rightward):
        for owner in range(shards):
            if owner != (last if rightward else 0):

                @pl.when(here == owner)
                def _():
                    hop_copy(name, owner, rightward, True).start()

    def hop(name, time, then=None):
        for at in range(shards):
            for rightward, owner, end in ((True, at - time, last), (False, at + time, 0)):
                if 0 <= owner <= last:

                    @pl.when(here == at)
                    def _():
                        hop_copy(name, owner, rightward, False).wait_recv()
                        if at != end:
                            hop_copy(name, owner, rightward, False).start()
                            if then is not None and owner in (0, last):
                                hop_copy(then, at, rightward, True).start()

    send_own("w", True)
    send_own("w", False)

    @pl.when(here == 0)
    def _():
        hop_copy("t", 0, True, True).start()

    @pl.when(here == last)
    def _():
        hop_copy("t", last, False, True).start()

    bias_copies = []
    for way in range(1, shards):
        copy = copy_to(
            bias_out.at[here], bias_out.at[here], next(slots), tensor=lax.rem(here + way, shards)
        )
        copy.start()
        bias_copies.append(copy)
    pending.extend(bias_copies)

    large = -MASKED
    segments = lax.broadcasted_iota(jnp.int32, (8, seq_len), 0)
    same = jnp.where(segments == ids_ref[...], 1.0, 0.0).astype(bf16)
    select = lax.broadcasted_iota(jnp.int32, (8, LANES), 1) - HEAD_DIM == lax.broadcasted_iota(
        jnp.int32, (8, LANES), 0
    )
    matched = contract_rows(same, jnp.where(select, 1.0, 0.0).astype(bf16))
    lane = lax.broadcasted_iota(jnp.int32, (seq_len, LANES), 1)
    segment_lane = (lane >= HEAD_DIM) & (lane < HEAD_DIM + 8)
    ones_lane = (lane >= HEAD_DIM + 8) & (lane < HEAD_DIM + 11)
    q_extra[...] = jnp.where(segment_lane, (matched - 1.0) * large, 0.0).astype(bf16)
    k_extra[...] = jnp.where(ones_lane, 1.0, matched).astype(bf16)
    ids = ids_ref[...]
    groups = bounds_out.shape[1]
    for group in range(groups):
        first = group * (seq_len // groups)
        last_row = first + seq_len // groups - 1
        before = jnp.sum(jnp.where(ids < ids_ref[:, first : first + 1], 1.0, 0.0))
        within = jnp.sum(jnp.where(ids <= ids_ref[:, last_row : last_row + 1], 1.0, 0.0))
        bounds_out[0, group] = before.astype(jnp.int32) // visit_block
        bounds_out[1, group] = (within.astype(jnp.int32) + visit_block - 1) // visit_block
    low_half = lax.broadcasted_iota(jnp.int32, (block, LANES), 1) < HEAD_DIM
    v_lane = lax.broadcasted_iota(jnp.int32, (block, LANES), 1)
    v_extra = jnp.where((v_lane >= HEAD_DIM) & (v_lane < HEAD_DIM + 3), 1.0, 0.0).astype(bf16)

    def rows_of(owner, count=block):
        return pl.ds(pl.multiple_of(owner * count, 16), count)

    def store(which, owner):
        rows = rows_of(owner)
        source, out = (
            (normed_all.at[rows], normed_out.at[rows]),
            (queries.at[:, rows], q_out.at[:, rows]),
            (keys.at[:, rows], k_out.at[:, rows]),
            (values.at[:, rows], v_out.at[:, rows]),
        )[which]
        return pltpu.make_async_copy(source, out, stored.at[which, owner])

    def project_block(source, owner):
        tokens = source.astype(f32)
        centred = tokens - jnp.mean(tokens, axis=1, keepdims=True)
        inverse = lax.rsqrt(jnp.mean(centred * centred, axis=1, keepdims=True) + eps_norm)
        normed = (centred * inverse * gain + shift).astype(bf16)
        rows = rows_of(owner)
        normed_all[rows, :] = normed
        for which, out in ((0, queries), (1, keys), (2, values)):
            product = times_transposed(normed, qkv_ref[which])
            if which != 1:
                product = product + qv_bias_ref[which // 2 : which // 2 + 1, :]
            if which == 0:
                product = product.astype(bf16).astype(f32) * HEAD_DIM**-0.5
            extra = v_extra if which == 2 else (q_extra if which == 0 else k_extra)[rows, :]
            for head in range(heads):
                first = (head // 2) * LANES
                tile = product[:, first : first + LANES]
                if tile.shape[1] < LANES:
                    blank = jnp.zeros((block, LANES - tile.shape[1]), f32)
                    tile = jnp.concatenate([tile, blank], axis=1)
                if head % 2:
                    tile = pltpu.roll(tile, HEAD_DIM, 1)
                out[head, rows, :] = jnp.where(low_half, tile, extra.astype(f32)).astype(bf16)
        store(0, owner).start()
        store(2, owner).start()
        store(3, owner).start()

    peaks[...] = jnp.full_like(peaks, -3e38)
    sums[...] = jnp.zeros_like(sums)

    def away(index):
        return jnp.maximum(index - here, here - index)

    def visit(owner, other):
        rows, across = rows_of(owner), rows_of(other)
        for head in range(heads):
            scores[head] = times_transposed(queries[head, rows, :], keys[head, across, :])
        for head in range(heads):
            old_peak = peaks[head, rows, :]
            new_peak = jnp.maximum(old_peak, jnp.max(scores[head], axis=1, keepdims=True))
            peaks[head, rows, :] = new_peak
            spread = jnp.concatenate([new_peak] * -(-block // LANES), axis=1)[:, :block]
            weights[head] = jnp.exp(scores[head] - spread).astype(bf16)
            sums[head, rows, :] = sums[head, rows, :] * jnp.exp(old_peak - new_peak)
        for head in range(heads):
            sums[head, rows, :] += jnp.dot(
                weights[head], values[head, across, :], preferred_element_type=f32
            )

    pair_slots = [next(slots) for _ in range(shards)]
    single_slots = [next(slots) for _ in range(shards)]

    def exchange(owner, source):
        half_block = block // 2
        return [
            pltpu.make_async_remote_copy(
                src_ref=out.at[rows_of(owner, count)],
                dst_ref=landing.at[source],
                send_sem=send.at[base + owner],
                recv_sem=recv.at[base + source],
                device_id={"tensor": owner},
                device_id_type=MESH,
            )
            for out, landing, count, base in (
                (pairs_out, pairs_here, block, pair_slots[0]),
                (singles_out, singles_here, half_block, single_slots[0]),
            )
        ]

    def complete(owner):
        rows, half_block = rows_of(owner), block // 2
        parts = []
        for head in range(heads):
            total = sums[head, rows, HEAD_DIM : HEAD_DIM + 1]
            parts.append(sums[head, rows, :] / total)
            high, middle_part, low = split_three(-(peaks[head, rows, :] + jnp.log(total)))
            kept = queries[head, rows, :].astype(f32)
            for at, value in enumerate((high, middle_part, low)):
                kept = jnp.where(v_lane == HEAD_DIM + 8 + at, value.astype(f32), kept)
            queries[head, rows, :] = kept.astype(bf16)
        pair = join_lanes(parts[0], parts[1]).astype(bf16)
        single = join_lanes(parts[2][:half_block], parts[2][half_block:]).astype(bf16)
        pairs_out[rows, :] = pair
        singles_out[rows_of(owner, half_block), :] = single
        store(1, owner).start()

        @pl.when(owner == here)
        def _():
            pairs_here[here] = pair
            singles_here[here] = single

        @pl.when(owner != here)
        def _():
            for copy in exchange(owner, here):
                copy.start()

    def attend_known(time):
        def each(at, carry):
            owner = lax.rem(here + shards // 2 + at, shards)

            def other_block(other, carry):
                near = jnp.maximum(owner - other, other - owner) <= reach
                known = jnp.maximum(jnp.maximum(away(owner), away(other)), 1)

                @pl.when(near & (known == time))
                def _():
                    visit(owner, other)

                return carry

            lax.fori_loop(0, shards, other_block, 0)
            final = jnp.maximum(
                away(jnp.maximum(owner - reach, 0)), away(jnp.minimum(owner + reach, last))
            )

            @pl.when(final == time)
            def _():
                complete(owner)

            return carry

        lax.fori_loop(0, shards, each, 0)

    project_block(tokens_ref[...], here)
    for time in range(1, shards):
        hop("w", time, "t")

    half = shards // 2
    stores = []
    for owner in range(shards):
        at = 2 + owner

        @pl.when(here == owner)
        def _():
            pltpu.make_async_copy(own, weights_out.at[own_piece, owner], local.at[at]).start()

        @pl.when(here != owner)
        def _():
            pltpu.make_async_copy(chain.at[owner], weights_out.at[own_piece, owner], local.at[at]).start()

        stores.append(pltpu.make_async_copy(own, weights_out.at[own_piece, owner], local.at[at]))
    for saved in stores:
        saved.wait()

    def part(low, pieces):
        owners = pl.ds(0, half) if low else pl.ds(half, shards - half)
        return weights_out.at[pieces, owners]

    def gather_stage(low, pieces, bit):
        return [start_dp(part(low, at), part(low, at), bit) for at in pieces]

    def wait_all(copies):
        for copy in copies:
            copy.wait_recv()

    stage = gather_stage(True, [own_piece], 2) + gather_stage(False, [own_piece], 1)

    def arrived(time):
        def each(at, carry):
            owner = here + (2 * at - 1) * time

            @pl.when((owner >= 0) & (owner <= last))
            def _():
                project_block(blocks[owner], owner)

            return carry

        lax.fori_loop(0, 2, each, 0)

    for time in range(1, shards):
        hop("t", time)
        arrived(time)
        if time == 1:
            wait_all(stage)
            stage = gather_stage(True, [pl.ds(core * 4 + x_bit * 2, 2)], 1) + gather_stage(
                False, [core * 4 + 2 * at + y_bit for at in range(2)], 2
            )
        attend_known(time)
        if time == 2:
            wait_all(stage)
            stage = [start_dp(weights_out.at[pl.ds(core * 4, 4)], weights_out.at[pl.ds(core * 4, 4)], 0)]
    for owner in range(shards):

        @pl.when(here != owner)
        def _():
            for copy in exchange(here, owner):
                copy.wait_recv()
            for copy in exchange(owner, here):
                copy.wait_send()

        for which in range(4):
            store(which, owner).wait()
    wait_all(stage)
    wait_all(bias_copies)
    for copy in pending:
        copy.wait_send()
    for name in chains:
        for at in range(shards):
            for owner in range(shards):
                if owner <= at < last:

                    @pl.when(here == at)
                    def _():
                        hop_copy(name, owner, True, False).wait_send()

                if owner >= at > 0:

                    @pl.when(here == at)
                    def _():
                        hop_copy(name, owner, False, False).wait_send()


def start(shards, members, visits, tokens, ids, gain, shift, qkv, qv_bias, fc1, fc2, proj, fc1_bias):
    dp_bits = members.bit_length() - 1
    assert members == 1 << dp_bits and dp_bits >= PIECE_BITS and shards >= 3
    f32, bf16 = jnp.float32, jnp.bfloat16
    block, width = tokens.shape
    seq_len = block * shards
    heads = qkv.shape[1] // HEAD_DIM
    rows = -(-(fc1.shape[0] + fc2.shape[0] + proj.shape[0]) // PIECES // 16) * 16
    copies = 6 * shards + (shards - 1) + 6
    vm = pltpu.VMEM
    on_chip = pl.BlockSpec(memory_space=vm)
    anywhere = pl.BlockSpec(memory_space=pl.ANY)
    head_rows = jax.ShapeDtypeStruct((heads, seq_len, LANES), bf16)
    return pl.pallas_call(
        partial(start_kernel, shards, dp_bits, visits[1]),
        in_specs=[on_chip] * 6 + [anywhere] * 2 + [on_chip] * 2,
        out_specs=[anywhere] * 4
        + [on_chip] * 4
        + [anywhere, on_chip, pl.BlockSpec(memory_space=pltpu.SMEM)],
        out_shape=[
            jax.ShapeDtypeStruct((seq_len, width), bf16),
            head_rows,
            head_rows,
            head_rows,
            jax.ShapeDtypeStruct((seq_len, LANES), bf16),
            jax.ShapeDtypeStruct((seq_len // 2, LANES), bf16),
            jax.ShapeDtypeStruct((shards, block, LANES), bf16),
            jax.ShapeDtypeStruct((shards, block // 2, LANES), bf16),
            jax.ShapeDtypeStruct((PIECES, shards, rows, width), bf16),
            jax.ShapeDtypeStruct((shards, 1, width), f32),
            jax.ShapeDtypeStruct((2, visits[0]), jnp.int32),
        ],
        scratch_shapes=[
            vm((shards, block, width), bf16),
            vm((seq_len, width), bf16),
            vm((heads, seq_len, LANES), bf16),
            vm((heads, seq_len, LANES), bf16),
            vm((heads, seq_len, LANES), bf16),
            vm((heads, seq_len, LANES), f32),
            vm((heads, seq_len, LANES), f32),
            vm((heads, block, block), f32),
            vm((heads, block, block), bf16),
            vm((seq_len, LANES), bf16),
            vm((seq_len, LANES), bf16),
            vm((rows, width), bf16),
            vm((shards, rows, width), bf16),
            pltpu.SemaphoreType.DMA((copies,)),
            pltpu.SemaphoreType.DMA((copies,)),
            pltpu.SemaphoreType.DMA((2 + shards,)),
            pltpu.SemaphoreType.DMA((4, shards)),
        ],
        compiler_params=pltpu.CompilerParams(
            collective_id=0, has_side_effects=True, vmem_limit_bytes=62 * 1024 * 1024
        ),
        name="start",
        cost_estimate=pl.CostEstimate(
            flops=6 * seq_len * width * heads * HEAD_DIM, transcendentals=0, bytes_accessed=40 * block * width
        ),
    )(tokens, ids, gain, shift, qkv, qv_bias, fc1, fc2, proj, fc1_bias)


CHUNK = 32


def middle_kernel(
    shards,
    dp_bits,
    pairs,
    singles,
    weights_ref,
    fc1_bias_ref,
    proj_bias_ref,
    scale_one_ref,
    gain_ref,
    shift_ref,
    fc2_bias_ref,
    scale_two_ref,
    tokens_ref,
    cotangent_ref,
    block_out,
    hidden_grad_out,
    pair_grads_out,
    single_grads_out,
    vectors_out,
    a_keep,
    a_away,
    b_keep,
    b_away,
    weights,
    attended,
    proj,
    branch,
    hidden,
    normed,
    wide,
    total,
    active,
    slope,
    grad_pre,
    grad_mlp,
    grad_branch,
    pair_grads,
    single_grads,
    got,
    send,
    recv,
    local,
):
    f32, bf16 = jnp.float32, jnp.bfloat16
    member, here = lax.axis_index("dp"), lax.axis_index("tensor")
    core, x_bit, y_bit = bit_of(member, 0), bit_of(member, 1), bit_of(member, 2)
    block, width = tokens_ref.shape
    columns = width // shards
    half = PIECES // 2
    fc_rows, proj_rows = width // PIECES, columns // PIECES
    proj_first = 2 * fc_rows
    slots = iter(range(send.shape[0]))
    proj_bias, scale_one, gain, shift, fc2_bias, scale_two = (
        ref[...].reshape(1, width)
        for ref in (proj_bias_ref, scale_one_ref, gain_ref, shift_ref, fc2_bias_ref, scale_two_ref)
    )

    def copy_to(src, dst, at, **peer):
        return pltpu.make_async_remote_copy(
            src_ref=src, dst_ref=dst, send_sem=send.at[at], recv_sem=recv.at[at], device_id=peer, device_id_type=MESH
        )

    loads = []
    for owner in range(shards):
        load = pltpu.make_async_copy(weights_ref.at[:, owner], weights.at[:, owner], local.at[owner])
        load.start()
        loads.append(load)
    greet(dp_bits, shards)

    for load in loads:
        load.wait()

    def fc1_of(owner):
        return weights[:, owner, :fc_rows, :].reshape(width, width)

    def fc2_of(owner):
        return weights[:, owner, fc_rows:proj_first, :].reshape(width, width)

    def proj_of(owner):
        return weights[:, owner, proj_first : proj_first + proj_rows, :].reshape(columns, width)

    def chunk(at):
        return pl.ds(pl.multiple_of(at * CHUNK, CHUNK), CHUNK)

    def each_chunk(body, init):
        return lax.fori_loop(0, block // CHUNK, body, init)

    def column_sum(value):
        return jnp.sum(value, axis=0, keepdims=True)

    def unit_of(value):
        centred = value - jnp.mean(value, axis=1, keepdims=True)
        inverse = lax.rsqrt(jnp.mean(centred * centred, axis=1, keepdims=True) + eps_norm)
        return centred * inverse, inverse

    third = shards * LANES
    for owner in range(shards):
        own_proj = proj_of(owner)
        proj[owner * LANES : (owner + 1) * LANES, :] = own_proj[:LANES]
        proj[third + owner * HEAD_DIM : third + (owner + 1) * HEAD_DIM, :] = own_proj[LANES:]
    middle_row = block // 2
    for owner in range(shards):
        attended[:, owner * LANES : (owner + 1) * LANES] = pairs[owner]
    lane = lax.broadcasted_iota(jnp.int32, (middle_row, LANES), 1)
    low_half = lane < HEAD_DIM

    def swapped(value):
        return pltpu.roll(value, HEAD_DIM, 1)

    for at in range(shards // 2):
        one, two = singles[2 * at].astype(f32), singles[2 * at + 1].astype(f32)
        columns_here = slice(third + at * LANES, third + (at + 1) * LANES)
        attended[:middle_row, columns_here] = jnp.where(low_half, one, swapped(two)).astype(bf16)
        attended[middle_row:, columns_here] = jnp.where(low_half, swapped(one), two).astype(bf16)
    product = jnp.dot(attended[...], proj[...], preferred_element_type=f32)
    branch[...] = product

    def enter(at, carry):
        rows = chunk(at)
        value = branch[rows, :] + proj_bias
        branch[rows, :] = value
        value = tokens_ref[rows, :].astype(f32) + scale_one * value
        hidden[rows, :] = value
        unit, _ = unit_of(value)
        normed[rows, :] = (unit * gain + shift).astype(bf16)
        return carry

    each_chunk(enter, 0)

    def forward(owner, carry):
        wide[:block, :] = jnp.dot(normed[...], fc1_of(owner), preferred_element_type=f32)
        bias = fc1_bias_ref[owner]

        def activate(at, carry):
            rows = chunk(at)
            value = wide[rows, :] + bias
            below = 0.5 * (1.0 + lax.erf(value * 0.5**0.5))
            active[owner, rows, :] = (value * below).astype(bf16)
            density = jnp.exp(value * value * -0.5) * (0.5 / math.pi) ** 0.5
            slope[owner, rows, :] = below + value * density
            return carry

        each_chunk(activate, 0)
        product = jnp.dot(active[owner], fc2_of(owner), preferred_element_type=f32)
        total[...] = jnp.where(owner == 0, product, total[...] + product)
        return carry

    lax.fori_loop(0, shards, forward, 0)
    empty = jnp.zeros((1, width), f32)

    def turn(at, sums):
        rows = chunk(at)
        value = total[rows, :] + fc2_bias
        block_out[rows, :] = (hidden[rows, :] + scale_two * value).astype(bf16)
        grad = cotangent_ref[rows, :].astype(f32)
        grad_mlp[rows, :] = (grad * scale_two).astype(bf16)
        return (
            sums[0] + column_sum(grad * value),
            sums[1] + column_sum(grad_mlp[rows, :].astype(f32)),
        )

    scale_two_sum, fc2_bias_sum = each_chunk(turn, (empty, empty))

    def backward(owner, carry):
        wide[:block, :] = times_transposed(grad_mlp[...], fc2_of(owner))

        def slopes(at, sums):
            rows = chunk(at)
            value = (wide[rows, :] * slope[owner, rows, :]).astype(bf16)
            grad_pre[owner, rows, :] = value
            return sums + column_sum(value.astype(f32))

        vectors_out[pl.ds(8 + owner, 1), :] = each_chunk(slopes, empty)
        product = times_transposed(grad_pre[owner], fc1_of(owner))
        total[...] = jnp.where(owner == 0, product, total[...] + product)
        return carry

    lax.fori_loop(0, shards, backward, 0)

    def leave(at, sums):
        rows = chunk(at)
        grad = total[rows, :]
        unit, inverse = unit_of(hidden[rows, :])
        scaled = grad * gain
        inner = (
            scaled
            - jnp.mean(scaled, axis=1, keepdims=True)
            - unit * jnp.mean(scaled * unit, axis=1, keepdims=True)
        )
        value = cotangent_ref[rows, :].astype(f32) + inverse * inner
        hidden_grad_out[rows, :] = value
        rounded = (value * scale_one).astype(bf16)
        grad_branch[rows, :] = rounded
        return (
            sums[0] + column_sum(grad * unit),
            sums[1] + column_sum(grad),
            sums[2] + column_sum(value * branch[rows, :]),
            sums[3] + column_sum(rounded.astype(f32)),
        )

    gain_sum, shift_sum, scale_one_sum, proj_bias_sum = each_chunk(leave, (empty,) * 4)
    for at, value in enumerate(
        (empty, empty, proj_bias_sum, scale_one_sum, gain_sum, shift_sum, fc2_bias_sum, scale_two_sum)
    ):
        vectors_out[at : at + 1, :] = value
    vectors_out[12:, :] = jnp.zeros((vectors_out.shape[0] - 12, width), f32)

    wide[:block, :] = times_transposed(grad_branch[...], proj[...])
    for owner in range(shards):
        pair_grads[owner] = wide[:block, owner * LANES : (owner + 1) * LANES].astype(bf16)
    for at in range(shards // 2):
        columns_here = slice(third + at * LANES, third + (at + 1) * LANES)
        upper, lower = wide[:middle_row, columns_here], wide[middle_row:block, columns_here]
        single_grads[2 * at] = jnp.where(low_half, upper, swapped(lower)).astype(bf16)
        single_grads[2 * at + 1] = jnp.where(low_half, swapped(upper), lower).astype(bf16)
    back = []
    for source, out in ((pair_grads, pair_grads_out), (single_grads, single_grads_out)):
        for way in range(1, shards):
            target = lax.rem(here + way, shards)
            copy = copy_to(source.at[target], out.at[here], next(slots), tensor=target)
            copy.start()
            back.append(copy)
        out[here] = source[here]

    first_slot = next(slots)

    def core_copy(owner):
        return pltpu.make_async_remote_copy(
            src_ref=weights.at[pl.ds((1 - core) * half, half), owner],
            dst_ref=got.at[:, owner],
            send_sem=send.at[first_slot + owner],
            recv_sem=recv.at[first_slot + owner],
            device_id={"dp": partner_of(member, 0)},
            device_id_type=MESH,
        )

    wide[...] = contract_rows(attended[:, :], grad_branch[...])
    for owner in range(shards):
        for piece in range(PIECES):
            first, end = piece * proj_rows, (piece + 1) * proj_rows
            for low, high, start_row in ((0, LANES, owner * LANES), (LANES, columns, third + owner * HEAD_DIM)):
                begin, stop = max(first, low), min(end, high)
                if begin < stop:
                    rows = slice(start_row + begin - low, start_row + stop - low)
                    to = slice(proj_first + begin - first, proj_first + stop - first)
                    weights[piece, owner, to, :] = wide[rows, :].astype(bf16)

    def weight_grads(owner, carry):
        for left, right, first, count in (
            (normed[...], grad_pre[owner], 0, fc_rows),
            (active[owner], grad_mlp[...], fc_rows, fc_rows),
        ):
            product = contract_rows(left, right).astype(bf16)
            weights[:, owner, first : first + count, :] = product.reshape(PIECES, count, width)
        core_copy(owner).start()
        return carry

    lax.fori_loop(0, shards, weight_grads, 0)
    split = shards // 2
    for owner in range(shards):
        core_copy(owner).wait_recv()
        if owner < split:
            for y in range(2):
                for out, x in ((a_keep, x_bit), (a_away, 1 - x_bit)):
                    out[y, owner] = rounded_sum(weights[core * half + x * 2 + y, owner], got[x * 2 + y, owner])
        else:
            for x in range(2):
                for out, y in ((b_keep, y_bit), (b_away, 1 - y_bit)):
                    out[x, owner - split] = rounded_sum(
                        weights[core * half + x * 2 + y, owner], got[x * 2 + y, owner]
                    )
    for copy in back:
        copy.wait_recv()
    for copy in back:
        copy.wait_send()
    for owner in range(shards):
        core_copy(owner).wait_send()


def middle(shards, members, pairs, singles, weights, fc1_bias, vectors, tokens, cotangent):
    dp_bits = members.bit_length() - 1
    f32, bf16 = jnp.float32, jnp.bfloat16
    block, width = tokens.shape
    rows = weights.shape[2]
    vm = pltpu.VMEM
    on_chip = pl.BlockSpec(memory_space=vm)
    quarter = jax.ShapeDtypeStruct((2, shards // 2, rows, width), bf16)
    copies = 2 * (shards - 1) + shards
    return pl.pallas_call(
        partial(middle_kernel, shards, dp_bits),
        in_specs=[on_chip, on_chip, pl.BlockSpec(memory_space=pl.ANY)] + [on_chip] * 9,
        out_specs=[on_chip] * 9,
        out_shape=[
            jax.ShapeDtypeStruct((block, width), bf16),
            jax.ShapeDtypeStruct((block, width), f32),
            jax.ShapeDtypeStruct((shards, block, LANES), bf16),
            jax.ShapeDtypeStruct((shards, block // 2, LANES), bf16),
            jax.ShapeDtypeStruct((16, width), f32),
            quarter,
            quarter,
            quarter,
            quarter,
        ],
        scratch_shapes=[
            vm(weights.shape, bf16),
            vm((block, width), bf16),
            vm((width, width), bf16),
            vm((block, width), f32),
            vm((block, width), f32),
            vm((block, width), bf16),
            vm((width, width), f32),
            vm((block, width), f32),
            vm((shards, block, width), bf16),
            vm((shards, block, width), f32),
            vm((shards, block, width), bf16),
            vm((block, width), bf16),
            vm((block, width), bf16),
            vm((shards, block, LANES), bf16),
            vm((shards, block // 2, LANES), bf16),
            vm((PIECES // 2, shards, rows, width), bf16),
            pltpu.SemaphoreType.DMA((copies,)),
            pltpu.SemaphoreType.DMA((copies,)),
            pltpu.SemaphoreType.DMA((shards,)),
        ],
        compiler_params=pltpu.CompilerParams(
            collective_id=2, has_side_effects=True, vmem_limit_bytes=62 * 1024 * 1024
        ),
        name="middle",
        cost_estimate=pl.CostEstimate(
            flops=12 * block * width * width * shards, transcendentals=0, bytes_accessed=40 * block * width
        ),
    )(pairs, singles, weights, fc1_bias, *vectors, tokens, cotangent)


eps_norm = 1e-06


def on_device(
    shards,
    members,
    tokens,
    segment_ids,
    ln1_gain,
    ln1_bias,
    qkv_weight,
    qv_bias,
    proj_weight,
    proj_bias,
    scale_one,
    ln2_gain,
    ln2_bias,
    fc1_weight,
    fc1_bias,
    fc2_weight,
    fc2_bias,
    scale_two,
    cotangent,
):
    f32, bf16 = jnp.float32, jnp.bfloat16
    seq_len = segment_ids.shape[1]
    rows_here, width = tokens.shape
    head_columns = qkv_weight.shape[2]
    heads = head_columns // HEAD_DIM
    hidden_here = fc1_weight.shape[1]
    ids = segment_ids[0]
    here = lax.axis_index("tensor")

    visits = (shards, seq_len // 6)
    turned = qkv_weight.transpose(0, 2, 1)
    full_one, queries, keys, values, pairs, singles, pairs_here, singles_here, gathered, fc1_bias_full, bounds = start(
        shards,
        members,
        visits,
        tokens,
        segment_ids,
        ln1_gain,
        ln1_bias,
        turned,
        qv_bias,
        fc1_weight,
        fc2_weight,
        proj_weight,
        fc1_bias,
    )
    params = (proj_bias, scale_one, ln2_gain, ln2_bias, fc2_bias, scale_two)
    block_out, grad_hidden, pair_grads, single_grads, vectors, a_keep, a_away, b_keep, b_away = middle(
        shards, members, pairs_here, singles_here, gathered, fc1_bias_full, params, tokens, cotangent
    )
    pair_grads = pair_grads.reshape(seq_len, LANES)
    single_grads = single_grads.reshape(seq_len // 2, LANES)

    def swap(value, bit):
        return lax.ppermute(value, "dp", [(j, j ^ (1 << bit)) for j in range(members)])

    a_got, b_got = swap(a_away, 1), swap(b_away, 2)
    grad_heads = attend_back(bounds, queries, keys, values, pairs, singles, pair_grads, single_grads, visits[1])
    grad_tokens, totals, qkv_pieces, weight_pieces = finish(
        shards,
        members,
        grad_heads,
        full_one,
        turned.reshape(3 * head_columns, width),
        ln1_gain,
        ln1_bias,
        vectors,
        tokens,
        grad_hidden,
        a_keep,
        a_got,
        b_keep,
        b_got,
    )
    fc1_grad, fc2_grad, proj_grad, qkv_grad, fc1_bias_grad, *sums = unpack(
        qkv_pieces, weight_pieces, totals, width // PIECES, head_columns // PIECES
    )
    qkv_grad = qkv_grad.reshape(3, head_columns, width).transpose(0, 2, 1)
    qv_sums = lax.dynamic_index_in_dim(totals, 12 + here, 0, keepdims=False)
    qv_grad = jnp.stack([qv_sums[:head_columns], qv_sums[2 * head_columns : 3 * head_columns]])
    return (
        block_out,
        grad_tokens,
        sums[0],
        sums[1],
        qkv_grad,
        qv_grad,
        proj_grad,
        sums[2],
        sums[3],
        sums[4],
        sums[5],
        fc1_grad,
        fc1_bias_grad,
        fc2_grad,
        sums[6],
        sums[7],
    )


def solution(mesh):
    rows = P(("dp", "tensor"), None)
    columns = P(None, "tensor")
    return jax.shard_map(
        partial(on_device, mesh.shape["tensor"], mesh.shape["dp"]),
        mesh=mesh,
        in_specs=(
            rows,
            P("dp", None),
            P(),
            P(),
            P(None, None, "tensor"),
            columns,
            P("tensor", None),
            P(),
            P(),
            P(),
            P(),
            columns,
            P("tensor"),
            P("tensor", None),
            P(),
            P(),
            rows,
        ),
        out_specs=(
            rows,
            rows,
            P(),
            P(),
            P(None, None, "tensor"),
            columns,
            P("tensor", None),
            P(),
            P(),
            P(),
            P(),
            columns,
            P("tensor"),
            P("tensor", None),
            P(),
            P(),
        ),
        check_vma=False,
    )
```

```python
from functools import partial
import math

import jax, jax.numpy as jnp
from jax import lax
from jax.experimental import pallas as pl
from jax.experimental.pallas import tpu as pltpu

from jax.sharding import PartitionSpec as P

HEAD_DIM = 64
LANES = 128
MOST_TOKENS = 1152
MASKED = -(2.0**100)


def contract_rows(left, right):
    return lax.dot_general(left, right, (((0,), (0,)), ((), ())), preferred_element_type=jnp.float32)


def times_transposed(left, right, precision=None):
    return lax.dot_general(
        left, right, (((1,), (1,)), ((), ())), preferred_element_type=jnp.float32, precision=precision
    )


def split_three(value):
    high = value.astype(jnp.bfloat16)
    rest = value - high.astype(jnp.float32)
    middle = rest.astype(jnp.bfloat16)
    low = (rest - middle.astype(jnp.float32)).astype(jnp.bfloat16)
    return (high, middle, low)


def join_lanes(low, high):
    lane = lax.broadcasted_iota(jnp.int32, low.shape, 1)
    return jnp.where(lane < HEAD_DIM, low, pltpu.roll(high, HEAD_DIM, 1))


MESH = pl.DeviceIdType.MESH
PIECES = 8
PIECE_BITS = 3


def rounded_sum(left, right):
    return (left.astype(jnp.float32) + right.astype(jnp.float32)).astype(jnp.bfloat16)


def bit_of(index, bit):
    return lax.rem(index // (1 << bit), 2)


def partner_of(index, bit):
    return index + (1 - 2 * bit_of(index, bit)) * (1 << bit)


def greet(dp_bits, shards):
    barrier = pltpu.get_barrier_semaphore()
    member, here = lax.axis_index("dp"), lax.axis_index("tensor")
    peers = [{"dp": partner_of(member, bit)} for bit in range(dp_bits)]
    peers += [{"tensor": lax.rem(here + way, shards)} for way in range(1, shards)]
    for peer in peers:
        pl.semaphore_signal(barrier, inc=1, device_id=peer, device_id_type=MESH)
    pl.semaphore_wait(barrier, len(peers))


def back_kernel(
    shards,
    dp_bits,
    q_ref,
    k_ref,
    v_ref,
    pair_ref,
    single_ref,
    pair_grad_ref,
    single_grad_ref,
    weight_ref,
    gain_ref,
    shift_ref,
    vectors_ref,
    rows_ref,
    tokens_ref,
    hidden_ref,
    a_keep,
    a_away,
    b_keep,
    b_away,
    tokens_out,
    vectors_out,
    qkv_out,
    weights_out,
    grad_heads,
    dq,
    dk,
    dv,
    probs,
    grad_scores,
    packed,
    rows_own,
    tokens_own,
    hidden_own,
    part,
    arrived,
    q_wide,
    column_sums,
    q_all,
    q_half,
    q_quarter,
    q_got_core,
    q_got_x,
    q_got_y,
    q_got_more,
    v_now,
    v_got,
    v_shards,
    a_sum,
    b_sum,
    a_got,
    b_got,
    a_second,
    b_second,
    pieces,
    pieces_more,
    z_got,
    send,
    recv,
    local,
):
    f32, bf16 = jnp.float32, jnp.bfloat16
    member, here = lax.axis_index("dp"), lax.axis_index("tensor")
    core, x_bit, y_bit = bit_of(member, 0), bit_of(member, 1), bit_of(member, 2)
    own_piece = core * 4 + x_bit * 2 + y_bit
    block, width = part.shape[1], part.shape[2]
    heads = q_ref.shape[0]
    columns = weight_ref.shape[0]
    half_rows = weights_out.shape[1] // 2
    last = shards - 1
    reach = -(-(MOST_TOKENS - 1) // block)
    gain, shift = (ref[...].reshape(1, width) for ref in (gain_ref, shift_ref))
    slots = iter(range(send.shape[0]))
    pending = []

    def copy_to(src, dst, at, **peer):
        return pltpu.make_async_remote_copy(
            src_ref=src, dst_ref=dst, send_sem=send.at[at], recv_sem=recv.at[at], device_id=peer, device_id_type=MESH
        )

    def start_dp(src, dst, bit, keep=True):
        copy = copy_to(src, dst, next(slots), dp=partner_of(member, bit))
        copy.start()
        if keep:
            pending.append(copy)
        return copy

    def load(at):
        source, landing = ((a_keep, a_sum), (b_keep, b_sum), (tokens_ref, tokens_own), (hidden_ref, hidden_own))[at]
        return pltpu.make_async_copy(source, landing, local.at[at])

    def load_rows(owner):
        rows = pl.ds(pl.multiple_of(owner * block, 16), block)
        return pltpu.make_async_copy(rows_ref.at[rows], rows_own, local.at[4])

    for at in range(4):
        load(at).start()
    load_rows(last).start()
    greet(dp_bits, shards)
    start_dp(a_away, a_got, 1)
    start_dp(b_away, b_got, 2)
    first_a, first_b = pending[-2:]
    second_slots = [next(slots) for _ in range(2)]

    def second(at):
        if at:
            return copy_to(b_sum.at[1 - x_bit], b_second, second_slots[1], dp=partner_of(member, 1))
        return copy_to(a_sum.at[1 - y_bit], a_second, second_slots[0], dp=partner_of(member, 2))

    z_slots = [next(slots) for _ in range(1, shards)]

    def piece_copy(way):
        target = lax.rem(here + way, shards)
        return copy_to(pieces.at[target], z_got.at[way - 1], z_slots[way - 1], tensor=target)

    more_slots = [next(slots) for _ in range(PIECE_BITS, dp_bits)]

    def sum_pairs(out, right):
        def step(at, carry):
            one, two = at // out.shape[1], lax.rem(at, out.shape[1])
            out[one, two] = rounded_sum(out[one, two], right[one, two])
            return carry

        lax.fori_loop(0, out.shape[0] * out.shape[1], step, 0)

    def second_exchange():
        first_a.wait_recv()
        first_b.wait_recv()
        load(0).wait()
        load(1).wait()
        sum_pairs(a_sum, a_got)
        sum_pairs(b_sum, b_got)
        second(0).start()
        second(1).start()

    def shard_exchange():
        second(0).wait_recv()
        second(1).wait_recv()
        split = shards // 2
        for at in range(split):
            pieces[at] = rounded_sum(a_sum[y_bit, at], a_second[at])
            pieces[split + at] = rounded_sum(b_sum[x_bit, at], b_second[at])
        for bit in range(PIECE_BITS, dp_bits):
            at = bit - PIECE_BITS
            extra = copy_to(pieces, pieces_more.at[at], more_slots[at], dp=partner_of(member, bit))
            extra.start()
            extra.wait_recv()
            extra.wait_send()

            def step(owner, carry):
                pieces[owner] = rounded_sum(pieces[owner], pieces_more[at, owner])
                return carry

            lax.fori_loop(0, shards, step, 0)
        for way in range(1, shards):
            piece_copy(way).start()

    right_slots = [next(slots) for _ in range(shards)]
    left_slots = [next(slots) for _ in range(shards)]

    def to_right(owner):
        return copy_to(part.at[owner], arrived.at[owner], right_slots[owner], tensor=lax.rem(here + 1, shards))

    def to_left(owner, target=None):
        to = lax.rem(here + last, shards) if target is None else target
        landing = jnp.where(owner == to, shards, owner)
        return copy_to(
            part.at[owner], arrived.at[landing], left_slots[owner], tensor=lax.rem(here + last, shards)
        )

    def add_arrived(owner, landing):
        def step(at, carry):
            rows = pl.ds(pl.multiple_of(at * (block // 4), 16), block // 4)
            part[owner, rows, :] = rounded_sum(part[owner, rows, :], arrived[landing, rows, :])
            return carry

        lax.fori_loop(0, 4, step, 0)

    def hop(moved, nth, rightward):
        owner, at = (last - nth, moved) if rightward else (nth, last - moved)
        if (at < owner) if rightward else (at > owner):

            @pl.when(here == at)
            def _():
                copy = to_right(owner) if rightward else to_left(owner)
                copy.wait_recv()
                add_arrived(owner, owner)
                copy.start()

    dq[...] = jnp.zeros_like(dq)
    dk[...] = jnp.zeros_like(dk)
    dv[...] = jnp.zeros_like(dv)
    q_wide[...] = jnp.zeros_like(q_wide)
    column_sums[...] = jnp.zeros_like(column_sums)
    source = lax.broadcasted_iota(jnp.int32, (LANES, LANES), 0)
    target = lax.broadcasted_iota(jnp.int32, (LANES, LANES), 1)
    gathers = (target >= HEAD_DIM) & (target < HEAD_DIM + 3)
    picks = []
    for odd in range(2):
        inside = (source >= HEAD_DIM * odd) & (source < HEAD_DIM * (odd + 1))
        summing = jnp.where(inside & gathers, -1.0, 0.0).astype(bf16)
        moving = jnp.where(inside & (source - HEAD_DIM * odd == target), 1.0, 0.0).astype(bf16)
        picks.append((summing, moving))
    half = block // 2
    lane = lax.broadcasted_iota(jnp.int32, (half, LANES), 1)

    def prepare(at, carry):
        for side in range(2):
            rows = pl.ds(pl.multiple_of((2 * at + side) * half, half), half)
            single_rows = pl.ds(pl.multiple_of(at * half, half), half)
            for head, odd, mixed, grad in (
                (0, 0, pair_ref[rows, :], pair_grad_ref[rows, :]),
                (1, 1, pair_ref[rows, :], pair_grad_ref[rows, :]),
                (2, side, single_ref[single_rows, :], single_grad_ref[single_rows, :]),
            ):
                summing, moving = picks[odd]
                product = grad.astype(f32) * mixed.astype(f32)
                high = product.astype(bf16)
                low = (product - high.astype(f32)).astype(bf16)
                shared = jnp.dot(high, summing, preferred_element_type=f32) + jnp.dot(
                    low, summing, preferred_element_type=f32
                )
                moved = jnp.dot(grad, moving, preferred_element_type=f32)
                for place, value in enumerate(split_three(shared)):
                    moved = jnp.where(lane == HEAD_DIM + place, value.astype(f32), moved)
                grad_heads[head, rows, :] = moved.astype(bf16)
        return carry

    lax.fori_loop(0, shards, prepare, 0)

    def rows_of(owner):
        return pl.ds(pl.multiple_of(owner * block, 16), block)

    def visit(owner, other):
        key_rows, query_rows = rows_of(owner), rows_of(other)
        for head in range(heads):
            prob = jnp.exp(times_transposed(k_ref[head, key_rows, :], q_ref[head, query_rows, :]))
            grad_prob = times_transposed(v_ref[head, key_rows, :], grad_heads[head, query_rows, :])
            probs[head] = prob.astype(bf16)
            grad_scores[head] = (prob * grad_prob).astype(bf16)
        for head in range(heads):
            dv[head, key_rows, :] += jnp.dot(
                probs[head], grad_heads[head, query_rows, :], preferred_element_type=f32
            )
            dk[head, key_rows, :] += jnp.dot(
                grad_scores[head], q_ref[head, query_rows, :], preferred_element_type=f32
            )
            dq[head, query_rows, :] += contract_rows(grad_scores[head], k_ref[head, key_rows, :])

    def close_block(owner, following):
        rows = rows_of(owner)
        scale = HEAD_DIM**-0.5
        for first, low, high in (
            (0, dq[0, rows, :] * scale, dq[1, rows, :] * scale),
            (1, dq[2, rows, :] * scale, dk[0, rows, :]),
            (2, dk[1, rows, :], dk[2, rows, :]),
            (3, dv[0, rows, :], dv[1, rows, :]),
        ):
            packed[:, first * LANES : (first + 1) * LANES] = join_lanes(low, high).astype(bf16)
        packed[:, 4 * LANES : columns] = dv[2, rows, :HEAD_DIM].astype(bf16)
        part[owner] = jnp.dot(packed[...], weight_ref[...], preferred_element_type=f32).astype(bf16)

        @pl.when((owner == last) & (here == 0))
        def _():
            to_right(last).start()

        @pl.when((owner == 0) & (here == last))
        def _():
            to_left(0).start()

        load_rows(owner).wait()
        q_wide[...] += contract_rows(packed[...], rows_own[...])
        column_sums[...] += jnp.dot(jnp.ones((8, block), bf16), packed[...], preferred_element_type=f32)

        @pl.when(following >= 0)
        def _():
            load_rows(following).start()

    order = []
    for near in range((shards + 1) // 2):
        for owner in (last - near, near):
            if owner not in order:
                order.append(owner)
    visits, closing = [], []
    for at, owner in enumerate(order):
        rest = order[at:]
        both = [(owner, owner)]
        for other in rest[1:]:
            if abs(owner - other) <= reach:
                both += [(owner, other), (other, owner)]
        visits += both
        closing.append(len(visits) - 1)
    total_visits = len(visits)

    def lookup(table, at):
        value = 0
        for place, entry in enumerate(table):
            value = value + jnp.where(at == place, entry, 0)
        return value

    closed = [order[closing.index(at)] if at in closing else -1 for at in range(total_visits)]
    later = [
        order[closing.index(at) + 1] if at in closing and at != closing[-1] else -1 for at in range(total_visits)
    ]
    events = {
        total_visits // 2: second_exchange,
        closing[1] + 1: lambda: hop(1, 0, True),
        closing[2]: shard_exchange,
    }
    assert len(events) == 3 and shards >= 4

    def each_visit(at, carry):
        visit(lookup([pair[0] for pair in visits], at), lookup([pair[1] for pair in visits], at))
        for when, event in events.items():

            @pl.when(at == when)
            def _():
                event()

        @pl.when(lookup([int(owner >= 0) for owner in closed], at) == 1)
        def _():
            close_block(lookup(closed, at), lookup(later, at))

        return carry

    lax.fori_loop(0, total_visits, each_visit, 0)
    for owner in range(last - 1, 0, -1):

        @pl.when(here == 0)
        def _():
            to_right(owner).start()

    for owner in range(1, last):

        @pl.when(here == last)
        def _():
            to_left(owner).start()

    sums = column_sums[...]
    weight = weight_ref[...].astype(f32)
    shift_sum = jnp.dot(sums, weight, preferred_element_type=f32, precision=lax.Precision.HIGHEST)[0:1]
    gain_sum = jnp.sum(weight * q_wide[...], axis=0, keepdims=True)
    v_now[0] = vectors_ref[...]
    v_now[0, 0:1, :] = (gain_sum - shift * shift_sum) / gain
    v_now[0, 1:2, :] = shift_sum
    v_now[0, pl.ds(12 + here, 1), 0:columns] = sums[0:1]
    count = q_all.shape[1]
    for piece in range(PIECES):
        q_all[piece] = q_wide[piece * count : (piece + 1) * count, :].astype(bf16)

    def vector_stage(bit):
        return start_dp(v_now.at[bit], v_got.at[bit], bit)

    q_core = start_dp(q_all.at[pl.ds((1 - core) * 4, 4)], q_got_core, 0)
    v_copy = vector_stage(0)
    hop(1, 0, False)
    hop(2, 0, True)
    q_core.wait_recv()
    for at in range(4):
        q_half[at] = rounded_sum(q_all[core * 4 + at], q_got_core[at])
    q_x = start_dp(q_half.at[pl.ds((1 - x_bit) * 2, 2)], q_got_x, 1)
    v_copy.wait_recv()
    v_now[1] = v_now[0] + v_got[0]
    v_copy = vector_stage(1)
    q_x.wait_recv()
    for at in range(2):
        q_quarter[at] = rounded_sum(q_half[x_bit * 2 + at], q_got_x[at])
    q_y = start_dp(q_quarter.at[1 - y_bit], q_got_y, 2)
    v_copy.wait_recv()
    v_now[2] = v_now[1] + v_got[1]
    v_copy = vector_stage(2)
    q_y.wait_recv()
    qkv_out[own_piece] = rounded_sum(q_quarter[y_bit], q_got_y[...])
    v_copy.wait_recv()
    v_now[3] = v_now[2] + v_got[2]
    for bit in range(PIECE_BITS, dp_bits):
        extra = start_dp(qkv_out.at[own_piece], q_got_more.at[bit - PIECE_BITS], bit, False)
        v_copy = vector_stage(bit)
        extra.wait_recv()
        extra.wait_send()
        qkv_out[own_piece] = rounded_sum(qkv_out[own_piece], q_got_more[bit - PIECE_BITS])
        v_copy.wait_recv()
        v_now[bit + 1] = v_now[bit] + v_got[bit]
    v_shards[here] = v_now[dp_bits]
    for way in range(1, shards):
        copy = copy_to(
            v_now.at[dp_bits], v_shards.at[here], next(slots), tensor=lax.rem(here + way, shards)
        )
        copy.start()
        pending.append(copy)
    v_waits = pending[-last:]
    q_back = start_dp(qkv_out.at[own_piece], qkv_out.at[own_piece], 2)
    q_back.wait_recv()
    q_back = start_dp(
        qkv_out.at[pl.ds(core * 4 + x_bit * 2, 2)], qkv_out.at[pl.ds(core * 4 + x_bit * 2, 2)], 1
    )
    q_back.wait_recv()
    q_back = start_dp(qkv_out.at[pl.ds(core * 4, 4)], qkv_out.at[pl.ds(core * 4, 4)], 0)

    for way in range(1, shards):
        piece_copy(way).wait_recv()
    total = pieces[here].astype(f32)
    for way in range(1, shards):
        total = total + z_got[way - 1].astype(f32)
    weights_out[own_piece] = total.astype(bf16)

    def own_half(low, *index):
        rows = pl.ds(0 if low else half_rows, half_rows)
        return weights_out.at[index[0], rows]

    back_a = start_dp(own_half(True, own_piece), own_half(True, own_piece), 2)
    back_b = start_dp(own_half(False, own_piece), own_half(False, own_piece), 1)
    back_a.wait_recv()
    span = pl.ds(core * 4 + x_bit * 2, 2)
    back_a = start_dp(own_half(True, span), own_half(True, span), 1)
    back_b.wait_recv()
    back_c = [
        start_dp(own_half(False, core * 4 + 2 * at + y_bit), own_half(False, core * 4 + 2 * at + y_bit), 2)
        for at in range(2)
    ]
    for moved in range(2, last):
        hop(moved, 0, False)
        if moved > 2:
            hop(moved, 0, True)
    for nth in range(1, last):
        for moved in range(1, last):
            hop(moved, nth, True)
            hop(moved, nth, False)
    back_a.wait_recv()
    for copy in back_c:
        copy.wait_recv()
    span = pl.ds(core * 4, 4)
    back_core = start_dp(weights_out.at[span], weights_out.at[span], 0)

    for copy in v_waits:
        copy.wait_recv()
    vectors_sum = v_shards[0]
    for at in range(1, shards):
        vectors_sum = vectors_sum + v_shards[at]
    vectors_out[...] = vectors_sum

    for owner in range(shards):

        @pl.when(here == owner)
        def _():
            if owner > 0:
                to_right(owner).wait_recv()
                add_arrived(owner, owner)
            if owner < last:
                to_left(owner, owner).wait_recv()
                add_arrived(owner, shards)

    load(2).wait()
    load(3).wait()

    def close(at, carry):
        rows = pl.ds(pl.multiple_of(at * (block // 4), 16), block // 4)
        tokens = tokens_own[rows, :].astype(f32)
        centred = tokens - jnp.mean(tokens, axis=1, keepdims=True)
        inverse = lax.rsqrt(jnp.mean(centred * centred, axis=1, keepdims=True) + eps_norm)
        unit = centred * inverse
        scaled = part[here, rows, :].astype(f32) * gain
        inner = (
            scaled
            - jnp.mean(scaled, axis=1, keepdims=True)
            - unit * jnp.mean(scaled * unit, axis=1, keepdims=True)
        )
        tokens_out[rows, :] = hidden_own[rows, :] + inverse * inner
        return carry

    lax.fori_loop(0, 4, close, 0)
    q_back.wait_recv()
    back_core.wait_recv()
    for copy in pending:
        copy.wait_send()
    for at in range(2):
        second(at).wait_send()
    for way in range(1, shards):
        piece_copy(way).wait_send()
    for owner in range(shards):

        @pl.when(here < owner)
        def _():
            to_right(owner).wait_send()

        @pl.when(here > owner)
        def _():
            to_left(owner).wait_send()


def back(shards, members, heads_in, pair_in, weight, gain, shift, vectors, rows, tokens, grad_hidden, exchanged):
    dp_bits = members.bit_length() - 1
    assert members == 1 << dp_bits and dp_bits >= PIECE_BITS
    f32, bf16 = jnp.float32, jnp.bfloat16
    heads, seq_len, _ = heads_in[0].shape
    columns, width = weight.shape
    block = tokens.shape[0]
    quarter = exchanged[0].shape
    piece_rows = quarter[2]
    count = columns // PIECES
    more = max(1, dp_bits - PIECE_BITS)
    copies = 20 + 2 * shards + 2 * (shards - 1) + 4 * dp_bits
    vm = pltpu.VMEM
    return pl.pallas_call(
        partial(back_kernel, shards, dp_bits),
        in_specs=[pl.BlockSpec(memory_space=vm)] * 11 + [pl.BlockSpec(memory_space=pl.ANY)] * 7,
        out_specs=[pl.BlockSpec(memory_space=vm)] * 4,
        out_shape=[
            jax.ShapeDtypeStruct((block, width), f32),
            jax.ShapeDtypeStruct(vectors.shape, f32),
            jax.ShapeDtypeStruct((PIECES, count, width), bf16),
            jax.ShapeDtypeStruct((PIECES, piece_rows, width), bf16),
        ],
        scratch_shapes=[
            vm((heads, seq_len, LANES), bf16),
            vm((heads, seq_len, LANES), f32),
            vm((heads, seq_len, LANES), f32),
            vm((heads, seq_len, LANES), f32),
            vm((heads, block, block), bf16),
            vm((heads, block, block), bf16),
            vm((block, columns), bf16),
            vm((block, width), bf16),
            vm((block, width), bf16),
            vm((block, width), f32),
            vm((shards, block, width), bf16),
            vm((shards + 1, block, width), bf16),
            vm((columns, width), f32),
            vm((8, columns), f32),
            vm((PIECES, count, width), bf16),
            vm((4, count, width), bf16),
            vm((2, count, width), bf16),
            vm((4, count, width), bf16),
            vm((2, count, width), bf16),
            vm((count, width), bf16),
            vm((more, count, width), bf16),
            vm((dp_bits + 1,) + vectors.shape, f32),
            vm((dp_bits,) + vectors.shape, f32),
            vm((shards,) + vectors.shape, f32),
            vm(quarter, bf16),
            vm(quarter, bf16),
            vm(quarter, bf16),
            vm(quarter, bf16),
            vm(quarter[1:], bf16),
            vm(quarter[1:], bf16),
            vm((shards, piece_rows, width), bf16),
            vm((more, shards, piece_rows, width), bf16),
            vm((shards - 1, piece_rows, width), bf16),
            pltpu.SemaphoreType.DMA((copies,)),
            pltpu.SemaphoreType.DMA((copies,)),
            pltpu.SemaphoreType.DMA((5,)),
        ],
        compiler_params=pltpu.CompilerParams(
            collective_id=1, has_side_effects=True, vmem_limit_bytes=67043328
        ),
        name="back",
        cost_estimate=pl.CostEstimate(
            flops=10 * heads * seq_len * seq_len * LANES, transcendentals=0, bytes_accessed=40 * block * width
        ),
    )(*heads_in, *pair_in, weight, gain, shift, vectors, rows, tokens, grad_hidden, *exchanged)


def unpack_kernel(qkv_ref, weights_ref, totals_ref, fc1_out, fc2_out, proj_out, qkv_out, fc1_bias_out, *vector_outs):
    fc_rows, proj_rows = fc1_out.shape[0], proj_out.shape[0]
    fc1_out[...] = weights_ref[0, :fc_rows].astype(jnp.float32)
    fc2_out[...] = weights_ref[0, fc_rows : 2 * fc_rows].astype(jnp.float32)
    proj_out[...] = weights_ref[0, 2 * fc_rows : 2 * fc_rows + proj_rows].astype(jnp.float32)
    qkv_out[...] = qkv_ref[0].astype(jnp.float32)

    @pl.when(pl.program_id(0) == 0)
    def _():
        width = totals_ref.shape[1]
        for at, out in enumerate(vector_outs):
            out[...] = totals_ref[at : at + 1, :].reshape(width)
        here = lax.axis_index("tensor")
        fc1_bias_out[...] = totals_ref[pl.ds(8 + here, 1), :].reshape(width)


def unpack(qkv, weights, totals, fc_rows, proj_rows):
    f32 = jnp.float32
    _, rows, width = weights.shape
    qkv_rows = qkv.shape[1]
    counts = (fc_rows, fc_rows, proj_rows, qkv_rows)
    vector = pl.BlockSpec((width,), lambda i: (0,))
    return pl.pallas_call(
        unpack_kernel,
        grid=(PIECES,),
        in_specs=[
            pl.BlockSpec((1, qkv_rows, width), lambda i: (i, 0, 0)),
            pl.BlockSpec((1, rows, width), lambda i: (i, 0, 0)),
            pl.BlockSpec(totals.shape, lambda i: (0, 0)),
        ],
        out_specs=[pl.BlockSpec((count, width), lambda i: (i, 0)) for count in counts] + [vector] * 9,
        out_shape=[jax.ShapeDtypeStruct((PIECES * count, width), f32) for count in counts]
        + [jax.ShapeDtypeStruct((width,), f32)] * 9,
        name="unpack",
    )(qkv, weights, totals)


def start_kernel(
    shards,
    dp_bits,
    tokens_ref,
    ids_ref,
    gain_ref,
    shift_ref,
    qkv_ref,
    qv_bias_ref,
    fc1_ref,
    fc2_ref,
    proj_ref,
    fc1_bias_ref,
    normed_out,
    q_out,
    k_out,
    v_out,
    pairs_out,
    singles_out,
    pairs_here,
    singles_here,
    weights_out,
    bias_out,
    blocks,
    normed_all,
    queries,
    keys,
    values,
    peaks,
    sums,
    scores,
    weights,
    q_extra,
    k_extra,
    own,
    chain,
    send,
    recv,
    local,
    stored,
):
    f32, bf16 = jnp.float32, jnp.bfloat16
    member, here = lax.axis_index("dp"), lax.axis_index("tensor")
    core, x_bit, y_bit = bit_of(member, 0), bit_of(member, 1), bit_of(member, 2)
    own_piece = core * 4 + x_bit * 2 + y_bit
    block, width = tokens_ref.shape
    heads = queries.shape[0]
    seq_len = ids_ref.shape[1]
    last = shards - 1
    reach = -(-(MOST_TOKENS - 1) // block)
    slots = iter(range(send.shape[0]))
    pending = []

    def copy_to(src, dst, at, **peer):
        return pltpu.make_async_remote_copy(
            src_ref=src, dst_ref=dst, send_sem=send.at[at], recv_sem=recv.at[at], device_id=peer, device_id_type=MESH
        )

    def start_dp(src, dst, bit):
        copy = copy_to(src, dst, next(slots), dp=partner_of(member, bit))
        copy.start()
        pending.append(copy)
        return copy

    fc1_rows, fc2_rows, proj_rows = (ref.shape[0] // PIECES for ref in (fc1_ref, fc2_ref, proj_ref))
    loads = []
    for at, (ref, first, count) in enumerate(
        ((fc1_ref, 0, fc1_rows), (fc2_ref, fc1_rows, fc2_rows))
    ):
        rows = pl.ds(pl.multiple_of(own_piece * count, 16), count)
        loads.append(pltpu.make_async_copy(ref.at[rows], own.at[first : first + count], local.at[at]))
        loads[-1].start()
    used = fc1_rows + fc2_rows
    rows = pl.ds(pl.multiple_of(own_piece * proj_rows, 8), proj_rows)
    own[used : used + proj_rows, :] = proj_ref[rows, :]
    used += proj_rows
    own[used:, :] = jnp.zeros((own.shape[0] - used, width), bf16)
    gain, shift = (ref[...].reshape(1, width) for ref in (gain_ref, shift_ref))
    bias_out[here] = fc1_bias_ref[...].reshape(1, width)
    greet(dp_bits, shards)
    for load in loads:
        load.wait()

    chains = {}
    for name, first, rest in (("w", own, chain), ("t", tokens_ref, blocks)):
        chains[name] = (
            first,
            rest,
            [next(slots) for _ in range(shards)],
            [next(slots) for _ in range(shards)],
        )

    def hop_copy(name, owner, rightward, from_own):
        first, rest, right_slots, left_slots = chains[name]
        src = first if from_own else rest.at[owner]
        step = 1 if rightward else last
        at = (right_slots if rightward else left_slots)[owner]
        return copy_to(src, rest.at[owner], at, tensor=lax.rem(here + step, shards))

    def send_own(name, rightward):
        for owner in range(shards):
            if owner != (last if rightward else 0):

                @pl.when(here == owner)
                def _():
                    hop_copy(name, owner, rightward, True).start()

    def hop(name, time, then=None):
        for at in range(shards):
            for rightward, owner, end in ((True, at - time, last), (False, at + time, 0)):
                if 0 <= owner <= last:

                    @pl.when(here == at)
                    def _():
                        hop_copy(name, owner, rightward, False).wait_recv()
                        if at != end:
                            hop_copy(name, owner, rightward, False).start()
                            if then is not None and owner in (0, last):
                                hop_copy(then, at, rightward, True).start()

    send_own("w", True)
    send_own("w", False)

    @pl.when(here == 0)
    def _():
        hop_copy("t", 0, True, True).start()

    @pl.when(here == last)
    def _():
        hop_copy("t", last, False, True).start()

    bias_copies = []
    for way in range(1, shards):
        copy = copy_to(
            bias_out.at[here], bias_out.at[here], next(slots), tensor=lax.rem(here + way, shards)
        )
        copy.start()
        bias_copies.append(copy)
    pending.extend(bias_copies)

    large = -MASKED
    segments = lax.broadcasted_iota(jnp.int32, (8, seq_len), 0)
    same = jnp.where(segments == ids_ref[...], 1.0, 0.0).astype(bf16)
    select = lax.broadcasted_iota(jnp.int32, (8, LANES), 1) - HEAD_DIM == lax.broadcasted_iota(
        jnp.int32, (8, LANES), 0
    )
    matched = contract_rows(same, jnp.where(select, 1.0, 0.0).astype(bf16))
    lane = lax.broadcasted_iota(jnp.int32, (seq_len, LANES), 1)
    segment_lane = (lane >= HEAD_DIM) & (lane < HEAD_DIM + 8)
    ones_lane = (lane >= HEAD_DIM + 8) & (lane < HEAD_DIM + 11)
    q_extra[...] = jnp.where(segment_lane, (matched - 1.0) * large, 0.0).astype(bf16)
    k_extra[...] = jnp.where(ones_lane, 1.0, matched).astype(bf16)
    low_half = lax.broadcasted_iota(jnp.int32, (block, LANES), 1) < HEAD_DIM
    v_lane = lax.broadcasted_iota(jnp.int32, (block, LANES), 1)
    v_extra = jnp.where((v_lane >= HEAD_DIM) & (v_lane < HEAD_DIM + 3), 1.0, 0.0).astype(bf16)

    def rows_of(owner, count=block):
        return pl.ds(pl.multiple_of(owner * count, 16), count)

    def store(which, owner):
        rows = rows_of(owner)
        source, out = (
            (normed_all.at[rows], normed_out.at[rows]),
            (queries.at[:, rows], q_out.at[:, rows]),
            (keys.at[:, rows], k_out.at[:, rows]),
            (values.at[:, rows], v_out.at[:, rows]),
        )[which]
        return pltpu.make_async_copy(source, out, stored.at[which, owner])

    def project_block(source, owner):
        tokens = source.astype(f32)
        centred = tokens - jnp.mean(tokens, axis=1, keepdims=True)
        inverse = lax.rsqrt(jnp.mean(centred * centred, axis=1, keepdims=True) + eps_norm)
        normed = (centred * inverse * gain + shift).astype(bf16)
        rows = rows_of(owner)
        normed_all[rows, :] = normed
        for which, out in ((0, queries), (1, keys), (2, values)):
            product = times_transposed(normed, qkv_ref[which])
            if which != 1:
                product = product + qv_bias_ref[which // 2 : which // 2 + 1, :]
            if which == 0:
                product = product.astype(bf16).astype(f32) * HEAD_DIM**-0.5
            extra = v_extra if which == 2 else (q_extra if which == 0 else k_extra)[rows, :]
            for head in range(heads):
                first = (head // 2) * LANES
                tile = product[:, first : first + LANES]
                if tile.shape[1] < LANES:
                    blank = jnp.zeros((block, LANES - tile.shape[1]), f32)
                    tile = jnp.concatenate([tile, blank], axis=1)
                if head % 2:
                    tile = pltpu.roll(tile, HEAD_DIM, 1)
                out[head, rows, :] = jnp.where(low_half, tile, extra.astype(f32)).astype(bf16)
        store(0, owner).start()
        store(2, owner).start()
        store(3, owner).start()

    peaks[...] = jnp.full_like(peaks, -3e38)
    sums[...] = jnp.zeros_like(sums)

    def away(index):
        return jnp.maximum(index - here, here - index)

    def visit(owner, other):
        rows, across = rows_of(owner), rows_of(other)
        for head in range(heads):
            scores[head] = times_transposed(queries[head, rows, :], keys[head, across, :])
        for head in range(heads):
            old_peak = peaks[head, rows, :]
            new_peak = jnp.maximum(old_peak, jnp.max(scores[head], axis=1, keepdims=True))
            peaks[head, rows, :] = new_peak
            spread = jnp.concatenate([new_peak] * -(-block // LANES), axis=1)[:, :block]
            weights[head] = jnp.exp(scores[head] - spread).astype(bf16)
            sums[head, rows, :] = sums[head, rows, :] * jnp.exp(old_peak - new_peak)
        for head in range(heads):
            sums[head, rows, :] += jnp.dot(
                weights[head], values[head, across, :], preferred_element_type=f32
            )

    pair_slots = [next(slots) for _ in range(shards)]
    single_slots = [next(slots) for _ in range(shards)]

    def exchange(owner, source):
        half_block = block // 2
        return [
            pltpu.make_async_remote_copy(
                src_ref=out.at[rows_of(owner, count)],
                dst_ref=landing.at[source],
                send_sem=send.at[base + owner],
                recv_sem=recv.at[base + source],
                device_id={"tensor": owner},
                device_id_type=MESH,
            )
            for out, landing, count, base in (
                (pairs_out, pairs_here, block, pair_slots[0]),
                (singles_out, singles_here, half_block, single_slots[0]),
            )
        ]

    def complete(owner):
        rows, half_block = rows_of(owner), block // 2
        parts = []
        for head in range(heads):
            total = sums[head, rows, HEAD_DIM : HEAD_DIM + 1]
            parts.append(sums[head, rows, :] / total)
            high, middle_part, low = split_three(-(peaks[head, rows, :] + jnp.log(total)))
            kept = queries[head, rows, :].astype(f32)
            for at, value in enumerate((high, middle_part, low)):
                kept = jnp.where(v_lane == HEAD_DIM + 8 + at, value.astype(f32), kept)
            queries[head, rows, :] = kept.astype(bf16)
        pair = join_lanes(parts[0], parts[1]).astype(bf16)
        single = join_lanes(parts[2][:half_block], parts[2][half_block:]).astype(bf16)
        pairs_out[rows, :] = pair
        singles_out[rows_of(owner, half_block), :] = single
        store(1, owner).start()

        @pl.when(owner == here)
        def _():
            pairs_here[here] = pair
            singles_here[here] = single

        @pl.when(owner != here)
        def _():
            for copy in exchange(owner, here):
                copy.start()

    def attend_known(time):
        def each(at, carry):
            owner = lax.rem(here + shards // 2 + at, shards)

            def other_block(other, carry):
                near = jnp.maximum(owner - other, other - owner) <= reach
                known = jnp.maximum(jnp.maximum(away(owner), away(other)), 1)

                @pl.when(near & (known == time))
                def _():
                    visit(owner, other)

                return carry

            lax.fori_loop(0, shards, other_block, 0)
            final = jnp.maximum(
                away(jnp.maximum(owner - reach, 0)), away(jnp.minimum(owner + reach, last))
            )

            @pl.when(final == time)
            def _():
                complete(owner)

            return carry

        lax.fori_loop(0, shards, each, 0)

    project_block(tokens_ref[...], here)
    for time in range(1, shards):
        hop("w", time, "t")

    half = shards // 2
    stores = []
    for owner in range(shards):
        at = 2 + owner

        @pl.when(here == owner)
        def _():
            pltpu.make_async_copy(own, weights_out.at[own_piece, owner], local.at[at]).start()

        @pl.when(here != owner)
        def _():
            pltpu.make_async_copy(chain.at[owner], weights_out.at[own_piece, owner], local.at[at]).start()

        stores.append(pltpu.make_async_copy(own, weights_out.at[own_piece, owner], local.at[at]))
    for saved in stores:
        saved.wait()

    def part(low, pieces):
        owners = pl.ds(0, half) if low else pl.ds(half, shards - half)
        return weights_out.at[pieces, owners]

    def gather_stage(low, pieces, bit):
        return [start_dp(part(low, at), part(low, at), bit) for at in pieces]

    def wait_all(copies):
        for copy in copies:
            copy.wait_recv()

    stage = gather_stage(True, [own_piece], 2) + gather_stage(False, [own_piece], 1)

    def arrived(time):
        def each(at, carry):
            owner = here + (2 * at - 1) * time

            @pl.when((owner >= 0) & (owner <= last))
            def _():
                project_block(blocks[owner], owner)

            return carry

        lax.fori_loop(0, 2, each, 0)

    for time in range(1, shards):
        hop("t", time)
        arrived(time)
        if time == 1:
            wait_all(stage)
            stage = gather_stage(True, [pl.ds(core * 4 + x_bit * 2, 2)], 1) + gather_stage(
                False, [core * 4 + 2 * at + y_bit for at in range(2)], 2
            )
        attend_known(time)
        if time == 2:
            wait_all(stage)
            stage = [start_dp(weights_out.at[pl.ds(core * 4, 4)], weights_out.at[pl.ds(core * 4, 4)], 0)]
    for owner in range(shards):

        @pl.when(here != owner)
        def _():
            for copy in exchange(here, owner):
                copy.wait_recv()
            for copy in exchange(owner, here):
                copy.wait_send()

        for which in range(4):
            store(which, owner).wait()
    wait_all(stage)
    wait_all(bias_copies)
    for copy in pending:
        copy.wait_send()
    for name in chains:
        for at in range(shards):
            for owner in range(shards):
                if owner <= at < last:

                    @pl.when(here == at)
                    def _():
                        hop_copy(name, owner, True, False).wait_send()

                if owner >= at > 0:

                    @pl.when(here == at)
                    def _():
                        hop_copy(name, owner, False, False).wait_send()


def start(shards, members, tokens, ids, gain, shift, qkv, qv_bias, fc1, fc2, proj, fc1_bias):
    dp_bits = members.bit_length() - 1
    assert members == 1 << dp_bits and dp_bits >= PIECE_BITS and shards >= 3
    f32, bf16 = jnp.float32, jnp.bfloat16
    block, width = tokens.shape
    seq_len = block * shards
    heads = qkv.shape[1] // HEAD_DIM
    rows = -(-(fc1.shape[0] + fc2.shape[0] + proj.shape[0]) // PIECES // 16) * 16
    copies = 6 * shards + (shards - 1) + 6
    vm = pltpu.VMEM
    on_chip = pl.BlockSpec(memory_space=vm)
    anywhere = pl.BlockSpec(memory_space=pl.ANY)
    head_rows = jax.ShapeDtypeStruct((heads, seq_len, LANES), bf16)
    return pl.pallas_call(
        partial(start_kernel, shards, dp_bits),
        in_specs=[on_chip] * 6 + [anywhere] * 2 + [on_chip] * 2,
        out_specs=[anywhere] * 4
        + [on_chip] * 4
        + [anywhere, on_chip],
        out_shape=[
            jax.ShapeDtypeStruct((seq_len, width), bf16),
            head_rows,
            head_rows,
            head_rows,
            jax.ShapeDtypeStruct((seq_len, LANES), bf16),
            jax.ShapeDtypeStruct((seq_len // 2, LANES), bf16),
            jax.ShapeDtypeStruct((shards, block, LANES), bf16),
            jax.ShapeDtypeStruct((shards, block // 2, LANES), bf16),
            jax.ShapeDtypeStruct((PIECES, shards, rows, width), bf16),
            jax.ShapeDtypeStruct((shards, 1, width), f32),
        ],
        scratch_shapes=[
            vm((shards, block, width), bf16),
            vm((seq_len, width), bf16),
            vm((heads, seq_len, LANES), bf16),
            vm((heads, seq_len, LANES), bf16),
            vm((heads, seq_len, LANES), bf16),
            vm((heads, seq_len, LANES), f32),
            vm((heads, seq_len, LANES), f32),
            vm((heads, block, block), f32),
            vm((heads, block, block), bf16),
            vm((seq_len, LANES), bf16),
            vm((seq_len, LANES), bf16),
            vm((rows, width), bf16),
            vm((shards, rows, width), bf16),
            pltpu.SemaphoreType.DMA((copies,)),
            pltpu.SemaphoreType.DMA((copies,)),
            pltpu.SemaphoreType.DMA((2 + shards,)),
            pltpu.SemaphoreType.DMA((4, shards)),
        ],
        compiler_params=pltpu.CompilerParams(
            collective_id=0, has_side_effects=True, vmem_limit_bytes=62 * 1024 * 1024
        ),
        name="start",
        cost_estimate=pl.CostEstimate(
            flops=6 * seq_len * width * heads * HEAD_DIM, transcendentals=0, bytes_accessed=40 * block * width
        ),
    )(tokens, ids, gain, shift, qkv, qv_bias, fc1, fc2, proj, fc1_bias)


CHUNK = 32


def middle_kernel(
    shards,
    dp_bits,
    pairs,
    singles,
    weights_ref,
    fc1_bias_ref,
    proj_bias_ref,
    scale_one_ref,
    gain_ref,
    shift_ref,
    fc2_bias_ref,
    scale_two_ref,
    tokens_ref,
    cotangent_ref,
    block_out,
    hidden_grad_out,
    pair_grads_out,
    single_grads_out,
    vectors_out,
    a_keep,
    a_away,
    b_keep,
    b_away,
    weights,
    attended,
    proj,
    branch,
    hidden,
    normed,
    wide,
    total,
    active,
    slope,
    grad_pre,
    grad_mlp,
    grad_branch,
    pair_grads,
    single_grads,
    got,
    send,
    recv,
    local,
):
    f32, bf16 = jnp.float32, jnp.bfloat16
    member, here = lax.axis_index("dp"), lax.axis_index("tensor")
    core, x_bit, y_bit = bit_of(member, 0), bit_of(member, 1), bit_of(member, 2)
    block, width = tokens_ref.shape
    columns = width // shards
    half = PIECES // 2
    fc_rows, proj_rows = width // PIECES, columns // PIECES
    proj_first = 2 * fc_rows
    slots = iter(range(send.shape[0]))
    proj_bias, scale_one, gain, shift, fc2_bias, scale_two = (
        ref[...].reshape(1, width)
        for ref in (proj_bias_ref, scale_one_ref, gain_ref, shift_ref, fc2_bias_ref, scale_two_ref)
    )

    def copy_to(src, dst, at, **peer):
        return pltpu.make_async_remote_copy(
            src_ref=src, dst_ref=dst, send_sem=send.at[at], recv_sem=recv.at[at], device_id=peer, device_id_type=MESH
        )

    loads = []
    for owner in range(shards):
        load = pltpu.make_async_copy(weights_ref.at[:, owner], weights.at[:, owner], local.at[owner])
        load.start()
        loads.append(load)
    greet(dp_bits, shards)

    for load in loads:
        load.wait()

    def fc1_of(owner):
        return weights[:, owner, :fc_rows, :].reshape(width, width)

    def fc2_of(owner):
        return weights[:, owner, fc_rows:proj_first, :].reshape(width, width)

    def proj_of(owner):
        return weights[:, owner, proj_first : proj_first + proj_rows, :].reshape(columns, width)

    def chunk(at):
        return pl.ds(pl.multiple_of(at * CHUNK, CHUNK), CHUNK)

    def each_chunk(body, init):
        return lax.fori_loop(0, block // CHUNK, body, init)

    def column_sum(value):
        return jnp.sum(value, axis=0, keepdims=True)

    def unit_of(value):
        centred = value - jnp.mean(value, axis=1, keepdims=True)
        inverse = lax.rsqrt(jnp.mean(centred * centred, axis=1, keepdims=True) + eps_norm)
        return centred * inverse, inverse

    third = shards * LANES
    for owner in range(shards):
        own_proj = proj_of(owner)
        proj[owner * LANES : (owner + 1) * LANES, :] = own_proj[:LANES]
        proj[third + owner * HEAD_DIM : third + (owner + 1) * HEAD_DIM, :] = own_proj[LANES:]
    middle_row = block // 2
    for owner in range(shards):
        attended[:, owner * LANES : (owner + 1) * LANES] = pairs[owner]
    lane = lax.broadcasted_iota(jnp.int32, (middle_row, LANES), 1)
    low_half = lane < HEAD_DIM

    def swapped(value):
        return pltpu.roll(value, HEAD_DIM, 1)

    for at in range(shards // 2):
        one, two = singles[2 * at].astype(f32), singles[2 * at + 1].astype(f32)
        columns_here = slice(third + at * LANES, third + (at + 1) * LANES)
        attended[:middle_row, columns_here] = jnp.where(low_half, one, swapped(two)).astype(bf16)
        attended[middle_row:, columns_here] = jnp.where(low_half, swapped(one), two).astype(bf16)
    product = jnp.dot(attended[...], proj[...], preferred_element_type=f32)
    branch[...] = product

    def enter(at, carry):
        rows = chunk(at)
        value = branch[rows, :] + proj_bias
        branch[rows, :] = value
        value = tokens_ref[rows, :].astype(f32) + scale_one * value
        hidden[rows, :] = value
        unit, _ = unit_of(value)
        normed[rows, :] = (unit * gain + shift).astype(bf16)
        return carry

    each_chunk(enter, 0)

    def forward(owner, carry):
        wide[:block, :] = jnp.dot(normed[...], fc1_of(owner), preferred_element_type=f32)
        bias = fc1_bias_ref[owner]

        def activate(at, carry):
            rows = chunk(at)
            value = wide[rows, :] + bias
            below = 0.5 * (1.0 + lax.erf(value * 0.5**0.5))
            active[owner, rows, :] = (value * below).astype(bf16)
            density = jnp.exp(value * value * -0.5) * (0.5 / math.pi) ** 0.5
            slope[owner, rows, :] = below + value * density
            return carry

        each_chunk(activate, 0)
        product = jnp.dot(active[owner], fc2_of(owner), preferred_element_type=f32)
        total[...] = jnp.where(owner == 0, product, total[...] + product)
        return carry

    lax.fori_loop(0, shards, forward, 0)
    empty = jnp.zeros((1, width), f32)

    def turn(at, sums):
        rows = chunk(at)
        value = total[rows, :] + fc2_bias
        block_out[rows, :] = (hidden[rows, :] + scale_two * value).astype(bf16)
        grad = cotangent_ref[rows, :].astype(f32)
        grad_mlp[rows, :] = (grad * scale_two).astype(bf16)
        return (
            sums[0] + column_sum(grad * value),
            sums[1] + column_sum(grad_mlp[rows, :].astype(f32)),
        )

    scale_two_sum, fc2_bias_sum = each_chunk(turn, (empty, empty))

    def backward(owner, carry):
        wide[:block, :] = times_transposed(grad_mlp[...], fc2_of(owner))

        def slopes(at, sums):
            rows = chunk(at)
            value = (wide[rows, :] * slope[owner, rows, :]).astype(bf16)
            grad_pre[owner, rows, :] = value
            return sums + column_sum(value.astype(f32))

        vectors_out[pl.ds(8 + owner, 1), :] = each_chunk(slopes, empty)
        product = times_transposed(grad_pre[owner], fc1_of(owner))
        total[...] = jnp.where(owner == 0, product, total[...] + product)
        return carry

    lax.fori_loop(0, shards, backward, 0)

    def leave(at, sums):
        rows = chunk(at)
        grad = total[rows, :]
        unit, inverse = unit_of(hidden[rows, :])
        scaled = grad * gain
        inner = (
            scaled
            - jnp.mean(scaled, axis=1, keepdims=True)
            - unit * jnp.mean(scaled * unit, axis=1, keepdims=True)
        )
        value = cotangent_ref[rows, :].astype(f32) + inverse * inner
        hidden_grad_out[rows, :] = value
        rounded = (value * scale_one).astype(bf16)
        grad_branch[rows, :] = rounded
        return (
            sums[0] + column_sum(grad * unit),
            sums[1] + column_sum(grad),
            sums[2] + column_sum(value * branch[rows, :]),
            sums[3] + column_sum(rounded.astype(f32)),
        )

    gain_sum, shift_sum, scale_one_sum, proj_bias_sum = each_chunk(leave, (empty,) * 4)
    for at, value in enumerate(
        (empty, empty, proj_bias_sum, scale_one_sum, gain_sum, shift_sum, fc2_bias_sum, scale_two_sum)
    ):
        vectors_out[at : at + 1, :] = value
    vectors_out[12:, :] = jnp.zeros((vectors_out.shape[0] - 12, width), f32)

    wide[:block, :] = times_transposed(grad_branch[...], proj[...])
    for owner in range(shards):
        pair_grads[owner] = wide[:block, owner * LANES : (owner + 1) * LANES].astype(bf16)
    for at in range(shards // 2):
        columns_here = slice(third + at * LANES, third + (at + 1) * LANES)
        upper, lower = wide[:middle_row, columns_here], wide[middle_row:block, columns_here]
        single_grads[2 * at] = jnp.where(low_half, upper, swapped(lower)).astype(bf16)
        single_grads[2 * at + 1] = jnp.where(low_half, swapped(upper), lower).astype(bf16)
    back = []
    for source, out in ((pair_grads, pair_grads_out), (single_grads, single_grads_out)):
        for way in range(1, shards):
            target = lax.rem(here + way, shards)
            copy = copy_to(source.at[target], out.at[here], next(slots), tensor=target)
            copy.start()
            back.append(copy)
        out[here] = source[here]

    first_slot = next(slots)

    def core_copy(owner):
        return pltpu.make_async_remote_copy(
            src_ref=weights.at[pl.ds((1 - core) * half, half), owner],
            dst_ref=got.at[:, owner],
            send_sem=send.at[first_slot + owner],
            recv_sem=recv.at[first_slot + owner],
            device_id={"dp": partner_of(member, 0)},
            device_id_type=MESH,
        )

    wide[...] = contract_rows(attended[:, :], grad_branch[...])
    for owner in range(shards):
        for piece in range(PIECES):
            first, end = piece * proj_rows, (piece + 1) * proj_rows
            for low, high, start_row in ((0, LANES, owner * LANES), (LANES, columns, third + owner * HEAD_DIM)):
                begin, stop = max(first, low), min(end, high)
                if begin < stop:
                    rows = slice(start_row + begin - low, start_row + stop - low)
                    to = slice(proj_first + begin - first, proj_first + stop - first)
                    weights[piece, owner, to, :] = wide[rows, :].astype(bf16)

    def weight_grads(owner, carry):
        for left, right, first, count in (
            (normed[...], grad_pre[owner], 0, fc_rows),
            (active[owner], grad_mlp[...], fc_rows, fc_rows),
        ):
            product = contract_rows(left, right).astype(bf16)
            weights[:, owner, first : first + count, :] = product.reshape(PIECES, count, width)
        core_copy(owner).start()
        return carry

    lax.fori_loop(0, shards, weight_grads, 0)
    split = shards // 2
    for owner in range(shards):
        core_copy(owner).wait_recv()
        if owner < split:
            for y in range(2):
                for out, x in ((a_keep, x_bit), (a_away, 1 - x_bit)):
                    out[y, owner] = rounded_sum(weights[core * half + x * 2 + y, owner], got[x * 2 + y, owner])
        else:
            for x in range(2):
                for out, y in ((b_keep, y_bit), (b_away, 1 - y_bit)):
                    out[x, owner - split] = rounded_sum(
                        weights[core * half + x * 2 + y, owner], got[x * 2 + y, owner]
                    )
    for copy in back:
        copy.wait_recv()
    for copy in back:
        copy.wait_send()
    for owner in range(shards):
        core_copy(owner).wait_send()


def middle(shards, members, pairs, singles, weights, fc1_bias, vectors, tokens, cotangent):
    dp_bits = members.bit_length() - 1
    f32, bf16 = jnp.float32, jnp.bfloat16
    block, width = tokens.shape
    rows = weights.shape[2]
    vm = pltpu.VMEM
    on_chip = pl.BlockSpec(memory_space=vm)
    quarter = jax.ShapeDtypeStruct((2, shards // 2, rows, width), bf16)
    copies = 2 * (shards - 1) + shards
    return pl.pallas_call(
        partial(middle_kernel, shards, dp_bits),
        in_specs=[on_chip, on_chip, pl.BlockSpec(memory_space=pl.ANY)] + [on_chip] * 9,
        out_specs=[on_chip] * 9,
        out_shape=[
            jax.ShapeDtypeStruct((block, width), bf16),
            jax.ShapeDtypeStruct((block, width), f32),
            jax.ShapeDtypeStruct((shards, block, LANES), bf16),
            jax.ShapeDtypeStruct((shards, block // 2, LANES), bf16),
            jax.ShapeDtypeStruct((16, width), f32),
            quarter,
            quarter,
            quarter,
            quarter,
        ],
        scratch_shapes=[
            vm(weights.shape, bf16),
            vm((block, width), bf16),
            vm((width, width), bf16),
            vm((block, width), f32),
            vm((block, width), f32),
            vm((block, width), bf16),
            vm((width, width), f32),
            vm((block, width), f32),
            vm((shards, block, width), bf16),
            vm((shards, block, width), f32),
            vm((shards, block, width), bf16),
            vm((block, width), bf16),
            vm((block, width), bf16),
            vm((shards, block, LANES), bf16),
            vm((shards, block // 2, LANES), bf16),
            vm((PIECES // 2, shards, rows, width), bf16),
            pltpu.SemaphoreType.DMA((copies,)),
            pltpu.SemaphoreType.DMA((copies,)),
            pltpu.SemaphoreType.DMA((shards,)),
        ],
        compiler_params=pltpu.CompilerParams(
            collective_id=2, has_side_effects=True, vmem_limit_bytes=62 * 1024 * 1024
        ),
        name="middle",
        cost_estimate=pl.CostEstimate(
            flops=12 * block * width * width * shards, transcendentals=0, bytes_accessed=40 * block * width
        ),
    )(pairs, singles, weights, fc1_bias, *vectors, tokens, cotangent)


eps_norm = 1e-06


def on_device(
    shards,
    members,
    tokens,
    segment_ids,
    ln1_gain,
    ln1_bias,
    qkv_weight,
    qv_bias,
    proj_weight,
    proj_bias,
    scale_one,
    ln2_gain,
    ln2_bias,
    fc1_weight,
    fc1_bias,
    fc2_weight,
    fc2_bias,
    scale_two,
    cotangent,
):
    f32, bf16 = jnp.float32, jnp.bfloat16
    seq_len = segment_ids.shape[1]
    rows_here, width = tokens.shape
    head_columns = qkv_weight.shape[2]
    heads = head_columns // HEAD_DIM
    hidden_here = fc1_weight.shape[1]
    ids = segment_ids[0]
    here = lax.axis_index("tensor")

    turned = qkv_weight.transpose(0, 2, 1)
    full_one, queries, keys, values, pairs, singles, pairs_here, singles_here, gathered, fc1_bias_full = start(
        shards,
        members,
        tokens,
        segment_ids,
        ln1_gain,
        ln1_bias,
        turned,
        qv_bias,
        fc1_weight,
        fc2_weight,
        proj_weight,
        fc1_bias,
    )
    params = (proj_bias, scale_one, ln2_gain, ln2_bias, fc2_bias, scale_two)
    block_out, grad_hidden, pair_grads, single_grads, vectors, a_keep, a_away, b_keep, b_away = middle(
        shards, members, pairs_here, singles_here, gathered, fc1_bias_full, params, tokens, cotangent
    )
    pair_grads = pair_grads.reshape(seq_len, LANES)
    single_grads = single_grads.reshape(seq_len // 2, LANES)

    grad_tokens, totals, qkv_pieces, weight_pieces = back(
        shards,
        members,
        (queries, keys, values),
        (pairs, singles, pair_grads, single_grads),
        turned.reshape(3 * head_columns, width),
        ln1_gain,
        ln1_bias,
        vectors,
        full_one,
        tokens,
        grad_hidden,
        (a_keep, a_away, b_keep, b_away),
    )
    fc1_grad, fc2_grad, proj_grad, qkv_grad, fc1_bias_grad, *sums = unpack(
        qkv_pieces, weight_pieces, totals, width // PIECES, head_columns // PIECES
    )
    qkv_grad = qkv_grad.reshape(3, head_columns, width).transpose(0, 2, 1)
    qv_sums = lax.dynamic_index_in_dim(totals, 12 + here, 0, keepdims=False)
    qv_grad = jnp.stack([qv_sums[:head_columns], qv_sums[2 * head_columns : 3 * head_columns]])
    return (
        block_out,
        grad_tokens,
        sums[0],
        sums[1],
        qkv_grad,
        qv_grad,
        proj_grad,
        sums[2],
        sums[3],
        sums[4],
        sums[5],
        fc1_grad,
        fc1_bias_grad,
        fc2_grad,
        sums[6],
        sums[7],
    )


def solution(mesh):
    rows = P(("dp", "tensor"), None)
    columns = P(None, "tensor")
    return jax.shard_map(
        partial(on_device, mesh.shape["tensor"], mesh.shape["dp"]),
        mesh=mesh,
        in_specs=(
            rows,
            P("dp", None),
            P(),
            P(),
            P(None, None, "tensor"),
            columns,
            P("tensor", None),
            P(),
            P(),
            P(),
            P(),
            columns,
            P("tensor"),
            P("tensor", None),
            P(),
            P(),
            rows,
        ),
        out_specs=(
            rows,
            rows,
            P(),
            P(),
            P(None, None, "tensor"),
            columns,
            P("tensor", None),
            P(),
            P(),
            P(),
            P(),
            columns,
            P("tensor"),
            P("tensor", None),
            P(),
            P(),
        ),
        check_vma=False,
    )
```

```python
from functools import partial
import math

import jax, jax.numpy as jnp
from jax import lax
from jax.experimental import pallas as pl
from jax.experimental.pallas import tpu as pltpu

from jax.sharding import PartitionSpec as P

HEAD_DIM = 64
LANES = 128
MOST_TOKENS = 1152
MASKED = -(2.0**100)


def contract_rows(left, right):
    return lax.dot_general(left, right, (((0,), (0,)), ((), ())), preferred_element_type=jnp.float32)


def times_transposed(left, right, precision=None):
    return lax.dot_general(
        left, right, (((1,), (1,)), ((), ())), preferred_element_type=jnp.float32, precision=precision
    )


def split_three(value):
    high = value.astype(jnp.bfloat16)
    rest = value - high.astype(jnp.float32)
    middle = rest.astype(jnp.bfloat16)
    low = (rest - middle.astype(jnp.float32)).astype(jnp.bfloat16)
    return (high, middle, low)


def join_lanes(low, high):
    lane = lax.broadcasted_iota(jnp.int32, low.shape, 1)
    return jnp.where(lane < HEAD_DIM, low, pltpu.roll(high, HEAD_DIM, 1))


MESH = pl.DeviceIdType.MESH
PIECES = 8
PIECE_BITS = 3


def rounded_sum(left, right):
    return (left.astype(jnp.float32) + right.astype(jnp.float32)).astype(jnp.bfloat16)


def bit_of(index, bit):
    return lax.rem(index // (1 << bit), 2)


def partner_of(index, bit):
    return index + (1 - 2 * bit_of(index, bit)) * (1 << bit)


def greet(dp_bits, shards):
    barrier = pltpu.get_barrier_semaphore()
    member, here = lax.axis_index("dp"), lax.axis_index("tensor")
    peers = [{"dp": partner_of(member, bit)} for bit in range(dp_bits)]
    peers += [{"tensor": lax.rem(here + way, shards)} for way in range(1, shards)]
    for peer in peers:
        pl.semaphore_signal(barrier, inc=1, device_id=peer, device_id_type=MESH)
    pl.semaphore_wait(barrier, len(peers))


def back_kernel(
    shards,
    dp_bits,
    q_ref,
    k_ref,
    v_ref,
    pair_ref,
    single_ref,
    pair_grad_ref,
    single_grad_ref,
    weight_ref,
    gain_ref,
    shift_ref,
    vectors_ref,
    rows_ref,
    tokens_ref,
    hidden_ref,
    a_keep,
    a_away,
    b_keep,
    b_away,
    early,
    tokens_out,
    vectors_out,
    qkv_out,
    weights_out,
    grad_heads,
    dq,
    dk,
    dv,
    probs,
    grad_scores,
    packed,
    rows_own,
    tokens_own,
    hidden_own,
    part,
    arrived,
    q_wide,
    column_sums,
    q_all,
    q_half,
    q_quarter,
    q_got_core,
    q_got_x,
    q_got_y,
    q_got_more,
    v_now,
    v_got,
    v_shards,
    a_sum,
    b_sum,
    a_got,
    b_got,
    a_second,
    b_second,
    pieces,
    early_own,
    pieces_more,
    early_more,
    z_got,
    early_got,
    send,
    recv,
    local,
):
    f32, bf16 = jnp.float32, jnp.bfloat16
    member, here = lax.axis_index("dp"), lax.axis_index("tensor")
    core, x_bit, y_bit = bit_of(member, 0), bit_of(member, 1), bit_of(member, 2)
    own_piece = core * 4 + x_bit * 2 + y_bit
    block, width = part.shape[1], part.shape[2]
    heads = q_ref.shape[0]
    columns = weight_ref.shape[0]
    half_rows = weights_out.shape[1] // 2
    last = shards - 1
    reach = -(-(MOST_TOKENS - 1) // block)
    gain, shift = (ref[...].reshape(1, width) for ref in (gain_ref, shift_ref))
    slots = iter(range(send.shape[0]))
    pending = []

    def copy_to(src, dst, at, **peer):
        return pltpu.make_async_remote_copy(
            src_ref=src, dst_ref=dst, send_sem=send.at[at], recv_sem=recv.at[at], device_id=peer, device_id_type=MESH
        )

    def start_dp(src, dst, bit, keep=True):
        copy = copy_to(src, dst, next(slots), dp=partner_of(member, bit))
        copy.start()
        if keep:
            pending.append(copy)
        return copy

    def load(at):
        source, landing = (
            (a_keep, a_sum),
            (b_keep, b_sum),
            (tokens_ref, tokens_own),
            (hidden_ref, hidden_own),
            (early, early_own),
        )[at]
        return pltpu.make_async_copy(source, landing, local.at[at])

    def load_rows(owner):
        rows = pl.ds(pl.multiple_of(owner * block, 16), block)
        return pltpu.make_async_copy(rows_ref.at[rows], rows_own, local.at[5])

    for at in range(5):
        load(at).start()
    load_rows(last).start()
    greet(dp_bits, shards)
    start_dp(a_away, a_got, 1)
    start_dp(b_away, b_got, 2)
    first_a, first_b = pending[-2:]
    second_slots = [next(slots) for _ in range(2)]

    def second(at):
        if at:
            return copy_to(b_sum.at[1 - x_bit], b_second, second_slots[1], dp=partner_of(member, 1))
        return copy_to(a_sum.at[1 - y_bit], a_second, second_slots[0], dp=partner_of(member, 2))

    z_slots = [[next(slots) for _ in range(1, shards)] for _ in range(2)]

    def piece_copy(way, first=False):
        target = lax.rem(here + way, shards)
        source, landing = (early_own, early_got) if first else (pieces, z_got)
        return copy_to(source.at[target], landing.at[way - 1], z_slots[first][way - 1], tensor=target)

    more_slots = [[next(slots) for _ in range(PIECE_BITS, dp_bits)] for _ in range(2)]

    def send_pieces(first):
        source, landing = (early_own, early_more) if first else (pieces, pieces_more)
        for bit in range(PIECE_BITS, dp_bits):
            at = bit - PIECE_BITS
            extra = copy_to(source, landing.at[at], more_slots[first][at], dp=partner_of(member, bit))
            extra.start()
            extra.wait_recv()
            extra.wait_send()

            def step(owner, carry):
                source[owner] = rounded_sum(source[owner], landing[at, owner])
                return carry

            lax.fori_loop(0, shards, step, 0)
        for way in range(1, shards):
            piece_copy(way, first).start()

    load(4).wait()
    send_pieces(True)

    def sum_pairs(out, right):
        def step(at, carry):
            one, two = at // out.shape[1], lax.rem(at, out.shape[1])
            out[one, two] = rounded_sum(out[one, two], right[one, two])
            return carry

        lax.fori_loop(0, out.shape[0] * out.shape[1], step, 0)

    def second_exchange():
        first_a.wait_recv()
        first_b.wait_recv()
        load(0).wait()
        load(1).wait()
        sum_pairs(a_sum, a_got)
        sum_pairs(b_sum, b_got)
        second(0).start()
        second(1).start()

    def shard_exchange():
        second(0).wait_recv()
        second(1).wait_recv()
        split = shards // 2
        for at in range(split):
            pieces[at] = rounded_sum(a_sum[y_bit, at], a_second[at])
            pieces[split + at] = rounded_sum(b_sum[x_bit, at], b_second[at])
        send_pieces(False)

    right_slots = [next(slots) for _ in range(shards)]
    left_slots = [next(slots) for _ in range(shards)]

    def to_right(owner):
        return copy_to(part.at[owner], arrived.at[owner], right_slots[owner], tensor=lax.rem(here + 1, shards))

    def to_left(owner, target=None):
        to = lax.rem(here + last, shards) if target is None else target
        landing = jnp.where(owner == to, shards, owner)
        return copy_to(
            part.at[owner], arrived.at[landing], left_slots[owner], tensor=lax.rem(here + last, shards)
        )

    def add_arrived(owner, landing):
        def step(at, carry):
            rows = pl.ds(pl.multiple_of(at * (block // 4), 16), block // 4)
            part[owner, rows, :] = rounded_sum(part[owner, rows, :], arrived[landing, rows, :])
            return carry

        lax.fori_loop(0, 4, step, 0)

    def hop(moved, nth, rightward):
        owner, at = (last - nth, moved) if rightward else (nth, last - moved)
        if (at < owner) if rightward else (at > owner):

            @pl.when(here == at)
            def _():
                copy = to_right(owner) if rightward else to_left(owner)
                copy.wait_recv()
                add_arrived(owner, owner)
                copy.start()

    dq[...] = jnp.zeros_like(dq)
    dk[...] = jnp.zeros_like(dk)
    dv[...] = jnp.zeros_like(dv)
    q_wide[...] = jnp.zeros_like(q_wide)
    column_sums[...] = jnp.zeros_like(column_sums)
    source = lax.broadcasted_iota(jnp.int32, (LANES, LANES), 0)
    target = lax.broadcasted_iota(jnp.int32, (LANES, LANES), 1)
    gathers = (target >= HEAD_DIM) & (target < HEAD_DIM + 3)
    picks = []
    for odd in range(2):
        inside = (source >= HEAD_DIM * odd) & (source < HEAD_DIM * (odd + 1))
        summing = jnp.where(inside & gathers, -1.0, 0.0).astype(bf16)
        moving = jnp.where(inside & (source - HEAD_DIM * odd == target), 1.0, 0.0).astype(bf16)
        picks.append((summing, moving))
    half = block // 2
    lane = lax.broadcasted_iota(jnp.int32, (half, LANES), 1)

    def prepare(at, carry):
        for side in range(2):
            rows = pl.ds(pl.multiple_of((2 * at + side) * half, half), half)
            single_rows = pl.ds(pl.multiple_of(at * half, half), half)
            for head, odd, mixed, grad in (
                (0, 0, pair_ref[rows, :], pair_grad_ref[rows, :]),
                (1, 1, pair_ref[rows, :], pair_grad_ref[rows, :]),
                (2, side, single_ref[single_rows, :], single_grad_ref[single_rows, :]),
            ):
                summing, moving = picks[odd]
                product = grad.astype(f32) * mixed.astype(f32)
                high = product.astype(bf16)
                low = (product - high.astype(f32)).astype(bf16)
                shared = jnp.dot(high, summing, preferred_element_type=f32) + jnp.dot(
                    low, summing, preferred_element_type=f32
                )
                moved = jnp.dot(grad, moving, preferred_element_type=f32)
                for place, value in enumerate(split_three(shared)):
                    moved = jnp.where(lane == HEAD_DIM + place, value.astype(f32), moved)
                grad_heads[head, rows, :] = moved.astype(bf16)
        return carry

    lax.fori_loop(0, shards, prepare, 0)

    def rows_of(owner):
        return pl.ds(pl.multiple_of(owner * block, 16), block)

    def visit(owner, other):
        key_rows, query_rows = rows_of(owner), rows_of(other)
        for head in range(heads):
            prob = jnp.exp(times_transposed(k_ref[head, key_rows, :], q_ref[head, query_rows, :]))
            grad_prob = times_transposed(v_ref[head, key_rows, :], grad_heads[head, query_rows, :])
            probs[head] = prob.astype(bf16)
            grad_scores[head] = (prob * grad_prob).astype(bf16)
        for head in range(heads):
            dv[head, key_rows, :] += jnp.dot(
                probs[head], grad_heads[head, query_rows, :], preferred_element_type=f32
            )
            dk[head, key_rows, :] += jnp.dot(
                grad_scores[head], q_ref[head, query_rows, :], preferred_element_type=f32
            )
            dq[head, query_rows, :] += contract_rows(grad_scores[head], k_ref[head, key_rows, :])

    def close_block(owner, following):
        rows = rows_of(owner)
        scale = HEAD_DIM**-0.5
        for first, low, high in (
            (0, dq[0, rows, :] * scale, dq[1, rows, :] * scale),
            (1, dq[2, rows, :] * scale, dk[0, rows, :]),
            (2, dk[1, rows, :], dk[2, rows, :]),
            (3, dv[0, rows, :], dv[1, rows, :]),
        ):
            packed[:, first * LANES : (first + 1) * LANES] = join_lanes(low, high).astype(bf16)
        packed[:, 4 * LANES : columns] = dv[2, rows, :HEAD_DIM].astype(bf16)
        part[owner] = jnp.dot(packed[...], weight_ref[...], preferred_element_type=f32).astype(bf16)

        @pl.when((owner == last) & (here == 0))
        def _():
            to_right(last).start()

        @pl.when((owner == 0) & (here == last))
        def _():
            to_left(0).start()

        load_rows(owner).wait()
        q_wide[...] += contract_rows(packed[...], rows_own[...])
        column_sums[...] += jnp.dot(jnp.ones((8, block), bf16), packed[...], preferred_element_type=f32)

        @pl.when(following >= 0)
        def _():
            load_rows(following).start()

    order = []
    for near in range((shards + 1) // 2):
        for owner in (last - near, near):
            if owner not in order:
                order.append(owner)
    visits, closing = [], []
    for at, owner in enumerate(order):
        rest = order[at:]
        both = [(owner, owner)]
        for other in rest[1:]:
            if abs(owner - other) <= reach:
                both += [(owner, other), (other, owner)]
        visits += both
        closing.append(len(visits) - 1)
    total_visits = len(visits)

    def lookup(table, at):
        value = 0
        for place, entry in enumerate(table):
            value = value + jnp.where(at == place, entry, 0)
        return value

    closed = [order[closing.index(at)] if at in closing else -1 for at in range(total_visits)]
    later = [
        order[closing.index(at) + 1] if at in closing and at != closing[-1] else -1 for at in range(total_visits)
    ]
    events = {
        closing[0] - 1: second_exchange,
        closing[0] + 2: shard_exchange,
        closing[1] + 1: lambda: hop(1, 0, True),
    }
    assert len(events) == 3 and shards >= 4

    def each_visit(at, carry):
        visit(lookup([pair[0] for pair in visits], at), lookup([pair[1] for pair in visits], at))
        for when, event in events.items():

            @pl.when(at == when)
            def _():
                event()

        @pl.when(lookup([int(owner >= 0) for owner in closed], at) == 1)
        def _():
            close_block(lookup(closed, at), lookup(later, at))

        return carry

    lax.fori_loop(0, total_visits, each_visit, 0)
    for owner in range(last - 1, 0, -1):

        @pl.when(here == 0)
        def _():
            to_right(owner).start()

    for owner in range(1, last):

        @pl.when(here == last)
        def _():
            to_left(owner).start()

    sums = column_sums[...]
    weight = weight_ref[...].astype(f32)
    shift_sum = jnp.dot(sums, weight, preferred_element_type=f32, precision=lax.Precision.HIGHEST)[0:1]
    gain_sum = jnp.sum(weight * q_wide[...], axis=0, keepdims=True)
    v_now[0] = vectors_ref[...]
    v_now[0, 0:1, :] = (gain_sum - shift * shift_sum) / gain
    v_now[0, 1:2, :] = shift_sum
    v_now[0, pl.ds(12 + here, 1), 0:columns] = sums[0:1]
    count = q_all.shape[1]
    for piece in range(PIECES):
        q_all[piece] = q_wide[piece * count : (piece + 1) * count, :].astype(bf16)

    def vector_stage(bit):
        return start_dp(v_now.at[bit], v_got.at[bit], bit)

    q_core = start_dp(q_all.at[pl.ds((1 - core) * 4, 4)], q_got_core, 0)
    v_copy = vector_stage(0)
    hop(1, 0, False)
    hop(2, 0, True)
    q_core.wait_recv()
    for at in range(4):
        q_half[at] = rounded_sum(q_all[core * 4 + at], q_got_core[at])
    q_x = start_dp(q_half.at[pl.ds((1 - x_bit) * 2, 2)], q_got_x, 1)
    v_copy.wait_recv()
    v_now[1] = v_now[0] + v_got[0]
    v_copy = vector_stage(1)
    q_x.wait_recv()
    for at in range(2):
        q_quarter[at] = rounded_sum(q_half[x_bit * 2 + at], q_got_x[at])
    q_y = start_dp(q_quarter.at[1 - y_bit], q_got_y, 2)
    v_copy.wait_recv()
    v_now[2] = v_now[1] + v_got[1]
    v_copy = vector_stage(2)
    q_y.wait_recv()
    qkv_out[own_piece] = rounded_sum(q_quarter[y_bit], q_got_y[...])
    v_copy.wait_recv()
    v_now[3] = v_now[2] + v_got[2]
    for bit in range(PIECE_BITS, dp_bits):
        extra = start_dp(qkv_out.at[own_piece], q_got_more.at[bit - PIECE_BITS], bit, False)
        v_copy = vector_stage(bit)
        extra.wait_recv()
        extra.wait_send()
        qkv_out[own_piece] = rounded_sum(qkv_out[own_piece], q_got_more[bit - PIECE_BITS])
        v_copy.wait_recv()
        v_now[bit + 1] = v_now[bit] + v_got[bit]
    v_shards[here] = v_now[dp_bits]
    for way in range(1, shards):
        copy = copy_to(
            v_now.at[dp_bits], v_shards.at[here], next(slots), tensor=lax.rem(here + way, shards)
        )
        copy.start()
        pending.append(copy)
    v_waits = pending[-last:]
    q_back = start_dp(qkv_out.at[own_piece], qkv_out.at[own_piece], 2)
    q_back.wait_recv()
    q_back = start_dp(
        qkv_out.at[pl.ds(core * 4 + x_bit * 2, 2)], qkv_out.at[pl.ds(core * 4 + x_bit * 2, 2)], 1
    )
    q_back.wait_recv()
    q_back = start_dp(qkv_out.at[pl.ds(core * 4, 4)], qkv_out.at[pl.ds(core * 4, 4)], 0)

    split_row = early_own.shape[1]
    for first, source, landing, rows in (
        (True, early_own, early_got, slice(0, split_row)),
        (False, pieces, z_got, slice(split_row, 2 * half_rows)),
    ):
        for way in range(1, shards):
            piece_copy(way, first).wait_recv()
        total = source[here].astype(f32)
        for way in range(1, shards):
            total = total + landing[way - 1].astype(f32)
        weights_out[own_piece, rows, :] = total.astype(bf16)

    def own_half(low, *index):
        rows = pl.ds(0 if low else half_rows, half_rows)
        return weights_out.at[index[0], rows]

    back_a = start_dp(own_half(True, own_piece), own_half(True, own_piece), 2)
    back_b = start_dp(own_half(False, own_piece), own_half(False, own_piece), 1)
    back_a.wait_recv()
    span = pl.ds(core * 4 + x_bit * 2, 2)
    back_a = start_dp(own_half(True, span), own_half(True, span), 1)
    back_b.wait_recv()
    back_c = [
        start_dp(own_half(False, core * 4 + 2 * at + y_bit), own_half(False, core * 4 + 2 * at + y_bit), 2)
        for at in range(2)
    ]
    for moved in range(2, last):
        hop(moved, 0, False)
        if moved > 2:
            hop(moved, 0, True)
    for nth in range(1, last):
        for moved in range(1, last):
            hop(moved, nth, True)
            hop(moved, nth, False)
    back_a.wait_recv()
    for copy in back_c:
        copy.wait_recv()
    span = pl.ds(core * 4, 4)
    back_core = start_dp(weights_out.at[span], weights_out.at[span], 0)

    for copy in v_waits:
        copy.wait_recv()
    vectors_sum = v_shards[0]
    for at in range(1, shards):
        vectors_sum = vectors_sum + v_shards[at]
    vectors_out[...] = vectors_sum

    for owner in range(shards):

        @pl.when(here == owner)
        def _():
            if owner > 0:
                to_right(owner).wait_recv()
                add_arrived(owner, owner)
            if owner < last:
                to_left(owner, owner).wait_recv()
                add_arrived(owner, shards)

    load(2).wait()
    load(3).wait()

    def close(at, carry):
        rows = pl.ds(pl.multiple_of(at * (block // 4), 16), block // 4)
        tokens = tokens_own[rows, :].astype(f32)
        centred = tokens - jnp.mean(tokens, axis=1, keepdims=True)
        inverse = lax.rsqrt(jnp.mean(centred * centred, axis=1, keepdims=True) + eps_norm)
        unit = centred * inverse
        scaled = part[here, rows, :].astype(f32) * gain
        inner = (
            scaled
            - jnp.mean(scaled, axis=1, keepdims=True)
            - unit * jnp.mean(scaled * unit, axis=1, keepdims=True)
        )
        tokens_out[rows, :] = hidden_own[rows, :] + inverse * inner
        return carry

    lax.fori_loop(0, 4, close, 0)
    q_back.wait_recv()
    back_core.wait_recv()
    for copy in pending:
        copy.wait_send()
    for at in range(2):
        second(at).wait_send()
    for way in range(1, shards):
        piece_copy(way, True).wait_send()
        piece_copy(way).wait_send()
    for owner in range(shards):

        @pl.when(here < owner)
        def _():
            to_right(owner).wait_send()

        @pl.when(here > owner)
        def _():
            to_left(owner).wait_send()


def back(shards, members, heads_in, pair_in, weight, gain, shift, vectors, rows, tokens, grad_hidden, exchanged):
    dp_bits = members.bit_length() - 1
    assert members == 1 << dp_bits and dp_bits >= PIECE_BITS
    f32, bf16 = jnp.float32, jnp.bfloat16
    heads, seq_len, _ = heads_in[0].shape
    columns, width = weight.shape
    block = tokens.shape[0]
    quarter = exchanged[0].shape
    early_rows = exchanged[4].shape[1]
    late_rows = quarter[2]
    count = columns // PIECES
    more = max(1, dp_bits - PIECE_BITS)
    copies = 20 + 2 * shards + 3 * (shards - 1) + 5 * dp_bits
    vm = pltpu.VMEM
    return pl.pallas_call(
        partial(back_kernel, shards, dp_bits),
        in_specs=[pl.BlockSpec(memory_space=vm)] * 11 + [pl.BlockSpec(memory_space=pl.ANY)] * 8,
        out_specs=[pl.BlockSpec(memory_space=vm)] * 4,
        out_shape=[
            jax.ShapeDtypeStruct((block, width), f32),
            jax.ShapeDtypeStruct(vectors.shape, f32),
            jax.ShapeDtypeStruct((PIECES, count, width), bf16),
            jax.ShapeDtypeStruct((PIECES, early_rows + late_rows, width), bf16),
        ],
        scratch_shapes=[
            vm((heads, seq_len, LANES), bf16),
            vm((heads, seq_len, LANES), f32),
            vm((heads, seq_len, LANES), f32),
            vm((heads, seq_len, LANES), f32),
            vm((heads, block, block), bf16),
            vm((heads, block, block), bf16),
            vm((block, columns), bf16),
            vm((block, width), bf16),
            vm((block, width), bf16),
            vm((block, width), f32),
            vm((shards, block, width), bf16),
            vm((shards + 1, block, width), bf16),
            vm((columns, width), f32),
            vm((8, columns), f32),
            vm((PIECES, count, width), bf16),
            vm((4, count, width), bf16),
            vm((2, count, width), bf16),
            vm((4, count, width), bf16),
            vm((2, count, width), bf16),
            vm((count, width), bf16),
            vm((more, count, width), bf16),
            vm((dp_bits + 1,) + vectors.shape, f32),
            vm((dp_bits,) + vectors.shape, f32),
            vm((shards,) + vectors.shape, f32),
            vm(quarter, bf16),
            vm(quarter, bf16),
            vm(quarter, bf16),
            vm(quarter, bf16),
            vm(quarter[1:], bf16),
            vm(quarter[1:], bf16),
            vm((shards, late_rows, width), bf16),
            vm((shards, early_rows, width), bf16),
            vm((more, shards, late_rows, width), bf16),
            vm((more, shards, early_rows, width), bf16),
            vm((shards - 1, late_rows, width), bf16),
            vm((shards - 1, early_rows, width), bf16),
            pltpu.SemaphoreType.DMA((copies,)),
            pltpu.SemaphoreType.DMA((copies,)),
            pltpu.SemaphoreType.DMA((6,)),
        ],
        compiler_params=pltpu.CompilerParams(
            collective_id=1, has_side_effects=True, vmem_limit_bytes=67043328
        ),
        name="back",
        cost_estimate=pl.CostEstimate(
            flops=10 * heads * seq_len * seq_len * LANES, transcendentals=0, bytes_accessed=40 * block * width
        ),
    )(*heads_in, *pair_in, weight, gain, shift, vectors, rows, tokens, grad_hidden, *exchanged)


def unpack_kernel(qkv_ref, weights_ref, totals_ref, fc1_out, fc2_out, proj_out, qkv_out, fc1_bias_out, *vector_outs):
    fc_rows, proj_rows = fc1_out.shape[0], proj_out.shape[0]
    fc2_out[...] = weights_ref[0, :fc_rows].astype(jnp.float32)
    fc1_out[...] = weights_ref[0, fc_rows : 2 * fc_rows].astype(jnp.float32)
    proj_out[...] = weights_ref[0, 2 * fc_rows : 2 * fc_rows + proj_rows].astype(jnp.float32)
    qkv_out[...] = qkv_ref[0].astype(jnp.float32)

    @pl.when(pl.program_id(0) == 0)
    def _():
        width = totals_ref.shape[1]
        for at, out in enumerate(vector_outs):
            out[...] = totals_ref[at : at + 1, :].reshape(width)
        here = lax.axis_index("tensor")
        fc1_bias_out[...] = totals_ref[pl.ds(8 + here, 1), :].reshape(width)


def unpack(qkv, weights, totals, fc_rows, proj_rows):
    f32 = jnp.float32
    _, rows, width = weights.shape
    qkv_rows = qkv.shape[1]
    counts = (fc_rows, fc_rows, proj_rows, qkv_rows)
    vector = pl.BlockSpec((width,), lambda i: (0,))
    return pl.pallas_call(
        unpack_kernel,
        grid=(PIECES,),
        in_specs=[
            pl.BlockSpec((1, qkv_rows, width), lambda i: (i, 0, 0)),
            pl.BlockSpec((1, rows, width), lambda i: (i, 0, 0)),
            pl.BlockSpec(totals.shape, lambda i: (0, 0)),
        ],
        out_specs=[pl.BlockSpec((count, width), lambda i: (i, 0)) for count in counts] + [vector] * 9,
        out_shape=[jax.ShapeDtypeStruct((PIECES * count, width), f32) for count in counts]
        + [jax.ShapeDtypeStruct((width,), f32)] * 9,
        name="unpack",
    )(qkv, weights, totals)


def start_kernel(
    shards,
    dp_bits,
    tokens_ref,
    ids_ref,
    gain_ref,
    shift_ref,
    qkv_ref,
    qv_bias_ref,
    fc1_ref,
    fc2_ref,
    proj_ref,
    fc1_bias_ref,
    normed_out,
    q_out,
    k_out,
    v_out,
    pairs_out,
    singles_out,
    pairs_here,
    singles_here,
    weights_out,
    bias_out,
    blocks,
    normed_all,
    queries,
    keys,
    values,
    peaks,
    sums,
    scores,
    weights,
    q_extra,
    k_extra,
    own,
    chain,
    send,
    recv,
    local,
    stored,
):
    f32, bf16 = jnp.float32, jnp.bfloat16
    member, here = lax.axis_index("dp"), lax.axis_index("tensor")
    core, x_bit, y_bit = bit_of(member, 0), bit_of(member, 1), bit_of(member, 2)
    own_piece = core * 4 + x_bit * 2 + y_bit
    block, width = tokens_ref.shape
    heads = queries.shape[0]
    seq_len = ids_ref.shape[1]
    last = shards - 1
    reach = -(-(MOST_TOKENS - 1) // block)
    slots = iter(range(send.shape[0]))
    pending = []

    def copy_to(src, dst, at, **peer):
        return pltpu.make_async_remote_copy(
            src_ref=src, dst_ref=dst, send_sem=send.at[at], recv_sem=recv.at[at], device_id=peer, device_id_type=MESH
        )

    def start_dp(src, dst, bit):
        copy = copy_to(src, dst, next(slots), dp=partner_of(member, bit))
        copy.start()
        pending.append(copy)
        return copy

    fc1_rows, fc2_rows, proj_rows = (ref.shape[0] // PIECES for ref in (fc1_ref, fc2_ref, proj_ref))
    loads = []
    for at, (ref, first, count) in enumerate(
        ((fc2_ref, 0, fc2_rows), (fc1_ref, fc2_rows, fc1_rows))
    ):
        rows = pl.ds(pl.multiple_of(own_piece * count, 16), count)
        loads.append(pltpu.make_async_copy(ref.at[rows], own.at[first : first + count], local.at[at]))
        loads[-1].start()
    used = fc1_rows + fc2_rows
    rows = pl.ds(pl.multiple_of(own_piece * proj_rows, 8), proj_rows)
    own[used : used + proj_rows, :] = proj_ref[rows, :]
    used += proj_rows
    own[used:, :] = jnp.zeros((own.shape[0] - used, width), bf16)
    gain, shift = (ref[...].reshape(1, width) for ref in (gain_ref, shift_ref))
    bias_out[here] = fc1_bias_ref[...].reshape(1, width)
    greet(dp_bits, shards)
    for load in loads:
        load.wait()

    chains = {}
    for name, first, rest in (("w", own, chain), ("t", tokens_ref, blocks)):
        chains[name] = (
            first,
            rest,
            [next(slots) for _ in range(shards)],
            [next(slots) for _ in range(shards)],
        )

    def hop_copy(name, owner, rightward, from_own):
        first, rest, right_slots, left_slots = chains[name]
        src = first if from_own else rest.at[owner]
        step = 1 if rightward else last
        at = (right_slots if rightward else left_slots)[owner]
        return copy_to(src, rest.at[owner], at, tensor=lax.rem(here + step, shards))

    def send_own(name, rightward):
        for owner in range(shards):
            if owner != (last if rightward else 0):

                @pl.when(here == owner)
                def _():
                    hop_copy(name, owner, rightward, True).start()

    def hop(name, time, then=None):
        for at in range(shards):
            for rightward, owner, end in ((True, at - time, last), (False, at + time, 0)):
                if 0 <= owner <= last:

                    @pl.when(here == at)
                    def _():
                        hop_copy(name, owner, rightward, False).wait_recv()
                        if at != end:
                            hop_copy(name, owner, rightward, False).start()
                            if then is not None and owner in (0, last):
                                hop_copy(then, at, rightward, True).start()

    send_own("w", True)
    send_own("w", False)

    @pl.when(here == 0)
    def _():
        hop_copy("t", 0, True, True).start()

    @pl.when(here == last)
    def _():
        hop_copy("t", last, False, True).start()

    bias_copies = []
    for way in range(1, shards):
        copy = copy_to(
            bias_out.at[here], bias_out.at[here], next(slots), tensor=lax.rem(here + way, shards)
        )
        copy.start()
        bias_copies.append(copy)
    pending.extend(bias_copies)

    large = -MASKED
    segments = lax.broadcasted_iota(jnp.int32, (8, seq_len), 0)
    same = jnp.where(segments == ids_ref[...], 1.0, 0.0).astype(bf16)
    select = lax.broadcasted_iota(jnp.int32, (8, LANES), 1) - HEAD_DIM == lax.broadcasted_iota(
        jnp.int32, (8, LANES), 0
    )
    matched = contract_rows(same, jnp.where(select, 1.0, 0.0).astype(bf16))
    lane = lax.broadcasted_iota(jnp.int32, (seq_len, LANES), 1)
    segment_lane = (lane >= HEAD_DIM) & (lane < HEAD_DIM + 8)
    ones_lane = (lane >= HEAD_DIM + 8) & (lane < HEAD_DIM + 11)
    q_extra[...] = jnp.where(segment_lane, (matched - 1.0) * large, 0.0).astype(bf16)
    k_extra[...] = jnp.where(ones_lane, 1.0, matched).astype(bf16)
    low_half = lax.broadcasted_iota(jnp.int32, (block, LANES), 1) < HEAD_DIM
    v_lane = lax.broadcasted_iota(jnp.int32, (block, LANES), 1)
    v_extra = jnp.where((v_lane >= HEAD_DIM) & (v_lane < HEAD_DIM + 3), 1.0, 0.0).astype(bf16)

    def rows_of(owner, count=block):
        return pl.ds(pl.multiple_of(owner * count, 16), count)

    def store(which, owner):
        rows = rows_of(owner)
        source, out = (
            (normed_all.at[rows], normed_out.at[rows]),
            (queries.at[:, rows], q_out.at[:, rows]),
            (keys.at[:, rows], k_out.at[:, rows]),
            (values.at[:, rows], v_out.at[:, rows]),
        )[which]
        return pltpu.make_async_copy(source, out, stored.at[which, owner])

    def project_block(source, owner):
        tokens = source.astype(f32)
        centred = tokens - jnp.mean(tokens, axis=1, keepdims=True)
        inverse = lax.rsqrt(jnp.mean(centred * centred, axis=1, keepdims=True) + eps_norm)
        normed = (centred * inverse * gain + shift).astype(bf16)
        rows = rows_of(owner)
        normed_all[rows, :] = normed
        for which, out in ((0, queries), (1, keys), (2, values)):
            product = times_transposed(normed, qkv_ref[which])
            if which != 1:
                product = product + qv_bias_ref[which // 2 : which // 2 + 1, :]
            if which == 0:
                product = product.astype(bf16).astype(f32) * HEAD_DIM**-0.5
            extra = v_extra if which == 2 else (q_extra if which == 0 else k_extra)[rows, :]
            for head in range(heads):
                first = (head // 2) * LANES
                tile = product[:, first : first + LANES]
                if tile.shape[1] < LANES:
                    blank = jnp.zeros((block, LANES - tile.shape[1]), f32)
                    tile = jnp.concatenate([tile, blank], axis=1)
                if head % 2:
                    tile = pltpu.roll(tile, HEAD_DIM, 1)
                out[head, rows, :] = jnp.where(low_half, tile, extra.astype(f32)).astype(bf16)
        store(0, owner).start()
        store(2, owner).start()
        store(3, owner).start()

    peaks[...] = jnp.full_like(peaks, -3e38)
    sums[...] = jnp.zeros_like(sums)

    def away(index):
        return jnp.maximum(index - here, here - index)

    def visit(owner, other):
        rows, across = rows_of(owner), rows_of(other)
        for head in range(heads):
            scores[head] = times_transposed(queries[head, rows, :], keys[head, across, :])
        for head in range(heads):
            old_peak = peaks[head, rows, :]
            new_peak = jnp.maximum(old_peak, jnp.max(scores[head], axis=1, keepdims=True))
            peaks[head, rows, :] = new_peak
            spread = jnp.concatenate([new_peak] * -(-block // LANES), axis=1)[:, :block]
            weights[head] = jnp.exp(scores[head] - spread).astype(bf16)
            sums[head, rows, :] = sums[head, rows, :] * jnp.exp(old_peak - new_peak)
        for head in range(heads):
            sums[head, rows, :] += jnp.dot(
                weights[head], values[head, across, :], preferred_element_type=f32
            )

    pair_slots = [next(slots) for _ in range(shards)]
    single_slots = [next(slots) for _ in range(shards)]

    def exchange(owner, source):
        half_block = block // 2
        return [
            pltpu.make_async_remote_copy(
                src_ref=out.at[rows_of(owner, count)],
                dst_ref=landing.at[source],
                send_sem=send.at[base + owner],
                recv_sem=recv.at[base + source],
                device_id={"tensor": owner},
                device_id_type=MESH,
            )
            for out, landing, count, base in (
                (pairs_out, pairs_here, block, pair_slots[0]),
                (singles_out, singles_here, half_block, single_slots[0]),
            )
        ]

    def complete(owner):
        rows, half_block = rows_of(owner), block // 2
        parts = []
        for head in range(heads):
            total = sums[head, rows, HEAD_DIM : HEAD_DIM + 1]
            parts.append(sums[head, rows, :] / total)
            high, middle_part, low = split_three(-(peaks[head, rows, :] + jnp.log(total)))
            kept = queries[head, rows, :].astype(f32)
            for at, value in enumerate((high, middle_part, low)):
                kept = jnp.where(v_lane == HEAD_DIM + 8 + at, value.astype(f32), kept)
            queries[head, rows, :] = kept.astype(bf16)
        pair = join_lanes(parts[0], parts[1]).astype(bf16)
        single = join_lanes(parts[2][:half_block], parts[2][half_block:]).astype(bf16)
        pairs_out[rows, :] = pair
        singles_out[rows_of(owner, half_block), :] = single
        store(1, owner).start()

        @pl.when(owner == here)
        def _():
            pairs_here[here] = pair
            singles_here[here] = single

        @pl.when(owner != here)
        def _():
            for copy in exchange(owner, here):
                copy.start()

    def attend_known(time):
        def each(at, carry):
            owner = lax.rem(here + shards // 2 + at, shards)

            def other_block(other, carry):
                near = jnp.maximum(owner - other, other - owner) <= reach
                known = jnp.maximum(jnp.maximum(away(owner), away(other)), 1)

                @pl.when(near & (known == time))
                def _():
                    visit(owner, other)

                return carry

            lax.fori_loop(0, shards, other_block, 0)
            final = jnp.maximum(
                away(jnp.maximum(owner - reach, 0)), away(jnp.minimum(owner + reach, last))
            )

            @pl.when(final == time)
            def _():
                complete(owner)

            return carry

        lax.fori_loop(0, shards, each, 0)

    project_block(tokens_ref[...], here)
    for time in range(1, shards):
        hop("w", time, "t")

    half = shards // 2
    stores = []
    for owner in range(shards):
        at = 2 + owner

        @pl.when(here == owner)
        def _():
            pltpu.make_async_copy(own, weights_out.at[own_piece, owner], local.at[at]).start()

        @pl.when(here != owner)
        def _():
            pltpu.make_async_copy(chain.at[owner], weights_out.at[own_piece, owner], local.at[at]).start()

        stores.append(pltpu.make_async_copy(own, weights_out.at[own_piece, owner], local.at[at]))
    for saved in stores:
        saved.wait()

    def part(low, pieces):
        owners = pl.ds(0, half) if low else pl.ds(half, shards - half)
        return weights_out.at[pieces, owners]

    def gather_stage(low, pieces, bit):
        return [start_dp(part(low, at), part(low, at), bit) for at in pieces]

    def wait_all(copies):
        for copy in copies:
            copy.wait_recv()

    stage = gather_stage(True, [own_piece], 2) + gather_stage(False, [own_piece], 1)

    def arrived(time):
        def each(at, carry):
            owner = here + (2 * at - 1) * time

            @pl.when((owner >= 0) & (owner <= last))
            def _():
                project_block(blocks[owner], owner)

            return carry

        lax.fori_loop(0, 2, each, 0)

    for time in range(1, shards):
        hop("t", time)
        arrived(time)
        if time == 1:
            wait_all(stage)
            stage = gather_stage(True, [pl.ds(core * 4 + x_bit * 2, 2)], 1) + gather_stage(
                False, [core * 4 + 2 * at + y_bit for at in range(2)], 2
            )
        attend_known(time)
        if time == 2:
            wait_all(stage)
            stage = [start_dp(weights_out.at[pl.ds(core * 4, 4)], weights_out.at[pl.ds(core * 4, 4)], 0)]
    for owner in range(shards):

        @pl.when(here != owner)
        def _():
            for copy in exchange(here, owner):
                copy.wait_recv()
            for copy in exchange(owner, here):
                copy.wait_send()

        for which in range(4):
            store(which, owner).wait()
    wait_all(stage)
    wait_all(bias_copies)
    for copy in pending:
        copy.wait_send()
    for name in chains:
        for at in range(shards):
            for owner in range(shards):
                if owner <= at < last:

                    @pl.when(here == at)
                    def _():
                        hop_copy(name, owner, True, False).wait_send()

                if owner >= at > 0:

                    @pl.when(here == at)
                    def _():
                        hop_copy(name, owner, False, False).wait_send()


def start(shards, members, tokens, ids, gain, shift, qkv, qv_bias, fc1, fc2, proj, fc1_bias):
    dp_bits = members.bit_length() - 1
    assert members == 1 << dp_bits and dp_bits >= PIECE_BITS and shards >= 3
    f32, bf16 = jnp.float32, jnp.bfloat16
    block, width = tokens.shape
    seq_len = block * shards
    heads = qkv.shape[1] // HEAD_DIM
    rows = -(-(fc1.shape[0] + fc2.shape[0] + proj.shape[0]) // PIECES // 16) * 16
    copies = 6 * shards + (shards - 1) + 6
    vm = pltpu.VMEM
    on_chip = pl.BlockSpec(memory_space=vm)
    anywhere = pl.BlockSpec(memory_space=pl.ANY)
    head_rows = jax.ShapeDtypeStruct((heads, seq_len, LANES), bf16)
    return pl.pallas_call(
        partial(start_kernel, shards, dp_bits),
        in_specs=[on_chip] * 6 + [anywhere] * 2 + [on_chip] * 2,
        out_specs=[anywhere] * 4
        + [on_chip] * 4
        + [anywhere, on_chip],
        out_shape=[
            jax.ShapeDtypeStruct((seq_len, width), bf16),
            head_rows,
            head_rows,
            head_rows,
            jax.ShapeDtypeStruct((seq_len, LANES), bf16),
            jax.ShapeDtypeStruct((seq_len // 2, LANES), bf16),
            jax.ShapeDtypeStruct((shards, block, LANES), bf16),
            jax.ShapeDtypeStruct((shards, block // 2, LANES), bf16),
            jax.ShapeDtypeStruct((PIECES, shards, rows, width), bf16),
            jax.ShapeDtypeStruct((shards, 1, width), f32),
        ],
        scratch_shapes=[
            vm((shards, block, width), bf16),
            vm((seq_len, width), bf16),
            vm((heads, seq_len, LANES), bf16),
            vm((heads, seq_len, LANES), bf16),
            vm((heads, seq_len, LANES), bf16),
            vm((heads, seq_len, LANES), f32),
            vm((heads, seq_len, LANES), f32),
            vm((heads, block, block), f32),
            vm((heads, block, block), bf16),
            vm((seq_len, LANES), bf16),
            vm((seq_len, LANES), bf16),
            vm((rows, width), bf16),
            vm((shards, rows, width), bf16),
            pltpu.SemaphoreType.DMA((copies,)),
            pltpu.SemaphoreType.DMA((copies,)),
            pltpu.SemaphoreType.DMA((2 + shards,)),
            pltpu.SemaphoreType.DMA((4, shards)),
        ],
        compiler_params=pltpu.CompilerParams(
            collective_id=0, has_side_effects=True, vmem_limit_bytes=62 * 1024 * 1024
        ),
        name="start",
        cost_estimate=pl.CostEstimate(
            flops=6 * seq_len * width * heads * HEAD_DIM, transcendentals=0, bytes_accessed=40 * block * width
        ),
    )(tokens, ids, gain, shift, qkv, qv_bias, fc1, fc2, proj, fc1_bias)


CHUNK = 32


def middle_kernel(
    shards,
    dp_bits,
    pairs,
    singles,
    weights_ref,
    fc1_bias_ref,
    proj_bias_ref,
    scale_one_ref,
    gain_ref,
    shift_ref,
    fc2_bias_ref,
    scale_two_ref,
    tokens_ref,
    cotangent_ref,
    block_out,
    hidden_grad_out,
    pair_grads_out,
    single_grads_out,
    vectors_out,
    a_keep,
    a_away,
    b_keep,
    b_away,
    early_out,
    weights,
    attended,
    proj,
    branch,
    hidden,
    normed,
    wide,
    total,
    active,
    slope,
    grad_pre,
    grad_mlp,
    grad_branch,
    pair_grads,
    single_grads,
    got_early,
    got,
    a_got,
    b_got,
    a_second,
    b_second,
    send,
    recv,
    local,
):
    f32, bf16 = jnp.float32, jnp.bfloat16
    member, here = lax.axis_index("dp"), lax.axis_index("tensor")
    core, x_bit, y_bit = bit_of(member, 0), bit_of(member, 1), bit_of(member, 2)
    block, width = tokens_ref.shape
    columns = width // shards
    half = PIECES // 2
    fc_rows, proj_rows = width // PIECES, columns // PIECES
    proj_first = 2 * fc_rows
    slots = iter(range(send.shape[0]))
    proj_bias, scale_one, gain, shift, fc2_bias, scale_two = (
        ref[...].reshape(1, width)
        for ref in (proj_bias_ref, scale_one_ref, gain_ref, shift_ref, fc2_bias_ref, scale_two_ref)
    )

    def copy_to(src, dst, at, **peer):
        return pltpu.make_async_remote_copy(
            src_ref=src, dst_ref=dst, send_sem=send.at[at], recv_sem=recv.at[at], device_id=peer, device_id_type=MESH
        )

    loads = []
    for owner in range(shards):
        load = pltpu.make_async_copy(weights_ref.at[:, owner], weights.at[:, owner], local.at[owner])
        load.start()
        loads.append(load)
    greet(dp_bits, shards)

    for load in loads:
        load.wait()

    def fc1_of(owner):
        return weights[:, owner, fc_rows:proj_first, :].reshape(width, width)

    def fc2_of(owner):
        return weights[:, owner, :fc_rows, :].reshape(width, width)

    def proj_of(owner):
        return weights[:, owner, proj_first : proj_first + proj_rows, :].reshape(columns, width)

    def chunk(at):
        return pl.ds(pl.multiple_of(at * CHUNK, CHUNK), CHUNK)

    def each_chunk(body, init):
        return lax.fori_loop(0, block // CHUNK, body, init)

    def column_sum(value):
        return jnp.sum(value, axis=0, keepdims=True)

    def unit_of(value):
        centred = value - jnp.mean(value, axis=1, keepdims=True)
        inverse = lax.rsqrt(jnp.mean(centred * centred, axis=1, keepdims=True) + eps_norm)
        return centred * inverse, inverse

    third = shards * LANES
    for owner in range(shards):
        own_proj = proj_of(owner)
        proj[owner * LANES : (owner + 1) * LANES, :] = own_proj[:LANES]
        proj[third + owner * HEAD_DIM : third + (owner + 1) * HEAD_DIM, :] = own_proj[LANES:]
    middle_row = block // 2
    for owner in range(shards):
        attended[:, owner * LANES : (owner + 1) * LANES] = pairs[owner]
    lane = lax.broadcasted_iota(jnp.int32, (middle_row, LANES), 1)
    low_half = lane < HEAD_DIM

    def swapped(value):
        return pltpu.roll(value, HEAD_DIM, 1)

    for at in range(shards // 2):
        one, two = singles[2 * at].astype(f32), singles[2 * at + 1].astype(f32)
        columns_here = slice(third + at * LANES, third + (at + 1) * LANES)
        attended[:middle_row, columns_here] = jnp.where(low_half, one, swapped(two)).astype(bf16)
        attended[middle_row:, columns_here] = jnp.where(low_half, swapped(one), two).astype(bf16)
    product = jnp.dot(attended[...], proj[...], preferred_element_type=f32)
    branch[...] = product

    def enter(at, carry):
        rows = chunk(at)
        value = branch[rows, :] + proj_bias
        branch[rows, :] = value
        value = tokens_ref[rows, :].astype(f32) + scale_one * value
        hidden[rows, :] = value
        unit, _ = unit_of(value)
        normed[rows, :] = (unit * gain + shift).astype(bf16)
        return carry

    each_chunk(enter, 0)

    def forward(owner, carry):
        wide[:block, :] = jnp.dot(normed[...], fc1_of(owner), preferred_element_type=f32)
        bias = fc1_bias_ref[owner]

        def activate(at, carry):
            rows = chunk(at)
            value = wide[rows, :] + bias
            below = 0.5 * (1.0 + lax.erf(value * 0.5**0.5))
            active[owner, rows, :] = (value * below).astype(bf16)
            density = jnp.exp(value * value * -0.5) * (0.5 / math.pi) ** 0.5
            slope[owner, rows, :] = below + value * density
            return carry

        each_chunk(activate, 0)
        product = jnp.dot(active[owner], fc2_of(owner), preferred_element_type=f32)
        total[...] = jnp.where(owner == 0, product, total[...] + product)
        return carry

    lax.fori_loop(0, shards, forward, 0)
    empty = jnp.zeros((1, width), f32)

    def turn(at, sums):
        rows = chunk(at)
        value = total[rows, :] + fc2_bias
        block_out[rows, :] = (hidden[rows, :] + scale_two * value).astype(bf16)
        grad = cotangent_ref[rows, :].astype(f32)
        grad_mlp[rows, :] = (grad * scale_two).astype(bf16)
        return (
            sums[0] + column_sum(grad * value),
            sums[1] + column_sum(grad_mlp[rows, :].astype(f32)),
        )

    scale_two_sum, fc2_bias_sum = each_chunk(turn, (empty, empty))

    split = shards // 2

    def slot_row():
        return [next(slots) for _ in range(shards)]

    early_slots, late_slots = slot_row(), slot_row()

    def core_copy(owner, early):
        rows = pl.ds(0, fc_rows) if early else pl.ds(fc_rows, weights.shape[2] - fc_rows)
        base = (early_slots if early else late_slots)[0]
        return pltpu.make_async_remote_copy(
            src_ref=weights.at[pl.ds((1 - core) * half, half), owner, rows],
            dst_ref=(got_early if early else got).at[:, owner],
            send_sem=send.at[base + owner],
            recv_sem=recv.at[base + owner],
            device_id={"dp": partner_of(member, 0)},
            device_id_type=MESH,
        )

    piece_rows = pl.ds(0, fc_rows)
    own = core * half
    side_slots = [next(slots) for _ in range(5)]

    def side_copies(stage):
        first_half, second_half = pl.ds(0, split), pl.ds(split, shards - split)
        if stage == 0:
            moves = [(weights.at[pl.ds(own + (1 - x_bit) * 2, 2), first_half, piece_rows], a_got, 1)]
            moves += [
                (weights.at[own + 2 * x + 1 - y_bit, second_half, piece_rows], b_got.at[x], 2) for x in range(2)
            ]
        else:
            moves = [
                (weights.at[own + 2 * x_bit + 1 - y_bit, first_half, piece_rows], a_second, 2),
                (weights.at[own + 2 * (1 - x_bit) + y_bit, second_half, piece_rows], b_second, 1),
            ]
        return [
            copy_to(source, landing, side_slots[3 * stage + at], dp=partner_of(member, bit))
            for at, (source, landing, bit) in enumerate(moves)
        ]

    def grow_piece(piece, owner, other):
        weights[piece, owner, piece_rows, :] = rounded_sum(weights[piece, owner, piece_rows, :], other)

    def early_pairs():
        for owner in range(shards):
            core_copy(owner, True).wait_recv()

        def step(at, carry):
            piece, owner = at // shards, lax.rem(at, shards)
            grow_piece(own + piece, owner, got_early[piece, owner])
            return carry

        lax.fori_loop(0, half * shards, step, 0)
        for copy in side_copies(0):
            copy.start()

    def early_sides():
        for copy in side_copies(0):
            copy.wait_recv()
        for owner in range(split):
            for at in range(2):
                grow_piece(own + 2 * x_bit + at, owner, a_got[at, owner])
                grow_piece(own + 2 * at + y_bit, split + owner, b_got[at, owner])
        for copy in side_copies(1):
            copy.start()

    def early_end():
        for copy in side_copies(1):
            copy.wait_recv()
        mine = own + 2 * x_bit + y_bit
        for owner in range(split):
            early_out[owner] = rounded_sum(weights[mine, owner, piece_rows, :], a_second[owner])
            early_out[split + owner] = rounded_sum(weights[mine, split + owner, piece_rows, :], b_second[owner])

    def backward(owner, carry):
        wide[:block, :] = times_transposed(grad_mlp[...], fc2_of(owner))

        def slopes(at, sums):
            rows = chunk(at)
            value = (wide[rows, :] * slope[owner, rows, :]).astype(bf16)
            grad_pre[owner, rows, :] = value
            return sums + column_sum(value.astype(f32))

        vectors_out[pl.ds(8 + owner, 1), :] = each_chunk(slopes, empty)
        product = times_transposed(grad_pre[owner], fc1_of(owner))
        total[...] = jnp.where(owner == 0, product, total[...] + product)
        product = contract_rows(active[owner], grad_mlp[...]).astype(bf16)
        weights[:, owner, :fc_rows, :] = product.reshape(PIECES, fc_rows, width)
        core_copy(owner, True).start()
        return carry

    lax.fori_loop(0, shards, backward, 0)
    early_pairs()

    def leave(at, sums):
        rows = chunk(at)
        grad = total[rows, :]
        unit, inverse = unit_of(hidden[rows, :])
        scaled = grad * gain
        inner = (
            scaled
            - jnp.mean(scaled, axis=1, keepdims=True)
            - unit * jnp.mean(scaled * unit, axis=1, keepdims=True)
        )
        value = cotangent_ref[rows, :].astype(f32) + inverse * inner
        hidden_grad_out[rows, :] = value
        rounded = (value * scale_one).astype(bf16)
        grad_branch[rows, :] = rounded
        return (
            sums[0] + column_sum(grad * unit),
            sums[1] + column_sum(grad),
            sums[2] + column_sum(value * branch[rows, :]),
            sums[3] + column_sum(rounded.astype(f32)),
        )

    gain_sum, shift_sum, scale_one_sum, proj_bias_sum = each_chunk(leave, (empty,) * 4)
    for at, value in enumerate(
        (empty, empty, proj_bias_sum, scale_one_sum, gain_sum, shift_sum, fc2_bias_sum, scale_two_sum)
    ):
        vectors_out[at : at + 1, :] = value
    vectors_out[12:, :] = jnp.zeros((vectors_out.shape[0] - 12, width), f32)

    wide[:block, :] = times_transposed(grad_branch[...], proj[...])
    for owner in range(shards):
        pair_grads[owner] = wide[:block, owner * LANES : (owner + 1) * LANES].astype(bf16)
    for at in range(shards // 2):
        columns_here = slice(third + at * LANES, third + (at + 1) * LANES)
        upper, lower = wide[:middle_row, columns_here], wide[middle_row:block, columns_here]
        single_grads[2 * at] = jnp.where(low_half, upper, swapped(lower)).astype(bf16)
        single_grads[2 * at + 1] = jnp.where(low_half, swapped(upper), lower).astype(bf16)
    back = []
    for source, out in ((pair_grads, pair_grads_out), (single_grads, single_grads_out)):
        for way in range(1, shards):
            target = lax.rem(here + way, shards)
            copy = copy_to(source.at[target], out.at[here], next(slots), tensor=target)
            copy.start()
            back.append(copy)
        out[here] = source[here]

    wide[...] = contract_rows(attended[:, :], grad_branch[...])
    for owner in range(shards):
        for piece in range(PIECES):
            first, end = piece * proj_rows, (piece + 1) * proj_rows
            for low, high, start_row in ((0, LANES, owner * LANES), (LANES, columns, third + owner * HEAD_DIM)):
                begin, stop = max(first, low), min(end, high)
                if begin < stop:
                    rows = slice(start_row + begin - low, start_row + stop - low)
                    to = slice(proj_first + begin - first, proj_first + stop - first)
                    weights[piece, owner, to, :] = wide[rows, :].astype(bf16)

    def weight_grads(owner, carry):
        product = contract_rows(normed[...], grad_pre[owner]).astype(bf16)
        weights[:, owner, fc_rows:proj_first, :] = product.reshape(PIECES, fc_rows, width)
        core_copy(owner, False).start()
        return carry

    lax.fori_loop(0, shards, weight_grads, 0)
    early_sides()
    for owner in range(shards):
        core_copy(owner, False).wait_recv()
        for x in range(2):
            for y in range(2):
                piece = x * 2 + y
                if owner < split:
                    moves = [(out, y, owner, at == x) for out, at in ((a_keep, x_bit), (a_away, 1 - x_bit))]
                else:
                    moves = [(out, x, owner - split, at == y) for out, at in ((b_keep, y_bit), (b_away, 1 - y_bit))]
                for out, first, second, wanted in moves:

                    @pl.when(wanted)
                    def _():
                        out[first, second] = rounded_sum(
                            weights[own + piece, owner, fc_rows:, :], got[piece, owner]
                        )

    early_end()
    for copy in back:
        copy.wait_recv()
    for copy in back + side_copies(0) + side_copies(1):
        copy.wait_send()
    for owner in range(shards):
        core_copy(owner, True).wait_send()
        core_copy(owner, False).wait_send()


def middle(shards, members, pairs, singles, weights, fc1_bias, vectors, tokens, cotangent):
    dp_bits = members.bit_length() - 1
    f32, bf16 = jnp.float32, jnp.bfloat16
    block, width = tokens.shape
    rows = weights.shape[2]
    vm = pltpu.VMEM
    on_chip = pl.BlockSpec(memory_space=vm)
    fc_rows = width // PIECES
    quarter = jax.ShapeDtypeStruct((2, shards // 2, rows - fc_rows, width), bf16)
    copies = 2 * (shards - 1) + 2 * shards + 5
    return pl.pallas_call(
        partial(middle_kernel, shards, dp_bits),
        in_specs=[on_chip, on_chip, pl.BlockSpec(memory_space=pl.ANY)] + [on_chip] * 9,
        out_specs=[on_chip] * 10,
        out_shape=[
            jax.ShapeDtypeStruct((block, width), bf16),
            jax.ShapeDtypeStruct((block, width), f32),
            jax.ShapeDtypeStruct((shards, block, LANES), bf16),
            jax.ShapeDtypeStruct((shards, block // 2, LANES), bf16),
            jax.ShapeDtypeStruct((16, width), f32),
            quarter,
            quarter,
            quarter,
            quarter,
            jax.ShapeDtypeStruct((shards, fc_rows, width), bf16),
        ],
        scratch_shapes=[
            vm(weights.shape, bf16),
            vm((block, width), bf16),
            vm((width, width), bf16),
            vm((block, width), f32),
            vm((block, width), f32),
            vm((block, width), bf16),
            vm((width, width), f32),
            vm((block, width), f32),
            vm((shards, block, width), bf16),
            vm((shards, block, width), f32),
            vm((shards, block, width), bf16),
            vm((block, width), bf16),
            vm((block, width), bf16),
            vm((shards, block, LANES), bf16),
            vm((shards, block // 2, LANES), bf16),
            vm((PIECES // 2, shards, fc_rows, width), bf16),
            vm((PIECES // 2, shards, rows - fc_rows, width), bf16),
            vm((2, shards // 2, fc_rows, width), bf16),
            vm((2, shards // 2, fc_rows, width), bf16),
            vm((shards // 2, fc_rows, width), bf16),
            vm((shards // 2, fc_rows, width), bf16),
            pltpu.SemaphoreType.DMA((copies,)),
            pltpu.SemaphoreType.DMA((copies,)),
            pltpu.SemaphoreType.DMA((shards,)),
        ],
        compiler_params=pltpu.CompilerParams(
            collective_id=2, has_side_effects=True, vmem_limit_bytes=62 * 1024 * 1024
        ),
        name="middle",
        cost_estimate=pl.CostEstimate(
            flops=12 * block * width * width * shards, transcendentals=0, bytes_accessed=40 * block * width
        ),
    )(pairs, singles, weights, fc1_bias, *vectors, tokens, cotangent)


eps_norm = 1e-06


def on_device(
    shards,
    members,
    tokens,
    segment_ids,
    ln1_gain,
    ln1_bias,
    qkv_weight,
    qv_bias,
    proj_weight,
    proj_bias,
    scale_one,
    ln2_gain,
    ln2_bias,
    fc1_weight,
    fc1_bias,
    fc2_weight,
    fc2_bias,
    scale_two,
    cotangent,
):
    f32, bf16 = jnp.float32, jnp.bfloat16
    seq_len = segment_ids.shape[1]
    rows_here, width = tokens.shape
    head_columns = qkv_weight.shape[2]
    heads = head_columns // HEAD_DIM
    hidden_here = fc1_weight.shape[1]
    ids = segment_ids[0]
    here = lax.axis_index("tensor")

    turned = qkv_weight.transpose(0, 2, 1)
    full_one, queries, keys, values, pairs, singles, pairs_here, singles_here, gathered, fc1_bias_full = start(
        shards,
        members,
        tokens,
        segment_ids,
        ln1_gain,
        ln1_bias,
        turned,
        qv_bias,
        fc1_weight,
        fc2_weight,
        proj_weight,
        fc1_bias,
    )
    params = (proj_bias, scale_one, ln2_gain, ln2_bias, fc2_bias, scale_two)
    block_out, grad_hidden, pair_grads, single_grads, vectors, *exchanged = middle(
        shards, members, pairs_here, singles_here, gathered, fc1_bias_full, params, tokens, cotangent
    )
    pair_grads = pair_grads.reshape(seq_len, LANES)
    single_grads = single_grads.reshape(seq_len // 2, LANES)

    grad_tokens, totals, qkv_pieces, weight_pieces = back(
        shards,
        members,
        (queries, keys, values),
        (pairs, singles, pair_grads, single_grads),
        turned.reshape(3 * head_columns, width),
        ln1_gain,
        ln1_bias,
        vectors,
        full_one,
        tokens,
        grad_hidden,
        exchanged,
    )
    fc1_grad, fc2_grad, proj_grad, qkv_grad, fc1_bias_grad, *sums = unpack(
        qkv_pieces, weight_pieces, totals, width // PIECES, head_columns // PIECES
    )
    qkv_grad = qkv_grad.reshape(3, head_columns, width).transpose(0, 2, 1)
    qv_sums = lax.dynamic_index_in_dim(totals, 12 + here, 0, keepdims=False)
    qv_grad = jnp.stack([qv_sums[:head_columns], qv_sums[2 * head_columns : 3 * head_columns]])
    return (
        block_out,
        grad_tokens,
        sums[0],
        sums[1],
        qkv_grad,
        qv_grad,
        proj_grad,
        sums[2],
        sums[3],
        sums[4],
        sums[5],
        fc1_grad,
        fc1_bias_grad,
        fc2_grad,
        sums[6],
        sums[7],
    )


def solution(mesh):
    rows = P(("dp", "tensor"), None)
    columns = P(None, "tensor")
    return jax.shard_map(
        partial(on_device, mesh.shape["tensor"], mesh.shape["dp"]),
        mesh=mesh,
        in_specs=(
            rows,
            P("dp", None),
            P(),
            P(),
            P(None, None, "tensor"),
            columns,
            P("tensor", None),
            P(),
            P(),
            P(),
            P(),
            columns,
            P("tensor"),
            P("tensor", None),
            P(),
            P(),
            rows,
        ),
        out_specs=(
            rows,
            rows,
            P(),
            P(),
            P(None, None, "tensor"),
            columns,
            P("tensor", None),
            P(),
            P(),
            P(),
            P(),
            columns,
            P("tensor"),
            P("tensor", None),
            P(),
            P(),
        ),
        check_vma=False,
    )
```

```python
from functools import partial
import math

import jax, jax.numpy as jnp
from jax import lax
from jax.experimental import pallas as pl
from jax.experimental.pallas import tpu as pltpu

from jax.sharding import PartitionSpec as P

HEAD_DIM = 64
LANES = 128
MOST_TOKENS = 1152
MASKED = -(2.0**100)


def contract_rows(left, right):
    return lax.dot_general(left, right, (((0,), (0,)), ((), ())), preferred_element_type=jnp.float32)


def times_transposed(left, right, precision=None):
    return lax.dot_general(
        left, right, (((1,), (1,)), ((), ())), preferred_element_type=jnp.float32, precision=precision
    )


def split_three(value):
    high = value.astype(jnp.bfloat16)
    rest = value - high.astype(jnp.float32)
    middle = rest.astype(jnp.bfloat16)
    low = (rest - middle.astype(jnp.float32)).astype(jnp.bfloat16)
    return (high, middle, low)


def join_lanes(low, high):
    lane = lax.broadcasted_iota(jnp.int32, low.shape, 1)
    return jnp.where(lane < HEAD_DIM, low, pltpu.roll(high, HEAD_DIM, 1))


MESH = pl.DeviceIdType.MESH
PIECES = 8
PIECE_BITS = 3


def rounded_sum(left, right):
    return (left.astype(jnp.float32) + right.astype(jnp.float32)).astype(jnp.bfloat16)


def bit_of(index, bit):
    return lax.rem(index // (1 << bit), 2)


def partner_of(index, bit):
    return index + (1 - 2 * bit_of(index, bit)) * (1 << bit)


def greet(dp_bits, shards):
    barrier = pltpu.get_barrier_semaphore()
    member, here = lax.axis_index("dp"), lax.axis_index("tensor")
    peers = [{"dp": partner_of(member, bit)} for bit in range(dp_bits)]
    peers += [{"tensor": lax.rem(here + way, shards)} for way in range(1, shards)]
    for peer in peers:
        pl.semaphore_signal(barrier, inc=1, device_id=peer, device_id_type=MESH)
    pl.semaphore_wait(barrier, len(peers))


def back_kernel(
    shards,
    dp_bits,
    q_ref,
    k_ref,
    v_ref,
    pair_ref,
    single_ref,
    pair_grad_ref,
    single_grad_ref,
    weight_ref,
    gain_ref,
    shift_ref,
    vectors_ref,
    rows_ref,
    tokens_ref,
    hidden_ref,
    a_keep,
    a_away,
    b_keep,
    b_away,
    a_early,
    a_early_away,
    b_early,
    b_early_away,
    tokens_out,
    vectors_out,
    qkv_out,
    weights_out,
    grad_heads,
    dq,
    dk,
    dv,
    probs,
    grad_scores,
    packed,
    rows_own,
    tokens_own,
    hidden_own,
    part,
    arrived,
    q_wide,
    column_sums,
    q_all,
    q_half,
    q_quarter,
    q_got_core,
    q_got_x,
    q_got_y,
    q_got_more,
    v_now,
    v_got,
    v_shards,
    a_sum,
    b_sum,
    a_got,
    b_got,
    a_second,
    b_second,
    pieces,
    early_own,
    pieces_more,
    early_more,
    z_got,
    early_got,
    early_side,
    send,
    recv,
    local,
):
    f32, bf16 = jnp.float32, jnp.bfloat16
    member, here = lax.axis_index("dp"), lax.axis_index("tensor")
    core, x_bit, y_bit = bit_of(member, 0), bit_of(member, 1), bit_of(member, 2)
    own_piece = core * 4 + x_bit * 2 + y_bit
    block, width = part.shape[1], part.shape[2]
    heads = q_ref.shape[0]
    columns = weight_ref.shape[0]
    half_rows = weights_out.shape[1] // 2
    last = shards - 1
    reach = -(-(MOST_TOKENS - 1) // block)
    gain, shift = (ref[...].reshape(1, width) for ref in (gain_ref, shift_ref))
    slots = iter(range(send.shape[0]))
    pending = []

    def copy_to(src, dst, at, **peer):
        return pltpu.make_async_remote_copy(
            src_ref=src, dst_ref=dst, send_sem=send.at[at], recv_sem=recv.at[at], device_id=peer, device_id_type=MESH
        )

    def start_dp(src, dst, bit, keep=True):
        copy = copy_to(src, dst, next(slots), dp=partner_of(member, bit))
        copy.start()
        if keep:
            pending.append(copy)
        return copy

    def load(at):
        source, landing = (
            (a_keep, a_sum),
            (b_keep, b_sum),
            (tokens_ref, tokens_own),
            (hidden_ref, hidden_own),
            (a_early, early_own.at[pl.ds(0, shards // 2)]),
            (b_early, early_own.at[pl.ds(shards // 2, shards // 2)]),
        )[at]
        return pltpu.make_async_copy(source, landing, local.at[at])

    def load_rows(owner):
        rows = pl.ds(pl.multiple_of(owner * block, 16), block)
        return pltpu.make_async_copy(rows_ref.at[rows], rows_own, local.at[6])

    for at in range(6):
        load(at).start()
    load_rows(last).start()
    greet(dp_bits, shards)
    start_dp(a_early_away, early_side.at[pl.ds(0, shards // 2)], 2)
    start_dp(b_early_away, early_side.at[pl.ds(shards // 2, shards // 2)], 1)
    early_sides = pending[-2:]
    start_dp(a_away, a_got, 1)
    start_dp(b_away, b_got, 2)
    first_a, first_b = pending[-2:]
    second_slots = [next(slots) for _ in range(2)]

    def second(at):
        if at:
            return copy_to(b_sum.at[1 - x_bit], b_second, second_slots[1], dp=partner_of(member, 1))
        return copy_to(a_sum.at[1 - y_bit], a_second, second_slots[0], dp=partner_of(member, 2))

    z_slots = [[next(slots) for _ in range(1, shards)] for _ in range(2)]

    def piece_copy(way, first=False):
        target = lax.rem(here + way, shards)
        source, landing = (early_own, early_got) if first else (pieces, z_got)
        return copy_to(source.at[target], landing.at[way - 1], z_slots[first][way - 1], tensor=target)

    more_slots = [[next(slots) for _ in range(PIECE_BITS, dp_bits)] for _ in range(2)]

    def send_pieces(first):
        source, landing = (early_own, early_more) if first else (pieces, pieces_more)
        for bit in range(PIECE_BITS, dp_bits):
            at = bit - PIECE_BITS
            extra = copy_to(source, landing.at[at], more_slots[first][at], dp=partner_of(member, bit))
            extra.start()
            extra.wait_recv()
            extra.wait_send()

            def step(owner, carry):
                source[owner] = rounded_sum(source[owner], landing[at, owner])
                return carry

            lax.fori_loop(0, shards, step, 0)
        for way in range(1, shards):
            piece_copy(way, first).start()

    def early_exchange():
        for at, copy in enumerate(early_sides):
            load(4 + at).wait()
            copy.wait_recv()
        for owner in range(shards):
            early_own[owner] = rounded_sum(early_own[owner], early_side[owner])
        send_pieces(True)


    def sum_pairs(out, right):
        def step(at, carry):
            one, two = at // out.shape[1], lax.rem(at, out.shape[1])
            out[one, two] = rounded_sum(out[one, two], right[one, two])
            return carry

        lax.fori_loop(0, out.shape[0] * out.shape[1], step, 0)

    def second_exchange():
        first_a.wait_recv()
        first_b.wait_recv()
        load(0).wait()
        load(1).wait()
        sum_pairs(a_sum, a_got)
        sum_pairs(b_sum, b_got)
        second(0).start()
        second(1).start()

    def shard_exchange():
        second(0).wait_recv()
        second(1).wait_recv()
        split = shards // 2
        for at in range(split):
            pieces[at] = rounded_sum(a_sum[y_bit, at], a_second[at])
            pieces[split + at] = rounded_sum(b_sum[x_bit, at], b_second[at])
        send_pieces(False)

    split_row = early_own.shape[1]
    gather_slots = [[next(slots) for _ in range(count)] for count in (2, 3, 1)]

    def gather_copies(stage):
        first_rows, other_rows = pl.ds(0, half_rows), pl.ds(half_rows, half_rows)
        if stage == 0:
            moves = [(own_piece, first_rows, 2), (own_piece, other_rows, 1)]
        elif stage == 1:
            moves = [(pl.ds(core * 4 + x_bit * 2, 2), first_rows, 1)]
            moves += [(core * 4 + 2 * at + y_bit, other_rows, 2) for at in range(2)]
        else:
            moves = [(pl.ds(core * 4, 4), pl.ds(0, 2 * half_rows), 0)]
        return [
            copy_to(
                weights_out.at[piece, rows],
                weights_out.at[piece, rows],
                gather_slots[stage][at],
                dp=partner_of(member, bit),
            )
            for at, (piece, rows, bit) in enumerate(moves)
        ]

    def gather_start(stage):
        for copy in gather_copies(stage):
            copy.start()

    def gather_wait(stage):
        for copy in gather_copies(stage):
            copy.wait_recv()

    def sum_shards():
        for first, source, landing, rows in (
            (True, early_own, early_got, slice(0, split_row)),
            (False, pieces, z_got, slice(split_row, 2 * half_rows)),
        ):
            for way in range(1, shards):
                piece_copy(way, first).wait_recv()
            total = source[here].astype(f32)
            for way in range(1, shards):
                total = total + landing[way - 1].astype(f32)
            weights_out[own_piece, rows, :] = total.astype(bf16)
        gather_start(0)

    right_slots = [next(slots) for _ in range(shards)]
    left_slots = [next(slots) for _ in range(shards)]

    def to_right(owner):
        return copy_to(part.at[owner], arrived.at[owner], right_slots[owner], tensor=lax.rem(here + 1, shards))

    def to_left(owner, target=None):
        to = lax.rem(here + last, shards) if target is None else target
        landing = jnp.where(owner == to, shards, owner)
        return copy_to(
            part.at[owner], arrived.at[landing], left_slots[owner], tensor=lax.rem(here + last, shards)
        )

    def add_arrived(owner, landing):
        def step(at, carry):
            rows = pl.ds(pl.multiple_of(at * (block // 4), 16), block // 4)
            part[owner, rows, :] = rounded_sum(part[owner, rows, :], arrived[landing, rows, :])
            return carry

        lax.fori_loop(0, 4, step, 0)

    def hop(moved, nth, rightward):
        owner, at = (last - nth, moved) if rightward else (nth, last - moved)
        if (at < owner) if rightward else (at > owner):

            @pl.when(here == at)
            def _():
                copy = to_right(owner) if rightward else to_left(owner)
                copy.wait_recv()
                add_arrived(owner, owner)
                copy.start()

    dq[...] = jnp.zeros_like(dq)
    dk[...] = jnp.zeros_like(dk)
    dv[...] = jnp.zeros_like(dv)
    q_wide[...] = jnp.zeros_like(q_wide)
    column_sums[...] = jnp.zeros_like(column_sums)
    source = lax.broadcasted_iota(jnp.int32, (LANES, LANES), 0)
    target = lax.broadcasted_iota(jnp.int32, (LANES, LANES), 1)
    gathers = (target >= HEAD_DIM) & (target < HEAD_DIM + 3)
    picks = []
    for odd in range(2):
        inside = (source >= HEAD_DIM * odd) & (source < HEAD_DIM * (odd + 1))
        summing = jnp.where(inside & gathers, -1.0, 0.0).astype(bf16)
        moving = jnp.where(inside & (source - HEAD_DIM * odd == target), 1.0, 0.0).astype(bf16)
        picks.append((summing, moving))
    half = block // 2
    lane = lax.broadcasted_iota(jnp.int32, (half, LANES), 1)

    def prepare(at, carry):
        for side in range(2):
            rows = pl.ds(pl.multiple_of((2 * at + side) * half, half), half)
            single_rows = pl.ds(pl.multiple_of(at * half, half), half)
            for head, odd, mixed, grad in (
                (0, 0, pair_ref[rows, :], pair_grad_ref[rows, :]),
                (1, 1, pair_ref[rows, :], pair_grad_ref[rows, :]),
                (2, side, single_ref[single_rows, :], single_grad_ref[single_rows, :]),
            ):
                summing, moving = picks[odd]
                product = grad.astype(f32) * mixed.astype(f32)
                high = product.astype(bf16)
                low = (product - high.astype(f32)).astype(bf16)
                shared = jnp.dot(high, summing, preferred_element_type=f32) + jnp.dot(
                    low, summing, preferred_element_type=f32
                )
                moved = jnp.dot(grad, moving, preferred_element_type=f32)
                for place, value in enumerate(split_three(shared)):
                    moved = jnp.where(lane == HEAD_DIM + place, value.astype(f32), moved)
                grad_heads[head, rows, :] = moved.astype(bf16)
        return carry

    lax.fori_loop(0, shards, prepare, 0)

    def rows_of(owner):
        return pl.ds(pl.multiple_of(owner * block, 16), block)

    def visit(owner, other):
        key_rows, query_rows = rows_of(owner), rows_of(other)
        for head in range(heads):
            prob = jnp.exp(times_transposed(k_ref[head, key_rows, :], q_ref[head, query_rows, :]))
            grad_prob = times_transposed(v_ref[head, key_rows, :], grad_heads[head, query_rows, :])
            probs[head] = prob.astype(bf16)
            grad_scores[head] = (prob * grad_prob).astype(bf16)
        for head in range(heads):
            dv[head, key_rows, :] += jnp.dot(
                probs[head], grad_heads[head, query_rows, :], preferred_element_type=f32
            )
            dk[head, key_rows, :] += jnp.dot(
                grad_scores[head], q_ref[head, query_rows, :], preferred_element_type=f32
            )
            dq[head, query_rows, :] += contract_rows(grad_scores[head], k_ref[head, key_rows, :])

    def close_block(owner, following):
        rows = rows_of(owner)
        scale = HEAD_DIM**-0.5
        for first, low, high in (
            (0, dq[0, rows, :] * scale, dq[1, rows, :] * scale),
            (1, dq[2, rows, :] * scale, dk[0, rows, :]),
            (2, dk[1, rows, :], dk[2, rows, :]),
            (3, dv[0, rows, :], dv[1, rows, :]),
        ):
            packed[:, first * LANES : (first + 1) * LANES] = join_lanes(low, high).astype(bf16)
        packed[:, 4 * LANES : columns] = dv[2, rows, :HEAD_DIM].astype(bf16)
        part[owner] = jnp.dot(packed[...], weight_ref[...], preferred_element_type=f32).astype(bf16)

        @pl.when((owner == last) & (here == 0))
        def _():
            to_right(last).start()

        @pl.when((owner == 0) & (here == last))
        def _():
            to_left(0).start()

        load_rows(owner).wait()
        q_wide[...] += contract_rows(packed[...], rows_own[...])
        column_sums[...] += jnp.dot(jnp.ones((8, block), bf16), packed[...], preferred_element_type=f32)

        @pl.when(following >= 0)
        def _():
            load_rows(following).start()

    order = []
    for near in range((shards + 1) // 2):
        for owner in (last - near, near):
            if owner not in order:
                order.append(owner)
    visits, closing = [], []
    for at, owner in enumerate(order):
        rest = order[at:]
        both = [(owner, owner)]
        for other in rest[1:]:
            if abs(owner - other) <= reach:
                both += [(owner, other), (other, owner)]
        visits += both
        closing.append(len(visits) - 1)
    total_visits = len(visits)

    def lookup(table, at):
        value = 0
        for place, entry in enumerate(table):
            value = value + jnp.where(at == place, entry, 0)
        return value

    closed = [order[closing.index(at)] if at in closing else -1 for at in range(total_visits)]
    later = [
        order[closing.index(at) + 1] if at in closing and at != closing[-1] else -1 for at in range(total_visits)
    ]
    events = {
        1: early_exchange,
        closing[0] + 1: second_exchange,
        closing[0] + 4: shard_exchange,
        closing[1] + 2: lambda: hop(1, 0, True),
        closing[-1]: sum_shards,
    }
    assert len(events) == 5 and shards >= 4

    def each_visit(at, carry):
        visit(lookup([pair[0] for pair in visits], at), lookup([pair[1] for pair in visits], at))
        for when, event in events.items():

            @pl.when(at == when)
            def _():
                event()

        @pl.when(lookup([int(owner >= 0) for owner in closed], at) == 1)
        def _():
            close_block(lookup(closed, at), lookup(later, at))

        return carry

    lax.fori_loop(0, total_visits, each_visit, 0)
    def end_sends(nths):
        for nth in nths:

            @pl.when(here == 0)
            def _():
                to_right(last - nth).start()

            @pl.when(here == last)
            def _():
                to_left(nth).start()

    end_sends(range(1, last - 1))
    gather_wait(0)
    gather_start(1)

    sums = column_sums[...]
    weight = weight_ref[...].astype(f32)
    shift_sum = jnp.dot(sums, weight, preferred_element_type=f32, precision=lax.Precision.HIGHEST)[0:1]
    gain_sum = jnp.sum(weight * q_wide[...], axis=0, keepdims=True)
    v_now[0] = vectors_ref[...]
    v_now[0, 0:1, :] = (gain_sum - shift * shift_sum) / gain
    v_now[0, 1:2, :] = shift_sum
    v_now[0, pl.ds(12 + here, 1), 0:columns] = sums[0:1]
    count = q_all.shape[1]
    for piece in range(PIECES):
        q_all[piece] = q_wide[piece * count : (piece + 1) * count, :].astype(bf16)

    def vector_stage(bit):
        return start_dp(v_now.at[bit], v_got.at[bit], bit)

    q_core = start_dp(q_all.at[pl.ds((1 - core) * 4, 4)], q_got_core, 0)
    v_copy = vector_stage(0)
    q_core.wait_recv()
    for at in range(4):
        q_half[at] = rounded_sum(q_all[core * 4 + at], q_got_core[at])
    q_x = start_dp(q_half.at[pl.ds((1 - x_bit) * 2, 2)], q_got_x, 1)
    v_copy.wait_recv()
    v_now[1] = v_now[0] + v_got[0]
    v_copy = vector_stage(1)
    hop(1, 0, False)
    for moved in range(2, last):
        hop(moved, 0, True)
    gather_wait(1)
    gather_start(2)
    q_x.wait_recv()
    for at in range(2):
        q_quarter[at] = rounded_sum(q_half[x_bit * 2 + at], q_got_x[at])
    q_y = start_dp(q_quarter.at[1 - y_bit], q_got_y, 2)
    v_copy.wait_recv()
    v_now[2] = v_now[1] + v_got[1]
    v_copy = vector_stage(2)
    q_y.wait_recv()
    qkv_out[own_piece] = rounded_sum(q_quarter[y_bit], q_got_y[...])
    v_copy.wait_recv()
    v_now[3] = v_now[2] + v_got[2]
    for bit in range(PIECE_BITS, dp_bits):
        extra = start_dp(qkv_out.at[own_piece], q_got_more.at[bit - PIECE_BITS], bit, False)
        v_copy = vector_stage(bit)
        extra.wait_recv()
        extra.wait_send()
        qkv_out[own_piece] = rounded_sum(qkv_out[own_piece], q_got_more[bit - PIECE_BITS])
        v_copy.wait_recv()
        v_now[bit + 1] = v_now[bit] + v_got[bit]
    q_back = start_dp(qkv_out.at[own_piece], qkv_out.at[own_piece], 2)
    v_shards[here] = v_now[dp_bits]
    for way in range(1, shards):
        copy = copy_to(
            v_now.at[dp_bits], v_shards.at[here], next(slots), tensor=lax.rem(here + way, shards)
        )
        copy.start()
        pending.append(copy)
    v_waits = pending[-last:]
    end_sends([last - 1])
    q_back.wait_recv()
    span = pl.ds(core * 4 + x_bit * 2, 2)
    q_back = start_dp(qkv_out.at[span], qkv_out.at[span], 1)
    for nth in range(1, last):
        for moved in range(1, last):
            hop(moved, nth, True)
            hop(moved, nth, False)
        if nth == 1:
            for moved in range(2, last):
                hop(moved, 0, False)
    q_back.wait_recv()
    span = pl.ds(core * 4, 4)
    q_back = start_dp(qkv_out.at[span], qkv_out.at[span], 0)
    gather_wait(2)
    for copy in v_waits:
        copy.wait_recv()
    vectors_sum = v_shards[0]
    for at in range(1, shards):
        vectors_sum = vectors_sum + v_shards[at]
    vectors_out[...] = vectors_sum

    for owner in range(shards):

        @pl.when(here == owner)
        def _():
            if owner > 0:
                to_right(owner).wait_recv()
                add_arrived(owner, owner)
            if owner < last:
                to_left(owner, owner).wait_recv()
                add_arrived(owner, shards)

    load(2).wait()
    load(3).wait()

    def close(at, carry):
        rows = pl.ds(pl.multiple_of(at * (block // 4), 16), block // 4)
        tokens = tokens_own[rows, :].astype(f32)
        centred = tokens - jnp.mean(tokens, axis=1, keepdims=True)
        inverse = lax.rsqrt(jnp.mean(centred * centred, axis=1, keepdims=True) + eps_norm)
        unit = centred * inverse
        scaled = part[here, rows, :].astype(f32) * gain
        inner = (
            scaled
            - jnp.mean(scaled, axis=1, keepdims=True)
            - unit * jnp.mean(scaled * unit, axis=1, keepdims=True)
        )
        tokens_out[rows, :] = hidden_own[rows, :] + inverse * inner
        return carry

    lax.fori_loop(0, 4, close, 0)
    q_back.wait_recv()
    for copy in pending:
        copy.wait_send()
    for at in range(2):
        second(at).wait_send()
    for stage in range(3):
        for copy in gather_copies(stage):
            copy.wait_send()
    for way in range(1, shards):
        piece_copy(way, True).wait_send()
        piece_copy(way).wait_send()
    for owner in range(shards):

        @pl.when(here < owner)
        def _():
            to_right(owner).wait_send()

        @pl.when(here > owner)
        def _():
            to_left(owner).wait_send()


def back(shards, members, heads_in, pair_in, weight, gain, shift, vectors, rows, tokens, grad_hidden, exchanged):
    dp_bits = members.bit_length() - 1
    assert members == 1 << dp_bits and dp_bits >= PIECE_BITS
    f32, bf16 = jnp.float32, jnp.bfloat16
    heads, seq_len, _ = heads_in[0].shape
    columns, width = weight.shape
    block = tokens.shape[0]
    quarter = exchanged[0].shape
    early_rows = exchanged[4].shape[1]
    late_rows = quarter[2]
    count = columns // PIECES
    more = max(1, dp_bits - PIECE_BITS)
    copies = 26 + 2 * shards + 3 * (shards - 1) + 5 * dp_bits
    vm = pltpu.VMEM
    return pl.pallas_call(
        partial(back_kernel, shards, dp_bits),
        in_specs=[pl.BlockSpec(memory_space=vm)] * 11 + [pl.BlockSpec(memory_space=pl.ANY)] * 11,
        out_specs=[pl.BlockSpec(memory_space=vm)] * 4,
        out_shape=[
            jax.ShapeDtypeStruct((block, width), f32),
            jax.ShapeDtypeStruct(vectors.shape, f32),
            jax.ShapeDtypeStruct((PIECES, count, width), bf16),
            jax.ShapeDtypeStruct((PIECES, early_rows + late_rows, width), bf16),
        ],
        scratch_shapes=[
            vm((heads, seq_len, LANES), bf16),
            vm((heads, seq_len, LANES), f32),
            vm((heads, seq_len, LANES), f32),
            vm((heads, seq_len, LANES), f32),
            vm((heads, block, block), bf16),
            vm((heads, block, block), bf16),
            vm((block, columns), bf16),
            vm((block, width), bf16),
            vm((block, width), bf16),
            vm((block, width), f32),
            vm((shards, block, width), bf16),
            vm((shards + 1, block, width), bf16),
            vm((columns, width), f32),
            vm((8, columns), f32),
            vm((PIECES, count, width), bf16),
            vm((4, count, width), bf16),
            vm((2, count, width), bf16),
            vm((4, count, width), bf16),
            vm((2, count, width), bf16),
            vm((count, width), bf16),
            vm((more, count, width), bf16),
            vm((dp_bits + 1,) + vectors.shape, f32),
            vm((dp_bits,) + vectors.shape, f32),
            vm((shards,) + vectors.shape, f32),
            vm(quarter, bf16),
            vm(quarter, bf16),
            vm(quarter, bf16),
            vm(quarter, bf16),
            vm(quarter[1:], bf16),
            vm(quarter[1:], bf16),
            vm((shards, late_rows, width), bf16),
            vm((shards, early_rows, width), bf16),
            vm((more, shards, late_rows, width), bf16),
            vm((more, shards, early_rows, width), bf16),
            vm((shards - 1, late_rows, width), bf16),
            vm((shards - 1, early_rows, width), bf16),
            vm((shards, early_rows, width), bf16),
            pltpu.SemaphoreType.DMA((copies,)),
            pltpu.SemaphoreType.DMA((copies,)),
            pltpu.SemaphoreType.DMA((7,)),
        ],
        compiler_params=pltpu.CompilerParams(
            collective_id=1, has_side_effects=True, vmem_limit_bytes=67043328
        ),
        name="back",
        cost_estimate=pl.CostEstimate(
            flops=10 * heads * seq_len * seq_len * LANES, transcendentals=0, bytes_accessed=40 * block * width
        ),
    )(*heads_in, *pair_in, weight, gain, shift, vectors, rows, tokens, grad_hidden, *exchanged)


def unpack_kernel(qkv_ref, weights_ref, totals_ref, fc1_out, fc2_out, proj_out, qkv_out, fc1_bias_out, *vector_outs):
    fc_rows, proj_rows = fc1_out.shape[0], proj_out.shape[0]
    fc2_out[...] = weights_ref[0, :fc_rows].astype(jnp.float32)
    fc1_out[...] = weights_ref[0, fc_rows : 2 * fc_rows].astype(jnp.float32)
    proj_out[...] = weights_ref[0, 2 * fc_rows : 2 * fc_rows + proj_rows].astype(jnp.float32)
    qkv_out[...] = qkv_ref[0].astype(jnp.float32)

    @pl.when(pl.program_id(0) == 0)
    def _():
        width = totals_ref.shape[1]
        for at, out in enumerate(vector_outs):
            out[...] = totals_ref[at : at + 1, :].reshape(width)
        here = lax.axis_index("tensor")
        fc1_bias_out[...] = totals_ref[pl.ds(8 + here, 1), :].reshape(width)


def unpack(qkv, weights, totals, fc_rows, proj_rows):
    f32 = jnp.float32
    _, rows, width = weights.shape
    qkv_rows = qkv.shape[1]
    counts = (fc_rows, fc_rows, proj_rows, qkv_rows)
    vector = pl.BlockSpec((width,), lambda i: (0,))
    return pl.pallas_call(
        unpack_kernel,
        grid=(PIECES,),
        in_specs=[
            pl.BlockSpec((1, qkv_rows, width), lambda i: (i, 0, 0)),
            pl.BlockSpec((1, rows, width), lambda i: (i, 0, 0)),
            pl.BlockSpec(totals.shape, lambda i: (0, 0)),
        ],
        out_specs=[pl.BlockSpec((count, width), lambda i: (i, 0)) for count in counts] + [vector] * 9,
        out_shape=[jax.ShapeDtypeStruct((PIECES * count, width), f32) for count in counts]
        + [jax.ShapeDtypeStruct((width,), f32)] * 9,
        name="unpack",
    )(qkv, weights, totals)


def start_kernel(
    shards,
    dp_bits,
    tokens_ref,
    ids_ref,
    gain_ref,
    shift_ref,
    qkv_ref,
    qv_bias_ref,
    fc1_ref,
    fc2_ref,
    proj_ref,
    fc1_bias_ref,
    normed_out,
    q_out,
    k_out,
    v_out,
    pairs_out,
    singles_out,
    pairs_here,
    singles_here,
    weights_out,
    bias_out,
    blocks,
    normed_all,
    queries,
    keys,
    values,
    peaks,
    sums,
    scores,
    weights,
    q_extra,
    k_extra,
    own,
    chain,
    send,
    recv,
    local,
    stored,
):
    f32, bf16 = jnp.float32, jnp.bfloat16
    member, here = lax.axis_index("dp"), lax.axis_index("tensor")
    core, x_bit, y_bit = bit_of(member, 0), bit_of(member, 1), bit_of(member, 2)
    own_piece = core * 4 + x_bit * 2 + y_bit
    block, width = tokens_ref.shape
    heads = queries.shape[0]
    seq_len = ids_ref.shape[1]
    last = shards - 1
    reach = -(-(MOST_TOKENS - 1) // block)
    slots = iter(range(send.shape[0]))
    pending = []

    def copy_to(src, dst, at, **peer):
        return pltpu.make_async_remote_copy(
            src_ref=src, dst_ref=dst, send_sem=send.at[at], recv_sem=recv.at[at], device_id=peer, device_id_type=MESH
        )

    def start_dp(src, dst, bit):
        copy = copy_to(src, dst, next(slots), dp=partner_of(member, bit))
        copy.start()
        pending.append(copy)
        return copy

    fc1_rows, fc2_rows, proj_rows = (ref.shape[0] // PIECES for ref in (fc1_ref, fc2_ref, proj_ref))
    loads = []
    for at, (ref, first, count) in enumerate(
        ((fc2_ref, 0, fc2_rows), (fc1_ref, fc2_rows, fc1_rows))
    ):
        rows = pl.ds(pl.multiple_of(own_piece * count, 16), count)
        loads.append(pltpu.make_async_copy(ref.at[rows], own.at[first : first + count], local.at[at]))
        loads[-1].start()
    used = fc1_rows + fc2_rows
    rows = pl.ds(pl.multiple_of(own_piece * proj_rows, 8), proj_rows)
    own[used : used + proj_rows, :] = proj_ref[rows, :]
    used += proj_rows
    own[used:, :] = jnp.zeros((own.shape[0] - used, width), bf16)
    gain, shift = (ref[...].reshape(1, width) for ref in (gain_ref, shift_ref))
    bias_out[here] = fc1_bias_ref[...].reshape(1, width)
    greet(dp_bits, shards)
    for load in loads:
        load.wait()

    chains = {}
    for name, first, rest in (("w", own, chain), ("t", tokens_ref, blocks)):
        chains[name] = (
            first,
            rest,
            [next(slots) for _ in range(shards)],
            [next(slots) for _ in range(shards)],
        )

    def hop_copy(name, owner, rightward, from_own):
        first, rest, right_slots, left_slots = chains[name]
        src = first if from_own else rest.at[owner]
        step = 1 if rightward else last
        at = (right_slots if rightward else left_slots)[owner]
        return copy_to(src, rest.at[owner], at, tensor=lax.rem(here + step, shards))

    def send_own(name, rightward):
        for owner in range(shards):
            if owner != (last if rightward else 0):

                @pl.when(here == owner)
                def _():
                    hop_copy(name, owner, rightward, True).start()

    def hop(name, time, then=None):
        for at in range(shards):
            for rightward, owner, end in ((True, at - time, last), (False, at + time, 0)):
                if 0 <= owner <= last:

                    @pl.when(here == at)
                    def _():
                        hop_copy(name, owner, rightward, False).wait_recv()
                        if at != end:
                            hop_copy(name, owner, rightward, False).start()
                            if then is not None and owner in (0, last):
                                hop_copy(then, at, rightward, True).start()

    send_own("w", True)
    send_own("w", False)

    @pl.when(here == 0)
    def _():
        hop_copy("t", 0, True, True).start()

    @pl.when(here == last)
    def _():
        hop_copy("t", last, False, True).start()

    bias_copies = []
    for way in range(1, shards):
        copy = copy_to(
            bias_out.at[here], bias_out.at[here], next(slots), tensor=lax.rem(here + way, shards)
        )
        copy.start()
        bias_copies.append(copy)
    pending.extend(bias_copies)

    large = -MASKED
    segments = lax.broadcasted_iota(jnp.int32, (8, seq_len), 0)
    same = jnp.where(segments == ids_ref[...], 1.0, 0.0).astype(bf16)
    select = lax.broadcasted_iota(jnp.int32, (8, LANES), 1) - HEAD_DIM == lax.broadcasted_iota(
        jnp.int32, (8, LANES), 0
    )
    matched = contract_rows(same, jnp.where(select, 1.0, 0.0).astype(bf16))
    lane = lax.broadcasted_iota(jnp.int32, (seq_len, LANES), 1)
    segment_lane = (lane >= HEAD_DIM) & (lane < HEAD_DIM + 8)
    ones_lane = (lane >= HEAD_DIM + 8) & (lane < HEAD_DIM + 11)
    q_extra[...] = jnp.where(segment_lane, (matched - 1.0) * large, 0.0).astype(bf16)
    k_extra[...] = jnp.where(ones_lane, 1.0, matched).astype(bf16)
    low_half = lax.broadcasted_iota(jnp.int32, (block, LANES), 1) < HEAD_DIM
    v_lane = lax.broadcasted_iota(jnp.int32, (block, LANES), 1)
    v_extra = jnp.where((v_lane >= HEAD_DIM) & (v_lane < HEAD_DIM + 3), 1.0, 0.0).astype(bf16)

    def rows_of(owner, count=block):
        return pl.ds(pl.multiple_of(owner * count, 16), count)

    def store(which, owner):
        rows = rows_of(owner)
        source, out = (
            (normed_all.at[rows], normed_out.at[rows]),
            (queries.at[:, rows], q_out.at[:, rows]),
            (keys.at[:, rows], k_out.at[:, rows]),
            (values.at[:, rows], v_out.at[:, rows]),
        )[which]
        return pltpu.make_async_copy(source, out, stored.at[which, owner])

    def project_block(source, owner):
        tokens = source.astype(f32)
        centred = tokens - jnp.mean(tokens, axis=1, keepdims=True)
        inverse = lax.rsqrt(jnp.mean(centred * centred, axis=1, keepdims=True) + eps_norm)
        normed = (centred * inverse * gain + shift).astype(bf16)
        rows = rows_of(owner)
        normed_all[rows, :] = normed
        for which, out in ((0, queries), (1, keys), (2, values)):
            product = times_transposed(normed, qkv_ref[which])
            if which != 1:
                product = product + qv_bias_ref[which // 2 : which // 2 + 1, :]
            if which == 0:
                product = product.astype(bf16).astype(f32) * HEAD_DIM**-0.5
            extra = v_extra if which == 2 else (q_extra if which == 0 else k_extra)[rows, :]
            for head in range(heads):
                first = (head // 2) * LANES
                tile = product[:, first : first + LANES]
                if tile.shape[1] < LANES:
                    blank = jnp.zeros((block, LANES - tile.shape[1]), f32)
                    tile = jnp.concatenate([tile, blank], axis=1)
                if head % 2:
                    tile = pltpu.roll(tile, HEAD_DIM, 1)
                out[head, rows, :] = jnp.where(low_half, tile, extra.astype(f32)).astype(bf16)
        store(0, owner).start()
        store(2, owner).start()
        store(3, owner).start()

    peaks[...] = jnp.full_like(peaks, -3e38)
    sums[...] = jnp.zeros_like(sums)

    def away(index):
        return jnp.maximum(index - here, here - index)

    def visit(owner, other):
        rows, across = rows_of(owner), rows_of(other)
        for head in range(heads):
            scores[head] = times_transposed(queries[head, rows, :], keys[head, across, :])
        for head in range(heads):
            old_peak = peaks[head, rows, :]
            new_peak = jnp.maximum(old_peak, jnp.max(scores[head], axis=1, keepdims=True))
            peaks[head, rows, :] = new_peak
            spread = jnp.concatenate([new_peak] * -(-block // LANES), axis=1)[:, :block]
            weights[head] = jnp.exp(scores[head] - spread).astype(bf16)
            sums[head, rows, :] = sums[head, rows, :] * jnp.exp(old_peak - new_peak)
        for head in range(heads):
            sums[head, rows, :] += jnp.dot(
                weights[head], values[head, across, :], preferred_element_type=f32
            )

    pair_slots = [next(slots) for _ in range(shards)]
    single_slots = [next(slots) for _ in range(shards)]

    def exchange(owner, source):
        half_block = block // 2
        return [
            pltpu.make_async_remote_copy(
                src_ref=out.at[rows_of(owner, count)],
                dst_ref=landing.at[source],
                send_sem=send.at[base + owner],
                recv_sem=recv.at[base + source],
                device_id={"tensor": owner},
                device_id_type=MESH,
            )
            for out, landing, count, base in (
                (pairs_out, pairs_here, block, pair_slots[0]),
                (singles_out, singles_here, half_block, single_slots[0]),
            )
        ]

    def complete(owner):
        rows, half_block = rows_of(owner), block // 2
        parts = []
        for head in range(heads):
            total = sums[head, rows, HEAD_DIM : HEAD_DIM + 1]
            parts.append(sums[head, rows, :] / total)
            high, middle_part, low = split_three(-(peaks[head, rows, :] + jnp.log(total)))
            kept = queries[head, rows, :].astype(f32)
            for at, value in enumerate((high, middle_part, low)):
                kept = jnp.where(v_lane == HEAD_DIM + 8 + at, value.astype(f32), kept)
            queries[head, rows, :] = kept.astype(bf16)
        pair = join_lanes(parts[0], parts[1]).astype(bf16)
        single = join_lanes(parts[2][:half_block], parts[2][half_block:]).astype(bf16)
        pairs_out[rows, :] = pair
        singles_out[rows_of(owner, half_block), :] = single
        store(1, owner).start()

        @pl.when(owner == here)
        def _():
            pairs_here[here] = pair
            singles_here[here] = single

        @pl.when(owner != here)
        def _():
            for copy in exchange(owner, here):
                copy.start()

    def attend_known(time):
        def each(at, carry):
            owner = lax.rem(here + shards // 2 + at, shards)

            def other_block(other, carry):
                near = jnp.maximum(owner - other, other - owner) <= reach
                known = jnp.maximum(jnp.maximum(away(owner), away(other)), 1)

                @pl.when(near & (known == time))
                def _():
                    visit(owner, other)

                return carry

            lax.fori_loop(0, shards, other_block, 0)
            final = jnp.maximum(
                away(jnp.maximum(owner - reach, 0)), away(jnp.minimum(owner + reach, last))
            )

            @pl.when(final == time)
            def _():
                complete(owner)

            return carry

        lax.fori_loop(0, shards, each, 0)

    project_block(tokens_ref[...], here)
    for time in range(1, shards):
        hop("w", time, "t")

    half = shards // 2
    stores = []
    for owner in range(shards):
        at = 2 + owner

        @pl.when(here == owner)
        def _():
            pltpu.make_async_copy(own, weights_out.at[own_piece, owner], local.at[at]).start()

        @pl.when(here != owner)
        def _():
            pltpu.make_async_copy(chain.at[owner], weights_out.at[own_piece, owner], local.at[at]).start()

        stores.append(pltpu.make_async_copy(own, weights_out.at[own_piece, owner], local.at[at]))
    for saved in stores:
        saved.wait()

    def part(low, pieces):
        owners = pl.ds(0, half) if low else pl.ds(half, shards - half)
        return weights_out.at[pieces, owners]

    def gather_stage(low, pieces, bit):
        return [start_dp(part(low, at), part(low, at), bit) for at in pieces]

    def wait_all(copies):
        for copy in copies:
            copy.wait_recv()

    stage = gather_stage(True, [own_piece], 2) + gather_stage(False, [own_piece], 1)

    def arrived(time):
        def each(at, carry):
            owner = here + (2 * at - 1) * time

            @pl.when((owner >= 0) & (owner <= last))
            def _():
                project_block(blocks[owner], owner)

            return carry

        lax.fori_loop(0, 2, each, 0)

    for time in range(1, shards):
        hop("t", time)
        arrived(time)
        if time == 1:
            wait_all(stage)
            stage = gather_stage(True, [pl.ds(core * 4 + x_bit * 2, 2)], 1) + gather_stage(
                False, [core * 4 + 2 * at + y_bit for at in range(2)], 2
            )
        attend_known(time)
        if time == 2:
            wait_all(stage)
            stage = [start_dp(weights_out.at[pl.ds(core * 4, 4)], weights_out.at[pl.ds(core * 4, 4)], 0)]
    for owner in range(shards):

        @pl.when(here != owner)
        def _():
            for copy in exchange(here, owner):
                copy.wait_recv()
            for copy in exchange(owner, here):
                copy.wait_send()

        for which in range(4):
            store(which, owner).wait()
    wait_all(stage)
    wait_all(bias_copies)
    for copy in pending:
        copy.wait_send()
    for name in chains:
        for at in range(shards):
            for owner in range(shards):
                if owner <= at < last:

                    @pl.when(here == at)
                    def _():
                        hop_copy(name, owner, True, False).wait_send()

                if owner >= at > 0:

                    @pl.when(here == at)
                    def _():
                        hop_copy(name, owner, False, False).wait_send()


def start(shards, members, tokens, ids, gain, shift, qkv, qv_bias, fc1, fc2, proj, fc1_bias):
    dp_bits = members.bit_length() - 1
    assert members == 1 << dp_bits and dp_bits >= PIECE_BITS and shards >= 3
    f32, bf16 = jnp.float32, jnp.bfloat16
    block, width = tokens.shape
    seq_len = block * shards
    heads = qkv.shape[1] // HEAD_DIM
    rows = -(-(fc1.shape[0] + fc2.shape[0] + proj.shape[0]) // PIECES // 16) * 16
    copies = 6 * shards + (shards - 1) + 6
    vm = pltpu.VMEM
    on_chip = pl.BlockSpec(memory_space=vm)
    anywhere = pl.BlockSpec(memory_space=pl.ANY)
    head_rows = jax.ShapeDtypeStruct((heads, seq_len, LANES), bf16)
    return pl.pallas_call(
        partial(start_kernel, shards, dp_bits),
        in_specs=[on_chip] * 6 + [anywhere] * 2 + [on_chip] * 2,
        out_specs=[anywhere] * 4
        + [on_chip] * 4
        + [anywhere, on_chip],
        out_shape=[
            jax.ShapeDtypeStruct((seq_len, width), bf16),
            head_rows,
            head_rows,
            head_rows,
            jax.ShapeDtypeStruct((seq_len, LANES), bf16),
            jax.ShapeDtypeStruct((seq_len // 2, LANES), bf16),
            jax.ShapeDtypeStruct((shards, block, LANES), bf16),
            jax.ShapeDtypeStruct((shards, block // 2, LANES), bf16),
            jax.ShapeDtypeStruct((PIECES, shards, rows, width), bf16),
            jax.ShapeDtypeStruct((shards, 1, width), f32),
        ],
        scratch_shapes=[
            vm((shards, block, width), bf16),
            vm((seq_len, width), bf16),
            vm((heads, seq_len, LANES), bf16),
            vm((heads, seq_len, LANES), bf16),
            vm((heads, seq_len, LANES), bf16),
            vm((heads, seq_len, LANES), f32),
            vm((heads, seq_len, LANES), f32),
            vm((heads, block, block), f32),
            vm((heads, block, block), bf16),
            vm((seq_len, LANES), bf16),
            vm((seq_len, LANES), bf16),
            vm((rows, width), bf16),
            vm((shards, rows, width), bf16),
            pltpu.SemaphoreType.DMA((copies,)),
            pltpu.SemaphoreType.DMA((copies,)),
            pltpu.SemaphoreType.DMA((2 + shards,)),
            pltpu.SemaphoreType.DMA((4, shards)),
        ],
        compiler_params=pltpu.CompilerParams(
            collective_id=0, has_side_effects=True, vmem_limit_bytes=62 * 1024 * 1024
        ),
        name="start",
        cost_estimate=pl.CostEstimate(
            flops=6 * seq_len * width * heads * HEAD_DIM, transcendentals=0, bytes_accessed=40 * block * width
        ),
    )(tokens, ids, gain, shift, qkv, qv_bias, fc1, fc2, proj, fc1_bias)


CHUNK = 32


def middle_kernel(
    shards,
    dp_bits,
    pairs,
    singles,
    weights_ref,
    fc1_bias_ref,
    proj_bias_ref,
    scale_one_ref,
    gain_ref,
    shift_ref,
    fc2_bias_ref,
    scale_two_ref,
    tokens_ref,
    cotangent_ref,
    block_out,
    hidden_grad_out,
    pair_grads_out,
    single_grads_out,
    vectors_out,
    a_keep,
    a_away,
    b_keep,
    b_away,
    a_early,
    a_early_away,
    b_early,
    b_early_away,
    weights,
    attended,
    proj,
    branch,
    hidden,
    normed,
    wide,
    total,
    active,
    slope,
    grad_pre,
    grad_mlp,
    grad_branch,
    pair_grads,
    single_grads,
    got_early,
    got,
    a_got,
    b_got,
    send,
    recv,
    local,
):
    f32, bf16 = jnp.float32, jnp.bfloat16
    member, here = lax.axis_index("dp"), lax.axis_index("tensor")
    core, x_bit, y_bit = bit_of(member, 0), bit_of(member, 1), bit_of(member, 2)
    block, width = tokens_ref.shape
    columns = width // shards
    half = PIECES // 2
    fc_rows, proj_rows = width // PIECES, columns // PIECES
    proj_first = 2 * fc_rows
    slots = iter(range(send.shape[0]))
    proj_bias, scale_one, gain, shift, fc2_bias, scale_two = (
        ref[...].reshape(1, width)
        for ref in (proj_bias_ref, scale_one_ref, gain_ref, shift_ref, fc2_bias_ref, scale_two_ref)
    )

    def copy_to(src, dst, at, **peer):
        return pltpu.make_async_remote_copy(
            src_ref=src, dst_ref=dst, send_sem=send.at[at], recv_sem=recv.at[at], device_id=peer, device_id_type=MESH
        )

    loads = []
    for owner in range(shards):
        load = pltpu.make_async_copy(weights_ref.at[:, owner], weights.at[:, owner], local.at[owner])
        load.start()
        loads.append(load)
    greet(dp_bits, shards)

    for load in loads:
        load.wait()

    def fc1_of(owner):
        return weights[:, owner, fc_rows:proj_first, :].reshape(width, width)

    def fc2_of(owner):
        return weights[:, owner, :fc_rows, :].reshape(width, width)

    def proj_of(owner):
        return weights[:, owner, proj_first : proj_first + proj_rows, :].reshape(columns, width)

    def chunk(at):
        return pl.ds(pl.multiple_of(at * CHUNK, CHUNK), CHUNK)

    def each_chunk(body, init):
        return lax.fori_loop(0, block // CHUNK, body, init)

    def column_sum(value):
        return jnp.sum(value, axis=0, keepdims=True)

    def unit_of(value):
        centred = value - jnp.mean(value, axis=1, keepdims=True)
        inverse = lax.rsqrt(jnp.mean(centred * centred, axis=1, keepdims=True) + eps_norm)
        return centred * inverse, inverse

    third = shards * LANES
    for owner in range(shards):
        own_proj = proj_of(owner)
        proj[owner * LANES : (owner + 1) * LANES, :] = own_proj[:LANES]
        proj[third + owner * HEAD_DIM : third + (owner + 1) * HEAD_DIM, :] = own_proj[LANES:]
    middle_row = block // 2
    for owner in range(shards):
        attended[:, owner * LANES : (owner + 1) * LANES] = pairs[owner]
    lane = lax.broadcasted_iota(jnp.int32, (middle_row, LANES), 1)
    low_half = lane < HEAD_DIM

    def swapped(value):
        return pltpu.roll(value, HEAD_DIM, 1)

    for at in range(shards // 2):
        one, two = singles[2 * at].astype(f32), singles[2 * at + 1].astype(f32)
        columns_here = slice(third + at * LANES, third + (at + 1) * LANES)
        attended[:middle_row, columns_here] = jnp.where(low_half, one, swapped(two)).astype(bf16)
        attended[middle_row:, columns_here] = jnp.where(low_half, swapped(one), two).astype(bf16)
    product = jnp.dot(attended[...], proj[...], preferred_element_type=f32)
    branch[...] = product

    def enter(at, carry):
        rows = chunk(at)
        value = branch[rows, :] + proj_bias
        branch[rows, :] = value
        value = tokens_ref[rows, :].astype(f32) + scale_one * value
        hidden[rows, :] = value
        unit, _ = unit_of(value)
        normed[rows, :] = (unit * gain + shift).astype(bf16)
        return carry

    each_chunk(enter, 0)

    def forward(owner, carry):
        wide[:block, :] = jnp.dot(normed[...], fc1_of(owner), preferred_element_type=f32)
        bias = fc1_bias_ref[owner]

        def activate(at, carry):
            rows = chunk(at)
            value = wide[rows, :] + bias
            below = 0.5 * (1.0 + lax.erf(value * 0.5**0.5))
            active[owner, rows, :] = (value * below).astype(bf16)
            density = jnp.exp(value * value * -0.5) * (0.5 / math.pi) ** 0.5
            slope[owner, rows, :] = below + value * density
            return carry

        each_chunk(activate, 0)
        product = jnp.dot(active[owner], fc2_of(owner), preferred_element_type=f32)
        total[...] = jnp.where(owner == 0, product, total[...] + product)
        return carry

    lax.fori_loop(0, shards, forward, 0)
    empty = jnp.zeros((1, width), f32)

    def turn(at, sums):
        rows = chunk(at)
        value = total[rows, :] + fc2_bias
        block_out[rows, :] = (hidden[rows, :] + scale_two * value).astype(bf16)
        grad = cotangent_ref[rows, :].astype(f32)
        grad_mlp[rows, :] = (grad * scale_two).astype(bf16)
        return (
            sums[0] + column_sum(grad * value),
            sums[1] + column_sum(grad_mlp[rows, :].astype(f32)),
        )

    scale_two_sum, fc2_bias_sum = each_chunk(turn, (empty, empty))

    split = shards // 2

    def slot_row():
        return [next(slots) for _ in range(shards)]

    early_slots, late_slots = slot_row(), slot_row()

    def core_copy(owner, early):
        rows = pl.ds(0, fc_rows) if early else pl.ds(fc_rows, weights.shape[2] - fc_rows)
        base = (early_slots if early else late_slots)[0]
        return pltpu.make_async_remote_copy(
            src_ref=weights.at[pl.ds((1 - core) * half, half), owner, rows],
            dst_ref=(got_early if early else got).at[:, owner],
            send_sem=send.at[base + owner],
            recv_sem=recv.at[base + owner],
            device_id={"dp": partner_of(member, 0)},
            device_id_type=MESH,
        )

    piece_rows = pl.ds(0, fc_rows)
    own = core * half
    side_slots = [next(slots) for _ in range(3)]

    def side_copies():
        first_half, second_half = pl.ds(0, split), pl.ds(split, shards - split)
        moves = [(weights.at[pl.ds(own + (1 - x_bit) * 2, 2), first_half, piece_rows], a_got, 1)]
        moves += [
            (weights.at[own + 2 * x + 1 - y_bit, second_half, piece_rows], b_got.at[x], 2) for x in range(2)
        ]
        return [
            copy_to(source, landing, side_slots[at], dp=partner_of(member, bit))
            for at, (source, landing, bit) in enumerate(moves)
        ]

    def grow_piece(piece, owner, other):
        weights[piece, owner, piece_rows, :] = rounded_sum(weights[piece, owner, piece_rows, :], other)

    def early_pairs():
        for owner in range(shards):
            core_copy(owner, True).wait_recv()

        def step(at, carry):
            piece, owner = at // shards, lax.rem(at, shards)
            grow_piece(own + piece, owner, got_early[piece, owner])
            return carry

        lax.fori_loop(0, half * shards, step, 0)
        for copy in side_copies():
            copy.start()

    def early_sides():
        for copy in side_copies():
            copy.wait_recv()
        for owner in range(split):
            for keep, away, side, got_side, y_side in (
                (a_early, a_early_away, x_bit, a_got, True),
                (b_early, b_early_away, y_bit, b_got, False),
            ):
                for out, at in ((keep, y_bit if y_side else x_bit), (away, 1 - (y_bit if y_side else x_bit))):
                    piece = own + (2 * side + at if y_side else 2 * at + side)
                    shard = owner if y_side else split + owner
                    out[owner] = rounded_sum(weights[piece, shard, piece_rows, :], got_side[at, owner])

    def backward(owner, carry):
        wide[:block, :] = times_transposed(grad_mlp[...], fc2_of(owner))

        def slopes(at, sums):
            rows = chunk(at)
            value = (wide[rows, :] * slope[owner, rows, :]).astype(bf16)
            grad_pre[owner, rows, :] = value
            return sums + column_sum(value.astype(f32))

        vectors_out[pl.ds(8 + owner, 1), :] = each_chunk(slopes, empty)
        product = times_transposed(grad_pre[owner], fc1_of(owner))
        total[...] = jnp.where(owner == 0, product, total[...] + product)
        return carry

    lax.fori_loop(0, shards, backward, 0)

    def leave(at, sums):
        rows = chunk(at)
        grad = total[rows, :]
        unit, inverse = unit_of(hidden[rows, :])
        scaled = grad * gain
        inner = (
            scaled
            - jnp.mean(scaled, axis=1, keepdims=True)
            - unit * jnp.mean(scaled * unit, axis=1, keepdims=True)
        )
        value = cotangent_ref[rows, :].astype(f32) + inverse * inner
        hidden_grad_out[rows, :] = value
        rounded = (value * scale_one).astype(bf16)
        grad_branch[rows, :] = rounded
        return (
            sums[0] + column_sum(grad * unit),
            sums[1] + column_sum(grad),
            sums[2] + column_sum(value * branch[rows, :]),
            sums[3] + column_sum(rounded.astype(f32)),
        )

    gain_sum, shift_sum, scale_one_sum, proj_bias_sum = each_chunk(leave, (empty,) * 4)
    for at, value in enumerate(
        (empty, empty, proj_bias_sum, scale_one_sum, gain_sum, shift_sum, fc2_bias_sum, scale_two_sum)
    ):
        vectors_out[at : at + 1, :] = value
    vectors_out[12:, :] = jnp.zeros((vectors_out.shape[0] - 12, width), f32)

    wide[:block, :] = times_transposed(grad_branch[...], proj[...])
    for owner in range(shards):
        pair_grads[owner] = wide[:block, owner * LANES : (owner + 1) * LANES].astype(bf16)
    for at in range(shards // 2):
        columns_here = slice(third + at * LANES, third + (at + 1) * LANES)
        upper, lower = wide[:middle_row, columns_here], wide[middle_row:block, columns_here]
        single_grads[2 * at] = jnp.where(low_half, upper, swapped(lower)).astype(bf16)
        single_grads[2 * at + 1] = jnp.where(low_half, swapped(upper), lower).astype(bf16)
    back = []
    for source, out in ((pair_grads, pair_grads_out), (single_grads, single_grads_out)):
        for way in range(1, shards):
            target = lax.rem(here + way, shards)
            copy = copy_to(source.at[target], out.at[here], next(slots), tensor=target)
            copy.start()
            back.append(copy)
        out[here] = source[here]

    def early_grads(owner, carry):
        product = contract_rows(active[owner], grad_mlp[...]).astype(bf16)
        weights[:, owner, :fc_rows, :] = product.reshape(PIECES, fc_rows, width)
        core_copy(owner, True).start()
        return carry

    lax.fori_loop(0, shards, early_grads, 0)
    wide[...] = contract_rows(attended[:, :], grad_branch[...])
    for owner in range(shards):
        for piece in range(PIECES):
            first, end = piece * proj_rows, (piece + 1) * proj_rows
            for low, high, start_row in ((0, LANES, owner * LANES), (LANES, columns, third + owner * HEAD_DIM)):
                begin, stop = max(first, low), min(end, high)
                if begin < stop:
                    rows = slice(start_row + begin - low, start_row + stop - low)
                    to = slice(proj_first + begin - first, proj_first + stop - first)
                    weights[piece, owner, to, :] = wide[rows, :].astype(bf16)

    early_pairs()

    def weight_grads(owner, carry):
        product = contract_rows(normed[...], grad_pre[owner]).astype(bf16)
        weights[:, owner, fc_rows:proj_first, :] = product.reshape(PIECES, fc_rows, width)
        core_copy(owner, False).start()
        return carry

    lax.fori_loop(0, shards, weight_grads, 0)
    for owner in range(shards):
        core_copy(owner, False).wait_recv()
        for x in range(2):
            for y in range(2):
                piece = x * 2 + y
                if owner < split:
                    moves = [(out, y, owner, at == x) for out, at in ((a_keep, x_bit), (a_away, 1 - x_bit))]
                else:
                    moves = [(out, x, owner - split, at == y) for out, at in ((b_keep, y_bit), (b_away, 1 - y_bit))]
                for out, first, second, wanted in moves:

                    @pl.when(wanted)
                    def _():
                        out[first, second] = rounded_sum(
                            weights[own + piece, owner, fc_rows:, :], got[piece, owner]
                        )

    early_sides()
    for copy in back:
        copy.wait_recv()
    for copy in back + side_copies():
        copy.wait_send()
    for owner in range(shards):
        core_copy(owner, True).wait_send()
        core_copy(owner, False).wait_send()


def middle(shards, members, pairs, singles, weights, fc1_bias, vectors, tokens, cotangent):
    dp_bits = members.bit_length() - 1
    f32, bf16 = jnp.float32, jnp.bfloat16
    block, width = tokens.shape
    rows = weights.shape[2]
    vm = pltpu.VMEM
    on_chip = pl.BlockSpec(memory_space=vm)
    fc_rows = width // PIECES
    quarter = jax.ShapeDtypeStruct((2, shards // 2, rows - fc_rows, width), bf16)
    early_half = jax.ShapeDtypeStruct((shards // 2, fc_rows, width), bf16)
    copies = 2 * (shards - 1) + 2 * shards + 3
    return pl.pallas_call(
        partial(middle_kernel, shards, dp_bits),
        in_specs=[on_chip, on_chip, pl.BlockSpec(memory_space=pl.ANY)] + [on_chip] * 9,
        out_specs=[on_chip] * 13,
        out_shape=[
            jax.ShapeDtypeStruct((block, width), bf16),
            jax.ShapeDtypeStruct((block, width), f32),
            jax.ShapeDtypeStruct((shards, block, LANES), bf16),
            jax.ShapeDtypeStruct((shards, block // 2, LANES), bf16),
            jax.ShapeDtypeStruct((16, width), f32),
            quarter,
            quarter,
            quarter,
            quarter,
            early_half,
            early_half,
            early_half,
            early_half,
        ],
        scratch_shapes=[
            vm(weights.shape, bf16),
            vm((block, width), bf16),
            vm((width, width), bf16),
            vm((block, width), f32),
            vm((block, width), f32),
            vm((block, width), bf16),
            vm((width, width), f32),
            vm((block, width), f32),
            vm((shards, block, width), bf16),
            vm((shards, block, width), f32),
            vm((shards, block, width), bf16),
            vm((block, width), bf16),
            vm((block, width), bf16),
            vm((shards, block, LANES), bf16),
            vm((shards, block // 2, LANES), bf16),
            vm((PIECES // 2, shards, fc_rows, width), bf16),
            vm((PIECES // 2, shards, rows - fc_rows, width), bf16),
            vm((2, shards // 2, fc_rows, width), bf16),
            vm((2, shards // 2, fc_rows, width), bf16),
            pltpu.SemaphoreType.DMA((copies,)),
            pltpu.SemaphoreType.DMA((copies,)),
            pltpu.SemaphoreType.DMA((shards,)),
        ],
        compiler_params=pltpu.CompilerParams(
            collective_id=2, has_side_effects=True, vmem_limit_bytes=62 * 1024 * 1024
        ),
        name="middle",
        cost_estimate=pl.CostEstimate(
            flops=12 * block * width * width * shards, transcendentals=0, bytes_accessed=40 * block * width
        ),
    )(pairs, singles, weights, fc1_bias, *vectors, tokens, cotangent)


eps_norm = 1e-06


def on_device(
    shards,
    members,
    tokens,
    segment_ids,
    ln1_gain,
    ln1_bias,
    qkv_weight,
    qv_bias,
    proj_weight,
    proj_bias,
    scale_one,
    ln2_gain,
    ln2_bias,
    fc1_weight,
    fc1_bias,
    fc2_weight,
    fc2_bias,
    scale_two,
    cotangent,
):
    f32, bf16 = jnp.float32, jnp.bfloat16
    seq_len = segment_ids.shape[1]
    rows_here, width = tokens.shape
    head_columns = qkv_weight.shape[2]
    heads = head_columns // HEAD_DIM
    hidden_here = fc1_weight.shape[1]
    ids = segment_ids[0]
    here = lax.axis_index("tensor")

    turned = qkv_weight.transpose(0, 2, 1)
    full_one, queries, keys, values, pairs, singles, pairs_here, singles_here, gathered, fc1_bias_full = start(
        shards,
        members,
        tokens,
        segment_ids,
        ln1_gain,
        ln1_bias,
        turned,
        qv_bias,
        fc1_weight,
        fc2_weight,
        proj_weight,
        fc1_bias,
    )
    params = (proj_bias, scale_one, ln2_gain, ln2_bias, fc2_bias, scale_two)
    block_out, grad_hidden, pair_grads, single_grads, vectors, *exchanged = middle(
        shards, members, pairs_here, singles_here, gathered, fc1_bias_full, params, tokens, cotangent
    )
    pair_grads = pair_grads.reshape(seq_len, LANES)
    single_grads = single_grads.reshape(seq_len // 2, LANES)

    grad_tokens, totals, qkv_pieces, weight_pieces = back(
        shards,
        members,
        (queries, keys, values),
        (pairs, singles, pair_grads, single_grads),
        turned.reshape(3 * head_columns, width),
        ln1_gain,
        ln1_bias,
        vectors,
        full_one,
        tokens,
        grad_hidden,
        exchanged,
    )
    fc1_grad, fc2_grad, proj_grad, qkv_grad, fc1_bias_grad, *sums = unpack(
        qkv_pieces, weight_pieces, totals, width // PIECES, head_columns // PIECES
    )
    qkv_grad = qkv_grad.reshape(3, head_columns, width).transpose(0, 2, 1)
    qv_sums = lax.dynamic_index_in_dim(totals, 12 + here, 0, keepdims=False)
    qv_grad = jnp.stack([qv_sums[:head_columns], qv_sums[2 * head_columns : 3 * head_columns]])
    return (
        block_out,
        grad_tokens,
        sums[0],
        sums[1],
        qkv_grad,
        qv_grad,
        proj_grad,
        sums[2],
        sums[3],
        sums[4],
        sums[5],
        fc1_grad,
        fc1_bias_grad,
        fc2_grad,
        sums[6],
        sums[7],
    )


def solution(mesh):
    rows = P(("dp", "tensor"), None)
    columns = P(None, "tensor")
    return jax.shard_map(
        partial(on_device, mesh.shape["tensor"], mesh.shape["dp"]),
        mesh=mesh,
        in_specs=(
            rows,
            P("dp", None),
            P(),
            P(),
            P(None, None, "tensor"),
            columns,
            P("tensor", None),
            P(),
            P(),
            P(),
            P(),
            columns,
            P("tensor"),
            P("tensor", None),
            P(),
            P(),
            rows,
        ),
        out_specs=(
            rows,
            rows,
            P(),
            P(),
            P(None, None, "tensor"),
            columns,
            P("tensor", None),
            P(),
            P(),
            P(),
            P(),
            columns,
            P("tensor"),
            P("tensor", None),
            P(),
            P(),
        ),
        check_vma=False,
    )
```

```python
from functools import partial
import math

import jax, jax.numpy as jnp
from jax import lax
from jax.experimental import pallas as pl
from jax.experimental.pallas import tpu as pltpu

from jax.sharding import PartitionSpec as P

HEAD_DIM = 64
LANES = 128
MOST_TOKENS = 1152
MASKED = -(2.0**100)


def contract_rows(left, right):
    return lax.dot_general(left, right, (((0,), (0,)), ((), ())), preferred_element_type=jnp.float32)


def times_transposed(left, right, precision=None):
    return lax.dot_general(
        left, right, (((1,), (1,)), ((), ())), preferred_element_type=jnp.float32, precision=precision
    )


def split_three(value):
    high = value.astype(jnp.bfloat16)
    rest = value - high.astype(jnp.float32)
    middle = rest.astype(jnp.bfloat16)
    low = (rest - middle.astype(jnp.float32)).astype(jnp.bfloat16)
    return (high, middle, low)


def join_lanes(low, high):
    lane = lax.broadcasted_iota(jnp.int32, low.shape, 1)
    return jnp.where(lane < HEAD_DIM, low, pltpu.roll(high, HEAD_DIM, 1))


MESH = pl.DeviceIdType.MESH
PIECES = 8
PIECE_BITS = 3


def rounded_sum(left, right):
    return (left.astype(jnp.float32) + right.astype(jnp.float32)).astype(jnp.bfloat16)


def bit_of(index, bit):
    return lax.rem(index // (1 << bit), 2)


def partner_of(index, bit):
    return index + (1 - 2 * bit_of(index, bit)) * (1 << bit)


def greet(dp_bits, shards, ahead=None):
    barrier = pltpu.get_barrier_semaphore()
    member, here = lax.axis_index("dp"), lax.axis_index("tensor")
    peers = [{"dp": partner_of(member, bit)} for bit in range(dp_bits)]
    peers += [{"tensor": lax.rem(here + way, shards)} for way in range(1, shards)]
    for peer in peers:
        pl.semaphore_signal(barrier, inc=1, device_id=peer, device_id_type=MESH)
    if ahead is not None:
        ahead()
    pl.semaphore_wait(barrier, len(peers))


def back_kernel(
    shards,
    dp_bits,
    q_ref,
    k_ref,
    v_ref,
    pair_ref,
    single_ref,
    pair_grad_ref,
    single_grad_ref,
    weight_ref,
    gain_ref,
    shift_ref,
    vectors_ref,
    rows_ref,
    tokens_ref,
    hidden_ref,
    a_keep,
    a_away,
    b_keep,
    b_away,
    a_early,
    a_early_away,
    b_early,
    b_early_away,
    tokens_out,
    vectors_out,
    qkv_out,
    weights_out,
    grad_heads,
    dq,
    dk,
    dv,
    probs,
    grad_scores,
    packed,
    rows_own,
    tokens_own,
    hidden_own,
    part,
    arrived,
    q_wide,
    column_sums,
    q_all,
    q_half,
    q_quarter,
    q_got_core,
    q_got_x,
    q_got_y,
    q_got_more,
    v_now,
    v_got,
    v_shards,
    a_sum,
    b_sum,
    a_got,
    b_got,
    a_second,
    b_second,
    pieces,
    early_own,
    pieces_more,
    early_more,
    z_got,
    early_got,
    early_side,
    send,
    recv,
    local,
):
    f32, bf16 = jnp.float32, jnp.bfloat16
    member, here = lax.axis_index("dp"), lax.axis_index("tensor")
    core, x_bit, y_bit = bit_of(member, 0), bit_of(member, 1), bit_of(member, 2)
    own_piece = core * 4 + x_bit * 2 + y_bit
    block, width = part.shape[1], part.shape[2]
    heads = q_ref.shape[0]
    columns = weight_ref.shape[0]
    half_rows = weights_out.shape[1] // 2
    last = shards - 1
    reach = -(-(MOST_TOKENS - 1) // block)
    gain, shift = (ref[...].reshape(1, width) for ref in (gain_ref, shift_ref))
    slots = iter(range(send.shape[0]))
    pending = []

    def copy_to(src, dst, at, **peer):
        return pltpu.make_async_remote_copy(
            src_ref=src, dst_ref=dst, send_sem=send.at[at], recv_sem=recv.at[at], device_id=peer, device_id_type=MESH
        )

    def start_dp(src, dst, bit, keep=True):
        copy = copy_to(src, dst, next(slots), dp=partner_of(member, bit))
        copy.start()
        if keep:
            pending.append(copy)
        return copy

    def load(at):
        source, landing = (
            (a_keep, a_sum),
            (b_keep, b_sum),
            (tokens_ref, tokens_own),
            (hidden_ref, hidden_own),
            (a_early, early_own.at[pl.ds(0, shards // 2)]),
            (b_early, early_own.at[pl.ds(shards // 2, shards // 2)]),
        )[at]
        return pltpu.make_async_copy(source, landing, local.at[at])

    def load_rows(owner):
        rows = pl.ds(pl.multiple_of(owner * block, 16), block)
        return pltpu.make_async_copy(rows_ref.at[rows], rows_own, local.at[6])

    for at in range(6):
        load(at).start()
    flipped = here >= shards // 2

    def mirrored(owner):
        return jnp.where(flipped, last - owner, owner)

    load_rows(mirrored(last)).start()
    def set_up():
        dq[...] = jnp.zeros_like(dq)
        dk[...] = jnp.zeros_like(dk)
        dv[...] = jnp.zeros_like(dv)
        q_wide[...] = jnp.zeros_like(q_wide)
        column_sums[...] = jnp.zeros_like(column_sums)
        source = lax.broadcasted_iota(jnp.int32, (LANES, LANES), 0)
        target = lax.broadcasted_iota(jnp.int32, (LANES, LANES), 1)
        gathers = (target >= HEAD_DIM) & (target < HEAD_DIM + 3)
        picks = []
        for odd in range(2):
            inside = (source >= HEAD_DIM * odd) & (source < HEAD_DIM * (odd + 1))
            summing = jnp.where(inside & gathers, -1.0, 0.0).astype(bf16)
            moving = jnp.where(inside & (source - HEAD_DIM * odd == target), 1.0, 0.0).astype(bf16)
            picks.append((summing, moving))
        half = block // 2
        lane = lax.broadcasted_iota(jnp.int32, (half, LANES), 1)

        def prepare(at, carry):
            for side in range(2):
                rows = pl.ds(pl.multiple_of((2 * at + side) * half, half), half)
                single_rows = pl.ds(pl.multiple_of(at * half, half), half)
                for head, odd, mixed, grad in (
                    (0, 0, pair_ref[rows, :], pair_grad_ref[rows, :]),
                    (1, 1, pair_ref[rows, :], pair_grad_ref[rows, :]),
                    (2, side, single_ref[single_rows, :], single_grad_ref[single_rows, :]),
                ):
                    summing, moving = picks[odd]
                    product = grad.astype(f32) * mixed.astype(f32)
                    high = product.astype(bf16)
                    low = (product - high.astype(f32)).astype(bf16)
                    shared = jnp.dot(high, summing, preferred_element_type=f32) + jnp.dot(
                        low, summing, preferred_element_type=f32
                    )
                    moved = jnp.dot(grad, moving, preferred_element_type=f32)
                    for place, value in enumerate(split_three(shared)):
                        moved = jnp.where(lane == HEAD_DIM + place, value.astype(f32), moved)
                    grad_heads[head, rows, :] = moved.astype(bf16)
            return carry

        lax.fori_loop(0, shards, prepare, 0)

    greet(dp_bits, shards, set_up)
    start_dp(a_early_away, early_side.at[pl.ds(0, shards // 2)], 2)
    start_dp(b_early_away, early_side.at[pl.ds(shards // 2, shards // 2)], 1)
    early_sides = pending[-2:]
    start_dp(a_away, a_got, 1)
    start_dp(b_away, b_got, 2)
    first_a, first_b = pending[-2:]
    second_slots = [next(slots) for _ in range(2)]

    def second(at):
        if at:
            return copy_to(b_sum.at[1 - x_bit], b_second, second_slots[1], dp=partner_of(member, 1))
        return copy_to(a_sum.at[1 - y_bit], a_second, second_slots[0], dp=partner_of(member, 2))

    z_slots = [[next(slots) for _ in range(1, shards)] for _ in range(2)]

    def piece_copy(way, first=False):
        target = lax.rem(here + way, shards)
        source, landing = (early_own, early_got) if first else (pieces, z_got)
        return copy_to(source.at[target], landing.at[way - 1], z_slots[first][way - 1], tensor=target)

    more_slots = [[next(slots) for _ in range(PIECE_BITS, dp_bits)] for _ in range(2)]

    def send_pieces(first):
        source, landing = (early_own, early_more) if first else (pieces, pieces_more)
        for bit in range(PIECE_BITS, dp_bits):
            at = bit - PIECE_BITS
            extra = copy_to(source, landing.at[at], more_slots[first][at], dp=partner_of(member, bit))
            extra.start()
            extra.wait_recv()
            extra.wait_send()

            def step(owner, carry):
                source[owner] = rounded_sum(source[owner], landing[at, owner])
                return carry

            lax.fori_loop(0, shards, step, 0)
        for way in range(1, shards):
            piece_copy(way, first).start()

    def early_exchange():
        for at, copy in enumerate(early_sides):
            load(4 + at).wait()
            copy.wait_recv()
        for owner in range(shards):
            early_own[owner] = rounded_sum(early_own[owner], early_side[owner])
        send_pieces(True)


    def sum_pairs(out, right):
        def step(at, carry):
            one, two = at // out.shape[1], lax.rem(at, out.shape[1])
            out[one, two] = rounded_sum(out[one, two], right[one, two])
            return carry

        lax.fori_loop(0, out.shape[0] * out.shape[1], step, 0)

    def second_exchange():
        first_a.wait_recv()
        first_b.wait_recv()
        load(0).wait()
        load(1).wait()
        sum_pairs(a_sum, a_got)
        sum_pairs(b_sum, b_got)
        second(0).start()
        second(1).start()

    def shard_exchange():
        second(0).wait_recv()
        second(1).wait_recv()
        split = shards // 2
        for at in range(split):
            pieces[at] = rounded_sum(a_sum[y_bit, at], a_second[at])
            pieces[split + at] = rounded_sum(b_sum[x_bit, at], b_second[at])
        send_pieces(False)

    split_row = early_own.shape[1]
    gather_slots = [[next(slots) for _ in range(count)] for count in (2, 3, 1)]

    def gather_copies(stage):
        first_rows, other_rows = pl.ds(0, half_rows), pl.ds(half_rows, half_rows)
        if stage == 0:
            moves = [(own_piece, first_rows, 2), (own_piece, other_rows, 1)]
        elif stage == 1:
            moves = [(pl.ds(core * 4 + x_bit * 2, 2), first_rows, 1)]
            moves += [(core * 4 + 2 * at + y_bit, other_rows, 2) for at in range(2)]
        else:
            moves = [(pl.ds(core * 4, 4), pl.ds(0, 2 * half_rows), 0)]
        return [
            copy_to(
                weights_out.at[piece, rows],
                weights_out.at[piece, rows],
                gather_slots[stage][at],
                dp=partner_of(member, bit),
            )
            for at, (piece, rows, bit) in enumerate(moves)
        ]

    def gather_start(stage):
        for copy in gather_copies(stage):
            copy.start()

    def gather_wait(stage):
        for copy in gather_copies(stage):
            copy.wait_recv()

    def sum_shards():
        for first, source, landing, rows in (
            (True, early_own, early_got, slice(0, split_row)),
            (False, pieces, z_got, slice(split_row, 2 * half_rows)),
        ):
            for way in range(1, shards):
                piece_copy(way, first).wait_recv()
            total = source[here].astype(f32)
            for way in range(1, shards):
                total = total + landing[way - 1].astype(f32)
            weights_out[own_piece, rows, :] = total.astype(bf16)
        gather_start(0)

    right_slots = [next(slots) for _ in range(shards)]
    left_slots = [next(slots) for _ in range(shards)]

    def to_right(owner):
        return copy_to(part.at[owner], arrived.at[owner], right_slots[0] + owner, tensor=lax.rem(here + 1, shards))

    def to_left(owner, target=None):
        to = lax.rem(here + last, shards) if target is None else target
        landing = jnp.where(owner == to, shards, owner)
        return copy_to(
            part.at[owner], arrived.at[landing], left_slots[0] + owner, tensor=lax.rem(here + last, shards)
        )

    def add_arrived(owner, landing):
        def step(at, carry):
            rows = pl.ds(pl.multiple_of(at * (block // 4), 16), block // 4)
            part[owner, rows, :] = rounded_sum(part[owner, rows, :], arrived[landing, rows, :])
            return carry

        lax.fori_loop(0, 4, step, 0)

    def hop(moved, nth, rightward):
        owner, at = (last - nth, moved) if rightward else (nth, last - moved)
        if (at < owner) if rightward else (at > owner):

            @pl.when(here == at)
            def _():
                copy = to_right(owner) if rightward else to_left(owner)
                copy.wait_recv()
                add_arrived(owner, owner)
                copy.start()

    def rows_of(owner):
        return pl.ds(pl.multiple_of(owner * block, 16), block)

    def visit(owner, other):
        key_rows, query_rows = rows_of(owner), rows_of(other)
        for head in range(heads):
            prob = jnp.exp(times_transposed(k_ref[head, key_rows, :], q_ref[head, query_rows, :]))
            grad_prob = times_transposed(v_ref[head, key_rows, :], grad_heads[head, query_rows, :])
            probs[head] = prob.astype(bf16)
            grad_scores[head] = (prob * grad_prob).astype(bf16)
        for head in range(heads):
            dv[head, key_rows, :] += jnp.dot(
                probs[head], grad_heads[head, query_rows, :], preferred_element_type=f32
            )
            dk[head, key_rows, :] += jnp.dot(
                grad_scores[head], q_ref[head, query_rows, :], preferred_element_type=f32
            )
            dq[head, query_rows, :] += contract_rows(grad_scores[head], k_ref[head, key_rows, :])

    def close_block(owner, following):
        rows = rows_of(owner)
        scale = HEAD_DIM**-0.5
        for first, low, high in (
            (0, dq[0, rows, :] * scale, dq[1, rows, :] * scale),
            (1, dq[2, rows, :] * scale, dk[0, rows, :]),
            (2, dk[1, rows, :], dk[2, rows, :]),
            (3, dv[0, rows, :], dv[1, rows, :]),
        ):
            packed[:, first * LANES : (first + 1) * LANES] = join_lanes(low, high).astype(bf16)
        packed[:, 4 * LANES : columns] = dv[2, rows, :HEAD_DIM].astype(bf16)
        part[owner] = jnp.dot(packed[...], weight_ref[...], preferred_element_type=f32).astype(bf16)

        @pl.when((owner > 1) & (here == 0))
        def _():
            to_right(owner).start()

        @pl.when((owner < last - 1) & (here == last))
        def _():
            to_left(owner).start()

        load_rows(owner).wait()
        q_wide[...] += contract_rows(packed[...], rows_own[...])
        column_sums[...] += jnp.dot(jnp.ones((8, block), bf16), packed[...], preferred_element_type=f32)

        @pl.when(following >= 0)
        def _():
            load_rows(following).start()

    order = []
    for near in range((shards + 1) // 2):
        for owner in (last - near, near):
            if owner not in order:
                order.append(owner)
    visits, closing = [], []
    for at, owner in enumerate(order):
        rest = order[at:]
        both = [(owner, owner)]
        for other in rest[1:]:
            if abs(owner - other) <= reach:
                both += [(owner, other), (other, owner)]
        visits += both
        closing.append(len(visits) - 1)
    total_visits = len(visits)

    def lookup(table, at):
        value = 0
        for place, entry in enumerate(table):
            value = value + jnp.where(at == place, entry, 0)
        return value

    closed = [order[closing.index(at)] if at in closing else -1 for at in range(total_visits)]
    later = [
        order[closing.index(at) + 1] if at in closing and at != closing[-1] else -1 for at in range(total_visits)
    ]
    def first_hops():
        hop(1, 0, True)
        hop(1, 0, False)

    events = {
        1: early_exchange,
        closing[0] + 1: second_exchange,
        closing[0] + 4: shard_exchange,
        closing[1] + 1: first_hops,
        closing[-1]: sum_shards,
    }
    assert len(events) == 5 and shards >= 4

    def each_visit(at, carry):
        visit(*(mirrored(lookup([pair[side] for pair in visits], at)) for side in range(2)))
        for when, event in events.items():

            @pl.when(at == when)
            def _():
                event()

        @pl.when(lookup([int(owner >= 0) for owner in closed], at) == 1)
        def _():
            following = lookup(later, at)
            close_block(mirrored(lookup(closed, at)), jnp.where(following < 0, -1, mirrored(following)))

        return carry

    lax.fori_loop(0, total_visits, each_visit, 0)
    def end_sends(nths):
        for nth in nths:

            @pl.when(here == 0)
            def _():
                to_right(last - nth).start()

            @pl.when(here == last)
            def _():
                to_left(nth).start()

    gather_wait(0)
    gather_start(1)

    sums = column_sums[...]
    weight = weight_ref[...].astype(f32)
    shift_sum = jnp.dot(sums, weight, preferred_element_type=f32, precision=lax.Precision.HIGHEST)[0:1]
    gain_sum = jnp.sum(weight * q_wide[...], axis=0, keepdims=True)
    v_now[0] = vectors_ref[...]
    v_now[0, 0:1, :] = (gain_sum - shift * shift_sum) / gain
    v_now[0, 1:2, :] = shift_sum
    v_now[0, pl.ds(12 + here, 1), 0:columns] = sums[0:1]
    count = q_all.shape[1]
    for piece in range(PIECES):
        q_all[piece] = q_wide[piece * count : (piece + 1) * count, :].astype(bf16)

    def vector_stage(bit):
        return start_dp(v_now.at[bit], v_got.at[bit], bit)

    q_core = start_dp(q_all.at[pl.ds((1 - core) * 4, 4)], q_got_core, 0)
    v_copy = vector_stage(0)
    q_core.wait_recv()
    for at in range(4):
        q_half[at] = rounded_sum(q_all[core * 4 + at], q_got_core[at])
    q_x = start_dp(q_half.at[pl.ds((1 - x_bit) * 2, 2)], q_got_x, 1)
    v_copy.wait_recv()
    v_now[1] = v_now[0] + v_got[0]
    v_copy = vector_stage(1)
    for moved in range(2, last):
        hop(moved, 0, True)
        hop(moved, 0, False)
    gather_wait(1)
    gather_start(2)
    q_x.wait_recv()
    for at in range(2):
        q_quarter[at] = rounded_sum(q_half[x_bit * 2 + at], q_got_x[at])
    q_y = start_dp(q_quarter.at[1 - y_bit], q_got_y, 2)
    v_copy.wait_recv()
    v_now[2] = v_now[1] + v_got[1]
    v_copy = vector_stage(2)
    q_y.wait_recv()
    qkv_out[own_piece] = rounded_sum(q_quarter[y_bit], q_got_y[...])
    v_copy.wait_recv()
    v_now[3] = v_now[2] + v_got[2]
    for bit in range(PIECE_BITS, dp_bits):
        extra = start_dp(qkv_out.at[own_piece], q_got_more.at[bit - PIECE_BITS], bit, False)
        v_copy = vector_stage(bit)
        extra.wait_recv()
        extra.wait_send()
        qkv_out[own_piece] = rounded_sum(qkv_out[own_piece], q_got_more[bit - PIECE_BITS])
        v_copy.wait_recv()
        v_now[bit + 1] = v_now[bit] + v_got[bit]
    q_back = start_dp(qkv_out.at[own_piece], qkv_out.at[own_piece], 2)
    v_shards[here] = v_now[dp_bits]
    for way in range(1, shards):
        copy = copy_to(
            v_now.at[dp_bits], v_shards.at[here], next(slots), tensor=lax.rem(here + way, shards)
        )
        copy.start()
        pending.append(copy)
    v_waits = pending[-last:]
    end_sends([last - 1])
    q_back.wait_recv()
    span = pl.ds(core * 4 + x_bit * 2, 2)
    q_back = start_dp(qkv_out.at[span], qkv_out.at[span], 1)
    for nth in range(1, last):
        for moved in range(1, last):
            hop(moved, nth, True)
            hop(moved, nth, False)
    q_back.wait_recv()
    span = pl.ds(core * 4, 4)
    q_back = start_dp(qkv_out.at[span], qkv_out.at[span], 0)
    gather_wait(2)
    for copy in v_waits:
        copy.wait_recv()
    vectors_sum = v_shards[0]
    for at in range(1, shards):
        vectors_sum = vectors_sum + v_shards[at]
    vectors_out[...] = vectors_sum

    for owner in range(shards):

        @pl.when(here == owner)
        def _():
            if owner > 0:
                to_right(owner).wait_recv()
                add_arrived(owner, owner)
            if owner < last:
                to_left(owner, owner).wait_recv()
                add_arrived(owner, shards)

    load(2).wait()
    load(3).wait()

    def close(at, carry):
        rows = pl.ds(pl.multiple_of(at * (block // 4), 16), block // 4)
        tokens = tokens_own[rows, :].astype(f32)
        centred = tokens - jnp.mean(tokens, axis=1, keepdims=True)
        inverse = lax.rsqrt(jnp.mean(centred * centred, axis=1, keepdims=True) + eps_norm)
        unit = centred * inverse
        scaled = part[here, rows, :].astype(f32) * gain
        inner = (
            scaled
            - jnp.mean(scaled, axis=1, keepdims=True)
            - unit * jnp.mean(scaled * unit, axis=1, keepdims=True)
        )
        tokens_out[rows, :] = hidden_own[rows, :] + inverse * inner
        return carry

    lax.fori_loop(0, 4, close, 0)
    q_back.wait_recv()
    for copy in pending:
        copy.wait_send()
    for at in range(2):
        second(at).wait_send()
    for stage in range(3):
        for copy in gather_copies(stage):
            copy.wait_send()
    for way in range(1, shards):
        piece_copy(way, True).wait_send()
        piece_copy(way).wait_send()
    for owner in range(shards):

        @pl.when(here < owner)
        def _():
            to_right(owner).wait_send()

        @pl.when(here > owner)
        def _():
            to_left(owner).wait_send()


def back(shards, members, heads_in, pair_in, weight, gain, shift, vectors, rows, tokens, grad_hidden, exchanged):
    dp_bits = members.bit_length() - 1
    assert members == 1 << dp_bits and dp_bits >= PIECE_BITS
    f32, bf16 = jnp.float32, jnp.bfloat16
    heads, seq_len, _ = heads_in[0].shape
    columns, width = weight.shape
    block = tokens.shape[0]
    quarter = exchanged[0].shape
    early_rows = exchanged[4].shape[1]
    late_rows = quarter[2]
    count = columns // PIECES
    more = max(1, dp_bits - PIECE_BITS)
    copies = 26 + 2 * shards + 3 * (shards - 1) + 5 * dp_bits
    vm = pltpu.VMEM
    return pl.pallas_call(
        partial(back_kernel, shards, dp_bits),
        in_specs=[pl.BlockSpec(memory_space=vm)] * 11 + [pl.BlockSpec(memory_space=pl.ANY)] * 11,
        out_specs=[pl.BlockSpec(memory_space=vm)] * 4,
        out_shape=[
            jax.ShapeDtypeStruct((block, width), f32),
            jax.ShapeDtypeStruct(vectors.shape, f32),
            jax.ShapeDtypeStruct((PIECES, count, width), bf16),
            jax.ShapeDtypeStruct((PIECES, early_rows + late_rows, width), bf16),
        ],
        scratch_shapes=[
            vm((heads, seq_len, LANES), bf16),
            vm((heads, seq_len, LANES), f32),
            vm((heads, seq_len, LANES), f32),
            vm((heads, seq_len, LANES), f32),
            vm((heads, block, block), bf16),
            vm((heads, block, block), bf16),
            vm((block, columns), bf16),
            vm((block, width), bf16),
            vm((block, width), bf16),
            vm((block, width), f32),
            vm((shards, block, width), bf16),
            vm((shards + 1, block, width), bf16),
            vm((columns, width), f32),
            vm((8, columns), f32),
            vm((PIECES, count, width), bf16),
            vm((4, count, width), bf16),
            vm((2, count, width), bf16),
            vm((4, count, width), bf16),
            vm((2, count, width), bf16),
            vm((count, width), bf16),
            vm((more, count, width), bf16),
            vm((dp_bits + 1,) + vectors.shape, f32),
            vm((dp_bits,) + vectors.shape, f32),
            vm((shards,) + vectors.shape, f32),
            vm(quarter, bf16),
            vm(quarter, bf16),
            vm(quarter, bf16),
            vm(quarter, bf16),
            vm(quarter[1:], bf16),
            vm(quarter[1:], bf16),
            vm((shards, late_rows, width), bf16),
            vm((shards, early_rows, width), bf16),
            vm((more, shards, late_rows, width), bf16),
            vm((more, shards, early_rows, width), bf16),
            vm((shards - 1, late_rows, width), bf16),
            vm((shards - 1, early_rows, width), bf16),
            vm((shards, early_rows, width), bf16),
            pltpu.SemaphoreType.DMA((copies,)),
            pltpu.SemaphoreType.DMA((copies,)),
            pltpu.SemaphoreType.DMA((7,)),
        ],
        compiler_params=pltpu.CompilerParams(
            collective_id=1, has_side_effects=True, vmem_limit_bytes=67043328
        ),
        name="back",
        cost_estimate=pl.CostEstimate(
            flops=10 * heads * seq_len * seq_len * LANES, transcendentals=0, bytes_accessed=40 * block * width
        ),
    )(*heads_in, *pair_in, weight, gain, shift, vectors, rows, tokens, grad_hidden, *exchanged)


def unpack_kernel(
    qkv_ref,
    weights_ref,
    totals_ref,
    tokens_ref,
    rows_ref,
    fc1_out,
    fc2_out,
    proj_out,
    qkv_out,
    tokens_out,
    rows_out,
    qv_out,
    fc1_bias_out,
    *vector_outs
):
    fc_rows, proj_rows = fc1_out.shape[0], proj_out.shape[0]
    fc2_out[...] = weights_ref[0, :fc_rows].astype(jnp.float32)
    fc1_out[...] = weights_ref[0, fc_rows : 2 * fc_rows].astype(jnp.float32)
    proj_out[...] = weights_ref[0, 2 * fc_rows : 2 * fc_rows + proj_rows].astype(jnp.float32)
    qkv_out[...] = qkv_ref[0].astype(jnp.float32)
    tokens_out[...] = tokens_ref[...]
    rows_out[...] = rows_ref[...]

    @pl.when(pl.program_id(0) == 0)
    def _():
        width = totals_ref.shape[1]
        for at, out in enumerate(vector_outs):
            out[...] = totals_ref[at : at + 1, :].reshape(width)
        here = lax.axis_index("tensor")
        fc1_bias_out[...] = totals_ref[pl.ds(8 + here, 1), :].reshape(width)
        columns = qv_out.shape[1]
        row = totals_ref[pl.ds(12 + here, 1), :]
        qv_out[0:1, :] = row[:, :columns]
        qv_out[1:2, :] = row[:, 2 * columns : 3 * columns]


def unpack(qkv, weights, totals, tokens, rows_in, fc_rows, proj_rows):
    f32 = jnp.float32
    _, rows, width = weights.shape
    qkv_rows = qkv.shape[1]
    token_rows = tokens.shape[0] // PIECES
    columns = proj_rows * PIECES
    counts = (fc_rows, fc_rows, proj_rows, qkv_rows, token_rows)
    vector = pl.BlockSpec((width,), lambda i: (0,))
    token_spec = pl.BlockSpec((token_rows, width), lambda i: (i, 0))
    return pl.pallas_call(
        unpack_kernel,
        grid=(PIECES,),
        in_specs=[
            pl.BlockSpec((1, qkv_rows, width), lambda i: (i, 0, 0)),
            pl.BlockSpec((1, rows, width), lambda i: (i, 0, 0)),
            pl.BlockSpec(totals.shape, lambda i: (0, 0)),
            token_spec,
            token_spec,
        ],
        out_specs=[pl.BlockSpec((count, width), lambda i: (i, 0)) for count in counts]
        + [token_spec, pl.BlockSpec((2, columns), lambda i: (0, 0))]
        + [vector] * 9,
        out_shape=[jax.ShapeDtypeStruct((PIECES * count, width), f32) for count in counts]
        + [jax.ShapeDtypeStruct(rows_in.shape, rows_in.dtype), jax.ShapeDtypeStruct((2, columns), f32)]
        + [jax.ShapeDtypeStruct((width,), f32)] * 9,
        name="unpack",
    )(qkv, weights, totals, tokens, rows_in)


def start_kernel(
    shards,
    dp_bits,
    tokens_ref,
    ids_ref,
    gain_ref,
    shift_ref,
    qkv_ref,
    qv_bias_ref,
    fc1_ref,
    fc2_ref,
    proj_ref,
    fc1_bias_ref,
    normed_out,
    q_out,
    k_out,
    v_out,
    pairs_out,
    singles_out,
    pairs_here,
    singles_here,
    weights_out,
    bias_out,
    blocks,
    normed_all,
    queries,
    keys,
    values,
    peaks,
    sums,
    scores,
    weights,
    q_extra,
    k_extra,
    own,
    chain,
    send,
    recv,
    local,
    stored,
):
    f32, bf16 = jnp.float32, jnp.bfloat16
    member, here = lax.axis_index("dp"), lax.axis_index("tensor")
    core, x_bit, y_bit = bit_of(member, 0), bit_of(member, 1), bit_of(member, 2)
    own_piece = core * 4 + x_bit * 2 + y_bit
    block, width = tokens_ref.shape
    heads = queries.shape[0]
    seq_len = ids_ref.shape[1]
    last = shards - 1
    reach = -(-(MOST_TOKENS - 1) // block)
    slots = iter(range(send.shape[0]))
    pending = []

    def copy_to(src, dst, at, **peer):
        return pltpu.make_async_remote_copy(
            src_ref=src, dst_ref=dst, send_sem=send.at[at], recv_sem=recv.at[at], device_id=peer, device_id_type=MESH
        )

    def start_dp(src, dst, bit):
        copy = copy_to(src, dst, next(slots), dp=partner_of(member, bit))
        copy.start()
        pending.append(copy)
        return copy

    fc1_rows, fc2_rows, proj_rows = (ref.shape[0] // PIECES for ref in (fc1_ref, fc2_ref, proj_ref))
    loads = []
    for at, (ref, first, count) in enumerate(
        ((fc2_ref, 0, fc2_rows), (fc1_ref, fc2_rows, fc1_rows))
    ):
        rows = pl.ds(pl.multiple_of(own_piece * count, 16), count)
        loads.append(pltpu.make_async_copy(ref.at[rows], own.at[first : first + count], local.at[at]))
        loads[-1].start()
    used = fc1_rows + fc2_rows
    rows = pl.ds(pl.multiple_of(own_piece * proj_rows, 8), proj_rows)
    own[used : used + proj_rows, :] = proj_ref[rows, :]
    used += proj_rows
    own[used:, :] = jnp.zeros((own.shape[0] - used, width), bf16)
    gain, shift = (ref[...].reshape(1, width) for ref in (gain_ref, shift_ref))
    bias_out[here] = fc1_bias_ref[...].reshape(1, width)
    greet(dp_bits, shards)
    for load in loads:
        load.wait()

    chains = {}
    for name, first, rest in (("w", own, chain), ("t", tokens_ref, blocks)):
        chains[name] = (
            first,
            rest,
            [next(slots) for _ in range(shards)],
            [next(slots) for _ in range(shards)],
        )

    def hop_copy(name, owner, rightward, from_own):
        first, rest, right_slots, left_slots = chains[name]
        src = first if from_own else rest.at[owner]
        step = 1 if rightward else last
        at = (right_slots if rightward else left_slots)[owner]
        return copy_to(src, rest.at[owner], at, tensor=lax.rem(here + step, shards))

    def send_own(name, rightward):
        for owner in range(shards):
            if owner != (last if rightward else 0):

                @pl.when(here == owner)
                def _():
                    hop_copy(name, owner, rightward, True).start()

    def hop(name, time, then=None):
        for at in range(shards):
            for rightward, owner, end in ((True, at - time, last), (False, at + time, 0)):
                if 0 <= owner <= last:

                    @pl.when(here == at)
                    def _():
                        hop_copy(name, owner, rightward, False).wait_recv()
                        if at != end:
                            hop_copy(name, owner, rightward, False).start()
                            if then is not None and owner in (0, last):
                                hop_copy(then, at, rightward, True).start()

    send_own("w", True)
    send_own("w", False)

    @pl.when(here == 0)
    def _():
        hop_copy("t", 0, True, True).start()

    @pl.when(here == last)
    def _():
        hop_copy("t", last, False, True).start()

    bias_copies = []
    for way in range(1, shards):
        copy = copy_to(
            bias_out.at[here], bias_out.at[here], next(slots), tensor=lax.rem(here + way, shards)
        )
        copy.start()
        bias_copies.append(copy)
    pending.extend(bias_copies)

    large = -MASKED
    segments = lax.broadcasted_iota(jnp.int32, (8, seq_len), 0)
    same = jnp.where(segments == ids_ref[...], 1.0, 0.0).astype(bf16)
    select = lax.broadcasted_iota(jnp.int32, (8, LANES), 1) - HEAD_DIM == lax.broadcasted_iota(
        jnp.int32, (8, LANES), 0
    )
    matched = contract_rows(same, jnp.where(select, 1.0, 0.0).astype(bf16))
    lane = lax.broadcasted_iota(jnp.int32, (seq_len, LANES), 1)
    segment_lane = (lane >= HEAD_DIM) & (lane < HEAD_DIM + 8)
    ones_lane = (lane >= HEAD_DIM + 8) & (lane < HEAD_DIM + 11)
    q_extra[...] = jnp.where(segment_lane, (matched - 1.0) * large, 0.0).astype(bf16)
    k_extra[...] = jnp.where(ones_lane, 1.0, matched).astype(bf16)
    low_half = lax.broadcasted_iota(jnp.int32, (block, LANES), 1) < HEAD_DIM
    v_lane = lax.broadcasted_iota(jnp.int32, (block, LANES), 1)
    v_extra = jnp.where((v_lane >= HEAD_DIM) & (v_lane < HEAD_DIM + 3), 1.0, 0.0).astype(bf16)

    def rows_of(owner, count=block):
        return pl.ds(pl.multiple_of(owner * count, 16), count)

    def store(which, owner):
        rows = rows_of(owner)
        source, out = (
            (normed_all.at[rows], normed_out.at[rows]),
            (queries.at[:, rows], q_out.at[:, rows]),
            (keys.at[:, rows], k_out.at[:, rows]),
            (values.at[:, rows], v_out.at[:, rows]),
        )[which]
        return pltpu.make_async_copy(source, out, stored.at[which, owner])

    def project_block(source, owner):
        tokens = source.astype(f32)
        centred = tokens - jnp.mean(tokens, axis=1, keepdims=True)
        inverse = lax.rsqrt(jnp.mean(centred * centred, axis=1, keepdims=True) + eps_norm)
        normed = (centred * inverse * gain + shift).astype(bf16)
        rows = rows_of(owner)
        normed_all[rows, :] = normed
        for which, out in ((0, queries), (1, keys), (2, values)):
            product = times_transposed(normed, qkv_ref[which])
            if which != 1:
                product = product + qv_bias_ref[which // 2 : which // 2 + 1, :]
            if which == 0:
                product = product.astype(bf16).astype(f32) * HEAD_DIM**-0.5
            extra = v_extra if which == 2 else (q_extra if which == 0 else k_extra)[rows, :]
            for head in range(heads):
                first = (head // 2) * LANES
                tile = product[:, first : first + LANES]
                if tile.shape[1] < LANES:
                    blank = jnp.zeros((block, LANES - tile.shape[1]), f32)
                    tile = jnp.concatenate([tile, blank], axis=1)
                if head % 2:
                    tile = pltpu.roll(tile, HEAD_DIM, 1)
                out[head, rows, :] = jnp.where(low_half, tile, extra.astype(f32)).astype(bf16)
        store(0, owner).start()
        store(2, owner).start()
        store(3, owner).start()

    peaks[...] = jnp.full_like(peaks, -3e38)
    sums[...] = jnp.zeros_like(sums)

    def away(index):
        return jnp.maximum(index - here, here - index)

    def visit(owner, other):
        rows, across = rows_of(owner), rows_of(other)
        for head in range(heads):
            scores[head] = times_transposed(queries[head, rows, :], keys[head, across, :])
        for head in range(heads):
            old_peak = peaks[head, rows, :]
            new_peak = jnp.maximum(old_peak, jnp.max(scores[head], axis=1, keepdims=True))
            peaks[head, rows, :] = new_peak
            spread = jnp.concatenate([new_peak] * -(-block // LANES), axis=1)[:, :block]
            weights[head] = jnp.exp(scores[head] - spread).astype(bf16)
            sums[head, rows, :] = sums[head, rows, :] * jnp.exp(old_peak - new_peak)
        for head in range(heads):
            sums[head, rows, :] += jnp.dot(
                weights[head], values[head, across, :], preferred_element_type=f32
            )

    pair_slots = [next(slots) for _ in range(shards)]
    single_slots = [next(slots) for _ in range(shards)]

    def exchange(owner, source):
        half_block = block // 2
        return [
            pltpu.make_async_remote_copy(
                src_ref=out.at[rows_of(owner, count)],
                dst_ref=landing.at[source],
                send_sem=send.at[base + owner],
                recv_sem=recv.at[base + source],
                device_id={"tensor": owner},
                device_id_type=MESH,
            )
            for out, landing, count, base in (
                (pairs_out, pairs_here, block, pair_slots[0]),
                (singles_out, singles_here, half_block, single_slots[0]),
            )
        ]

    def complete(owner):
        rows, half_block = rows_of(owner), block // 2
        parts = []
        for head in range(heads):
            total = sums[head, rows, HEAD_DIM : HEAD_DIM + 1]
            parts.append(sums[head, rows, :] / total)
            high, middle_part, low = split_three(-(peaks[head, rows, :] + jnp.log(total)))
            kept = queries[head, rows, :].astype(f32)
            for at, value in enumerate((high, middle_part, low)):
                kept = jnp.where(v_lane == HEAD_DIM + 8 + at, value.astype(f32), kept)
            queries[head, rows, :] = kept.astype(bf16)
        pair = join_lanes(parts[0], parts[1]).astype(bf16)
        single = join_lanes(parts[2][:half_block], parts[2][half_block:]).astype(bf16)
        pairs_out[rows, :] = pair
        singles_out[rows_of(owner, half_block), :] = single
        store(1, owner).start()

        @pl.when(owner == here)
        def _():
            pairs_here[here] = pair
            singles_here[here] = single

        @pl.when(owner != here)
        def _():
            for copy in exchange(owner, here):
                copy.start()

    def attend_known(time):
        def each(at, carry):
            owner = lax.rem(here + shards // 2 + at, shards)

            def other_block(other, carry):
                near = jnp.maximum(owner - other, other - owner) <= reach
                known = jnp.maximum(jnp.maximum(away(owner), away(other)), 1)

                @pl.when(near & (known == time))
                def _():
                    visit(owner, other)

                return carry

            lax.fori_loop(0, shards, other_block, 0)
            final = jnp.maximum(
                away(jnp.maximum(owner - reach, 0)), away(jnp.minimum(owner + reach, last))
            )

            @pl.when(final == time)
            def _():
                complete(owner)

            return carry

        lax.fori_loop(0, shards, each, 0)

    project_block(tokens_ref[...], here)
    for time in range(1, shards):
        hop("w", time, "t")

    half = shards // 2
    stores = []
    for owner in range(shards):
        at = 2 + owner

        @pl.when(here == owner)
        def _():
            pltpu.make_async_copy(own, weights_out.at[own_piece, owner], local.at[at]).start()

        @pl.when(here != owner)
        def _():
            pltpu.make_async_copy(chain.at[owner], weights_out.at[own_piece, owner], local.at[at]).start()

        stores.append(pltpu.make_async_copy(own, weights_out.at[own_piece, owner], local.at[at]))
    for saved in stores:
        saved.wait()

    def part(low, pieces):
        owners = pl.ds(0, half) if low else pl.ds(half, shards - half)
        return weights_out.at[pieces, owners]

    def gather_stage(low, pieces, bit):
        return [start_dp(part(low, at), part(low, at), bit) for at in pieces]

    def wait_all(copies):
        for copy in copies:
            copy.wait_recv()

    stage = gather_stage(True, [own_piece], 2) + gather_stage(False, [own_piece], 1)

    def arrived(time):
        def each(at, carry):
            owner = here + (2 * at - 1) * time

            @pl.when((owner >= 0) & (owner <= last))
            def _():
                project_block(blocks[owner], owner)

            return carry

        lax.fori_loop(0, 2, each, 0)

    for time in range(1, shards):
        hop("t", time)
        arrived(time)
        if time == 1:
            wait_all(stage)
            stage = gather_stage(True, [pl.ds(core * 4 + x_bit * 2, 2)], 1) + gather_stage(
                False, [core * 4 + 2 * at + y_bit for at in range(2)], 2
            )
        attend_known(time)
        if time == 2:
            wait_all(stage)
            stage = [start_dp(weights_out.at[pl.ds(core * 4, 4)], weights_out.at[pl.ds(core * 4, 4)], 0)]
    for owner in range(shards):

        @pl.when(here != owner)
        def _():
            for copy in exchange(here, owner):
                copy.wait_recv()
            for copy in exchange(owner, here):
                copy.wait_send()

        for which in range(4):
            store(which, owner).wait()
    wait_all(stage)
    wait_all(bias_copies)
    for copy in pending:
        copy.wait_send()
    for name in chains:
        for at in range(shards):
            for owner in range(shards):
                if owner <= at < last:

                    @pl.when(here == at)
                    def _():
                        hop_copy(name, owner, True, False).wait_send()

                if owner >= at > 0:

                    @pl.when(here == at)
                    def _():
                        hop_copy(name, owner, False, False).wait_send()


def start(shards, members, tokens, ids, gain, shift, qkv, qv_bias, fc1, fc2, proj, fc1_bias):
    dp_bits = members.bit_length() - 1
    assert members == 1 << dp_bits and dp_bits >= PIECE_BITS and shards >= 3
    f32, bf16 = jnp.float32, jnp.bfloat16
    block, width = tokens.shape
    seq_len = block * shards
    heads = qkv.shape[1] // HEAD_DIM
    rows = -(-(fc1.shape[0] + fc2.shape[0] + proj.shape[0]) // PIECES // 16) * 16
    copies = 6 * shards + (shards - 1) + 6
    vm = pltpu.VMEM
    on_chip = pl.BlockSpec(memory_space=vm)
    anywhere = pl.BlockSpec(memory_space=pl.ANY)
    head_rows = jax.ShapeDtypeStruct((heads, seq_len, LANES), bf16)
    return pl.pallas_call(
        partial(start_kernel, shards, dp_bits),
        in_specs=[on_chip] * 6 + [anywhere] * 2 + [on_chip] * 2,
        out_specs=[anywhere] * 4
        + [on_chip] * 4
        + [anywhere, on_chip],
        out_shape=[
            jax.ShapeDtypeStruct((seq_len, width), bf16),
            head_rows,
            head_rows,
            head_rows,
            jax.ShapeDtypeStruct((seq_len, LANES), bf16),
            jax.ShapeDtypeStruct((seq_len // 2, LANES), bf16),
            jax.ShapeDtypeStruct((shards, block, LANES), bf16),
            jax.ShapeDtypeStruct((shards, block // 2, LANES), bf16),
            jax.ShapeDtypeStruct((PIECES, shards, rows, width), bf16),
            jax.ShapeDtypeStruct((shards, 1, width), f32),
        ],
        scratch_shapes=[
            vm((shards, block, width), bf16),
            vm((seq_len, width), bf16),
            vm((heads, seq_len, LANES), bf16),
            vm((heads, seq_len, LANES), bf16),
            vm((heads, seq_len, LANES), bf16),
            vm((heads, seq_len, LANES), f32),
            vm((heads, seq_len, LANES), f32),
            vm((heads, block, block), f32),
            vm((heads, block, block), bf16),
            vm((seq_len, LANES), bf16),
            vm((seq_len, LANES), bf16),
            vm((rows, width), bf16),
            vm((shards, rows, width), bf16),
            pltpu.SemaphoreType.DMA((copies,)),
            pltpu.SemaphoreType.DMA((copies,)),
            pltpu.SemaphoreType.DMA((2 + shards,)),
            pltpu.SemaphoreType.DMA((4, shards)),
        ],
        compiler_params=pltpu.CompilerParams(
            collective_id=0, has_side_effects=True, vmem_limit_bytes=62 * 1024 * 1024
        ),
        name="start",
        cost_estimate=pl.CostEstimate(
            flops=6 * seq_len * width * heads * HEAD_DIM, transcendentals=0, bytes_accessed=40 * block * width
        ),
    )(tokens, ids, gain, shift, qkv, qv_bias, fc1, fc2, proj, fc1_bias)


CHUNK = 32


def middle_kernel(
    shards,
    dp_bits,
    pairs,
    singles,
    weights_ref,
    fc1_bias_ref,
    proj_bias_ref,
    scale_one_ref,
    gain_ref,
    shift_ref,
    fc2_bias_ref,
    scale_two_ref,
    tokens_ref,
    cotangent_ref,
    block_out,
    hidden_grad_out,
    pair_grads_out,
    single_grads_out,
    vectors_out,
    a_keep,
    a_away,
    b_keep,
    b_away,
    a_early,
    a_early_away,
    b_early,
    b_early_away,
    weights,
    attended,
    proj,
    branch,
    hidden,
    normed,
    wide,
    total,
    active,
    slope,
    grad_pre,
    grad_mlp,
    grad_branch,
    pair_grads,
    single_grads,
    got_early,
    got,
    a_got,
    b_got,
    send,
    recv,
    local,
):
    f32, bf16 = jnp.float32, jnp.bfloat16
    member, here = lax.axis_index("dp"), lax.axis_index("tensor")
    core, x_bit, y_bit = bit_of(member, 0), bit_of(member, 1), bit_of(member, 2)
    block, width = tokens_ref.shape
    columns = width // shards
    half = PIECES // 2
    fc_rows, proj_rows = width // PIECES, columns // PIECES
    proj_first = 2 * fc_rows
    slots = iter(range(send.shape[0]))
    proj_bias, scale_one, gain, shift, fc2_bias, scale_two = (
        ref[...].reshape(1, width)
        for ref in (proj_bias_ref, scale_one_ref, gain_ref, shift_ref, fc2_bias_ref, scale_two_ref)
    )

    def copy_to(src, dst, at, **peer):
        return pltpu.make_async_remote_copy(
            src_ref=src, dst_ref=dst, send_sem=send.at[at], recv_sem=recv.at[at], device_id=peer, device_id_type=MESH
        )

    loads = []
    for at, (first, end) in enumerate(
        ((proj_first, weights.shape[2]), (fc_rows, proj_first), (0, fc_rows))
    ):
        rows = pl.ds(first, end - first)
        loads.append(pltpu.make_async_copy(weights_ref.at[:, :, rows], weights.at[:, :, rows], local.at[at]))
        loads[-1].start()
    greet(dp_bits, shards)

    loads[0].wait()

    def fc1_of(owner):
        return weights[:, owner, fc_rows:proj_first, :].reshape(width, width)

    def fc2_of(owner):
        return weights[:, owner, :fc_rows, :].reshape(width, width)

    def proj_of(owner):
        return weights[:, owner, proj_first : proj_first + proj_rows, :].reshape(columns, width)

    def chunk(at):
        return pl.ds(pl.multiple_of(at * CHUNK, CHUNK), CHUNK)

    def each_chunk(body, init):
        return lax.fori_loop(0, block // CHUNK, body, init)

    def column_sum(value):
        return jnp.sum(value, axis=0, keepdims=True)

    def unit_of(value):
        centred = value - jnp.mean(value, axis=1, keepdims=True)
        inverse = lax.rsqrt(jnp.mean(centred * centred, axis=1, keepdims=True) + eps_norm)
        return centred * inverse, inverse

    third = shards * LANES
    for owner in range(shards):
        own_proj = proj_of(owner)
        proj[owner * LANES : (owner + 1) * LANES, :] = own_proj[:LANES]
        proj[third + owner * HEAD_DIM : third + (owner + 1) * HEAD_DIM, :] = own_proj[LANES:]
    middle_row = block // 2
    for owner in range(shards):
        attended[:, owner * LANES : (owner + 1) * LANES] = pairs[owner]
    lane = lax.broadcasted_iota(jnp.int32, (middle_row, LANES), 1)
    low_half = lane < HEAD_DIM

    def swapped(value):
        return pltpu.roll(value, HEAD_DIM, 1)

    for at in range(shards // 2):
        one, two = singles[2 * at].astype(f32), singles[2 * at + 1].astype(f32)
        columns_here = slice(third + at * LANES, third + (at + 1) * LANES)
        attended[:middle_row, columns_here] = jnp.where(low_half, one, swapped(two)).astype(bf16)
        attended[middle_row:, columns_here] = jnp.where(low_half, swapped(one), two).astype(bf16)
    product = jnp.dot(attended[...], proj[...], preferred_element_type=f32)
    branch[...] = product

    def enter(at, carry):
        rows = chunk(at)
        value = branch[rows, :] + proj_bias
        branch[rows, :] = value
        value = tokens_ref[rows, :].astype(f32) + scale_one * value
        hidden[rows, :] = value
        unit, _ = unit_of(value)
        normed[rows, :] = (unit * gain + shift).astype(bf16)
        return carry

    each_chunk(enter, 0)

    def forward(owner, carry):
        wide[:block, :] = jnp.dot(normed[...], fc1_of(owner), preferred_element_type=f32)
        bias = fc1_bias_ref[owner]

        def activate(at, carry):
            rows = chunk(at)
            value = wide[rows, :] + bias
            below = 0.5 * (1.0 + lax.erf(value * 0.5**0.5))
            active[owner, rows, :] = (value * below).astype(bf16)
            density = jnp.exp(value * value * -0.5) * (0.5 / math.pi) ** 0.5
            slope[owner, rows, :] = below + value * density
            return carry

        each_chunk(activate, 0)
        product = jnp.dot(active[owner], fc2_of(owner), preferred_element_type=f32)
        total[...] = jnp.where(owner == 0, product, total[...] + product)
        return carry

    for load in loads[1:]:
        load.wait()
    lax.fori_loop(0, shards, forward, 0)
    empty = jnp.zeros((1, width), f32)

    def turn(at, sums):
        rows = chunk(at)
        value = total[rows, :] + fc2_bias
        block_out[rows, :] = (hidden[rows, :] + scale_two * value).astype(bf16)
        grad = cotangent_ref[rows, :].astype(f32)
        grad_mlp[rows, :] = (grad * scale_two).astype(bf16)
        return (
            sums[0] + column_sum(grad * value),
            sums[1] + column_sum(grad_mlp[rows, :].astype(f32)),
        )

    scale_two_sum, fc2_bias_sum = each_chunk(turn, (empty, empty))

    split = shards // 2

    def slot_row():
        return [next(slots) for _ in range(shards)]

    early_slots, late_slots = slot_row(), slot_row()

    def core_copy(owner, early):
        rows = pl.ds(0, fc_rows) if early else pl.ds(fc_rows, weights.shape[2] - fc_rows)
        base = (early_slots if early else late_slots)[0]
        return pltpu.make_async_remote_copy(
            src_ref=weights.at[pl.ds((1 - core) * half, half), owner, rows],
            dst_ref=(got_early if early else got).at[:, owner],
            send_sem=send.at[base + owner],
            recv_sem=recv.at[base + owner],
            device_id={"dp": partner_of(member, 0)},
            device_id_type=MESH,
        )

    piece_rows = pl.ds(0, fc_rows)
    own = core * half
    side_slots = [next(slots) for _ in range(3)]

    def side_copies():
        first_half, second_half = pl.ds(0, split), pl.ds(split, shards - split)
        moves = [(weights.at[pl.ds(own + (1 - x_bit) * 2, 2), first_half, piece_rows], a_got, 1)]
        moves += [
            (weights.at[own + 2 * x + 1 - y_bit, second_half, piece_rows], b_got.at[x], 2) for x in range(2)
        ]
        return [
            copy_to(source, landing, side_slots[at], dp=partner_of(member, bit))
            for at, (source, landing, bit) in enumerate(moves)
        ]

    def grow_piece(piece, owner, other):
        weights[piece, owner, piece_rows, :] = rounded_sum(weights[piece, owner, piece_rows, :], other)

    def early_pairs():
        for owner in range(shards):
            core_copy(owner, True).wait_recv()

        def step(at, carry):
            piece, owner = at // shards, lax.rem(at, shards)
            grow_piece(own + piece, owner, got_early[piece, owner])
            return carry

        lax.fori_loop(0, half * shards, step, 0)
        for copy in side_copies():
            copy.start()

    def early_sides():
        for copy in side_copies():
            copy.wait_recv()
        for owner in range(split):
            for keep, away, side, got_side, y_side in (
                (a_early, a_early_away, x_bit, a_got, True),
                (b_early, b_early_away, y_bit, b_got, False),
            ):
                for out, at in ((keep, y_bit if y_side else x_bit), (away, 1 - (y_bit if y_side else x_bit))):
                    piece = own + (2 * side + at if y_side else 2 * at + side)
                    shard = owner if y_side else split + owner
                    out[owner] = rounded_sum(weights[piece, shard, piece_rows, :], got_side[at, owner])

    def backward(owner, carry):
        wide[:block, :] = times_transposed(grad_mlp[...], fc2_of(owner))

        def slopes(at, sums):
            rows = chunk(at)
            value = (wide[rows, :] * slope[owner, rows, :]).astype(bf16)
            grad_pre[owner, rows, :] = value
            return sums + column_sum(value.astype(f32))

        vectors_out[pl.ds(8 + owner, 1), :] = each_chunk(slopes, empty)
        product = times_transposed(grad_pre[owner], fc1_of(owner))
        total[...] = jnp.where(owner == 0, product, total[...] + product)
        return carry

    lax.fori_loop(0, shards, backward, 0)

    def leave(at, sums):
        rows = chunk(at)
        grad = total[rows, :]
        unit, inverse = unit_of(hidden[rows, :])
        scaled = grad * gain
        inner = (
            scaled
            - jnp.mean(scaled, axis=1, keepdims=True)
            - unit * jnp.mean(scaled * unit, axis=1, keepdims=True)
        )
        value = cotangent_ref[rows, :].astype(f32) + inverse * inner
        hidden_grad_out[rows, :] = value
        rounded = (value * scale_one).astype(bf16)
        grad_branch[rows, :] = rounded
        return (
            sums[0] + column_sum(grad * unit),
            sums[1] + column_sum(grad),
            sums[2] + column_sum(value * branch[rows, :]),
            sums[3] + column_sum(rounded.astype(f32)),
        )

    gain_sum, shift_sum, scale_one_sum, proj_bias_sum = each_chunk(leave, (empty,) * 4)
    for at, value in enumerate(
        (empty, empty, proj_bias_sum, scale_one_sum, gain_sum, shift_sum, fc2_bias_sum, scale_two_sum)
    ):
        vectors_out[at : at + 1, :] = value
    vectors_out[12:, :] = jnp.zeros((vectors_out.shape[0] - 12, width), f32)

    wide[:block, :] = times_transposed(grad_branch[...], proj[...])
    for owner in range(shards):
        pair_grads[owner] = wide[:block, owner * LANES : (owner + 1) * LANES].astype(bf16)
    for at in range(shards // 2):
        columns_here = slice(third + at * LANES, third + (at + 1) * LANES)
        upper, lower = wide[:middle_row, columns_here], wide[middle_row:block, columns_here]
        single_grads[2 * at] = jnp.where(low_half, upper, swapped(lower)).astype(bf16)
        single_grads[2 * at + 1] = jnp.where(low_half, swapped(upper), lower).astype(bf16)
    back = []
    for source, out in ((pair_grads, pair_grads_out), (single_grads, single_grads_out)):
        for way in range(1, shards):
            target = lax.rem(here + way, shards)
            copy = copy_to(source.at[target], out.at[here], next(slots), tensor=target)
            copy.start()
            back.append(copy)
        out[here] = source[here]

    def early_grads(owner, carry):
        product = contract_rows(active[owner], grad_mlp[...]).astype(bf16)
        weights[:, owner, :fc_rows, :] = product.reshape(PIECES, fc_rows, width)
        core_copy(owner, True).start()
        return carry

    lax.fori_loop(0, shards, early_grads, 0)
    wide[...] = contract_rows(attended[:, :], grad_branch[...])
    for owner in range(shards):
        for piece in range(PIECES):
            first, end = piece * proj_rows, (piece + 1) * proj_rows
            for low, high, start_row in ((0, LANES, owner * LANES), (LANES, columns, third + owner * HEAD_DIM)):
                begin, stop = max(first, low), min(end, high)
                if begin < stop:
                    rows = slice(start_row + begin - low, start_row + stop - low)
                    to = slice(proj_first + begin - first, proj_first + stop - first)
                    weights[piece, owner, to, :] = wide[rows, :].astype(bf16)

    early_pairs()

    def weight_grads(owner, carry):
        product = contract_rows(normed[...], grad_pre[owner]).astype(bf16)
        weights[:, owner, fc_rows:proj_first, :] = product.reshape(PIECES, fc_rows, width)
        core_copy(owner, False).start()
        return carry

    lax.fori_loop(0, shards, weight_grads, 0)
    for owner in range(shards):
        core_copy(owner, False).wait_recv()
        for x in range(2):
            for y in range(2):
                piece = x * 2 + y
                if owner < split:
                    moves = [(out, y, owner, at == x) for out, at in ((a_keep, x_bit), (a_away, 1 - x_bit))]
                else:
                    moves = [(out, x, owner - split, at == y) for out, at in ((b_keep, y_bit), (b_away, 1 - y_bit))]
                for out, first, second, wanted in moves:

                    @pl.when(wanted)
                    def _():
                        out[first, second] = rounded_sum(
                            weights[own + piece, owner, fc_rows:, :], got[piece, owner]
                        )

    early_sides()
    for copy in back:
        copy.wait_recv()
    for copy in back + side_copies():
        copy.wait_send()
    for owner in range(shards):
        core_copy(owner, True).wait_send()
        core_copy(owner, False).wait_send()


def middle(shards, members, pairs, singles, weights, fc1_bias, vectors, tokens, cotangent):
    dp_bits = members.bit_length() - 1
    f32, bf16 = jnp.float32, jnp.bfloat16
    block, width = tokens.shape
    rows = weights.shape[2]
    vm = pltpu.VMEM
    on_chip = pl.BlockSpec(memory_space=vm)
    fc_rows = width // PIECES
    quarter = jax.ShapeDtypeStruct((2, shards // 2, rows - fc_rows, width), bf16)
    early_half = jax.ShapeDtypeStruct((shards // 2, fc_rows, width), bf16)
    copies = 2 * (shards - 1) + 2 * shards + 3
    return pl.pallas_call(
        partial(middle_kernel, shards, dp_bits),
        in_specs=[on_chip, on_chip, pl.BlockSpec(memory_space=pl.ANY)] + [on_chip] * 9,
        out_specs=[on_chip] * 13,
        out_shape=[
            jax.ShapeDtypeStruct((block, width), bf16),
            jax.ShapeDtypeStruct((block, width), f32),
            jax.ShapeDtypeStruct((shards, block, LANES), bf16),
            jax.ShapeDtypeStruct((shards, block // 2, LANES), bf16),
            jax.ShapeDtypeStruct((16, width), f32),
            quarter,
            quarter,
            quarter,
            quarter,
            early_half,
            early_half,
            early_half,
            early_half,
        ],
        scratch_shapes=[
            vm(weights.shape, bf16),
            vm((block, width), bf16),
            vm((width, width), bf16),
            vm((block, width), f32),
            vm((block, width), f32),
            vm((block, width), bf16),
            vm((width, width), f32),
            vm((block, width), f32),
            vm((shards, block, width), bf16),
            vm((shards, block, width), f32),
            vm((shards, block, width), bf16),
            vm((block, width), bf16),
            vm((block, width), bf16),
            vm((shards, block, LANES), bf16),
            vm((shards, block // 2, LANES), bf16),
            vm((PIECES // 2, shards, fc_rows, width), bf16),
            vm((PIECES // 2, shards, rows - fc_rows, width), bf16),
            vm((2, shards // 2, fc_rows, width), bf16),
            vm((2, shards // 2, fc_rows, width), bf16),
            pltpu.SemaphoreType.DMA((copies,)),
            pltpu.SemaphoreType.DMA((copies,)),
            pltpu.SemaphoreType.DMA((shards,)),
        ],
        compiler_params=pltpu.CompilerParams(
            collective_id=2, has_side_effects=True, vmem_limit_bytes=62 * 1024 * 1024
        ),
        name="middle",
        cost_estimate=pl.CostEstimate(
            flops=12 * block * width * width * shards, transcendentals=0, bytes_accessed=40 * block * width
        ),
    )(pairs, singles, weights, fc1_bias, *vectors, tokens, cotangent)


eps_norm = 1e-06


def on_device(
    shards,
    members,
    tokens,
    segment_ids,
    ln1_gain,
    ln1_bias,
    qkv_weight,
    qv_bias,
    proj_weight,
    proj_bias,
    scale_one,
    ln2_gain,
    ln2_bias,
    fc1_weight,
    fc1_bias,
    fc2_weight,
    fc2_bias,
    scale_two,
    cotangent,
):
    f32, bf16 = jnp.float32, jnp.bfloat16
    seq_len = segment_ids.shape[1]
    rows_here, width = tokens.shape
    head_columns = qkv_weight.shape[2]
    heads = head_columns // HEAD_DIM
    hidden_here = fc1_weight.shape[1]
    ids = segment_ids[0]
    here = lax.axis_index("tensor")

    turned = qkv_weight.transpose(0, 2, 1)
    full_one, queries, keys, values, pairs, singles, pairs_here, singles_here, gathered, fc1_bias_full = start(
        shards,
        members,
        tokens,
        segment_ids,
        ln1_gain,
        ln1_bias,
        turned,
        qv_bias,
        fc1_weight,
        fc2_weight,
        proj_weight,
        fc1_bias,
    )
    params = (proj_bias, scale_one, ln2_gain, ln2_bias, fc2_bias, scale_two)
    block_out, grad_hidden, pair_grads, single_grads, vectors, *exchanged = middle(
        shards, members, pairs_here, singles_here, gathered, fc1_bias_full, params, tokens, cotangent
    )
    pair_grads = pair_grads.reshape(seq_len, LANES)
    single_grads = single_grads.reshape(seq_len // 2, LANES)

    grad_tokens, totals, qkv_pieces, weight_pieces = back(
        shards,
        members,
        (queries, keys, values),
        (pairs, singles, pair_grads, single_grads),
        turned.reshape(3 * head_columns, width),
        ln1_gain,
        ln1_bias,
        vectors,
        full_one,
        tokens,
        grad_hidden,
        exchanged,
    )
    fc1_grad, fc2_grad, proj_grad, qkv_grad, grad_tokens, block_out, qv_grad, fc1_bias_grad, *sums = unpack(
        qkv_pieces, weight_pieces, totals, grad_tokens, block_out, width // PIECES, head_columns // PIECES
    )
    qkv_grad = qkv_grad.reshape(3, head_columns, width).transpose(0, 2, 1)
    return (
        block_out,
        grad_tokens,
        sums[0],
        sums[1],
        qkv_grad,
        qv_grad,
        proj_grad,
        sums[2],
        sums[3],
        sums[4],
        sums[5],
        fc1_grad,
        fc1_bias_grad,
        fc2_grad,
        sums[6],
        sums[7],
    )


def solution(mesh):
    rows = P(("dp", "tensor"), None)
    columns = P(None, "tensor")
    return jax.shard_map(
        partial(on_device, mesh.shape["tensor"], mesh.shape["dp"]),
        mesh=mesh,
        in_specs=(
            rows,
            P("dp", None),
            P(),
            P(),
            P(None, None, "tensor"),
            columns,
            P("tensor", None),
            P(),
            P(),
            P(),
            P(),
            columns,
            P("tensor"),
            P("tensor", None),
            P(),
            P(),
            rows,
        ),
        out_specs=(
            rows,
            rows,
            P(),
            P(),
            P(None, None, "tensor"),
            columns,
            P("tensor", None),
            P(),
            P(),
            P(),
            P(),
            columns,
            P("tensor"),
            P("tensor", None),
            P(),
            P(),
        ),
        check_vma=False,
    )
```

```python
from functools import partial
import math

import jax, jax.numpy as jnp
from jax import lax
from jax.experimental import pallas as pl
from jax.experimental.pallas import tpu as pltpu

from jax.sharding import PartitionSpec as P

HEAD_DIM = 64
LANES = 128
MOST_TOKENS = 1152
MASKED = -(2.0**100)


def contract_rows(left, right):
    return lax.dot_general(left, right, (((0,), (0,)), ((), ())), preferred_element_type=jnp.float32)


def times_transposed(left, right, precision=None):
    return lax.dot_general(
        left, right, (((1,), (1,)), ((), ())), preferred_element_type=jnp.float32, precision=precision
    )


def split_three(value):
    high = value.astype(jnp.bfloat16)
    rest = value - high.astype(jnp.float32)
    middle = rest.astype(jnp.bfloat16)
    low = (rest - middle.astype(jnp.float32)).astype(jnp.bfloat16)
    return (high, middle, low)


def join_lanes(low, high):
    lane = lax.broadcasted_iota(jnp.int32, low.shape, 1)
    return jnp.where(lane < HEAD_DIM, low, pltpu.roll(high, HEAD_DIM, 1))


MESH = pl.DeviceIdType.MESH
PIECES = 8
PIECE_BITS = 3
UNPACK_STEPS = 2


def rounded_sum(left, right):
    return (left.astype(jnp.float32) + right.astype(jnp.float32)).astype(jnp.bfloat16)


def bit_of(index, bit):
    return lax.rem(index // (1 << bit), 2)


def partner_of(index, bit):
    return index + (1 - 2 * bit_of(index, bit)) * (1 << bit)


def greet(dp_bits, shards, ahead=None):
    barrier = pltpu.get_barrier_semaphore()
    member, here = lax.axis_index("dp"), lax.axis_index("tensor")
    peers = [{"dp": partner_of(member, bit)} for bit in range(dp_bits)]
    peers += [{"tensor": lax.rem(here + way, shards)} for way in range(1, shards)]
    for peer in peers:
        pl.semaphore_signal(barrier, inc=1, device_id=peer, device_id_type=MESH)
    if ahead is not None:
        ahead()
    pl.semaphore_wait(barrier, len(peers))


def back_kernel(
    shards,
    dp_bits,
    q_in,
    k_in,
    v_in,
    pair_ref,
    single_ref,
    pair_grad_ref,
    single_grad_ref,
    weight_ref,
    gain_ref,
    shift_ref,
    vectors_ref,
    rows_ref,
    tokens_ref,
    hidden_ref,
    a_keep,
    a_away,
    b_keep,
    b_away,
    a_early,
    a_early_away,
    b_early,
    b_early_away,
    tokens_out,
    vectors_out,
    qkv_result,
    weights_result,
    q_ref,
    k_ref,
    v_ref,
    qkv_out,
    weights_out,
    grad_heads,
    dq,
    dk,
    dv,
    probs,
    grad_scores,
    packed,
    rows_own,
    tokens_own,
    hidden_own,
    part,
    arrived,
    q_wide,
    column_sums,
    q_all,
    q_half,
    q_quarter,
    q_got_core,
    q_got_x,
    q_got_y,
    q_got_more,
    v_now,
    v_got,
    v_shards,
    a_sum,
    b_sum,
    a_got,
    b_got,
    a_second,
    b_second,
    pieces,
    early_own,
    pieces_more,
    early_more,
    z_got,
    early_got,
    early_side,
    send,
    recv,
    local,
):
    f32, bf16 = jnp.float32, jnp.bfloat16
    member, here = lax.axis_index("dp"), lax.axis_index("tensor")
    core, x_bit, y_bit = bit_of(member, 0), bit_of(member, 1), bit_of(member, 2)
    own_piece = core * 4 + x_bit * 2 + y_bit
    block, width = part.shape[1], part.shape[2]
    heads = q_ref.shape[0]
    columns = weight_ref.shape[0]
    half_rows = weights_out.shape[1] // 2
    last = shards - 1
    reach = -(-(MOST_TOKENS - 1) // block)
    gain, shift = (ref[...].reshape(1, width) for ref in (gain_ref, shift_ref))
    slots = iter(range(send.shape[0]))
    pending = []

    def copy_to(src, dst, at, **peer):
        return pltpu.make_async_remote_copy(
            src_ref=src, dst_ref=dst, send_sem=send.at[at], recv_sem=recv.at[at], device_id=peer, device_id_type=MESH
        )

    def start_dp(src, dst, bit, keep=True):
        copy = copy_to(src, dst, next(slots), dp=partner_of(member, bit))
        copy.start()
        if keep:
            pending.append(copy)
        return copy

    def load(at):
        source, landing = (
            (a_keep, a_sum),
            (b_keep, b_sum),
            (tokens_ref, tokens_own),
            (hidden_ref, hidden_own),
            (a_early, early_own.at[pl.ds(0, shards // 2)]),
            (b_early, early_own.at[pl.ds(shards // 2, shards // 2)]),
            (q_in, q_ref),
            (k_in, k_ref),
            (v_in, v_ref),
            (qkv_out, qkv_result),
            (weights_out, weights_result),
        )[at]
        return pltpu.make_async_copy(source, landing, local.at[at])

    def load_rows(owner):
        rows = pl.ds(pl.multiple_of(owner * block, 16), block)
        return pltpu.make_async_copy(rows_ref.at[rows], rows_own, local.at[11])

    for at in (6, 7, 8, 0, 1, 2, 3, 4, 5):
        load(at).start()
    flipped = here >= shards // 2

    def mirrored(owner):
        return jnp.where(flipped, last - owner, owner)

    load_rows(mirrored(last)).start()
    def set_up():
        dq[...] = jnp.zeros_like(dq)
        dk[...] = jnp.zeros_like(dk)
        dv[...] = jnp.zeros_like(dv)
        q_wide[...] = jnp.zeros_like(q_wide)
        column_sums[...] = jnp.zeros_like(column_sums)
        source = lax.broadcasted_iota(jnp.int32, (LANES, LANES), 0)
        target = lax.broadcasted_iota(jnp.int32, (LANES, LANES), 1)
        gathers = (target >= HEAD_DIM) & (target < HEAD_DIM + 3)
        picks = []
        for odd in range(2):
            inside = (source >= HEAD_DIM * odd) & (source < HEAD_DIM * (odd + 1))
            summing = jnp.where(inside & gathers, -1.0, 0.0).astype(bf16)
            moving = jnp.where(inside & (source - HEAD_DIM * odd == target), 1.0, 0.0).astype(bf16)
            picks.append((summing, moving))
        half = block // 2
        lane = lax.broadcasted_iota(jnp.int32, (half, LANES), 1)

        def prepare(at, carry):
            for side in range(2):
                rows = pl.ds(pl.multiple_of((2 * at + side) * half, half), half)
                single_rows = pl.ds(pl.multiple_of(at * half, half), half)
                for head, odd, mixed, grad in (
                    (0, 0, pair_ref[rows, :], pair_grad_ref[rows, :]),
                    (1, 1, pair_ref[rows, :], pair_grad_ref[rows, :]),
                    (2, side, single_ref[single_rows, :], single_grad_ref[single_rows, :]),
                ):
                    summing, moving = picks[odd]
                    product = grad.astype(f32) * mixed.astype(f32)
                    high = product.astype(bf16)
                    low = (product - high.astype(f32)).astype(bf16)
                    shared = jnp.dot(high, summing, preferred_element_type=f32) + jnp.dot(
                        low, summing, preferred_element_type=f32
                    )
                    moved = jnp.dot(grad, moving, preferred_element_type=f32)
                    for place, value in enumerate(split_three(shared)):
                        moved = jnp.where(lane == HEAD_DIM + place, value.astype(f32), moved)
                    grad_heads[head, rows, :] = moved.astype(bf16)
            return carry

        lax.fori_loop(0, shards, prepare, 0)

    greet(dp_bits, shards, set_up)
    start_dp(a_early_away, early_side.at[pl.ds(0, shards // 2)], 2)
    start_dp(b_early_away, early_side.at[pl.ds(shards // 2, shards // 2)], 1)
    early_sides = pending[-2:]
    start_dp(a_away, a_got, 1)
    start_dp(b_away, b_got, 2)
    first_a, first_b = pending[-2:]
    second_slots = [next(slots) for _ in range(2)]

    def second(at):
        if at:
            return copy_to(b_sum.at[1 - x_bit], b_second, second_slots[1], dp=partner_of(member, 1))
        return copy_to(a_sum.at[1 - y_bit], a_second, second_slots[0], dp=partner_of(member, 2))

    z_slots = [[next(slots) for _ in range(1, shards)] for _ in range(2)]

    def piece_copy(way, first=False):
        target = lax.rem(here + way, shards)
        source, landing = (early_own, early_got) if first else (pieces, z_got)
        return copy_to(source.at[target], landing.at[way - 1], z_slots[first][way - 1], tensor=target)

    more_slots = [[next(slots) for _ in range(PIECE_BITS, dp_bits)] for _ in range(2)]

    def send_pieces(first):
        source, landing = (early_own, early_more) if first else (pieces, pieces_more)
        for bit in range(PIECE_BITS, dp_bits):
            at = bit - PIECE_BITS
            extra = copy_to(source, landing.at[at], more_slots[first][at], dp=partner_of(member, bit))
            extra.start()
            extra.wait_recv()
            extra.wait_send()

            def step(owner, carry):
                source[owner] = rounded_sum(source[owner], landing[at, owner])
                return carry

            lax.fori_loop(0, shards, step, 0)
        for way in range(1, shards):
            piece_copy(way, first).start()

    def early_exchange():
        for at, copy in enumerate(early_sides):
            load(4 + at).wait()
            copy.wait_recv()
        for owner in range(shards):
            early_own[owner] = rounded_sum(early_own[owner], early_side[owner])
        send_pieces(True)


    def sum_pairs(out, right):
        def step(at, carry):
            one, two = at // out.shape[1], lax.rem(at, out.shape[1])
            out[one, two] = rounded_sum(out[one, two], right[one, two])
            return carry

        lax.fori_loop(0, out.shape[0] * out.shape[1], step, 0)

    def second_exchange():
        first_a.wait_recv()
        first_b.wait_recv()
        load(0).wait()
        load(1).wait()
        sum_pairs(a_sum, a_got)
        sum_pairs(b_sum, b_got)
        second(0).start()
        second(1).start()

    def shard_exchange():
        second(0).wait_recv()
        second(1).wait_recv()
        split = shards // 2
        for at in range(split):
            pieces[at] = rounded_sum(a_sum[y_bit, at], a_second[at])
            pieces[split + at] = rounded_sum(b_sum[x_bit, at], b_second[at])
        send_pieces(False)

    split_row = early_own.shape[1]
    gather_slots = [[next(slots) for _ in range(count)] for count in (2, 3, 1)]

    def gather_copies(stage):
        first_rows, other_rows = pl.ds(0, half_rows), pl.ds(half_rows, half_rows)
        if stage == 0:
            moves = [(own_piece, first_rows, 2), (own_piece, other_rows, 1)]
        elif stage == 1:
            moves = [(pl.ds(core * 4 + x_bit * 2, 2), first_rows, 1)]
            moves += [(core * 4 + 2 * at + y_bit, other_rows, 2) for at in range(2)]
        else:
            moves = [(pl.ds(core * 4, 4), pl.ds(0, 2 * half_rows), 0)]
        return [
            copy_to(
                weights_out.at[piece, rows],
                weights_out.at[piece, rows],
                gather_slots[stage][at],
                dp=partner_of(member, bit),
            )
            for at, (piece, rows, bit) in enumerate(moves)
        ]

    def gather_start(stage):
        for copy in gather_copies(stage):
            copy.start()

    def gather_wait(stage):
        for copy in gather_copies(stage):
            copy.wait_recv()

    def sum_shards():
        for first, source, landing, rows in (
            (True, early_own, early_got, slice(0, split_row)),
            (False, pieces, z_got, slice(split_row, 2 * half_rows)),
        ):
            for way in range(1, shards):
                piece_copy(way, first).wait_recv()
            total = source[here].astype(f32)
            for way in range(1, shards):
                total = total + landing[way - 1].astype(f32)
            weights_out[own_piece, rows, :] = total.astype(bf16)
        gather_start(0)

    right_slots = [next(slots) for _ in range(shards)]
    left_slots = [next(slots) for _ in range(shards)]

    def to_right(owner):
        return copy_to(part.at[owner], arrived.at[owner], right_slots[0] + owner, tensor=lax.rem(here + 1, shards))

    def to_left(owner, target=None):
        to = lax.rem(here + last, shards) if target is None else target
        landing = jnp.where(owner == to, shards, owner)
        return copy_to(
            part.at[owner], arrived.at[landing], left_slots[0] + owner, tensor=lax.rem(here + last, shards)
        )

    def add_arrived(owner, landing):
        def step(at, carry):
            rows = pl.ds(pl.multiple_of(at * (block // 4), 16), block // 4)
            part[owner, rows, :] = rounded_sum(part[owner, rows, :], arrived[landing, rows, :])
            return carry

        lax.fori_loop(0, 4, step, 0)

    def hop(moved, nth, rightward):
        owner, at = (last - nth, moved) if rightward else (nth, last - moved)
        if (at < owner) if rightward else (at > owner):

            @pl.when(here == at)
            def _():
                copy = to_right(owner) if rightward else to_left(owner)
                copy.wait_recv()
                add_arrived(owner, owner)
                copy.start()

    for at in (6, 7, 8):
        load(at).wait()

    def rows_of(owner):
        return pl.ds(pl.multiple_of(owner * block, 16), block)

    def visit(owner, other):
        key_rows, query_rows = rows_of(owner), rows_of(other)
        for head in range(heads):
            prob = jnp.exp(times_transposed(k_ref[head, key_rows, :], q_ref[head, query_rows, :]))
            grad_prob = times_transposed(v_ref[head, key_rows, :], grad_heads[head, query_rows, :])
            probs[head] = prob.astype(bf16)
            grad_scores[head] = (prob * grad_prob).astype(bf16)
        for head in range(heads):
            dv[head, key_rows, :] += jnp.dot(
                probs[head], grad_heads[head, query_rows, :], preferred_element_type=f32
            )
            dk[head, key_rows, :] += jnp.dot(
                grad_scores[head], q_ref[head, query_rows, :], preferred_element_type=f32
            )
            dq[head, query_rows, :] += contract_rows(grad_scores[head], k_ref[head, key_rows, :])

    def close_block(owner, following):
        rows = rows_of(owner)
        scale = HEAD_DIM**-0.5
        for first, low, high in (
            (0, dq[0, rows, :] * scale, dq[1, rows, :] * scale),
            (1, dq[2, rows, :] * scale, dk[0, rows, :]),
            (2, dk[1, rows, :], dk[2, rows, :]),
            (3, dv[0, rows, :], dv[1, rows, :]),
        ):
            packed[:, first * LANES : (first + 1) * LANES] = join_lanes(low, high).astype(bf16)
        packed[:, 4 * LANES : columns] = dv[2, rows, :HEAD_DIM].astype(bf16)
        part[owner] = jnp.dot(packed[...], weight_ref[...], preferred_element_type=f32).astype(bf16)

        @pl.when((owner > 1) & (here == 0))
        def _():
            to_right(owner).start()

        @pl.when((owner < last - 1) & (here == last))
        def _():
            to_left(owner).start()

        load_rows(owner).wait()
        q_wide[...] += contract_rows(packed[...], rows_own[...])
        column_sums[...] += jnp.dot(jnp.ones((8, block), bf16), packed[...], preferred_element_type=f32)

        @pl.when(following >= 0)
        def _():
            load_rows(following).start()

    order = []
    for near in range((shards + 1) // 2):
        for owner in (last - near, near):
            if owner not in order:
                order.append(owner)
    visits, closing = [], []
    for at, owner in enumerate(order):
        rest = order[at:]
        both = [(owner, owner)]
        for other in rest[1:]:
            if abs(owner - other) <= reach:
                both += [(owner, other), (other, owner)]
        visits += both
        closing.append(len(visits) - 1)
    total_visits = len(visits)

    def lookup(table, at):
        value = 0
        for place, entry in enumerate(table):
            value = value + jnp.where(at == place, entry, 0)
        return value

    closed = [order[closing.index(at)] if at in closing else -1 for at in range(total_visits)]
    later = [
        order[closing.index(at) + 1] if at in closing and at != closing[-1] else -1 for at in range(total_visits)
    ]
    def first_hops():
        hop(1, 0, True)
        hop(1, 0, False)

    events = {
        1: early_exchange,
        closing[0] + 1: second_exchange,
        closing[0] + 4: shard_exchange,
        closing[1] + 1: first_hops,
        closing[-1]: sum_shards,
    }
    assert len(events) == 5 and shards >= 4

    def each_visit(at, carry):
        visit(*(mirrored(lookup([pair[side] for pair in visits], at)) for side in range(2)))
        for when, event in events.items():

            @pl.when(at == when)
            def _():
                event()

        @pl.when(lookup([int(owner >= 0) for owner in closed], at) == 1)
        def _():
            following = lookup(later, at)
            close_block(mirrored(lookup(closed, at)), jnp.where(following < 0, -1, mirrored(following)))

        return carry

    lax.fori_loop(0, total_visits, each_visit, 0)
    def end_sends(nths):
        for nth in nths:

            @pl.when(here == 0)
            def _():
                to_right(last - nth).start()

            @pl.when(here == last)
            def _():
                to_left(nth).start()

    gather_wait(0)
    gather_start(1)

    sums = column_sums[...]
    weight = weight_ref[...].astype(f32)
    shift_sum = jnp.dot(sums, weight, preferred_element_type=f32, precision=lax.Precision.HIGHEST)[0:1]
    gain_sum = jnp.sum(weight * q_wide[...], axis=0, keepdims=True)
    v_now[0] = vectors_ref[...]
    v_now[0, 0:1, :] = (gain_sum - shift * shift_sum) / gain
    v_now[0, 1:2, :] = shift_sum
    v_now[0, pl.ds(12 + here, 1), 0:columns] = sums[0:1]
    count = q_all.shape[1]
    for piece in range(PIECES):
        q_all[piece] = q_wide[piece * count : (piece + 1) * count, :].astype(bf16)

    def vector_stage(bit):
        return start_dp(v_now.at[bit], v_got.at[bit], bit)

    q_core = start_dp(q_all.at[pl.ds((1 - core) * 4, 4)], q_got_core, 0)
    v_copy = vector_stage(0)
    q_core.wait_recv()
    for at in range(4):
        q_half[at] = rounded_sum(q_all[core * 4 + at], q_got_core[at])
    q_x = start_dp(q_half.at[pl.ds((1 - x_bit) * 2, 2)], q_got_x, 1)
    v_copy.wait_recv()
    v_now[1] = v_now[0] + v_got[0]
    v_copy = vector_stage(1)
    for moved in range(2, last):
        hop(moved, 0, True)
        hop(moved, 0, False)
    gather_wait(1)
    gather_start(2)
    q_x.wait_recv()
    for at in range(2):
        q_quarter[at] = rounded_sum(q_half[x_bit * 2 + at], q_got_x[at])
    q_y = start_dp(q_quarter.at[1 - y_bit], q_got_y, 2)
    v_copy.wait_recv()
    v_now[2] = v_now[1] + v_got[1]
    v_copy = vector_stage(2)
    q_y.wait_recv()
    qkv_out[own_piece] = rounded_sum(q_quarter[y_bit], q_got_y[...])
    v_copy.wait_recv()
    v_now[3] = v_now[2] + v_got[2]
    for bit in range(PIECE_BITS, dp_bits):
        extra = start_dp(qkv_out.at[own_piece], q_got_more.at[bit - PIECE_BITS], bit, False)
        v_copy = vector_stage(bit)
        extra.wait_recv()
        extra.wait_send()
        qkv_out[own_piece] = rounded_sum(qkv_out[own_piece], q_got_more[bit - PIECE_BITS])
        v_copy.wait_recv()
        v_now[bit + 1] = v_now[bit] + v_got[bit]
    q_back = start_dp(qkv_out.at[own_piece], qkv_out.at[own_piece], 2)
    v_shards[here] = v_now[dp_bits]
    for way in range(1, shards):
        copy = copy_to(
            v_now.at[dp_bits], v_shards.at[here], next(slots), tensor=lax.rem(here + way, shards)
        )
        copy.start()
        pending.append(copy)
    v_waits = pending[-last:]
    end_sends([last - 1])
    q_back.wait_recv()
    span = pl.ds(core * 4 + x_bit * 2, 2)
    q_back = start_dp(qkv_out.at[span], qkv_out.at[span], 1)
    for nth in range(1, last):
        for moved in range(1, last):
            hop(moved, nth, True)
            hop(moved, nth, False)
    q_back.wait_recv()
    span = pl.ds(core * 4, 4)
    q_back = start_dp(qkv_out.at[span], qkv_out.at[span], 0)
    gather_wait(2)
    load(10).start()
    for copy in v_waits:
        copy.wait_recv()
    vectors_sum = v_shards[0]
    for at in range(1, shards):
        vectors_sum = vectors_sum + v_shards[at]
    vectors_out[...] = vectors_sum

    for owner in range(shards):

        @pl.when(here == owner)
        def _():
            if owner > 0:
                to_right(owner).wait_recv()
                add_arrived(owner, owner)
            if owner < last:
                to_left(owner, owner).wait_recv()
                add_arrived(owner, shards)

    load(2).wait()
    load(3).wait()

    def close(at, carry):
        rows = pl.ds(pl.multiple_of(at * (block // 4), 16), block // 4)
        tokens = tokens_own[rows, :].astype(f32)
        centred = tokens - jnp.mean(tokens, axis=1, keepdims=True)
        inverse = lax.rsqrt(jnp.mean(centred * centred, axis=1, keepdims=True) + eps_norm)
        unit = centred * inverse
        scaled = part[here, rows, :].astype(f32) * gain
        inner = (
            scaled
            - jnp.mean(scaled, axis=1, keepdims=True)
            - unit * jnp.mean(scaled * unit, axis=1, keepdims=True)
        )
        tokens_out[rows, :] = hidden_own[rows, :] + inverse * inner
        return carry

    q_back.wait_recv()
    load(9).start()
    lax.fori_loop(0, 4, close, 0)
    load(9).wait()
    load(10).wait()
    for copy in pending:
        copy.wait_send()
    for at in range(2):
        second(at).wait_send()
    for stage in range(3):
        for copy in gather_copies(stage):
            copy.wait_send()
    for way in range(1, shards):
        piece_copy(way, True).wait_send()
        piece_copy(way).wait_send()
    for owner in range(shards):

        @pl.when(here < owner)
        def _():
            to_right(owner).wait_send()

        @pl.when(here > owner)
        def _():
            to_left(owner).wait_send()


def back(shards, members, heads_in, pair_in, weight, gain, shift, vectors, rows, tokens, grad_hidden, exchanged):
    dp_bits = members.bit_length() - 1
    assert members == 1 << dp_bits and dp_bits >= PIECE_BITS
    f32, bf16 = jnp.float32, jnp.bfloat16
    heads, seq_len, _ = heads_in[0].shape
    columns, width = weight.shape
    block = tokens.shape[0]
    quarter = exchanged[0].shape
    early_rows = exchanged[4].shape[1]
    late_rows = quarter[2]
    count = columns // PIECES
    more = max(1, dp_bits - PIECE_BITS)
    copies = 26 + 2 * shards + 3 * (shards - 1) + 5 * dp_bits
    vm = pltpu.VMEM
    return pl.pallas_call(
        partial(back_kernel, shards, dp_bits),
        in_specs=[pl.BlockSpec(memory_space=pl.ANY)] * 3
        + [pl.BlockSpec(memory_space=vm)] * 8
        + [pl.BlockSpec(memory_space=pl.ANY)] * 11,
        out_specs=[pl.BlockSpec(memory_space=vm)] * 2 + [pl.BlockSpec(memory_space=pl.ANY)] * 2,
        out_shape=[
            jax.ShapeDtypeStruct((block, width), f32),
            jax.ShapeDtypeStruct(vectors.shape, f32),
            jax.ShapeDtypeStruct((PIECES, count, width), bf16),
            jax.ShapeDtypeStruct((PIECES, early_rows + late_rows, width), bf16),
        ],
        scratch_shapes=[
            vm((heads, seq_len, LANES), bf16),
            vm((heads, seq_len, LANES), bf16),
            vm((heads, seq_len, LANES), bf16),
            vm((PIECES, count, width), bf16),
            vm((PIECES, early_rows + late_rows, width), bf16),
            vm((heads, seq_len, LANES), bf16),
            vm((heads, seq_len, LANES), f32),
            vm((heads, seq_len, LANES), f32),
            vm((heads, seq_len, LANES), f32),
            vm((heads, block, block), bf16),
            vm((heads, block, block), bf16),
            vm((block, columns), bf16),
            vm((block, width), bf16),
            vm((block, width), bf16),
            vm((block, width), f32),
            vm((shards, block, width), bf16),
            vm((shards + 1, block, width), bf16),
            vm((columns, width), f32),
            vm((8, columns), f32),
            vm((PIECES, count, width), bf16),
            vm((4, count, width), bf16),
            vm((2, count, width), bf16),
            vm((4, count, width), bf16),
            vm((2, count, width), bf16),
            vm((count, width), bf16),
            vm((more, count, width), bf16),
            vm((dp_bits + 1,) + vectors.shape, f32),
            vm((dp_bits,) + vectors.shape, f32),
            vm((shards,) + vectors.shape, f32),
            vm(quarter, bf16),
            vm(quarter, bf16),
            vm(quarter, bf16),
            vm(quarter, bf16),
            vm(quarter[1:], bf16),
            vm(quarter[1:], bf16),
            vm((shards, late_rows, width), bf16),
            vm((shards, early_rows, width), bf16),
            vm((more, shards, late_rows, width), bf16),
            vm((more, shards, early_rows, width), bf16),
            vm((shards - 1, late_rows, width), bf16),
            vm((shards - 1, early_rows, width), bf16),
            vm((shards, early_rows, width), bf16),
            pltpu.SemaphoreType.DMA((copies,)),
            pltpu.SemaphoreType.DMA((copies,)),
            pltpu.SemaphoreType.DMA((12,)),
        ],
        compiler_params=pltpu.CompilerParams(
            collective_id=1, has_side_effects=True, vmem_limit_bytes=67043328
        ),
        name="back",
        cost_estimate=pl.CostEstimate(
            flops=10 * heads * seq_len * seq_len * LANES, transcendentals=0, bytes_accessed=40 * block * width
        ),
    )(*heads_in, *pair_in, weight, gain, shift, vectors, rows, tokens, grad_hidden, *exchanged)


def unpack_kernel(
    qkv_ref,
    weights_ref,
    totals_ref,
    tokens_ref,
    rows_ref,
    fc1_out,
    fc2_out,
    proj_out,
    qkv_out,
    tokens_out,
    rows_out,
    qv_out,
    fc1_bias_out,
    *vector_outs
):
    group = weights_ref.shape[0]
    fc_rows, proj_rows, qkv_rows = (ref.shape[0] // group for ref in (fc1_out, proj_out, qkv_out))
    for at in range(group):
        for out, source, first, count in (
            (fc2_out, weights_ref, 0, fc_rows),
            (fc1_out, weights_ref, fc_rows, fc_rows),
            (proj_out, weights_ref, 2 * fc_rows, proj_rows),
            (qkv_out, qkv_ref, 0, qkv_rows),
        ):
            out[at * count : (at + 1) * count, :] = source[at, first : first + count].astype(jnp.float32)
    tokens_out[...] = tokens_ref[...]
    rows_out[...] = rows_ref[...]

    @pl.when(pl.program_id(0) == 0)
    def _():
        width = totals_ref.shape[1]
        for at, out in enumerate(vector_outs):
            out[...] = totals_ref[at : at + 1, :].reshape(width)
        here = lax.axis_index("tensor")
        fc1_bias_out[...] = totals_ref[pl.ds(8 + here, 1), :].reshape(width)
        columns = qv_out.shape[1]
        row = totals_ref[pl.ds(12 + here, 1), :]
        qv_out[0:1, :] = row[:, :columns]
        qv_out[1:2, :] = row[:, 2 * columns : 3 * columns]


def unpack(qkv, weights, totals, tokens, rows_in, fc_rows, proj_rows):
    f32 = jnp.float32
    _, rows, width = weights.shape
    qkv_rows = qkv.shape[1]
    steps = UNPACK_STEPS
    group = PIECES // steps
    token_rows = tokens.shape[0] // steps
    columns = proj_rows * PIECES
    counts = (*(group * count for count in (fc_rows, fc_rows, proj_rows, qkv_rows)), token_rows)
    vector = pl.BlockSpec((width,), lambda i: (0,))
    token_spec = pl.BlockSpec((token_rows, width), lambda i: (i, 0))
    return pl.pallas_call(
        unpack_kernel,
        grid=(steps,),
        in_specs=[
            pl.BlockSpec((group, qkv_rows, width), lambda i: (i, 0, 0)),
            pl.BlockSpec((group, rows, width), lambda i: (i, 0, 0)),
            pl.BlockSpec(totals.shape, lambda i: (0, 0)),
            token_spec,
            token_spec,
        ],
        out_specs=[pl.BlockSpec((count, width), lambda i: (i, 0)) for count in counts]
        + [token_spec, pl.BlockSpec((2, columns), lambda i: (0, 0))]
        + [vector] * 9,
        out_shape=[jax.ShapeDtypeStruct((steps * count, width), f32) for count in counts]
        + [jax.ShapeDtypeStruct(rows_in.shape, rows_in.dtype), jax.ShapeDtypeStruct((2, columns), f32)]
        + [jax.ShapeDtypeStruct((width,), f32)] * 9,
        name="unpack",
    )(qkv, weights, totals, tokens, rows_in)


def start_kernel(
    shards,
    dp_bits,
    tokens_ref,
    ids_ref,
    gain_ref,
    shift_ref,
    qkv_ref,
    qv_bias_ref,
    fc1_ref,
    fc2_ref,
    proj_ref,
    fc1_bias_ref,
    normed_out,
    q_out,
    k_out,
    v_out,
    pairs_out,
    singles_out,
    pairs_here,
    singles_here,
    weights_out,
    bias_out,
    blocks,
    normed_all,
    queries,
    keys,
    values,
    peaks,
    sums,
    scores,
    weights,
    q_extra,
    k_extra,
    own,
    chain,
    send,
    recv,
    local,
    stored,
):
    f32, bf16 = jnp.float32, jnp.bfloat16
    member, here = lax.axis_index("dp"), lax.axis_index("tensor")
    core, x_bit, y_bit = bit_of(member, 0), bit_of(member, 1), bit_of(member, 2)
    own_piece = core * 4 + x_bit * 2 + y_bit
    block, width = tokens_ref.shape
    heads = queries.shape[0]
    seq_len = ids_ref.shape[1]
    last = shards - 1
    reach = -(-(MOST_TOKENS - 1) // block)
    slots = iter(range(send.shape[0]))
    pending = []

    def copy_to(src, dst, at, **peer):
        return pltpu.make_async_remote_copy(
            src_ref=src, dst_ref=dst, send_sem=send.at[at], recv_sem=recv.at[at], device_id=peer, device_id_type=MESH
        )

    def start_dp(src, dst, bit):
        copy = copy_to(src, dst, next(slots), dp=partner_of(member, bit))
        copy.start()
        pending.append(copy)
        return copy

    fc1_rows, fc2_rows, proj_rows = (ref.shape[0] // PIECES for ref in (fc1_ref, fc2_ref, proj_ref))
    loads = []
    for at, (ref, first, count) in enumerate(
        ((fc2_ref, 0, fc2_rows), (fc1_ref, fc2_rows, fc1_rows))
    ):
        rows = pl.ds(pl.multiple_of(own_piece * count, 16), count)
        loads.append(pltpu.make_async_copy(ref.at[rows], own.at[first : first + count], local.at[at]))
        loads[-1].start()
    used = fc1_rows + fc2_rows
    rows = pl.ds(pl.multiple_of(own_piece * proj_rows, 8), proj_rows)
    own[used : used + proj_rows, :] = proj_ref[rows, :]
    used += proj_rows
    own[used:, :] = jnp.zeros((own.shape[0] - used, width), bf16)
    gain, shift = (ref[...].reshape(1, width) for ref in (gain_ref, shift_ref))
    bias_out[here] = fc1_bias_ref[...].reshape(1, width)
    greet(dp_bits, shards)
    for load in loads:
        load.wait()

    chains = {}
    for name, first, rest in (("w", own, chain), ("t", tokens_ref, blocks)):
        chains[name] = (
            first,
            rest,
            [next(slots) for _ in range(shards)],
            [next(slots) for _ in range(shards)],
        )

    def hop_copy(name, owner, rightward, from_own):
        first, rest, right_slots, left_slots = chains[name]
        src = first if from_own else rest.at[owner]
        step = 1 if rightward else last
        at = (right_slots if rightward else left_slots)[owner]
        return copy_to(src, rest.at[owner], at, tensor=lax.rem(here + step, shards))

    def send_own(name, rightward):
        for owner in range(shards):
            if owner != (last if rightward else 0):

                @pl.when(here == owner)
                def _():
                    hop_copy(name, owner, rightward, True).start()

    def hop(name, time, then=None):
        for at in range(shards):
            for rightward, owner, end in ((True, at - time, last), (False, at + time, 0)):
                if 0 <= owner <= last:

                    @pl.when(here == at)
                    def _():
                        hop_copy(name, owner, rightward, False).wait_recv()
                        if at != end:
                            hop_copy(name, owner, rightward, False).start()
                            if then is not None and owner in (0, last):
                                hop_copy(then, at, rightward, True).start()

    send_own("w", True)
    send_own("w", False)

    @pl.when(here == 0)
    def _():
        hop_copy("t", 0, True, True).start()

    @pl.when(here == last)
    def _():
        hop_copy("t", last, False, True).start()

    bias_copies = []
    for way in range(1, shards):
        copy = copy_to(
            bias_out.at[here], bias_out.at[here], next(slots), tensor=lax.rem(here + way, shards)
        )
        copy.start()
        bias_copies.append(copy)
    pending.extend(bias_copies)

    large = -MASKED
    segments = lax.broadcasted_iota(jnp.int32, (8, seq_len), 0)
    same = jnp.where(segments == ids_ref[...], 1.0, 0.0).astype(bf16)
    select = lax.broadcasted_iota(jnp.int32, (8, LANES), 1) - HEAD_DIM == lax.broadcasted_iota(
        jnp.int32, (8, LANES), 0
    )
    matched = contract_rows(same, jnp.where(select, 1.0, 0.0).astype(bf16))
    lane = lax.broadcasted_iota(jnp.int32, (seq_len, LANES), 1)
    segment_lane = (lane >= HEAD_DIM) & (lane < HEAD_DIM + 8)
    ones_lane = (lane >= HEAD_DIM + 8) & (lane < HEAD_DIM + 11)
    q_extra[...] = jnp.where(segment_lane, (matched - 1.0) * large, 0.0).astype(bf16)
    k_extra[...] = jnp.where(ones_lane, 1.0, matched).astype(bf16)
    low_half = lax.broadcasted_iota(jnp.int32, (block, LANES), 1) < HEAD_DIM
    v_lane = lax.broadcasted_iota(jnp.int32, (block, LANES), 1)
    v_extra = jnp.where((v_lane >= HEAD_DIM) & (v_lane < HEAD_DIM + 3), 1.0, 0.0).astype(bf16)

    def rows_of(owner, count=block):
        return pl.ds(pl.multiple_of(owner * count, 16), count)

    def store(which, owner):
        rows = rows_of(owner)
        source, out = (
            (normed_all.at[rows], normed_out.at[rows]),
            (queries.at[:, rows], q_out.at[:, rows]),
            (keys.at[:, rows], k_out.at[:, rows]),
            (values.at[:, rows], v_out.at[:, rows]),
        )[which]
        return pltpu.make_async_copy(source, out, stored.at[which, owner])

    def project_block(source, owner):
        tokens = source.astype(f32)
        centred = tokens - jnp.mean(tokens, axis=1, keepdims=True)
        inverse = lax.rsqrt(jnp.mean(centred * centred, axis=1, keepdims=True) + eps_norm)
        normed = (centred * inverse * gain + shift).astype(bf16)
        rows = rows_of(owner)
        normed_all[rows, :] = normed
        for which, out in ((0, queries), (1, keys), (2, values)):
            product = times_transposed(normed, qkv_ref[which])
            if which != 1:
                product = product + qv_bias_ref[which // 2 : which // 2 + 1, :]
            if which == 0:
                product = product.astype(bf16).astype(f32) * HEAD_DIM**-0.5
            extra = v_extra if which == 2 else (q_extra if which == 0 else k_extra)[rows, :]
            for head in range(heads):
                first = (head // 2) * LANES
                tile = product[:, first : first + LANES]
                if tile.shape[1] < LANES:
                    blank = jnp.zeros((block, LANES - tile.shape[1]), f32)
                    tile = jnp.concatenate([tile, blank], axis=1)
                if head % 2:
                    tile = pltpu.roll(tile, HEAD_DIM, 1)
                out[head, rows, :] = jnp.where(low_half, tile, extra.astype(f32)).astype(bf16)
        store(0, owner).start()
        store(2, owner).start()
        store(3, owner).start()

    peaks[...] = jnp.full_like(peaks, -3e38)
    sums[...] = jnp.zeros_like(sums)

    def away(index):
        return jnp.maximum(index - here, here - index)

    def visit(owner, other):
        rows, across = rows_of(owner), rows_of(other)
        for head in range(heads):
            scores[head] = times_transposed(queries[head, rows, :], keys[head, across, :])
        for head in range(heads):
            old_peak = peaks[head, rows, :]
            new_peak = jnp.maximum(old_peak, jnp.max(scores[head], axis=1, keepdims=True))
            peaks[head, rows, :] = new_peak
            spread = jnp.concatenate([new_peak] * -(-block // LANES), axis=1)[:, :block]
            weights[head] = jnp.exp(scores[head] - spread).astype(bf16)
            sums[head, rows, :] = sums[head, rows, :] * jnp.exp(old_peak - new_peak)
        for head in range(heads):
            sums[head, rows, :] += jnp.dot(
                weights[head], values[head, across, :], preferred_element_type=f32
            )

    pair_slots = [next(slots) for _ in range(shards)]
    single_slots = [next(slots) for _ in range(shards)]

    def exchange(owner, source):
        half_block = block // 2
        return [
            pltpu.make_async_remote_copy(
                src_ref=out.at[rows_of(owner, count)],
                dst_ref=landing.at[source],
                send_sem=send.at[base + owner],
                recv_sem=recv.at[base + source],
                device_id={"tensor": owner},
                device_id_type=MESH,
            )
            for out, landing, count, base in (
                (pairs_out, pairs_here, block, pair_slots[0]),
                (singles_out, singles_here, half_block, single_slots[0]),
            )
        ]

    def complete(owner):
        rows, half_block = rows_of(owner), block // 2
        parts = []
        for head in range(heads):
            total = sums[head, rows, HEAD_DIM : HEAD_DIM + 1]
            parts.append(sums[head, rows, :] / total)
            high, middle_part, low = split_three(-(peaks[head, rows, :] + jnp.log(total)))
            kept = queries[head, rows, :].astype(f32)
            for at, value in enumerate((high, middle_part, low)):
                kept = jnp.where(v_lane == HEAD_DIM + 8 + at, value.astype(f32), kept)
            queries[head, rows, :] = kept.astype(bf16)
        pair = join_lanes(parts[0], parts[1]).astype(bf16)
        single = join_lanes(parts[2][:half_block], parts[2][half_block:]).astype(bf16)
        pairs_out[rows, :] = pair
        singles_out[rows_of(owner, half_block), :] = single
        store(1, owner).start()

        @pl.when(owner == here)
        def _():
            pairs_here[here] = pair
            singles_here[here] = single

        @pl.when(owner != here)
        def _():
            for copy in exchange(owner, here):
                copy.start()

    def attend_known(time):
        def each(at, carry):
            owner = lax.rem(here + shards // 2 + at, shards)

            def other_block(other, carry):
                near = jnp.maximum(owner - other, other - owner) <= reach
                known = jnp.maximum(jnp.maximum(away(owner), away(other)), 1)

                @pl.when(near & (known == time))
                def _():
                    visit(owner, other)

                return carry

            lax.fori_loop(0, shards, other_block, 0)
            final = jnp.maximum(
                away(jnp.maximum(owner - reach, 0)), away(jnp.minimum(owner + reach, last))
            )

            @pl.when(final == time)
            def _():
                complete(owner)

            return carry

        lax.fori_loop(0, shards, each, 0)

    project_block(tokens_ref[...], here)
    for time in range(1, shards):
        hop("w", time, "t")

    half = shards // 2
    stores = []
    for owner in range(shards):
        at = 2 + owner

        @pl.when(here == owner)
        def _():
            pltpu.make_async_copy(own, weights_out.at[own_piece, owner], local.at[at]).start()

        @pl.when(here != owner)
        def _():
            pltpu.make_async_copy(chain.at[owner], weights_out.at[own_piece, owner], local.at[at]).start()

        stores.append(pltpu.make_async_copy(own, weights_out.at[own_piece, owner], local.at[at]))
    for saved in stores:
        saved.wait()

    def part(low, pieces):
        owners = pl.ds(0, half) if low else pl.ds(half, shards - half)
        return weights_out.at[pieces, owners]

    def gather_stage(low, pieces, bit):
        return [start_dp(part(low, at), part(low, at), bit) for at in pieces]

    def wait_all(copies):
        for copy in copies:
            copy.wait_recv()

    stage = gather_stage(True, [own_piece], 2) + gather_stage(False, [own_piece], 1)

    def arrived(time):
        def each(at, carry):
            owner = here + (2 * at - 1) * time

            @pl.when((owner >= 0) & (owner <= last))
            def _():
                project_block(blocks[owner], owner)

            return carry

        lax.fori_loop(0, 2, each, 0)

    for time in range(1, shards):
        hop("t", time)
        arrived(time)
        if time == 1:
            wait_all(stage)
            stage = gather_stage(True, [pl.ds(core * 4 + x_bit * 2, 2)], 1) + gather_stage(
                False, [core * 4 + 2 * at + y_bit for at in range(2)], 2
            )
        attend_known(time)
        if time == 2:
            wait_all(stage)
            stage = [start_dp(weights_out.at[pl.ds(core * 4, 4)], weights_out.at[pl.ds(core * 4, 4)], 0)]
    for owner in range(shards):

        @pl.when(here != owner)
        def _():
            for copy in exchange(here, owner):
                copy.wait_recv()
            for copy in exchange(owner, here):
                copy.wait_send()

        for which in range(4):
            store(which, owner).wait()
    wait_all(stage)
    wait_all(bias_copies)
    for copy in pending:
        copy.wait_send()
    for name in chains:
        for at in range(shards):
            for owner in range(shards):
                if owner <= at < last:

                    @pl.when(here == at)
                    def _():
                        hop_copy(name, owner, True, False).wait_send()

                if owner >= at > 0:

                    @pl.when(here == at)
                    def _():
                        hop_copy(name, owner, False, False).wait_send()


def start(shards, members, tokens, ids, gain, shift, qkv, qv_bias, fc1, fc2, proj, fc1_bias):
    dp_bits = members.bit_length() - 1
    assert members == 1 << dp_bits and dp_bits >= PIECE_BITS and shards >= 3
    f32, bf16 = jnp.float32, jnp.bfloat16
    block, width = tokens.shape
    seq_len = block * shards
    heads = qkv.shape[1] // HEAD_DIM
    rows = -(-(fc1.shape[0] + fc2.shape[0] + proj.shape[0]) // PIECES // 16) * 16
    copies = 6 * shards + (shards - 1) + 6
    vm = pltpu.VMEM
    on_chip = pl.BlockSpec(memory_space=vm)
    anywhere = pl.BlockSpec(memory_space=pl.ANY)
    head_rows = jax.ShapeDtypeStruct((heads, seq_len, LANES), bf16)
    return pl.pallas_call(
        partial(start_kernel, shards, dp_bits),
        in_specs=[on_chip] * 6 + [anywhere] * 2 + [on_chip] * 2,
        out_specs=[anywhere] * 4
        + [on_chip] * 4
        + [anywhere, on_chip],
        out_shape=[
            jax.ShapeDtypeStruct((seq_len, width), bf16),
            head_rows,
            head_rows,
            head_rows,
            jax.ShapeDtypeStruct((seq_len, LANES), bf16),
            jax.ShapeDtypeStruct((seq_len // 2, LANES), bf16),
            jax.ShapeDtypeStruct((shards, block, LANES), bf16),
            jax.ShapeDtypeStruct((shards, block // 2, LANES), bf16),
            jax.ShapeDtypeStruct((PIECES, shards, rows, width), bf16),
            jax.ShapeDtypeStruct((shards, 1, width), f32),
        ],
        scratch_shapes=[
            vm((shards, block, width), bf16),
            vm((seq_len, width), bf16),
            vm((heads, seq_len, LANES), bf16),
            vm((heads, seq_len, LANES), bf16),
            vm((heads, seq_len, LANES), bf16),
            vm((heads, seq_len, LANES), f32),
            vm((heads, seq_len, LANES), f32),
            vm((heads, block, block), f32),
            vm((heads, block, block), bf16),
            vm((seq_len, LANES), bf16),
            vm((seq_len, LANES), bf16),
            vm((rows, width), bf16),
            vm((shards, rows, width), bf16),
            pltpu.SemaphoreType.DMA((copies,)),
            pltpu.SemaphoreType.DMA((copies,)),
            pltpu.SemaphoreType.DMA((2 + shards,)),
            pltpu.SemaphoreType.DMA((4, shards)),
        ],
        compiler_params=pltpu.CompilerParams(
            collective_id=0, has_side_effects=True, vmem_limit_bytes=62 * 1024 * 1024
        ),
        name="start",
        cost_estimate=pl.CostEstimate(
            flops=6 * seq_len * width * heads * HEAD_DIM, transcendentals=0, bytes_accessed=40 * block * width
        ),
    )(tokens, ids, gain, shift, qkv, qv_bias, fc1, fc2, proj, fc1_bias)


CHUNK = 32


def middle_kernel(
    shards,
    dp_bits,
    pairs,
    singles,
    weights_ref,
    fc1_bias_ref,
    proj_bias_ref,
    scale_one_ref,
    gain_ref,
    shift_ref,
    fc2_bias_ref,
    scale_two_ref,
    tokens_ref,
    cotangent_ref,
    block_result,
    hidden_grad_result,
    pair_grads_out,
    single_grads_out,
    vectors_out,
    *rest,
):
    results, rest = rest[:8], rest[8:]
    parts, rest = rest[:8], rest[8:]
    middle_body(
        shards,
        dp_bits,
        (pairs, singles, weights_ref, fc1_bias_ref),
        (proj_bias_ref, scale_one_ref, gain_ref, shift_ref, fc2_bias_ref, scale_two_ref),
        (tokens_ref, cotangent_ref),
        (block_result, hidden_grad_result, *results),
        (pair_grads_out, single_grads_out, vectors_out),
        parts,
        *rest,
    )


def middle_body(
    shards,
    dp_bits,
    sources,
    parameter_refs,
    row_refs,
    results,
    outs,
    parts,
    block_out,
    hidden_grad_out,
    weights,
    attended,
    proj,
    branch,
    hidden,
    normed,
    wide,
    total,
    active,
    slope,
    grad_pre,
    grad_mlp,
    grad_branch,
    pair_grads,
    single_grads,
    got_early,
    got,
    a_got,
    b_got,
    send,
    recv,
    local,
    stored,
):
    pairs, singles, weights_ref, fc1_bias_ref = sources
    tokens_ref, cotangent_ref = row_refs
    pair_grads_out, single_grads_out, vectors_out = outs
    a_keep, a_away, b_keep, b_away, a_early, a_early_away, b_early, b_early_away = parts

    def store(at):
        return pltpu.make_async_copy((block_out, hidden_grad_out, *parts)[at], results[at], stored.at[at])

    f32, bf16 = jnp.float32, jnp.bfloat16
    member, here = lax.axis_index("dp"), lax.axis_index("tensor")
    core, x_bit, y_bit = bit_of(member, 0), bit_of(member, 1), bit_of(member, 2)
    block, width = tokens_ref.shape
    columns = width // shards
    half = PIECES // 2
    fc_rows, proj_rows = width // PIECES, columns // PIECES
    proj_first = 2 * fc_rows
    slots = iter(range(send.shape[0]))
    proj_bias, scale_one, gain, shift, fc2_bias, scale_two = (
        ref[...].reshape(1, width)
        for ref in parameter_refs
    )

    def copy_to(src, dst, at, **peer):
        return pltpu.make_async_remote_copy(
            src_ref=src, dst_ref=dst, send_sem=send.at[at], recv_sem=recv.at[at], device_id=peer, device_id_type=MESH
        )

    loads = []
    for at, (first, end) in enumerate(
        ((proj_first, weights.shape[2]), (fc_rows, proj_first), (0, fc_rows))
    ):
        rows = pl.ds(first, end - first)
        loads.append(pltpu.make_async_copy(weights_ref.at[:, :, rows], weights.at[:, :, rows], local.at[at]))
        loads[-1].start()
    greet(dp_bits, shards)

    loads[0].wait()

    def fc1_of(owner):
        return weights[:, owner, fc_rows:proj_first, :].reshape(width, width)

    def fc2_of(owner):
        return weights[:, owner, :fc_rows, :].reshape(width, width)

    def proj_of(owner):
        return weights[:, owner, proj_first : proj_first + proj_rows, :].reshape(columns, width)

    def chunk(at):
        return pl.ds(pl.multiple_of(at * CHUNK, CHUNK), CHUNK)

    def each_chunk(body, init):
        return lax.fori_loop(0, block // CHUNK, body, init)

    def column_sum(value):
        return jnp.sum(value, axis=0, keepdims=True)

    def unit_of(value):
        centred = value - jnp.mean(value, axis=1, keepdims=True)
        inverse = lax.rsqrt(jnp.mean(centred * centred, axis=1, keepdims=True) + eps_norm)
        return centred * inverse, inverse

    third = shards * LANES
    for owner in range(shards):
        own_proj = proj_of(owner)
        proj[owner * LANES : (owner + 1) * LANES, :] = own_proj[:LANES]
        proj[third + owner * HEAD_DIM : third + (owner + 1) * HEAD_DIM, :] = own_proj[LANES:]
    middle_row = block // 2
    for owner in range(shards):
        attended[:, owner * LANES : (owner + 1) * LANES] = pairs[owner]
    lane = lax.broadcasted_iota(jnp.int32, (middle_row, LANES), 1)
    low_half = lane < HEAD_DIM

    def swapped(value):
        return pltpu.roll(value, HEAD_DIM, 1)

    for at in range(shards // 2):
        one, two = singles[2 * at].astype(f32), singles[2 * at + 1].astype(f32)
        columns_here = slice(third + at * LANES, third + (at + 1) * LANES)
        attended[:middle_row, columns_here] = jnp.where(low_half, one, swapped(two)).astype(bf16)
        attended[middle_row:, columns_here] = jnp.where(low_half, swapped(one), two).astype(bf16)
    product = jnp.dot(attended[...], proj[...], preferred_element_type=f32)
    branch[...] = product

    def enter(at, carry):
        rows = chunk(at)
        value = branch[rows, :] + proj_bias
        branch[rows, :] = value
        value = tokens_ref[rows, :].astype(f32) + scale_one * value
        hidden[rows, :] = value
        unit, _ = unit_of(value)
        normed[rows, :] = (unit * gain + shift).astype(bf16)
        return carry

    each_chunk(enter, 0)

    def forward(owner, carry):
        wide[:block, :] = jnp.dot(normed[...], fc1_of(owner), preferred_element_type=f32)
        bias = fc1_bias_ref[owner]

        def activate(at, carry):
            rows = chunk(at)
            value = wide[rows, :] + bias
            below = 0.5 * (1.0 + lax.erf(value * 0.5**0.5))
            active[owner, rows, :] = (value * below).astype(bf16)
            density = jnp.exp(value * value * -0.5) * (0.5 / math.pi) ** 0.5
            slope[owner, rows, :] = below + value * density
            return carry

        each_chunk(activate, 0)
        product = jnp.dot(active[owner], fc2_of(owner), preferred_element_type=f32)
        total[...] = jnp.where(owner == 0, product, total[...] + product)
        return carry

    for load in loads[1:]:
        load.wait()
    lax.fori_loop(0, shards, forward, 0)
    empty = jnp.zeros((1, width), f32)

    def turn(at, sums):
        rows = chunk(at)
        value = total[rows, :] + fc2_bias
        block_out[rows, :] = (hidden[rows, :] + scale_two * value).astype(bf16)
        grad = cotangent_ref[rows, :].astype(f32)
        grad_mlp[rows, :] = (grad * scale_two).astype(bf16)
        return (
            sums[0] + column_sum(grad * value),
            sums[1] + column_sum(grad_mlp[rows, :].astype(f32)),
        )

    scale_two_sum, fc2_bias_sum = each_chunk(turn, (empty, empty))
    store(0).start()

    split = shards // 2

    def slot_row():
        return [next(slots) for _ in range(shards)]

    early_slots, late_slots = slot_row(), slot_row()

    def core_copy(owner, early):
        rows = pl.ds(0, fc_rows) if early else pl.ds(fc_rows, weights.shape[2] - fc_rows)
        base = (early_slots if early else late_slots)[0]
        return pltpu.make_async_remote_copy(
            src_ref=weights.at[pl.ds((1 - core) * half, half), owner, rows],
            dst_ref=(got_early if early else got).at[:, owner],
            send_sem=send.at[base + owner],
            recv_sem=recv.at[base + owner],
            device_id={"dp": partner_of(member, 0)},
            device_id_type=MESH,
        )

    piece_rows = pl.ds(0, fc_rows)
    own = core * half
    side_slots = [next(slots) for _ in range(3)]

    def side_copies():
        first_half, second_half = pl.ds(0, split), pl.ds(split, shards - split)
        moves = [(weights.at[pl.ds(own + (1 - x_bit) * 2, 2), first_half, piece_rows], a_got, 1)]
        moves += [
            (weights.at[own + 2 * x + 1 - y_bit, second_half, piece_rows], b_got.at[x], 2) for x in range(2)
        ]
        return [
            copy_to(source, landing, side_slots[at], dp=partner_of(member, bit))
            for at, (source, landing, bit) in enumerate(moves)
        ]

    def grow_piece(piece, owner, other):
        weights[piece, owner, piece_rows, :] = rounded_sum(weights[piece, owner, piece_rows, :], other)

    def early_pairs():
        for owner in range(shards):
            core_copy(owner, True).wait_recv()

        def step(at, carry):
            piece, owner = at // shards, lax.rem(at, shards)
            grow_piece(own + piece, owner, got_early[piece, owner])
            return carry

        lax.fori_loop(0, half * shards, step, 0)
        for copy in side_copies():
            copy.start()

    def early_sides():
        for copy in side_copies():
            copy.wait_recv()
        for owner in range(split):
            for keep, away, side, got_side, y_side in (
                (a_early, a_early_away, x_bit, a_got, True),
                (b_early, b_early_away, y_bit, b_got, False),
            ):
                for out, at in ((keep, y_bit if y_side else x_bit), (away, 1 - (y_bit if y_side else x_bit))):
                    piece = own + (2 * side + at if y_side else 2 * at + side)
                    shard = owner if y_side else split + owner
                    out[owner] = rounded_sum(weights[piece, shard, piece_rows, :], got_side[at, owner])

    def backward(owner, carry):
        wide[:block, :] = times_transposed(grad_mlp[...], fc2_of(owner))

        def slopes(at, sums):
            rows = chunk(at)
            value = (wide[rows, :] * slope[owner, rows, :]).astype(bf16)
            grad_pre[owner, rows, :] = value
            return sums + column_sum(value.astype(f32))

        vectors_out[pl.ds(8 + owner, 1), :] = each_chunk(slopes, empty)
        product = times_transposed(grad_pre[owner], fc1_of(owner))
        total[...] = jnp.where(owner == 0, product, total[...] + product)
        return carry

    lax.fori_loop(0, shards, backward, 0)

    def leave(at, sums):
        rows = chunk(at)
        grad = total[rows, :]
        unit, inverse = unit_of(hidden[rows, :])
        scaled = grad * gain
        inner = (
            scaled
            - jnp.mean(scaled, axis=1, keepdims=True)
            - unit * jnp.mean(scaled * unit, axis=1, keepdims=True)
        )
        value = cotangent_ref[rows, :].astype(f32) + inverse * inner
        hidden_grad_out[rows, :] = value
        rounded = (value * scale_one).astype(bf16)
        grad_branch[rows, :] = rounded
        return (
            sums[0] + column_sum(grad * unit),
            sums[1] + column_sum(grad),
            sums[2] + column_sum(value * branch[rows, :]),
            sums[3] + column_sum(rounded.astype(f32)),
        )

    gain_sum, shift_sum, scale_one_sum, proj_bias_sum = each_chunk(leave, (empty,) * 4)
    store(1).start()
    for at, value in enumerate(
        (empty, empty, proj_bias_sum, scale_one_sum, gain_sum, shift_sum, fc2_bias_sum, scale_two_sum)
    ):
        vectors_out[at : at + 1, :] = value
    vectors_out[12:, :] = jnp.zeros((vectors_out.shape[0] - 12, width), f32)

    wide[:block, :] = times_transposed(grad_branch[...], proj[...])
    for owner in range(shards):
        pair_grads[owner] = wide[:block, owner * LANES : (owner + 1) * LANES].astype(bf16)
    for at in range(shards // 2):
        columns_here = slice(third + at * LANES, third + (at + 1) * LANES)
        upper, lower = wide[:middle_row, columns_here], wide[middle_row:block, columns_here]
        single_grads[2 * at] = jnp.where(low_half, upper, swapped(lower)).astype(bf16)
        single_grads[2 * at + 1] = jnp.where(low_half, swapped(upper), lower).astype(bf16)
    back = []
    for source, out in ((pair_grads, pair_grads_out), (single_grads, single_grads_out)):
        for way in range(1, shards):
            target = lax.rem(here + way, shards)
            copy = copy_to(source.at[target], out.at[here], next(slots), tensor=target)
            copy.start()
            back.append(copy)
        out[here] = source[here]

    def early_grads(owner, carry):
        product = contract_rows(active[owner], grad_mlp[...]).astype(bf16)
        weights[:, owner, :fc_rows, :] = product.reshape(PIECES, fc_rows, width)
        core_copy(owner, True).start()
        return carry

    lax.fori_loop(0, shards, early_grads, 0)
    wide[...] = contract_rows(attended[:, :], grad_branch[...])
    for owner in range(shards):
        for piece in range(PIECES):
            first, end = piece * proj_rows, (piece + 1) * proj_rows
            for low, high, start_row in ((0, LANES, owner * LANES), (LANES, columns, third + owner * HEAD_DIM)):
                begin, stop = max(first, low), min(end, high)
                if begin < stop:
                    rows = slice(start_row + begin - low, start_row + stop - low)
                    to = slice(proj_first + begin - first, proj_first + stop - first)
                    weights[piece, owner, to, :] = wide[rows, :].astype(bf16)

    early_pairs()

    def weight_grads(owner, carry):
        product = contract_rows(normed[...], grad_pre[owner]).astype(bf16)
        weights[:, owner, fc_rows:proj_first, :] = product.reshape(PIECES, fc_rows, width)
        core_copy(owner, False).start()
        return carry

    lax.fori_loop(0, shards, weight_grads, 0)
    for owner in range(shards):
        core_copy(owner, False).wait_recv()
        for x in range(2):
            for y in range(2):
                piece = x * 2 + y
                if owner < split:
                    moves = [(out, y, owner, at == x) for out, at in ((a_keep, x_bit), (a_away, 1 - x_bit))]
                else:
                    moves = [(out, x, owner - split, at == y) for out, at in ((b_keep, y_bit), (b_away, 1 - y_bit))]
                for out, first, second, wanted in moves:

                    @pl.when(wanted)
                    def _():
                        out[first, second] = rounded_sum(
                            weights[own + piece, owner, fc_rows:, :], got[piece, owner]
                        )

    for at in range(2, 6):
        store(at).start()
    early_sides()
    for at in range(6, 10):
        store(at).start()
    for copy in back:
        copy.wait_recv()
    for at in range(10):
        store(at).wait()
    for copy in back + side_copies():
        copy.wait_send()
    for owner in range(shards):
        core_copy(owner, True).wait_send()
        core_copy(owner, False).wait_send()


def middle(shards, members, pairs, singles, weights, fc1_bias, vectors, tokens, cotangent):
    dp_bits = members.bit_length() - 1
    f32, bf16 = jnp.float32, jnp.bfloat16
    block, width = tokens.shape
    rows = weights.shape[2]
    vm = pltpu.VMEM
    on_chip = pl.BlockSpec(memory_space=vm)
    fc_rows = width // PIECES
    quarter = jax.ShapeDtypeStruct((2, shards // 2, rows - fc_rows, width), bf16)
    early_half = jax.ShapeDtypeStruct((shards // 2, fc_rows, width), bf16)
    copies = 2 * (shards - 1) + 2 * shards + 3
    return pl.pallas_call(
        partial(middle_kernel, shards, dp_bits),
        in_specs=[on_chip, on_chip, pl.BlockSpec(memory_space=pl.ANY)] + [on_chip] * 9,
        out_specs=[pl.BlockSpec(memory_space=pl.ANY)] * 2
        + [on_chip] * 3
        + [pl.BlockSpec(memory_space=pl.ANY)] * 8,
        out_shape=[
            jax.ShapeDtypeStruct((block, width), bf16),
            jax.ShapeDtypeStruct((block, width), f32),
            jax.ShapeDtypeStruct((shards, block, LANES), bf16),
            jax.ShapeDtypeStruct((shards, block // 2, LANES), bf16),
            jax.ShapeDtypeStruct((16, width), f32),
            quarter,
            quarter,
            quarter,
            quarter,
            early_half,
            early_half,
            early_half,
            early_half,
        ],
        scratch_shapes=[vm(quarter.shape, bf16)] * 4
        + [vm(early_half.shape, bf16)] * 4
        + [
            vm((block, width), bf16),
            vm((block, width), f32),
            vm(weights.shape, bf16),
            vm((block, width), bf16),
            vm((width, width), bf16),
            vm((block, width), f32),
            vm((block, width), f32),
            vm((block, width), bf16),
            vm((width, width), f32),
            vm((block, width), f32),
            vm((shards, block, width), bf16),
            vm((shards, block, width), f32),
            vm((shards, block, width), bf16),
            vm((block, width), bf16),
            vm((block, width), bf16),
            vm((shards, block, LANES), bf16),
            vm((shards, block // 2, LANES), bf16),
            vm((PIECES // 2, shards, fc_rows, width), bf16),
            vm((PIECES // 2, shards, rows - fc_rows, width), bf16),
            vm((2, shards // 2, fc_rows, width), bf16),
            vm((2, shards // 2, fc_rows, width), bf16),
            pltpu.SemaphoreType.DMA((copies,)),
            pltpu.SemaphoreType.DMA((copies,)),
            pltpu.SemaphoreType.DMA((shards,)),
            pltpu.SemaphoreType.DMA((10,)),
        ],
        compiler_params=pltpu.CompilerParams(
            collective_id=2, has_side_effects=True, vmem_limit_bytes=62 * 1024 * 1024
        ),
        name="middle",
        cost_estimate=pl.CostEstimate(
            flops=12 * block * width * width * shards, transcendentals=0, bytes_accessed=40 * block * width
        ),
    )(pairs, singles, weights, fc1_bias, *vectors, tokens, cotangent)


eps_norm = 1e-06


def on_device(
    shards,
    members,
    tokens,
    segment_ids,
    ln1_gain,
    ln1_bias,
    qkv_weight,
    qv_bias,
    proj_weight,
    proj_bias,
    scale_one,
    ln2_gain,
    ln2_bias,
    fc1_weight,
    fc1_bias,
    fc2_weight,
    fc2_bias,
    scale_two,
    cotangent,
):
    f32, bf16 = jnp.float32, jnp.bfloat16
    seq_len = segment_ids.shape[1]
    rows_here, width = tokens.shape
    head_columns = qkv_weight.shape[2]
    heads = head_columns // HEAD_DIM
    hidden_here = fc1_weight.shape[1]
    ids = segment_ids[0]
    here = lax.axis_index("tensor")

    turned = qkv_weight.transpose(0, 2, 1)
    full_one, queries, keys, values, pairs, singles, pairs_here, singles_here, gathered, fc1_bias_full = start(
        shards,
        members,
        tokens,
        segment_ids,
        ln1_gain,
        ln1_bias,
        turned,
        qv_bias,
        fc1_weight,
        fc2_weight,
        proj_weight,
        fc1_bias,
    )
    params = (proj_bias, scale_one, ln2_gain, ln2_bias, fc2_bias, scale_two)
    block_out, grad_hidden, pair_grads, single_grads, vectors, *exchanged = middle(
        shards, members, pairs_here, singles_here, gathered, fc1_bias_full, params, tokens, cotangent
    )
    pair_grads = pair_grads.reshape(seq_len, LANES)
    single_grads = single_grads.reshape(seq_len // 2, LANES)

    grad_tokens, totals, qkv_pieces, weight_pieces = back(
        shards,
        members,
        (queries, keys, values),
        (pairs, singles, pair_grads, single_grads),
        turned.reshape(3 * head_columns, width),
        ln1_gain,
        ln1_bias,
        vectors,
        full_one,
        tokens,
        grad_hidden,
        exchanged,
    )
    fc1_grad, fc2_grad, proj_grad, qkv_grad, grad_tokens, block_out, qv_grad, fc1_bias_grad, *sums = unpack(
        qkv_pieces, weight_pieces, totals, grad_tokens, block_out, width // PIECES, head_columns // PIECES
    )
    qkv_grad = qkv_grad.reshape(3, head_columns, width).transpose(0, 2, 1)
    return (
        block_out,
        grad_tokens,
        sums[0],
        sums[1],
        qkv_grad,
        qv_grad,
        proj_grad,
        sums[2],
        sums[3],
        sums[4],
        sums[5],
        fc1_grad,
        fc1_bias_grad,
        fc2_grad,
        sums[6],
        sums[7],
    )


def solution(mesh):
    rows = P(("dp", "tensor"), None)
    columns = P(None, "tensor")
    return jax.shard_map(
        partial(on_device, mesh.shape["tensor"], mesh.shape["dp"]),
        mesh=mesh,
        in_specs=(
            rows,
            P("dp", None),
            P(),
            P(),
            P(None, None, "tensor"),
            columns,
            P("tensor", None),
            P(),
            P(),
            P(),
            P(),
            columns,
            P("tensor"),
            P("tensor", None),
            P(),
            P(),
            rows,
        ),
        out_specs=(
            rows,
            rows,
            P(),
            P(),
            P(None, None, "tensor"),
            columns,
            P("tensor", None),
            P(),
            P(),
            P(),
            P(),
            columns,
            P("tensor"),
            P("tensor", None),
            P(),
            P(),
        ),
        check_vma=False,
    )
```

```python
from functools import partial
import math

import jax, jax.numpy as jnp
from jax import lax
from jax.experimental import pallas as pl
from jax.experimental.pallas import tpu as pltpu

from jax.sharding import PartitionSpec as P

HEAD_DIM = 64
LANES = 128
MOST_TOKENS = 1152
MASKED = -(2.0**100)


def contract_rows(left, right):
    return lax.dot_general(left, right, (((0,), (0,)), ((), ())), preferred_element_type=jnp.float32)


def times_transposed(left, right, precision=None):
    return lax.dot_general(
        left, right, (((1,), (1,)), ((), ())), preferred_element_type=jnp.float32, precision=precision
    )


def split_three(value):
    high = value.astype(jnp.bfloat16)
    rest = value - high.astype(jnp.float32)
    middle = rest.astype(jnp.bfloat16)
    low = (rest - middle.astype(jnp.float32)).astype(jnp.bfloat16)
    return (high, middle, low)


def join_lanes(low, high):
    lane = lax.broadcasted_iota(jnp.int32, low.shape, 1)
    return jnp.where(lane < HEAD_DIM, low, pltpu.roll(high, HEAD_DIM, 1))


MESH = pl.DeviceIdType.MESH
PIECES = 8
PIECE_BITS = 3
UNPACK_STEPS = 2


def rounded_sum(left, right):
    return (left.astype(jnp.float32) + right.astype(jnp.float32)).astype(jnp.bfloat16)


def bit_of(index, bit):
    return lax.rem(index // (1 << bit), 2)


def partner_of(index, bit):
    return index + (1 - 2 * bit_of(index, bit)) * (1 << bit)


def greet(dp_bits, shards, ahead=None):
    barrier = pltpu.get_barrier_semaphore()
    member, here = lax.axis_index("dp"), lax.axis_index("tensor")
    peers = [{"dp": partner_of(member, bit)} for bit in range(dp_bits)]
    peers += [{"tensor": lax.rem(here + way, shards)} for way in range(1, shards)]
    for peer in peers:
        pl.semaphore_signal(barrier, inc=1, device_id=peer, device_id_type=MESH)
    if ahead is not None:
        ahead()
    pl.semaphore_wait(barrier, len(peers))


def back_kernel(
    shards,
    dp_bits,
    q_in,
    k_in,
    v_in,
    pair_ref,
    single_ref,
    pair_grad_ref,
    single_grad_ref,
    weight_ref,
    gain_ref,
    shift_ref,
    vectors_ref,
    rows_ref,
    tokens_ref,
    hidden_ref,
    a_keep,
    a_away,
    b_keep,
    b_away,
    a_early,
    a_early_away,
    b_early,
    b_early_away,
    tokens_out,
    vectors_out,
    qkv_result,
    weights_result,
    q_ref,
    k_ref,
    v_ref,
    qkv_out,
    weights_out,
    grad_heads,
    dq,
    dk,
    dv,
    probs,
    grad_scores,
    packed,
    rows_own,
    tokens_own,
    hidden_own,
    part,
    arrived,
    q_wide,
    column_sums,
    q_all,
    q_half,
    q_quarter,
    q_got_core,
    q_got_x,
    q_got_y,
    q_got_more,
    v_now,
    v_got,
    v_shards,
    a_sum,
    b_sum,
    a_got,
    b_got,
    a_second,
    b_second,
    pieces,
    early_own,
    pieces_more,
    early_more,
    z_got,
    early_got,
    early_side,
    send,
    recv,
    local,
):
    f32, bf16 = jnp.float32, jnp.bfloat16
    member, here = lax.axis_index("dp"), lax.axis_index("tensor")
    core, x_bit, y_bit = bit_of(member, 0), bit_of(member, 1), bit_of(member, 2)
    own_piece = core * 4 + x_bit * 2 + y_bit
    block, width = part.shape[1], part.shape[2]
    heads = q_ref.shape[0]
    columns = weight_ref.shape[0]
    half_rows = weights_out.shape[1] // 2
    last = shards - 1
    reach = -(-(MOST_TOKENS - 1) // block)
    gain, shift = (ref[...].reshape(1, width) for ref in (gain_ref, shift_ref))
    slots = iter(range(send.shape[0]))
    pending = []

    def copy_to(src, dst, at, **peer):
        return pltpu.make_async_remote_copy(
            src_ref=src, dst_ref=dst, send_sem=send.at[at], recv_sem=recv.at[at], device_id=peer, device_id_type=MESH
        )

    def start_dp(src, dst, bit, keep=True):
        copy = copy_to(src, dst, next(slots), dp=partner_of(member, bit))
        copy.start()
        if keep:
            pending.append(copy)
        return copy

    def load(at):
        source, landing = (
            (a_keep, a_sum),
            (b_keep, b_sum),
            (tokens_ref, tokens_own),
            (hidden_ref, hidden_own),
            (a_early, early_own.at[pl.ds(0, shards // 2)]),
            (b_early, early_own.at[pl.ds(shards // 2, shards // 2)]),
            (q_in, q_ref),
            (k_in, k_ref),
            (v_in, v_ref),
            (qkv_out, qkv_result),
            (weights_out, weights_result),
        )[at]
        return pltpu.make_async_copy(source, landing, local.at[at])

    def load_rows(owner):
        rows = pl.ds(pl.multiple_of(owner * block, 16), block)
        return pltpu.make_async_copy(rows_ref.at[rows], rows_own, local.at[11])

    for at in (6, 7, 8, 0, 1, 2, 3, 4, 5):
        load(at).start()
    flipped = here >= shards // 2

    def mirrored(owner):
        return jnp.where(flipped, last - owner, owner)

    load_rows(mirrored(last)).start()
    def set_up():
        dq[...] = jnp.zeros_like(dq)
        dk[...] = jnp.zeros_like(dk)
        dv[...] = jnp.zeros_like(dv)
        q_wide[...] = jnp.zeros_like(q_wide)
        column_sums[...] = jnp.zeros_like(column_sums)
        source = lax.broadcasted_iota(jnp.int32, (LANES, LANES), 0)
        target = lax.broadcasted_iota(jnp.int32, (LANES, LANES), 1)
        gathers = (target >= HEAD_DIM) & (target < HEAD_DIM + 3)
        picks = []
        for odd in range(2):
            inside = (source >= HEAD_DIM * odd) & (source < HEAD_DIM * (odd + 1))
            summing = jnp.where(inside & gathers, -1.0, 0.0).astype(bf16)
            moving = jnp.where(inside & (source - HEAD_DIM * odd == target), 1.0, 0.0).astype(bf16)
            picks.append((summing, moving))
        half = block // 2
        lane = lax.broadcasted_iota(jnp.int32, (half, LANES), 1)

        def prepare(at, carry):
            for side in range(2):
                rows = pl.ds(pl.multiple_of((2 * at + side) * half, half), half)
                single_rows = pl.ds(pl.multiple_of(at * half, half), half)
                for head, odd, mixed, grad in (
                    (0, 0, pair_ref[rows, :], pair_grad_ref[rows, :]),
                    (1, 1, pair_ref[rows, :], pair_grad_ref[rows, :]),
                    (2, side, single_ref[single_rows, :], single_grad_ref[single_rows, :]),
                ):
                    summing, moving = picks[odd]
                    product = grad.astype(f32) * mixed.astype(f32)
                    high = product.astype(bf16)
                    low = (product - high.astype(f32)).astype(bf16)
                    shared = jnp.dot(high, summing, preferred_element_type=f32) + jnp.dot(
                        low, summing, preferred_element_type=f32
                    )
                    moved = jnp.dot(grad, moving, preferred_element_type=f32)
                    for place, value in enumerate(split_three(shared)):
                        moved = jnp.where(lane == HEAD_DIM + place, value.astype(f32), moved)
                    grad_heads[head, rows, :] = moved.astype(bf16)
            return carry

        lax.fori_loop(0, shards, prepare, 0)

    greet(dp_bits, shards, set_up)
    start_dp(a_early_away, early_side.at[pl.ds(0, shards // 2)], 2)
    start_dp(b_early_away, early_side.at[pl.ds(shards // 2, shards // 2)], 1)
    early_sides = pending[-2:]
    start_dp(a_away, a_got, 1)
    start_dp(b_away, b_got, 2)
    first_a, first_b = pending[-2:]
    second_slots = [next(slots) for _ in range(2)]

    def second(at):
        if at:
            return copy_to(b_sum.at[1 - x_bit], b_second, second_slots[1], dp=partner_of(member, 1))
        return copy_to(a_sum.at[1 - y_bit], a_second, second_slots[0], dp=partner_of(member, 2))

    z_slots = [[next(slots) for _ in range(1, shards)] for _ in range(2)]

    def piece_copy(way, first=False):
        target = lax.rem(here + way, shards)
        source, landing = (early_own, early_got) if first else (pieces, z_got)
        return copy_to(source.at[target], landing.at[way - 1], z_slots[first][way - 1], tensor=target)

    more_slots = [[next(slots) for _ in range(PIECE_BITS, dp_bits)] for _ in range(2)]

    def send_pieces(first):
        source, landing = (early_own, early_more) if first else (pieces, pieces_more)
        for bit in range(PIECE_BITS, dp_bits):
            at = bit - PIECE_BITS
            extra = copy_to(source, landing.at[at], more_slots[first][at], dp=partner_of(member, bit))
            extra.start()
            extra.wait_recv()
            extra.wait_send()

            def step(owner, carry):
                source[owner] = rounded_sum(source[owner], landing[at, owner])
                return carry

            lax.fori_loop(0, shards, step, 0)
        for way in range(1, shards):
            piece_copy(way, first).start()

    def early_exchange():
        for at, copy in enumerate(early_sides):
            load(4 + at).wait()
            copy.wait_recv()
        for owner in range(shards):
            early_own[owner] = rounded_sum(early_own[owner], early_side[owner])
        send_pieces(True)


    def sum_pairs(out, right):
        def step(at, carry):
            one, two = at // out.shape[1], lax.rem(at, out.shape[1])
            out[one, two] = rounded_sum(out[one, two], right[one, two])
            return carry

        lax.fori_loop(0, out.shape[0] * out.shape[1], step, 0)

    def second_exchange():
        first_a.wait_recv()
        first_b.wait_recv()
        load(0).wait()
        load(1).wait()
        sum_pairs(a_sum, a_got)
        sum_pairs(b_sum, b_got)
        second(0).start()
        second(1).start()

    def shard_exchange():
        second(0).wait_recv()
        second(1).wait_recv()
        split = shards // 2
        for at in range(split):
            pieces[at] = rounded_sum(a_sum[y_bit, at], a_second[at])
            pieces[split + at] = rounded_sum(b_sum[x_bit, at], b_second[at])
        send_pieces(False)

    split_row = early_own.shape[1]
    gather_slots = [[next(slots) for _ in range(count)] for count in (2, 3, 1)]

    def gather_copies(stage):
        first_rows, other_rows = pl.ds(0, half_rows), pl.ds(half_rows, half_rows)
        if stage == 0:
            moves = [(own_piece, first_rows, 2), (own_piece, other_rows, 1)]
        elif stage == 1:
            moves = [(pl.ds(core * 4 + x_bit * 2, 2), first_rows, 1)]
            moves += [(core * 4 + 2 * at + y_bit, other_rows, 2) for at in range(2)]
        else:
            moves = [(pl.ds(core * 4, 4), pl.ds(0, 2 * half_rows), 0)]
        return [
            copy_to(
                weights_out.at[piece, rows],
                weights_out.at[piece, rows],
                gather_slots[stage][at],
                dp=partner_of(member, bit),
            )
            for at, (piece, rows, bit) in enumerate(moves)
        ]

    def gather_start(stage):
        for copy in gather_copies(stage):
            copy.start()

    def gather_wait(stage):
        for copy in gather_copies(stage):
            copy.wait_recv()

    def sum_shards():
        for first, source, landing, rows in (
            (True, early_own, early_got, slice(0, split_row)),
            (False, pieces, z_got, slice(split_row, 2 * half_rows)),
        ):
            for way in range(1, shards):
                piece_copy(way, first).wait_recv()
            total = source[here].astype(f32)
            for way in range(1, shards):
                total = total + landing[way - 1].astype(f32)
            weights_out[own_piece, rows, :] = total.astype(bf16)
        gather_start(0)

    right_slots = [next(slots) for _ in range(shards)]
    left_slots = [next(slots) for _ in range(shards)]

    def to_right(owner):
        return copy_to(part.at[owner], arrived.at[owner], right_slots[0] + owner, tensor=lax.rem(here + 1, shards))

    def to_left(owner, target=None):
        to = lax.rem(here + last, shards) if target is None else target
        landing = jnp.where(owner == to, shards, owner)
        return copy_to(
            part.at[owner], arrived.at[landing], left_slots[0] + owner, tensor=lax.rem(here + last, shards)
        )

    def add_arrived(owner, landing):
        def step(at, carry):
            rows = pl.ds(pl.multiple_of(at * (block // 4), 16), block // 4)
            part[owner, rows, :] = rounded_sum(part[owner, rows, :], arrived[landing, rows, :])
            return carry

        lax.fori_loop(0, 4, step, 0)

    def hop(moved, nth, rightward):
        owner, at = (last - nth, moved) if rightward else (nth, last - moved)
        if (at < owner) if rightward else (at > owner):

            @pl.when(here == at)
            def _():
                copy = to_right(owner) if rightward else to_left(owner)
                copy.wait_recv()
                add_arrived(owner, owner)
                copy.start()

    for at in (6, 7, 8):
        load(at).wait()

    def rows_of(owner):
        return pl.ds(pl.multiple_of(owner * block, 16), block)

    def visit(owner, other):
        key_rows, query_rows = rows_of(owner), rows_of(other)
        for head in range(heads):
            prob = jnp.exp(times_transposed(k_ref[head, key_rows, :], q_ref[head, query_rows, :]))
            grad_prob = times_transposed(v_ref[head, key_rows, :], grad_heads[head, query_rows, :])
            probs[head] = prob.astype(bf16)
            grad_scores[head] = (prob * grad_prob).astype(bf16)
        for head in range(heads):
            dv[head, key_rows, :] += jnp.dot(
                probs[head], grad_heads[head, query_rows, :], preferred_element_type=f32
            )
            dk[head, key_rows, :] += jnp.dot(
                grad_scores[head], q_ref[head, query_rows, :], preferred_element_type=f32
            )
            dq[head, query_rows, :] += contract_rows(grad_scores[head], k_ref[head, key_rows, :])

    def close_block(owner, following):
        rows = rows_of(owner)
        scale = HEAD_DIM**-0.5
        for first, low, high in (
            (0, dq[0, rows, :] * scale, dq[1, rows, :] * scale),
            (1, dq[2, rows, :] * scale, dk[0, rows, :]),
            (2, dk[1, rows, :], dk[2, rows, :]),
            (3, dv[0, rows, :], dv[1, rows, :]),
        ):
            packed[:, first * LANES : (first + 1) * LANES] = join_lanes(low, high).astype(bf16)
        packed[:, 4 * LANES : columns] = dv[2, rows, :HEAD_DIM].astype(bf16)
        part[owner] = jnp.dot(packed[...], weight_ref[...], preferred_element_type=f32).astype(bf16)

        @pl.when((owner > 1) & (here == 0))
        def _():
            to_right(owner).start()

        @pl.when((owner < last - 1) & (here == last))
        def _():
            to_left(owner).start()

        load_rows(owner).wait()
        q_wide[...] += contract_rows(packed[...], rows_own[...])
        column_sums[...] += jnp.dot(jnp.ones((8, block), bf16), packed[...], preferred_element_type=f32)

        @pl.when(following >= 0)
        def _():
            load_rows(following).start()

    order = []
    for near in range((shards + 1) // 2):
        for owner in (last - near, near):
            if owner not in order:
                order.append(owner)
    visits, closing = [], []
    for at, owner in enumerate(order):
        rest = order[at:]
        both = [(owner, owner)]
        for other in rest[1:]:
            if abs(owner - other) <= reach:
                both += [(owner, other), (other, owner)]
        visits += both
        closing.append(len(visits) - 1)
    total_visits = len(visits)

    def lookup(table, at):
        value = 0
        for place, entry in enumerate(table):
            value = value + jnp.where(at == place, entry, 0)
        return value

    closed = [order[closing.index(at)] if at in closing else -1 for at in range(total_visits)]
    later = [
        order[closing.index(at) + 1] if at in closing and at != closing[-1] else -1 for at in range(total_visits)
    ]
    def first_hops():
        hop(1, 0, True)
        hop(1, 0, False)

    events = {
        1: early_exchange,
        closing[0] + 1: second_exchange,
        closing[0] + 4: shard_exchange,
        closing[1] + 1: first_hops,
        closing[-1]: sum_shards,
    }
    assert len(events) == 5 and shards >= 4

    def each_visit(at, carry):
        visit(*(mirrored(lookup([pair[side] for pair in visits], at)) for side in range(2)))
        for when, event in events.items():

            @pl.when(at == when)
            def _():
                event()

        @pl.when(lookup([int(owner >= 0) for owner in closed], at) == 1)
        def _():
            following = lookup(later, at)
            close_block(mirrored(lookup(closed, at)), jnp.where(following < 0, -1, mirrored(following)))

        return carry

    lax.fori_loop(0, total_visits, each_visit, 0)
    def end_sends(nths):
        for nth in nths:

            @pl.when(here == 0)
            def _():
                to_right(last - nth).start()

            @pl.when(here == last)
            def _():
                to_left(nth).start()

    gather_wait(0)
    gather_start(1)

    sums = column_sums[...]
    weight = weight_ref[...].astype(f32)
    shift_sum = jnp.dot(sums, weight, preferred_element_type=f32, precision=lax.Precision.HIGHEST)[0:1]
    gain_sum = jnp.sum(weight * q_wide[...], axis=0, keepdims=True)
    v_now[0] = vectors_ref[...]
    v_now[0, 0:1, :] = (gain_sum - shift * shift_sum) / gain
    v_now[0, 1:2, :] = shift_sum
    v_now[0, pl.ds(12 + here, 1), 0:columns] = sums[0:1]
    count = q_all.shape[1]
    for piece in range(PIECES):
        q_all[piece] = q_wide[piece * count : (piece + 1) * count, :].astype(bf16)

    def vector_stage(bit):
        return start_dp(v_now.at[bit], v_got.at[bit], bit)

    q_core = start_dp(q_all.at[pl.ds((1 - core) * 4, 4)], q_got_core, 0)
    v_copy = vector_stage(0)
    q_core.wait_recv()
    for at in range(4):
        q_half[at] = rounded_sum(q_all[core * 4 + at], q_got_core[at])
    q_x = start_dp(q_half.at[pl.ds((1 - x_bit) * 2, 2)], q_got_x, 1)
    v_copy.wait_recv()
    v_now[1] = v_now[0] + v_got[0]
    v_copy = vector_stage(1)
    for moved in range(2, last):
        hop(moved, 0, True)
        hop(moved, 0, False)
    gather_wait(1)
    gather_start(2)
    q_x.wait_recv()
    for at in range(2):
        q_quarter[at] = rounded_sum(q_half[x_bit * 2 + at], q_got_x[at])
    q_y = start_dp(q_quarter.at[1 - y_bit], q_got_y, 2)
    v_copy.wait_recv()
    v_now[2] = v_now[1] + v_got[1]
    v_copy = vector_stage(2)
    q_y.wait_recv()
    qkv_out[own_piece] = rounded_sum(q_quarter[y_bit], q_got_y[...])
    v_copy.wait_recv()
    v_now[3] = v_now[2] + v_got[2]
    for bit in range(PIECE_BITS, dp_bits):
        extra = start_dp(qkv_out.at[own_piece], q_got_more.at[bit - PIECE_BITS], bit, False)
        v_copy = vector_stage(bit)
        extra.wait_recv()
        extra.wait_send()
        qkv_out[own_piece] = rounded_sum(qkv_out[own_piece], q_got_more[bit - PIECE_BITS])
        v_copy.wait_recv()
        v_now[bit + 1] = v_now[bit] + v_got[bit]
    q_back = start_dp(qkv_out.at[own_piece], qkv_out.at[own_piece], 2)
    v_shards[here] = v_now[dp_bits]
    for way in range(1, shards):
        copy = copy_to(
            v_now.at[dp_bits], v_shards.at[here], next(slots), tensor=lax.rem(here + way, shards)
        )
        copy.start()
        pending.append(copy)
    v_waits = pending[-last:]
    end_sends([last - 1])
    q_back.wait_recv()
    span = pl.ds(core * 4 + x_bit * 2, 2)
    q_back = start_dp(qkv_out.at[span], qkv_out.at[span], 1)
    for nth in range(1, last):
        for moved in range(1, last):
            hop(moved, nth, True)
            hop(moved, nth, False)
    q_back.wait_recv()
    span = pl.ds(core * 4, 4)
    q_back = start_dp(qkv_out.at[span], qkv_out.at[span], 0)
    gather_wait(2)
    load(10).start()
    for copy in v_waits:
        copy.wait_recv()
    vectors_sum = v_shards[0]
    for at in range(1, shards):
        vectors_sum = vectors_sum + v_shards[at]
    vectors_out[...] = vectors_sum

    for owner in range(shards):

        @pl.when(here == owner)
        def _():
            if owner > 0:
                to_right(owner).wait_recv()
                add_arrived(owner, owner)
            if owner < last:
                to_left(owner, owner).wait_recv()
                add_arrived(owner, shards)

    load(2).wait()
    load(3).wait()

    def close(at, carry):
        rows = pl.ds(pl.multiple_of(at * (block // 4), 16), block // 4)
        tokens = tokens_own[rows, :].astype(f32)
        centred = tokens - jnp.mean(tokens, axis=1, keepdims=True)
        inverse = lax.rsqrt(jnp.mean(centred * centred, axis=1, keepdims=True) + eps_norm)
        unit = centred * inverse
        scaled = part[here, rows, :].astype(f32) * gain
        inner = (
            scaled
            - jnp.mean(scaled, axis=1, keepdims=True)
            - unit * jnp.mean(scaled * unit, axis=1, keepdims=True)
        )
        tokens_out[rows, :] = hidden_own[rows, :] + inverse * inner
        return carry

    q_back.wait_recv()
    load(9).start()
    lax.fori_loop(0, 4, close, 0)
    load(9).wait()
    load(10).wait()
    for copy in pending:
        copy.wait_send()
    for at in range(2):
        second(at).wait_send()
    for stage in range(3):
        for copy in gather_copies(stage):
            copy.wait_send()
    for way in range(1, shards):
        piece_copy(way, True).wait_send()
        piece_copy(way).wait_send()
    for owner in range(shards):

        @pl.when(here < owner)
        def _():
            to_right(owner).wait_send()

        @pl.when(here > owner)
        def _():
            to_left(owner).wait_send()


def back(shards, members, heads_in, pair_in, weight, gain, shift, vectors, rows, tokens, grad_hidden, exchanged):
    dp_bits = members.bit_length() - 1
    assert members == 1 << dp_bits and dp_bits >= PIECE_BITS
    f32, bf16 = jnp.float32, jnp.bfloat16
    heads, seq_len, _ = heads_in[0].shape
    columns, width = weight.shape
    block = tokens.shape[0]
    quarter = exchanged[0].shape
    early_rows = exchanged[4].shape[1]
    late_rows = quarter[2]
    count = columns // PIECES
    more = max(1, dp_bits - PIECE_BITS)
    copies = 26 + 2 * shards + 3 * (shards - 1) + 5 * dp_bits
    vm = pltpu.VMEM
    return pl.pallas_call(
        partial(back_kernel, shards, dp_bits),
        in_specs=[pl.BlockSpec(memory_space=pl.ANY)] * 3
        + [pl.BlockSpec(memory_space=vm)] * 8
        + [pl.BlockSpec(memory_space=pl.ANY)] * 11,
        out_specs=[pl.BlockSpec(memory_space=vm)] * 2 + [pl.BlockSpec(memory_space=pl.ANY)] * 2,
        out_shape=[
            jax.ShapeDtypeStruct((block, width), f32),
            jax.ShapeDtypeStruct(vectors.shape, f32),
            jax.ShapeDtypeStruct((PIECES, count, width), bf16),
            jax.ShapeDtypeStruct((PIECES, early_rows + late_rows, width), bf16),
        ],
        scratch_shapes=[
            vm((heads, seq_len, LANES), bf16),
            vm((heads, seq_len, LANES), bf16),
            vm((heads, seq_len, LANES), bf16),
            vm((PIECES, count, width), bf16),
            vm((PIECES, early_rows + late_rows, width), bf16),
            vm((heads, seq_len, LANES), bf16),
            vm((heads, seq_len, LANES), f32),
            vm((heads, seq_len, LANES), f32),
            vm((heads, seq_len, LANES), f32),
            vm((heads, block, block), bf16),
            vm((heads, block, block), bf16),
            vm((block, columns), bf16),
            vm((block, width), bf16),
            vm((block, width), bf16),
            vm((block, width), f32),
            vm((shards, block, width), bf16),
            vm((shards + 1, block, width), bf16),
            vm((columns, width), f32),
            vm((8, columns), f32),
            vm((PIECES, count, width), bf16),
            vm((4, count, width), bf16),
            vm((2, count, width), bf16),
            vm((4, count, width), bf16),
            vm((2, count, width), bf16),
            vm((count, width), bf16),
            vm((more, count, width), bf16),
            vm((dp_bits + 1,) + vectors.shape, f32),
            vm((dp_bits,) + vectors.shape, f32),
            vm((shards,) + vectors.shape, f32),
            vm(quarter, bf16),
            vm(quarter, bf16),
            vm(quarter, bf16),
            vm(quarter, bf16),
            vm(quarter[1:], bf16),
            vm(quarter[1:], bf16),
            vm((shards, late_rows, width), bf16),
            vm((shards, early_rows, width), bf16),
            vm((more, shards, late_rows, width), bf16),
            vm((more, shards, early_rows, width), bf16),
            vm((shards - 1, late_rows, width), bf16),
            vm((shards - 1, early_rows, width), bf16),
            vm((shards, early_rows, width), bf16),
            pltpu.SemaphoreType.DMA((copies,)),
            pltpu.SemaphoreType.DMA((copies,)),
            pltpu.SemaphoreType.DMA((12,)),
        ],
        compiler_params=pltpu.CompilerParams(
            collective_id=1, has_side_effects=True, vmem_limit_bytes=67043328
        ),
        name="back",
        cost_estimate=pl.CostEstimate(
            flops=10 * heads * seq_len * seq_len * LANES, transcendentals=0, bytes_accessed=40 * block * width
        ),
    )(*heads_in, *pair_in, weight, gain, shift, vectors, rows, tokens, grad_hidden, *exchanged)


def unpack_kernel(
    qkv_ref,
    weights_ref,
    totals_ref,
    tokens_ref,
    rows_ref,
    fc1_out,
    fc2_out,
    proj_out,
    qkv_out,
    tokens_out,
    rows_out,
    qv_out,
    fc1_bias_out,
    *vector_outs
):
    group = weights_ref.shape[0]
    fc_rows, proj_rows, qkv_rows = (ref.shape[0] // group for ref in (fc1_out, proj_out, qkv_out))
    for at in range(group):
        for out, source, first, count in (
            (fc2_out, weights_ref, 0, fc_rows),
            (fc1_out, weights_ref, fc_rows, fc_rows),
            (proj_out, weights_ref, 2 * fc_rows, proj_rows),
            (qkv_out, qkv_ref, 0, qkv_rows),
        ):
            out[at * count : (at + 1) * count, :] = source[at, first : first + count].astype(jnp.float32)
    tokens_out[...] = tokens_ref[...]
    rows_out[...] = rows_ref[...]

    @pl.when(pl.program_id(0) == 0)
    def _():
        width = totals_ref.shape[1]
        for at, out in enumerate(vector_outs):
            out[...] = totals_ref[at : at + 1, :].reshape(width)
        here = lax.axis_index("tensor")
        fc1_bias_out[...] = totals_ref[pl.ds(8 + here, 1), :].reshape(width)
        columns = qv_out.shape[1]
        row = totals_ref[pl.ds(12 + here, 1), :]
        qv_out[0:1, :] = row[:, :columns]
        qv_out[1:2, :] = row[:, 2 * columns : 3 * columns]


def unpack(qkv, weights, totals, tokens, rows_in, fc_rows, proj_rows):
    f32 = jnp.float32
    _, rows, width = weights.shape
    qkv_rows = qkv.shape[1]
    steps = UNPACK_STEPS
    group = PIECES // steps
    token_rows = tokens.shape[0] // steps
    columns = proj_rows * PIECES
    counts = (*(group * count for count in (fc_rows, fc_rows, proj_rows, qkv_rows)), token_rows)
    vector = pl.BlockSpec((width,), lambda i: (0,))
    token_spec = pl.BlockSpec((token_rows, width), lambda i: (i, 0))
    return pl.pallas_call(
        unpack_kernel,
        grid=(steps,),
        in_specs=[
            pl.BlockSpec((group, qkv_rows, width), lambda i: (i, 0, 0)),
            pl.BlockSpec((group, rows, width), lambda i: (i, 0, 0)),
            pl.BlockSpec(totals.shape, lambda i: (0, 0)),
            token_spec,
            token_spec,
        ],
        out_specs=[pl.BlockSpec((count, width), lambda i: (i, 0)) for count in counts]
        + [token_spec, pl.BlockSpec((2, columns), lambda i: (0, 0))]
        + [vector] * 9,
        out_shape=[jax.ShapeDtypeStruct((steps * count, width), f32) for count in counts]
        + [jax.ShapeDtypeStruct(rows_in.shape, rows_in.dtype), jax.ShapeDtypeStruct((2, columns), f32)]
        + [jax.ShapeDtypeStruct((width,), f32)] * 9,
        name="unpack",
    )(qkv, weights, totals, tokens, rows_in)


def start_kernel(
    shards,
    dp_bits,
    tokens_ref,
    ids_ref,
    gain_ref,
    shift_ref,
    qkv_ref,
    qv_bias_ref,
    fc1_ref,
    fc2_ref,
    proj_ref,
    fc1_bias_ref,
    normed_out,
    q_out,
    k_out,
    v_out,
    pairs_out,
    singles_out,
    pairs_here,
    singles_here,
    weights_out,
    bias_out,
    blocks,
    normed_all,
    queries,
    keys,
    values,
    peaks,
    sums,
    scores,
    weights,
    q_extra,
    k_extra,
    own,
    chain,
    send,
    recv,
    local,
    stored,
):
    f32, bf16 = jnp.float32, jnp.bfloat16
    member, here = lax.axis_index("dp"), lax.axis_index("tensor")
    core, x_bit, y_bit = bit_of(member, 0), bit_of(member, 1), bit_of(member, 2)
    own_piece = core * 4 + x_bit * 2 + y_bit
    block, width = tokens_ref.shape
    heads = queries.shape[0]
    seq_len = ids_ref.shape[1]
    last = shards - 1
    reach = -(-(MOST_TOKENS - 1) // block)
    slots = iter(range(send.shape[0]))
    pending = []

    def copy_to(src, dst, at, **peer):
        return pltpu.make_async_remote_copy(
            src_ref=src, dst_ref=dst, send_sem=send.at[at], recv_sem=recv.at[at], device_id=peer, device_id_type=MESH
        )

    def start_dp(src, dst, bit):
        copy = copy_to(src, dst, next(slots), dp=partner_of(member, bit))
        copy.start()
        pending.append(copy)
        return copy

    fc1_rows, fc2_rows, proj_rows = (ref.shape[0] // PIECES for ref in (fc1_ref, fc2_ref, proj_ref))
    loads = []
    for at, (ref, first, count) in enumerate(
        ((fc2_ref, 0, fc2_rows), (fc1_ref, fc2_rows, fc1_rows))
    ):
        rows = pl.ds(pl.multiple_of(own_piece * count, 16), count)
        loads.append(pltpu.make_async_copy(ref.at[rows], own.at[first : first + count], local.at[at]))
        loads[-1].start()
    used = fc1_rows + fc2_rows
    rows = pl.ds(pl.multiple_of(own_piece * proj_rows, 8), proj_rows)
    own[used : used + proj_rows, :] = proj_ref[rows, :]
    used += proj_rows
    own[used:, :] = jnp.zeros((own.shape[0] - used, width), bf16)
    gain, shift = (ref[...].reshape(1, width) for ref in (gain_ref, shift_ref))
    bias_out[here] = fc1_bias_ref[...].reshape(1, width)
    greet(dp_bits, shards)
    for load in loads:
        load.wait()

    chains = {}
    for name, first, rest in (("w", own, chain), ("t", tokens_ref, blocks)):
        chains[name] = (
            first,
            rest,
            [next(slots) for _ in range(shards)],
            [next(slots) for _ in range(shards)],
        )

    def hop_copy(name, owner, rightward, from_own):
        first, rest, right_slots, left_slots = chains[name]
        src = first if from_own else rest.at[owner]
        step = 1 if rightward else last
        at = (right_slots if rightward else left_slots)[owner]
        return copy_to(src, rest.at[owner], at, tensor=lax.rem(here + step, shards))

    def send_own(name, rightward):
        for owner in range(shards):
            if owner != (last if rightward else 0):

                @pl.when(here == owner)
                def _():
                    hop_copy(name, owner, rightward, True).start()

    def hop(name, time, then=None):
        for at in range(shards):
            for rightward, owner, end in ((True, at - time, last), (False, at + time, 0)):
                if 0 <= owner <= last:

                    @pl.when(here == at)
                    def _():
                        hop_copy(name, owner, rightward, False).wait_recv()
                        if at != end:
                            hop_copy(name, owner, rightward, False).start()
                            if then is not None and owner in (0, last):
                                hop_copy(then, at, rightward, True).start()

    send_own("w", True)
    send_own("w", False)

    @pl.when(here == 0)
    def _():
        hop_copy("t", 0, True, True).start()

    @pl.when(here == last)
    def _():
        hop_copy("t", last, False, True).start()

    bias_copies = []
    for way in range(1, shards):
        copy = copy_to(
            bias_out.at[here], bias_out.at[here], next(slots), tensor=lax.rem(here + way, shards)
        )
        copy.start()
        bias_copies.append(copy)
    pending.extend(bias_copies)

    large = -MASKED
    segments = lax.broadcasted_iota(jnp.int32, (8, seq_len), 0)
    same = jnp.where(segments == ids_ref[...], 1.0, 0.0).astype(bf16)
    select = lax.broadcasted_iota(jnp.int32, (8, LANES), 1) - HEAD_DIM == lax.broadcasted_iota(
        jnp.int32, (8, LANES), 0
    )
    matched = contract_rows(same, jnp.where(select, 1.0, 0.0).astype(bf16))
    lane = lax.broadcasted_iota(jnp.int32, (seq_len, LANES), 1)
    segment_lane = (lane >= HEAD_DIM) & (lane < HEAD_DIM + 8)
    ones_lane = (lane >= HEAD_DIM + 8) & (lane < HEAD_DIM + 11)
    q_extra[...] = jnp.where(segment_lane, (matched - 1.0) * large, 0.0).astype(bf16)
    k_extra[...] = jnp.where(ones_lane, 1.0, matched).astype(bf16)
    low_half = lax.broadcasted_iota(jnp.int32, (block, LANES), 1) < HEAD_DIM
    v_lane = lax.broadcasted_iota(jnp.int32, (block, LANES), 1)
    v_extra = jnp.where((v_lane >= HEAD_DIM) & (v_lane < HEAD_DIM + 3), 1.0, 0.0).astype(bf16)

    def rows_of(owner, count=block):
        return pl.ds(pl.multiple_of(owner * count, 16), count)

    def store(which, owner):
        rows = rows_of(owner)
        source, out = (
            (normed_all.at[rows], normed_out.at[rows]),
            (queries.at[:, rows], q_out.at[:, rows]),
            (keys.at[:, rows], k_out.at[:, rows]),
            (values.at[:, rows], v_out.at[:, rows]),
        )[which]
        return pltpu.make_async_copy(source, out, stored.at[which, owner])

    def project_block(source, owner):
        tokens = source.astype(f32)
        centred = tokens - jnp.mean(tokens, axis=1, keepdims=True)
        inverse = lax.rsqrt(jnp.mean(centred * centred, axis=1, keepdims=True) + eps_norm)
        normed = (centred * inverse * gain + shift).astype(bf16)
        rows = rows_of(owner)
        normed_all[rows, :] = normed
        for which, out in ((0, queries), (1, keys), (2, values)):
            product = times_transposed(normed, qkv_ref[which])
            if which != 1:
                product = product + qv_bias_ref[which // 2 : which // 2 + 1, :]
            if which == 0:
                product = product.astype(bf16).astype(f32) * HEAD_DIM**-0.5
            extra = v_extra if which == 2 else (q_extra if which == 0 else k_extra)[rows, :]
            for head in range(heads):
                first = (head // 2) * LANES
                tile = product[:, first : first + LANES]
                if tile.shape[1] < LANES:
                    blank = jnp.zeros((block, LANES - tile.shape[1]), f32)
                    tile = jnp.concatenate([tile, blank], axis=1)
                if head % 2:
                    tile = pltpu.roll(tile, HEAD_DIM, 1)
                out[head, rows, :] = jnp.where(low_half, tile, extra.astype(f32)).astype(bf16)
        store(0, owner).start()
        store(2, owner).start()
        store(3, owner).start()

    peaks[...] = jnp.full_like(peaks, -3e38)
    sums[...] = jnp.zeros_like(sums)

    def away(index):
        return jnp.maximum(index - here, here - index)

    def visit(owner, other):
        rows, across = rows_of(owner), rows_of(other)
        for head in range(heads):
            scores[head] = times_transposed(queries[head, rows, :], keys[head, across, :])
        for head in range(heads):
            old_peak = peaks[head, rows, :]
            new_peak = jnp.maximum(old_peak, jnp.max(scores[head], axis=1, keepdims=True))
            peaks[head, rows, :] = new_peak
            spread = jnp.concatenate([new_peak] * -(-block // LANES), axis=1)[:, :block]
            weights[head] = jnp.exp(scores[head] - spread).astype(bf16)
            sums[head, rows, :] = sums[head, rows, :] * jnp.exp(old_peak - new_peak)
        for head in range(heads):
            sums[head, rows, :] += jnp.dot(
                weights[head], values[head, across, :], preferred_element_type=f32
            )

    pair_slots = [next(slots) for _ in range(shards)]
    single_slots = [next(slots) for _ in range(shards)]

    def exchange(owner, source):
        half_block = block // 2
        return [
            pltpu.make_async_remote_copy(
                src_ref=out.at[rows_of(owner, count)],
                dst_ref=landing.at[source],
                send_sem=send.at[base + owner],
                recv_sem=recv.at[base + source],
                device_id={"tensor": owner},
                device_id_type=MESH,
            )
            for out, landing, count, base in (
                (pairs_out, pairs_here, block, pair_slots[0]),
                (singles_out, singles_here, half_block, single_slots[0]),
            )
        ]

    def complete(owner):
        rows, half_block = rows_of(owner), block // 2
        parts = []
        for head in range(heads):
            total = sums[head, rows, HEAD_DIM : HEAD_DIM + 1]
            parts.append(sums[head, rows, :] / total)
            high, middle_part, low = split_three(-(peaks[head, rows, :] + jnp.log(total)))
            kept = queries[head, rows, :].astype(f32)
            for at, value in enumerate((high, middle_part, low)):
                kept = jnp.where(v_lane == HEAD_DIM + 8 + at, value.astype(f32), kept)
            queries[head, rows, :] = kept.astype(bf16)
        pair = join_lanes(parts[0], parts[1]).astype(bf16)
        single = join_lanes(parts[2][:half_block], parts[2][half_block:]).astype(bf16)
        pairs_out[rows, :] = pair
        singles_out[rows_of(owner, half_block), :] = single
        store(1, owner).start()

        @pl.when(owner == here)
        def _():
            pairs_here[here] = pair
            singles_here[here] = single

        @pl.when(owner != here)
        def _():
            for copy in exchange(owner, here):
                copy.start()

    def attend_known(time):
        def each(at, carry):
            owner = lax.rem(here + shards // 2 + at, shards)

            def other_block(other, carry):
                near = jnp.maximum(owner - other, other - owner) <= reach
                known = jnp.maximum(jnp.maximum(away(owner), away(other)), 1)

                @pl.when(near & (known == time))
                def _():
                    visit(owner, other)

                return carry

            lax.fori_loop(0, shards, other_block, 0)
            final = jnp.maximum(
                away(jnp.maximum(owner - reach, 0)), away(jnp.minimum(owner + reach, last))
            )

            @pl.when(final == time)
            def _():
                complete(owner)

            return carry

        lax.fori_loop(0, shards, each, 0)

    project_block(tokens_ref[...], here)
    for time in range(1, shards):
        hop("w", time, "t")

    half = shards // 2
    stores = []
    for owner in range(shards):
        at = 2 + owner

        @pl.when(here == owner)
        def _():
            pltpu.make_async_copy(own, weights_out.at[own_piece, owner], local.at[at]).start()

        @pl.when(here != owner)
        def _():
            pltpu.make_async_copy(chain.at[owner], weights_out.at[own_piece, owner], local.at[at]).start()

        stores.append(pltpu.make_async_copy(own, weights_out.at[own_piece, owner], local.at[at]))
    for saved in stores:
        saved.wait()

    def part(low, pieces):
        owners = pl.ds(0, half) if low else pl.ds(half, shards - half)
        return weights_out.at[pieces, owners]

    def gather_stage(low, pieces, bit):
        return [start_dp(part(low, at), part(low, at), bit) for at in pieces]

    def wait_all(copies):
        for copy in copies:
            copy.wait_recv()

    stage = gather_stage(True, [own_piece], 2) + gather_stage(False, [own_piece], 1)

    def arrived(time):
        def each(at, carry):
            owner = here + (2 * at - 1) * time

            @pl.when((owner >= 0) & (owner <= last))
            def _():
                project_block(blocks[owner], owner)

            return carry

        lax.fori_loop(0, 2, each, 0)

    for time in range(1, shards):
        hop("t", time)
        arrived(time)
        if time == 1:
            wait_all(stage)
            stage = gather_stage(True, [pl.ds(core * 4 + x_bit * 2, 2)], 1) + gather_stage(
                False, [core * 4 + 2 * at + y_bit for at in range(2)], 2
            )
        attend_known(time)
        if time == 2:
            wait_all(stage)
            stage = [start_dp(weights_out.at[pl.ds(core * 4, 4)], weights_out.at[pl.ds(core * 4, 4)], 0)]
    for owner in range(shards):

        @pl.when(here != owner)
        def _():
            for copy in exchange(here, owner):
                copy.wait_recv()
            for copy in exchange(owner, here):
                copy.wait_send()

        for which in range(4):
            store(which, owner).wait()
    wait_all(stage)
    wait_all(bias_copies)
    for copy in pending:
        copy.wait_send()
    for name in chains:
        for at in range(shards):
            for owner in range(shards):
                if owner <= at < last:

                    @pl.when(here == at)
                    def _():
                        hop_copy(name, owner, True, False).wait_send()

                if owner >= at > 0:

                    @pl.when(here == at)
                    def _():
                        hop_copy(name, owner, False, False).wait_send()


def start(shards, members, tokens, ids, gain, shift, qkv, qv_bias, fc1, fc2, proj, fc1_bias):
    dp_bits = members.bit_length() - 1
    assert members == 1 << dp_bits and dp_bits >= PIECE_BITS and shards >= 3
    f32, bf16 = jnp.float32, jnp.bfloat16
    block, width = tokens.shape
    seq_len = block * shards
    heads = qkv.shape[1] // HEAD_DIM
    rows = -(-(fc1.shape[0] + fc2.shape[0] + proj.shape[0]) // PIECES // 16) * 16
    copies = 6 * shards + (shards - 1) + 6
    vm = pltpu.VMEM
    on_chip = pl.BlockSpec(memory_space=vm)
    anywhere = pl.BlockSpec(memory_space=pl.ANY)
    head_rows = jax.ShapeDtypeStruct((heads, seq_len, LANES), bf16)
    return pl.pallas_call(
        partial(start_kernel, shards, dp_bits),
        in_specs=[on_chip] * 6 + [anywhere] * 2 + [on_chip] * 2,
        out_specs=[anywhere] * 4
        + [on_chip] * 4
        + [anywhere, on_chip],
        out_shape=[
            jax.ShapeDtypeStruct((seq_len, width), bf16),
            head_rows,
            head_rows,
            head_rows,
            jax.ShapeDtypeStruct((seq_len, LANES), bf16),
            jax.ShapeDtypeStruct((seq_len // 2, LANES), bf16),
            jax.ShapeDtypeStruct((shards, block, LANES), bf16),
            jax.ShapeDtypeStruct((shards, block // 2, LANES), bf16),
            jax.ShapeDtypeStruct((PIECES, shards, rows, width), bf16),
            jax.ShapeDtypeStruct((shards, 1, width), f32),
        ],
        scratch_shapes=[
            vm((shards, block, width), bf16),
            vm((seq_len, width), bf16),
            vm((heads, seq_len, LANES), bf16),
            vm((heads, seq_len, LANES), bf16),
            vm((heads, seq_len, LANES), bf16),
            vm((heads, seq_len, LANES), f32),
            vm((heads, seq_len, LANES), f32),
            vm((heads, block, block), f32),
            vm((heads, block, block), bf16),
            vm((seq_len, LANES), bf16),
            vm((seq_len, LANES), bf16),
            vm((rows, width), bf16),
            vm((shards, rows, width), bf16),
            pltpu.SemaphoreType.DMA((copies,)),
            pltpu.SemaphoreType.DMA((copies,)),
            pltpu.SemaphoreType.DMA((2 + shards,)),
            pltpu.SemaphoreType.DMA((4, shards)),
        ],
        compiler_params=pltpu.CompilerParams(
            collective_id=0, has_side_effects=True, vmem_limit_bytes=62 * 1024 * 1024
        ),
        name="start",
        cost_estimate=pl.CostEstimate(
            flops=6 * seq_len * width * heads * HEAD_DIM, transcendentals=0, bytes_accessed=40 * block * width
        ),
    )(tokens, ids, gain, shift, qkv, qv_bias, fc1, fc2, proj, fc1_bias)


CHUNK = 192


def middle_kernel(
    shards,
    dp_bits,
    pairs,
    singles,
    weights_ref,
    fc1_bias_ref,
    proj_bias_ref,
    scale_one_ref,
    gain_ref,
    shift_ref,
    fc2_bias_ref,
    scale_two_ref,
    tokens_ref,
    cotangent_ref,
    block_result,
    hidden_grad_result,
    pair_grads_out,
    single_grads_out,
    vectors_out,
    *rest,
):
    results, rest = rest[:8], rest[8:]
    parts, rest = rest[:8], rest[8:]
    middle_body(
        shards,
        dp_bits,
        (pairs, singles, weights_ref, fc1_bias_ref),
        (proj_bias_ref, scale_one_ref, gain_ref, shift_ref, fc2_bias_ref, scale_two_ref),
        (tokens_ref, cotangent_ref),
        (block_result, hidden_grad_result, *results),
        (pair_grads_out, single_grads_out, vectors_out),
        parts,
        *rest,
    )


def middle_body(
    shards,
    dp_bits,
    sources,
    parameter_refs,
    row_refs,
    results,
    outs,
    parts,
    block_out,
    hidden_grad_out,
    weights,
    attended,
    proj,
    branch,
    hidden,
    normed,
    wide,
    total,
    active,
    slope,
    grad_pre,
    grad_mlp,
    grad_branch,
    pair_grads,
    single_grads,
    got_early,
    got,
    a_got,
    b_got,
    send,
    recv,
    local,
    stored,
):
    pairs, singles, weights_ref, fc1_bias_ref = sources
    tokens_ref, cotangent_ref = row_refs
    pair_grads_out, single_grads_out, vectors_out = outs
    a_keep, a_away, b_keep, b_away, a_early, a_early_away, b_early, b_early_away = parts

    def store(at):
        return pltpu.make_async_copy((block_out, hidden_grad_out, *parts)[at], results[at], stored.at[at])

    f32, bf16 = jnp.float32, jnp.bfloat16
    member, here = lax.axis_index("dp"), lax.axis_index("tensor")
    core, x_bit, y_bit = bit_of(member, 0), bit_of(member, 1), bit_of(member, 2)
    block, width = tokens_ref.shape
    columns = width // shards
    half = PIECES // 2
    fc_rows, proj_rows = width // PIECES, columns // PIECES
    proj_first = 2 * fc_rows
    slots = iter(range(send.shape[0]))
    proj_bias, scale_one, gain, shift, fc2_bias, scale_two = (
        ref[...].reshape(1, width)
        for ref in parameter_refs
    )

    def copy_to(src, dst, at, **peer):
        return pltpu.make_async_remote_copy(
            src_ref=src, dst_ref=dst, send_sem=send.at[at], recv_sem=recv.at[at], device_id=peer, device_id_type=MESH
        )

    loads = []
    for at, (first, end) in enumerate(
        ((proj_first, weights.shape[2]), (fc_rows, proj_first), (0, fc_rows))
    ):
        rows = pl.ds(first, end - first)
        loads.append(pltpu.make_async_copy(weights_ref.at[:, :, rows], weights.at[:, :, rows], local.at[at]))
        loads[-1].start()
    greet(dp_bits, shards)

    loads[0].wait()

    def fc1_of(owner):
        return weights[:, owner, fc_rows:proj_first, :].reshape(width, width)

    def fc2_of(owner):
        return weights[:, owner, :fc_rows, :].reshape(width, width)

    def proj_of(owner):
        return weights[:, owner, proj_first : proj_first + proj_rows, :].reshape(columns, width)

    def chunk(at):
        return pl.ds(pl.multiple_of(at * CHUNK, 16), CHUNK)

    def each_chunk(body, init):
        return lax.fori_loop(0, block // CHUNK, body, init)

    def column_sum(value):
        return jnp.sum(value, axis=0, keepdims=True)

    def unit_of(value):
        centred = value - jnp.mean(value, axis=1, keepdims=True)
        inverse = lax.rsqrt(jnp.mean(centred * centred, axis=1, keepdims=True) + eps_norm)
        return centred * inverse, inverse

    third = shards * LANES
    for owner in range(shards):
        own_proj = proj_of(owner)
        proj[owner * LANES : (owner + 1) * LANES, :] = own_proj[:LANES]
        proj[third + owner * HEAD_DIM : third + (owner + 1) * HEAD_DIM, :] = own_proj[LANES:]
    middle_row = block // 2
    for owner in range(shards):
        attended[:, owner * LANES : (owner + 1) * LANES] = pairs[owner]
    lane = lax.broadcasted_iota(jnp.int32, (middle_row, LANES), 1)
    low_half = lane < HEAD_DIM

    def swapped(value):
        return pltpu.roll(value, HEAD_DIM, 1)

    for at in range(shards // 2):
        one, two = singles[2 * at].astype(f32), singles[2 * at + 1].astype(f32)
        columns_here = slice(third + at * LANES, third + (at + 1) * LANES)
        attended[:middle_row, columns_here] = jnp.where(low_half, one, swapped(two)).astype(bf16)
        attended[middle_row:, columns_here] = jnp.where(low_half, swapped(one), two).astype(bf16)
    product = jnp.dot(attended[...], proj[...], preferred_element_type=f32)
    branch[...] = product

    def enter(at, carry):
        rows = chunk(at)
        value = branch[rows, :] + proj_bias
        branch[rows, :] = value
        value = tokens_ref[rows, :].astype(f32) + scale_one * value
        hidden[rows, :] = value
        unit, _ = unit_of(value)
        normed[rows, :] = (unit * gain + shift).astype(bf16)
        return carry

    each_chunk(enter, 0)

    def forward(owner, carry):
        wide[:block, :] = jnp.dot(normed[...], fc1_of(owner), preferred_element_type=f32)
        bias = fc1_bias_ref[owner]

        def activate(at, carry):
            rows = chunk(at)
            value = wide[rows, :] + bias
            below = 0.5 * (1.0 + lax.erf(value * 0.5**0.5))
            active[owner, rows, :] = (value * below).astype(bf16)
            density = jnp.exp(value * value * -0.5) * (0.5 / math.pi) ** 0.5
            slope[owner, rows, :] = below + value * density
            return carry

        each_chunk(activate, 0)
        product = jnp.dot(active[owner], fc2_of(owner), preferred_element_type=f32)
        total[...] = jnp.where(owner == 0, product, total[...] + product)
        return carry

    for load in loads[1:]:
        load.wait()
    lax.fori_loop(0, shards, forward, 0)
    empty = jnp.zeros((1, width), f32)

    def turn(at, sums):
        rows = chunk(at)
        value = total[rows, :] + fc2_bias
        block_out[rows, :] = (hidden[rows, :] + scale_two * value).astype(bf16)
        grad = cotangent_ref[rows, :].astype(f32)
        grad_mlp[rows, :] = (grad * scale_two).astype(bf16)
        return (
            sums[0] + column_sum(grad * value),
            sums[1] + column_sum(grad_mlp[rows, :].astype(f32)),
        )

    scale_two_sum, fc2_bias_sum = each_chunk(turn, (empty, empty))
    store(0).start()

    split = shards // 2

    def slot_row():
        return [next(slots) for _ in range(shards)]

    early_slots, late_slots = slot_row(), slot_row()

    def core_copy(owner, early):
        rows = pl.ds(0, fc_rows) if early else pl.ds(fc_rows, weights.shape[2] - fc_rows)
        base = (early_slots if early else late_slots)[0]
        return pltpu.make_async_remote_copy(
            src_ref=weights.at[pl.ds((1 - core) * half, half), owner, rows],
            dst_ref=(got_early if early else got).at[:, owner],
            send_sem=send.at[base + owner],
            recv_sem=recv.at[base + owner],
            device_id={"dp": partner_of(member, 0)},
            device_id_type=MESH,
        )

    piece_rows = pl.ds(0, fc_rows)
    own = core * half
    side_slots = [next(slots) for _ in range(3)]

    def side_copies():
        first_half, second_half = pl.ds(0, split), pl.ds(split, shards - split)
        moves = [(weights.at[pl.ds(own + (1 - x_bit) * 2, 2), first_half, piece_rows], a_got, 1)]
        moves += [
            (weights.at[own + 2 * x + 1 - y_bit, second_half, piece_rows], b_got.at[x], 2) for x in range(2)
        ]
        return [
            copy_to(source, landing, side_slots[at], dp=partner_of(member, bit))
            for at, (source, landing, bit) in enumerate(moves)
        ]

    def grow_piece(piece, owner, other):
        weights[piece, owner, piece_rows, :] = rounded_sum(weights[piece, owner, piece_rows, :], other)

    def early_pairs():
        for owner in range(shards):
            core_copy(owner, True).wait_recv()

        def step(at, carry):
            piece, owner = at // shards, lax.rem(at, shards)
            grow_piece(own + piece, owner, got_early[piece, owner])
            return carry

        lax.fori_loop(0, half * shards, step, 0)
        for copy in side_copies():
            copy.start()

    def early_sides():
        for copy in side_copies():
            copy.wait_recv()
        for owner in range(split):
            for keep, away, side, got_side, y_side in (
                (a_early, a_early_away, x_bit, a_got, True),
                (b_early, b_early_away, y_bit, b_got, False),
            ):
                for out, at in ((keep, y_bit if y_side else x_bit), (away, 1 - (y_bit if y_side else x_bit))):
                    piece = own + (2 * side + at if y_side else 2 * at + side)
                    shard = owner if y_side else split + owner
                    out[owner] = rounded_sum(weights[piece, shard, piece_rows, :], got_side[at, owner])

    def backward(owner, carry):
        wide[:block, :] = times_transposed(grad_mlp[...], fc2_of(owner))

        def slopes(at, sums):
            rows = chunk(at)
            value = (wide[rows, :] * slope[owner, rows, :]).astype(bf16)
            grad_pre[owner, rows, :] = value
            return sums + column_sum(value.astype(f32))

        vectors_out[pl.ds(8 + owner, 1), :] = each_chunk(slopes, empty)
        product = times_transposed(grad_pre[owner], fc1_of(owner))
        total[...] = jnp.where(owner == 0, product, total[...] + product)
        return carry

    lax.fori_loop(0, shards, backward, 0)

    def leave(at, sums):
        rows = chunk(at)
        grad = total[rows, :]
        unit, inverse = unit_of(hidden[rows, :])
        scaled = grad * gain
        inner = (
            scaled
            - jnp.mean(scaled, axis=1, keepdims=True)
            - unit * jnp.mean(scaled * unit, axis=1, keepdims=True)
        )
        value = cotangent_ref[rows, :].astype(f32) + inverse * inner
        hidden_grad_out[rows, :] = value
        rounded = (value * scale_one).astype(bf16)
        grad_branch[rows, :] = rounded
        return (
            sums[0] + column_sum(grad * unit),
            sums[1] + column_sum(grad),
            sums[2] + column_sum(value * branch[rows, :]),
            sums[3] + column_sum(rounded.astype(f32)),
        )

    gain_sum, shift_sum, scale_one_sum, proj_bias_sum = each_chunk(leave, (empty,) * 4)
    store(1).start()
    for at, value in enumerate(
        (empty, empty, proj_bias_sum, scale_one_sum, gain_sum, shift_sum, fc2_bias_sum, scale_two_sum)
    ):
        vectors_out[at : at + 1, :] = value
    vectors_out[12:, :] = jnp.zeros((vectors_out.shape[0] - 12, width), f32)

    wide[:block, :] = times_transposed(grad_branch[...], proj[...])
    for owner in range(shards):
        pair_grads[owner] = wide[:block, owner * LANES : (owner + 1) * LANES].astype(bf16)
    for at in range(shards // 2):
        columns_here = slice(third + at * LANES, third + (at + 1) * LANES)
        upper, lower = wide[:middle_row, columns_here], wide[middle_row:block, columns_here]
        single_grads[2 * at] = jnp.where(low_half, upper, swapped(lower)).astype(bf16)
        single_grads[2 * at + 1] = jnp.where(low_half, swapped(upper), lower).astype(bf16)
    back = []
    for source, out in ((pair_grads, pair_grads_out), (single_grads, single_grads_out)):
        for way in range(1, shards):
            target = lax.rem(here + way, shards)
            copy = copy_to(source.at[target], out.at[here], next(slots), tensor=target)
            copy.start()
            back.append(copy)
        out[here] = source[here]

    def early_grads(owner, carry):
        product = contract_rows(active[owner], grad_mlp[...]).astype(bf16)
        weights[:, owner, :fc_rows, :] = product.reshape(PIECES, fc_rows, width)
        core_copy(owner, True).start()
        return carry

    lax.fori_loop(0, shards, early_grads, 0)
    wide[...] = contract_rows(attended[:, :], grad_branch[...])
    for owner in range(shards):
        for piece in range(PIECES):
            first, end = piece * proj_rows, (piece + 1) * proj_rows
            for low, high, start_row in ((0, LANES, owner * LANES), (LANES, columns, third + owner * HEAD_DIM)):
                begin, stop = max(first, low), min(end, high)
                if begin < stop:
                    rows = slice(start_row + begin - low, start_row + stop - low)
                    to = slice(proj_first + begin - first, proj_first + stop - first)
                    weights[piece, owner, to, :] = wide[rows, :].astype(bf16)

    early_pairs()

    def weight_grads(owner, carry):
        product = contract_rows(normed[...], grad_pre[owner]).astype(bf16)
        weights[:, owner, fc_rows:proj_first, :] = product.reshape(PIECES, fc_rows, width)
        core_copy(owner, False).start()
        return carry

    lax.fori_loop(0, shards, weight_grads, 0)
    for owner in range(shards):
        core_copy(owner, False).wait_recv()
        for x in range(2):
            for y in range(2):
                piece = x * 2 + y
                if owner < split:
                    moves = [(out, y, owner, at == x) for out, at in ((a_keep, x_bit), (a_away, 1 - x_bit))]
                else:
                    moves = [(out, x, owner - split, at == y) for out, at in ((b_keep, y_bit), (b_away, 1 - y_bit))]
                for out, first, second, wanted in moves:

                    @pl.when(wanted)
                    def _():
                        out[first, second] = rounded_sum(
                            weights[own + piece, owner, fc_rows:, :], got[piece, owner]
                        )

    for at in range(2, 6):
        store(at).start()
    early_sides()
    for at in range(6, 10):
        store(at).start()
    for copy in back:
        copy.wait_recv()
    for at in range(10):
        store(at).wait()
    for copy in back + side_copies():
        copy.wait_send()
    for owner in range(shards):
        core_copy(owner, True).wait_send()
        core_copy(owner, False).wait_send()


def middle(shards, members, pairs, singles, weights, fc1_bias, vectors, tokens, cotangent):
    dp_bits = members.bit_length() - 1
    f32, bf16 = jnp.float32, jnp.bfloat16
    block, width = tokens.shape
    rows = weights.shape[2]
    vm = pltpu.VMEM
    on_chip = pl.BlockSpec(memory_space=vm)
    fc_rows = width // PIECES
    quarter = jax.ShapeDtypeStruct((2, shards // 2, rows - fc_rows, width), bf16)
    early_half = jax.ShapeDtypeStruct((shards // 2, fc_rows, width), bf16)
    copies = 2 * (shards - 1) + 2 * shards + 3
    return pl.pallas_call(
        partial(middle_kernel, shards, dp_bits),
        in_specs=[on_chip, on_chip, pl.BlockSpec(memory_space=pl.ANY)] + [on_chip] * 9,
        out_specs=[pl.BlockSpec(memory_space=pl.ANY)] * 2
        + [on_chip] * 3
        + [pl.BlockSpec(memory_space=pl.ANY)] * 8,
        out_shape=[
            jax.ShapeDtypeStruct((block, width), bf16),
            jax.ShapeDtypeStruct((block, width), f32),
            jax.ShapeDtypeStruct((shards, block, LANES), bf16),
            jax.ShapeDtypeStruct((shards, block // 2, LANES), bf16),
            jax.ShapeDtypeStruct((16, width), f32),
            quarter,
            quarter,
            quarter,
            quarter,
            early_half,
            early_half,
            early_half,
            early_half,
        ],
        scratch_shapes=[vm(quarter.shape, bf16)] * 4
        + [vm(early_half.shape, bf16)] * 4
        + [
            vm((block, width), bf16),
            vm((block, width), f32),
            vm(weights.shape, bf16),
            vm((block, width), bf16),
            vm((width, width), bf16),
            vm((block, width), f32),
            vm((block, width), f32),
            vm((block, width), bf16),
            vm((width, width), f32),
            vm((block, width), f32),
            vm((shards, block, width), bf16),
            vm((shards, block, width), f32),
            vm((shards, block, width), bf16),
            vm((block, width), bf16),
            vm((block, width), bf16),
            vm((shards, block, LANES), bf16),
            vm((shards, block // 2, LANES), bf16),
            vm((PIECES // 2, shards, fc_rows, width), bf16),
            vm((PIECES // 2, shards, rows - fc_rows, width), bf16),
            vm((2, shards // 2, fc_rows, width), bf16),
            vm((2, shards // 2, fc_rows, width), bf16),
            pltpu.SemaphoreType.DMA((copies,)),
            pltpu.SemaphoreType.DMA((copies,)),
            pltpu.SemaphoreType.DMA((shards,)),
            pltpu.SemaphoreType.DMA((10,)),
        ],
        compiler_params=pltpu.CompilerParams(
            collective_id=2, has_side_effects=True, vmem_limit_bytes=62 * 1024 * 1024
        ),
        name="middle",
        cost_estimate=pl.CostEstimate(
            flops=12 * block * width * width * shards, transcendentals=0, bytes_accessed=40 * block * width
        ),
    )(pairs, singles, weights, fc1_bias, *vectors, tokens, cotangent)


eps_norm = 1e-06


def on_device(
    shards,
    members,
    tokens,
    segment_ids,
    ln1_gain,
    ln1_bias,
    qkv_weight,
    qv_bias,
    proj_weight,
    proj_bias,
    scale_one,
    ln2_gain,
    ln2_bias,
    fc1_weight,
    fc1_bias,
    fc2_weight,
    fc2_bias,
    scale_two,
    cotangent,
):
    f32, bf16 = jnp.float32, jnp.bfloat16
    seq_len = segment_ids.shape[1]
    rows_here, width = tokens.shape
    head_columns = qkv_weight.shape[2]
    heads = head_columns // HEAD_DIM
    hidden_here = fc1_weight.shape[1]
    ids = segment_ids[0]
    here = lax.axis_index("tensor")

    turned = qkv_weight.transpose(0, 2, 1)
    full_one, queries, keys, values, pairs, singles, pairs_here, singles_here, gathered, fc1_bias_full = start(
        shards,
        members,
        tokens,
        segment_ids,
        ln1_gain,
        ln1_bias,
        turned,
        qv_bias,
        fc1_weight,
        fc2_weight,
        proj_weight,
        fc1_bias,
    )
    params = (proj_bias, scale_one, ln2_gain, ln2_bias, fc2_bias, scale_two)
    block_out, grad_hidden, pair_grads, single_grads, vectors, *exchanged = middle(
        shards, members, pairs_here, singles_here, gathered, fc1_bias_full, params, tokens, cotangent
    )
    pair_grads = pair_grads.reshape(seq_len, LANES)
    single_grads = single_grads.reshape(seq_len // 2, LANES)

    grad_tokens, totals, qkv_pieces, weight_pieces = back(
        shards,
        members,
        (queries, keys, values),
        (pairs, singles, pair_grads, single_grads),
        turned.reshape(3 * head_columns, width),
        ln1_gain,
        ln1_bias,
        vectors,
        full_one,
        tokens,
        grad_hidden,
        exchanged,
    )
    fc1_grad, fc2_grad, proj_grad, qkv_grad, grad_tokens, block_out, qv_grad, fc1_bias_grad, *sums = unpack(
        qkv_pieces, weight_pieces, totals, grad_tokens, block_out, width // PIECES, head_columns // PIECES
    )
    qkv_grad = qkv_grad.reshape(3, head_columns, width).transpose(0, 2, 1)
    return (
        block_out,
        grad_tokens,
        sums[0],
        sums[1],
        qkv_grad,
        qv_grad,
        proj_grad,
        sums[2],
        sums[3],
        sums[4],
        sums[5],
        fc1_grad,
        fc1_bias_grad,
        fc2_grad,
        sums[6],
        sums[7],
    )


def solution(mesh):
    rows = P(("dp", "tensor"), None)
    columns = P(None, "tensor")
    return jax.shard_map(
        partial(on_device, mesh.shape["tensor"], mesh.shape["dp"]),
        mesh=mesh,
        in_specs=(
            rows,
            P("dp", None),
            P(),
            P(),
            P(None, None, "tensor"),
            columns,
            P("tensor", None),
            P(),
            P(),
            P(),
            P(),
            columns,
            P("tensor"),
            P("tensor", None),
            P(),
            P(),
            rows,
        ),
        out_specs=(
            rows,
            rows,
            P(),
            P(),
            P(None, None, "tensor"),
            columns,
            P("tensor", None),
            P(),
            P(),
            P(),
            P(),
            columns,
            P("tensor"),
            P("tensor", None),
            P(),
            P(),
        ),
        check_vma=False,
    )
```
